32 devices in a mesh: fsdp: 4 (over z), ctx: 2 (over y), tp: 4 (over x, core).
Axes of the slice: x: 2, y: 2, z: 4, core: 2. Of those that a mesh axis runs over, the one named last changes fastest.
Arguments:
- inputs: bfloat16 [12288, 768], P(('fsdp', 'ctx')), may hold values from -6 to 6
- segments: int32 [4, 3072], P('fsdp', 'ctx'), may hold values from 0 to 11, never falling along the last dimension, each value on 1 to 512 neighbouring positions
- w_query: bfloat16 [768, 768], P('fsdp', 'tp'), may hold values from -0.21875 to 0.21875
- b_query: bfloat16 [768], P('tp'), may hold values from -4 to 4
- w_key: bfloat16 [768, 768], P('fsdp', 'tp'), may hold values from -0.21875 to 0.21875
- w_value: bfloat16 [768, 768], P('fsdp', 'tp'), may hold values from -0.21875 to 0.21875
- b_value: bfloat16 [768], P('tp'), may hold values from -4 to 4
- w_out: bfloat16 [768, 768], P('tp', 'fsdp'), may hold values from -3 to 3
- b_out: bfloat16 [768], replicated, may hold values from -4 to 4
- gain_one: bfloat16 [768], replicated, may hold values from 0.099609375 to 1.8984375
- shift_one: bfloat16 [768], replicated, may hold values from -4 to 4
- w_inner: bfloat16 [768, 3072], P('fsdp', 'tp'), may hold values from -0.21875 to 0.21875
- b_inner: bfloat16 [3072], P('tp'), may hold values from -4 to 4
- w_outer: bfloat16 [3072, 768], P('tp', 'fsdp'), may hold values from -0.109375 to 0.109375
- b_outer: bfloat16 [768], replicated, may hold values from -4 to 4
- gain_two: bfloat16 [768], replicated, may hold values from 0.099609375 to 1.8984375
- shift_two: bfloat16 [768], replicated, may hold values from -4 to 4
- grad_output: bfloat16 [12288, 768], P(('fsdp', 'ctx')), may hold values from -6 to 6
Outputs:
- output: bfloat16 [12288, 768], P(('fsdp', 'ctx'))
- grad_inputs: float32 [12288, 768], P(('fsdp', 'ctx'))
- grad_w_query: float32 [768, 768], P('fsdp', 'tp')
- grad_b_query: float32 [768], P('tp')
- grad_w_key: float32 [768, 768], P('fsdp', 'tp')
- grad_w_value: float32 [768, 768], P('fsdp', 'tp')
- grad_b_value: float32 [768], P('tp')
- grad_w_out: float32 [768, 768], P('tp', 'fsdp')
- grad_b_out: float32 [768], replicated
- grad_gain_one: float32 [768], replicated
- grad_shift_one: float32 [768], replicated
- grad_w_inner: float32 [768, 3072], P('fsdp', 'tp')
- grad_b_inner: float32 [3072], P('tp')
- grad_w_outer: float32 [3072, 768], P('tp', 'fsdp')
- grad_b_outer: float32 [768], replicated
- grad_gain_two: float32 [768], replicated
- grad_shift_two: float32 [768], replicated
The draws below stay inside these ranges and needn't reach their ends.
Inputs may be any that keep to these rules, and one draw needn't show every extreme that they name: `segments`: along each sequence the ids never fall and every id of 0 to 11 occurs; a document has 1 to 512 tokens, and one has exactly 512.
All inputs are finite; a program needn't handle non-finite values.
Results may differ from the reference program's by a relative error of at most 0.023.
Values may be sent and summed in bfloat16 or wider, within the bound.
No kernel may reach another device: no remote copies, remote signals or barrier semaphores. Data moves between devices by JAX's collectives and lax.ppermute only.
A program may use at most 128 MiB of HBM per device.

```python
import math
import jax
import jax.numpy as jnp
import numpy as np
from jax import lax

HEADS = 12
HEAD_DIM = 64
FF = 3072
MOST = 512
D = 768
SEQ_LEN = 3072
SEQS = 4
TOKENS = 12288
DOCS = 12


def steps_of(own_key, extent, pieces, low, top_value):
    loudness = 1.0
    for dim, blocks in pieces:
        heights = jax.random.uniform(jax.random.fold_in(jax.random.fold_in(own_key, 6), dim), (blocks,), jnp.float32, low / len(pieces), top_value / len(pieces))
        loudness = loudness * jnp.repeat(jnp.exp(heights), extent[dim] // blocks).reshape((-1,) + (1,) * (len(extent) - 1 - dim))
    return loudness


def profile(number_of, total, limit, skew):
    loads = [(1 << 20) // math.isqrt(rank ** skew) + 1 for rank in range(2, number_of + 1)]
    spare, given = total - limit - (number_of - 1), [1] * (number_of - 1)
    while spare > 0:
        candidates = [i for i in range(number_of - 1) if given[i] < limit]
        whole, remaining = sum([loads[i] for i in candidates]), spare
        for i in candidates:
            extra = min(limit - given[i], max(1, remaining * loads[i] // whole), spare)
            given[i] = given[i] + extra
            spare = spare - extra
    return np.array([limit] + given)


def uneven(key, number_of, total, bound, skew):
    if number_of == 2:
        one = jax.random.randint(key, (), max(1, total - bound), min(bound, total - 1) + 1)
        return jnp.stack([one, total - one])
    sizes = jnp.asarray(profile(number_of, total, bound, skew), jnp.int32)
    couples = (number_of - 1) // 2
    giver, sink = sizes[1:1 + 2 * couples:2], sizes[2:2 + 2 * couples:2]
    slack = jnp.minimum(giver - 1, bound - sink)
    moved = jax.random.randint(jax.random.fold_in(key, 1), (couples,), 0, 1 << 20) % (slack + 1)
    sizes = sizes.at[1:1 + 2 * couples:2].set(giver - moved).at[2:2 + 2 * couples:2].set(sink + moved)
    return sizes[jax.random.permutation(jax.random.fold_in(key, 2), number_of)]


def gaussian(key, extent, deviation, most, cuts=(), kind=jnp.bfloat16):
    values = deviation * jax.random.normal(key, extent, jnp.float32)
    if cuts:
        values = values * steps_of(key, extent, cuts, -0.22, 0.18)
    return jnp.clip(values, -most, most).astype(kind)


def setup_inputs(seed: int = 0) -> dict:
    key_of = jax.random.split(jax.random.key(seed), 19)
    inputs = gaussian(key_of[0], (TOKENS, D), 1.0, 6.0, ((0, 8),))
    segments = jax.vmap(lambda own: jnp.searchsorted(jnp.cumsum(uneven(own, DOCS, SEQ_LEN, MOST, 2)), jnp.arange(SEQ_LEN), side="right"))(jax.random.split(key_of[1], SEQS)).reshape((SEQS, SEQ_LEN)).astype(jnp.int32)
    w_query = gaussian(key_of[2], (D, D), D ** -0.5, 0.21875, ((0, 4), (1, 4)))
    b_query = gaussian(key_of[3], (D,), 0.3, 4.0, ((0, 4),))
    w_key = gaussian(key_of[4], (D, D), D ** -0.5, 0.21875, ((0, 4), (1, 4)))
    w_value = gaussian(key_of[5], (D, D), D ** -0.5, 0.21875, ((0, 4), (1, 4)))
    b_value = gaussian(key_of[6], (D,), 0.3, 4.0, ((0, 4),))
    w_out = gaussian(key_of[7], (D, D), 4 ** -0.5, 3.0, ((0, 4), (1, 4)))
    b_out = gaussian(key_of[8], (D,), 0.3, 4.0)
    gain_one = jnp.clip(1.0 + 0.18 * jax.random.normal(key_of[9], (D,), jnp.float32), 0.099609375, 1.8984375).astype(jnp.bfloat16)
    shift_one = gaussian(key_of[10], (D,), 0.3, 4.0)
    w_inner = gaussian(key_of[11], (D, FF), D ** -0.5, 0.21875, ((0, 4), (1, 4)))
    b_inner = gaussian(key_of[12], (FF,), 0.3, 4.0, ((0, 4),))
    w_outer = gaussian(key_of[13], (FF, D), FF ** -0.5, 0.109375, ((0, 4), (1, 4)))
    b_outer = gaussian(key_of[14], (D,), 0.3, 4.0)
    gain_two = jnp.clip(1.0 + 0.18 * jax.random.normal(key_of[15], (D,), jnp.float32), 0.099609375, 1.8984375).astype(jnp.bfloat16)
    shift_two = gaussian(key_of[16], (D,), 0.3, 4.0)
    grad_output = gaussian(key_of[17], (TOKENS, D), 1.0, 6.0, ((0, 8),))
    return dict(inputs=inputs, segments=segments, w_query=w_query, b_query=b_query, w_key=w_key, w_value=w_value, b_value=b_value, w_out=w_out, b_out=b_out, gain_one=gain_one, shift_one=shift_one, w_inner=w_inner, b_inner=b_inner, w_outer=w_outer, b_outer=b_outer, gain_two=gain_two, shift_two=shift_two, grad_output=grad_output)


@jax.custom_vjp
def low(v):
    return lax.optimization_barrier(v.astype(jnp.bfloat16)).astype(jnp.float32)

@jax.custom_vjp
def low_back(v):
    return v

def low_keep(v):
    return (low(v), None)

def low_pass(kept, grad):
    return (grad,)

def back_keep(v):
    return (v, None)

def back_low(kept, grad):
    return (low(grad),)
low.defvjp(low_keep, low_pass)
low_back.defvjp(back_keep, back_low)
layer_eps = 1e-12
masked_score = -1e+30

def matmul(left, right):
    return jnp.dot(left, right, precision=lax.Precision.HIGHEST, preferred_element_type=jnp.float32)

def layer_norm(hidden, gain, shift):
    average = lax.optimization_barrier(jnp.mean(hidden, axis=-1, keepdims=True))
    centred = hidden - average
    variance = lax.optimization_barrier(jnp.mean(centred * centred, axis=-1, keepdims=True))
    return centred * lax.rsqrt(variance + layer_eps) * gain + shift

def gelu_exact(values):
    return 0.5 * values * (1.0 + jax.scipy.special.erf(values * 0.7071067811865476))

def attend_block(query_block, seg_block, keys, values, seg_keys):
    scores = jnp.einsum('qhd,khd->hqk', query_block, keys, precision=lax.Precision.HIGHEST) / math.sqrt(HEAD_DIM)
    scores = low_back(scores)
    same = seg_block[None, :, None] == seg_keys[None, None, :]
    scores = jnp.where(same, scores, masked_score)
    shifted = scores - lax.optimization_barrier(jnp.max(scores, axis=-1, keepdims=True))
    expo = jnp.exp(shifted)
    weights = low(expo / lax.optimization_barrier(jnp.sum(expo, axis=-1, keepdims=True)))
    return jnp.einsum('hqk,khd->qhd', weights, values, precision=lax.Precision.HIGHEST)

def forward(inputs, segment, params):
    w_query, b_query, w_key, w_value, b_value, w_out, b_out, gain_one, shift_one, w_inner, b_inner, w_outer, b_outer, gain_two, shift_two = params
    queries = low_back(low(matmul(inputs, w_query) + b_query))
    keys = low_back(low(matmul(inputs, w_key)))
    values = low_back(low(matmul(inputs, w_value) + b_value))
    width = math.gcd(SEQ_LEN, 512)
    blocks = SEQ_LEN // width
    query_heads = queries.reshape(blocks, width, HEADS, HEAD_DIM)
    seg_blocks = segment.reshape(blocks, width)
    key_heads = keys.reshape(SEQ_LEN, HEADS, HEAD_DIM)
    value_heads = values.reshape(SEQ_LEN, HEADS, HEAD_DIM)
    checked = jax.checkpoint(attend_block)

    def visit(carry, item):
        return (carry, checked(item[0], item[1], key_heads, value_heads, segment))
    _, attended = lax.scan(visit, None, (query_heads, seg_blocks))
    attended = low_back(low(attended.reshape(SEQ_LEN, D)))
    branch = low_back(matmul(attended, w_out) + b_out)
    normed_one = layer_norm(inputs + branch, gain_one, shift_one)
    inner = low_back(matmul(low(normed_one), w_inner) + b_inner)
    activ = low(gelu_exact(inner))
    outer = low_back(matmul(activ, w_outer) + b_outer)
    return layer_norm(normed_one + outer, gain_two, shift_two)

def reference(inputs, segments, w_query, b_query, w_key, w_value, b_value, w_out, b_out, gain_one, shift_one, w_inner, b_inner, w_outer, b_outer, gain_two, shift_two, grad_output):
    params = tuple((weight.astype(jnp.float32) for weight in (w_query, b_query, w_key, w_value, b_value, w_out, b_out, gain_one, shift_one, w_inner, b_inner, w_outer, b_outer, gain_two, shift_two)))
    seq_inputs = inputs.astype(jnp.float32).reshape(SEQS, SEQ_LEN, D)
    seq_grads = grad_output.astype(jnp.float32).reshape(SEQS, SEQ_LEN, D)
    zeros = tuple((jnp.zeros_like(weight) for weight in params))

    def per_sequence(carry, item):
        seq_input, seq_segment, seq_grad = item
        result, pullback = jax.vjp(lambda activ_in, weights: forward(activ_in, seq_segment, weights), seq_input, params)
        grad_in, grad_params = pullback(seq_grad)
        carry = tuple((total + part for total, part in zip(carry, grad_params)))
        return (carry, (result, grad_in))
    totals, (results, grads) = lax.scan(per_sequence, zeros, (seq_inputs, segments, seq_grads))
    return (results.reshape(TOKENS, D).astype(jnp.bfloat16), grads.reshape(TOKENS, D), totals[0], totals[1], totals[2], totals[3], totals[4], totals[5], totals[6], totals[7], totals[8], totals[9], totals[10], totals[11], totals[12], totals[13], totals[14])
```

```python
import math

import jax
import jax.numpy as jnp
from jax import lax
from jax.experimental import pallas as pl
from jax.experimental.pallas import tpu as pltpu
from jax.sharding import PartitionSpec as P

HEAD_DIM = 64
MOST = 512
IDS = 64
NO_ID = 63
LSE_LANE = 60
FAR = -1e30

layer_eps = 1e-12
low = jnp.bfloat16
high = jnp.float32


def nn(left, right):
    return jnp.dot(left, right, preferred_element_type=high)


def nt(left, right):
    return lax.dot_general(left, right, (((1,), (1,)), ((), ())), preferred_element_type=high)


def tn(left, right):
    return lax.dot_general(left, right, (((0,), (0,)), ((), ())), preferred_element_type=high)


def swap(value, axis, bit):
    count = lax.axis_size(axis)
    return lax.ppermute(value, axis, [(i, i ^ bit) for i in range(count)])


def shift(value, axis, step):
    count = lax.axis_size(axis)
    return lax.ppermute(value, axis, [(i, (i + step) % count) for i in range(count)])


def place(whole, part, first):
    return lax.dynamic_update_slice_in_dim(whole, part, first, 0)


def take(whole, first, count):
    return lax.dynamic_slice_in_dim(whole, first, count, 0)


def norm_parts(hidden):
    average = jnp.mean(hidden, axis=-1, keepdims=True)
    centred = hidden - average
    variance = jnp.mean(centred * centred, axis=-1, keepdims=True)
    inverse = lax.rsqrt(variance + layer_eps)
    return centred * inverse, inverse


def norm_back(grad, hat, inverse, gain):
    scaled = grad * gain
    first = jnp.mean(scaled, axis=-1, keepdims=True)
    second = jnp.mean(scaled * hat, axis=-1, keepdims=True)
    return inverse * (scaled - first - hat * second)


def gelu_parts(inner):
    half = 0.5 * (1.0 + lax.erf(inner * 0.7071067811865476))
    slope = half + inner * (jnp.exp(-0.5 * inner * inner) * 0.3989422804014327)
    return inner * half, slope


def three(value):
    first = value.astype(low)
    rest = value - first.astype(high)
    second = rest.astype(low)
    third = (rest - second.astype(high)).astype(low)
    return first, second, third


def meets(seg_q, first_q, size_q, seg_k, first_k, size_k):
    return (seg_q[first_q + size_q - 1] >= seg_k[first_k]) & (
        seg_q[first_q] <= seg_k[first_k + size_k - 1]
    )


def attend_kernel(
    here, seg_q, seg_k, q_ref, k_ref, v_ref, mq_ref, mk_ref, out_ref, full_ref, qa_ref, ka_ref,
    vt_ref, acc_ref, top_ref, *, block, width, heads
):
    parts = out_ref.shape[0]
    keys = k_ref.shape[0]
    scale = 1.0 / math.sqrt(HEAD_DIM)
    mine = here[0]
    for h in range(heads):
        cols = slice(h * HEAD_DIM, (h + 1) * HEAD_DIM)
        ka_ref[h] = jnp.concatenate([k_ref[:, cols], mk_ref[...]], axis=1)
        qa_ref[h] = jnp.concatenate([q_ref[:, cols] * jnp.array(scale, low), mq_ref[...]], axis=1)
        vt_ref[h, :HEAD_DIM, :] = v_ref[:, cols].T
        vt_ref[h, HEAD_DIM:, :] = jnp.ones((vt_ref.shape[1] - HEAD_DIM, keys), low)

    def one_part(r, carry):
        first_q = (mine ^ r) * block
        acc_ref[...] = jnp.zeros_like(acc_ref)
        top_ref[...] = jnp.full_like(top_ref, 2 * FAR)

        def one_block(b, carry):
            first_k = b * width

            @pl.when(meets(seg_q, first_q, block, seg_k, first_k, width))
            def _():
                for h in range(heads):
                    scores = nt(ka_ref[h, pl.ds(first_k, width), :], qa_ref[h, pl.ds(first_q, block), :])
                    top = top_ref[h]
                    peak = jnp.maximum(top, jnp.max(scores, axis=0, keepdims=True))
                    weights = jnp.exp(scores - peak).astype(low)
                    acc_ref[h] = acc_ref[h] * jnp.exp(top - peak) + nn(
                        vt_ref[h, :, pl.ds(first_k, width)], weights
                    )
                    top_ref[h] = peak

            return carry

        lax.fori_loop(0, keys // width, one_block, 0)
        outs = []
        for h in range(heads):
            acc = acc_ref[h]
            total = acc[HEAD_DIM : HEAD_DIM + 1]
            lse = top_ref[h] + jnp.log(total)
            rows = jnp.concatenate(
                [acc[:HEAD_DIM] / total, jnp.broadcast_to(lse, (HEAD_DIM, block))], axis=0
            )
            turned = rows.T
            outs.append(turned[:, :HEAD_DIM])
            minus = three(-turned[:, HEAD_DIM:])
            lane = lax.broadcasted_iota(jnp.int32, (block, HEAD_DIM), 1)
            mask = mq_ref[pl.ds(first_q, block), :].astype(high)
            for i in range(3):
                mask = jnp.where(lane == LSE_LANE + i, minus[i].astype(high), mask)
            qa_ref[h, pl.ds(first_q, block), HEAD_DIM:] = mask.astype(low)
        joined = jnp.concatenate(outs, axis=1)
        full_ref[pl.ds(first_q, block), :] = joined
        out_ref[r] = joined.astype(low)
        return carry

    lax.fori_loop(0, parts, one_part, 0)


def attend(here, seg_q, seg_k, queries, keys, values, mask_q, mask_k, parts):
    rows, local = queries.shape
    count = keys.shape[0]
    heads = local // HEAD_DIM
    block = rows // parts
    width = 256
    vmem = pl.BlockSpec(memory_space=pltpu.VMEM)
    smem = pl.BlockSpec(memory_space=pltpu.SMEM)
    pairs = rows * 768 * heads
    return pl.pallas_call(
        lambda *refs: attend_kernel(*refs, block=block, width=width, heads=heads),
        name="attend",
        out_shape=(
            jax.ShapeDtypeStruct((parts, block, local), low),
            jax.ShapeDtypeStruct((rows, local), high),
            jax.ShapeDtypeStruct((heads, rows, 2 * HEAD_DIM), low),
            jax.ShapeDtypeStruct((heads, count, 2 * HEAD_DIM), low),
        ),
        in_specs=[smem] * 3 + [vmem] * 5,
        out_specs=(vmem,) * 4,
        scratch_shapes=[
            pltpu.VMEM((heads, HEAD_DIM + 16, count), low),
            pltpu.VMEM((heads, HEAD_DIM + 16, block), high),
            pltpu.VMEM((heads, 1, block), high),
        ],
        cost_estimate=pl.CostEstimate(flops=pairs * 256, transcendentals=pairs, bytes_accessed=8 << 20),
    )(here, seg_q, seg_k, queries, keys, values, mask_q, mask_k)


def attend_back_kernel(
    here, seg_q, seg_k, g_ref, full_ref, qa_ref, ka_ref, v_ref, dq_ref, dk_ref, dv_ref, kt_ref,
    va_ref, ga_ref, dka_ref, dva_ref, dqa_ref, *, block, width, heads
):
    parts = g_ref.shape[0]
    keys = v_ref.shape[0]
    scale = 1.0 / math.sqrt(HEAD_DIM)
    mine = here[0]
    for h in range(heads):
        cols = slice(h * HEAD_DIM, (h + 1) * HEAD_DIM)
        kt_ref[h] = ka_ref[h, :, :HEAD_DIM].T
        va_ref[h] = jnp.concatenate([v_ref[:, cols], jnp.ones((keys, HEAD_DIM), low)], axis=1)
    dka_ref[...] = jnp.zeros_like(dka_ref)
    dva_ref[...] = jnp.zeros_like(dva_ref)

    def one_part(r, carry):
        first_q = (mine ^ r) * block
        for h in range(heads):
            cols = slice(h * HEAD_DIM, (h + 1) * HEAD_DIM)
            grad = g_ref[r, :, cols]
            delta = jnp.sum(
                grad.astype(high) * full_ref[pl.ds(first_q, block), cols], axis=1, keepdims=True
            )
            lane = lax.broadcasted_iota(jnp.int32, (block, HEAD_DIM), 1)
            extra = jnp.zeros((block, HEAD_DIM), high)
            for i, piece in enumerate(three(-delta)):
                extra = jnp.where(lane == i, piece.astype(high), extra)
            ga_ref[h] = jnp.concatenate([grad, extra.astype(low)], axis=1)
        dqa_ref[...] = jnp.zeros_like(dqa_ref)

        def one_block(b, carry):
            first_k = b * width

            @pl.when(meets(seg_q, first_q, block, seg_k, first_k, width))
            def _():
                for h in range(heads):
                    span = pl.ds(first_k, width)
                    asks = qa_ref[h, pl.ds(first_q, block), :]
                    probs = jnp.exp(nt(ka_ref[h, span, :], asks))
                    slopes = (probs * nt(va_ref[h, span, :], ga_ref[h])).astype(low)
                    dva_ref[h, span, :] += nn(probs.astype(low), ga_ref[h, :, :HEAD_DIM])
                    dka_ref[h, span, :] += nn(slopes, asks[:, :HEAD_DIM])
                    dqa_ref[h] += nn(kt_ref[h, :, span], slopes)

            return carry

        lax.fori_loop(0, keys // width, one_block, 0)
        dq_ref[pl.ds(first_q, block), :] = jnp.concatenate(
            [(dqa_ref[h] * scale).T for h in range(heads)], axis=1
        ).astype(low)
        return carry

    lax.fori_loop(0, parts, one_part, 0)
    for h in range(heads):
        cols = slice(h * HEAD_DIM, (h + 1) * HEAD_DIM)
        dk_ref[:, cols] = dka_ref[h].astype(low)
        dv_ref[:, cols] = dva_ref[h].astype(low)


def attend_back(here, seg_q, seg_k, grads, full, asks, keys, values):
    parts, block, local = grads.shape
    rows = parts * block
    count = values.shape[0]
    heads = local // HEAD_DIM
    width = 256
    vmem = pl.BlockSpec(memory_space=pltpu.VMEM)
    smem = pl.BlockSpec(memory_space=pltpu.SMEM)
    pairs = rows * 768 * heads
    return pl.pallas_call(
        lambda *refs: attend_back_kernel(*refs, block=block, width=width, heads=heads),
        name="attend_back",
        out_shape=(
            jax.ShapeDtypeStruct((rows, local), low),
            jax.ShapeDtypeStruct((count, local), low),
            jax.ShapeDtypeStruct((count, local), low),
        ),
        in_specs=[smem] * 3 + [vmem] * 5,
        out_specs=(vmem,) * 3,
        scratch_shapes=[
            pltpu.VMEM((heads, HEAD_DIM, count), low),
            pltpu.VMEM((heads, count, 2 * HEAD_DIM), low),
            pltpu.VMEM((heads, block, 2 * HEAD_DIM), low),
            pltpu.VMEM((heads, count, HEAD_DIM), high),
            pltpu.VMEM((heads, count, HEAD_DIM), high),
            pltpu.VMEM((heads, HEAD_DIM, block), high),
        ],
        cost_estimate=pl.CostEstimate(flops=pairs * 640, transcendentals=pairs, bytes_accessed=8 << 20),
    )(here, seg_q, seg_k, grads, full, asks, keys, values)


def gather_fast(shard, f, c):
    rows = shard.shape[0]
    half = rows // 2
    n_f = lax.axis_size("fsdp")
    own = take(shard, c * half, half)
    whole = jnp.zeros((n_f * rows,) + shard.shape[1:], shard.dtype)
    whole = place(whole, shard, f * rows)
    for s in range(1, n_f):
        got = shift(own, "fsdp", s)
        other = swap(got, "ctx", 1)
        first = (f - s) % n_f * rows
        whole = place(whole, got, first + c * half)
        whole = place(whole, other, first + (1 - c) * half)
    return whole


def halo_of(value, c, span):
    rows = value.shape[0]
    return take(value, (1 - c) * (rows - span), span)


def shards(
    inputs, segments, w_query, b_query, w_key, w_value, b_value, w_out, b_out, gain_one, shift_one,
    w_inner, b_inner, w_outer, b_outer, gain_two, shift_two, grad_output,
):
    rows, width = inputs.shape
    local = w_query.shape[1]
    hidden = w_inner.shape[1]
    n_f, n_c, n_t = (lax.axis_size(a) for a in ("fsdp", "ctx", "tp"))
    f, c, t = (lax.axis_index(a) for a in ("fsdp", "ctx", "tp"))
    tokens = rows // n_t
    rim = MOST
    quick = n_f == 4 and n_c == 2 and n_t == 4
    piece = width // n_f
    flip = [t ^ r for r in range(n_t)]

    bundle_a = jnp.concatenate([w_query, w_key, w_value, w_out.T], axis=1)
    if quick:
        whole_a = gather_fast(bundle_a, f, c)
    else:
        whole_a = lax.all_gather(bundle_a, "fsdp", axis=0, tiled=True)
    bundle_f = jnp.concatenate([w_inner, w_outer.T], axis=1)
    bias_row = jnp.pad(b_inner[None], ((0, 7), (0, hidden)))
    if quick:
        half = piece // 2
        own = take(bundle_f, c * half, half)
        base = jnp.zeros((width + 8, 2 * hidden), low)
        near = place(place(base, bias_row, width), bundle_f, f * piece)
        far_own = swap(jnp.concatenate([bundle_f, bias_row], axis=0), "tp", 2)
        far = place(place(base, far_own[piece:], width), far_own[:piece], f * piece)
        for s in range(1, n_f):
            first = (f - s) % n_f * piece
            got = shift(own, "fsdp", s)
            side = swap(got, "ctx", 1)
            got_x = swap(got, "tp", 2)
            side_x = swap(side, "tp", 2) if s == 2 else swap(got_x, "ctx", 1)
            near = place(place(near, got, first + c * half), side, first + (1 - c) * half)
            far = place(place(far, got_x, first + c * half), side_x, first + (1 - c) * half)
        pieces_f = [near, swap(near, "tp", 1), far, swap(far, "tp", 1)]
    else:
        gathered = lax.all_gather(bundle_f, "fsdp", axis=0, tiled=True)
        gathered = lax.all_gather(jnp.concatenate([gathered, bias_row], axis=0), "tp", axis=0)
        pieces_f = [lax.dynamic_index_in_dim(gathered, i, 0, keepdims=False) for i in flip]
    w_in = [p[:width, :hidden] for p in pieces_f]
    w_ot = [p[:width, hidden:] for p in pieces_f]
    b_in = [p[width : width + 1, :hidden].astype(high) for p in pieces_f]

    seg_own = segments.reshape(rows)
    if n_c == 2:
        sent = halo_of(inputs, c, rim)
        if quick:
            part = rim // 2
            got = swap(take(sent, (t & 1) * part, part), "ctx", 1)
            mate = swap(got, "tp", 1)
            even = (t & 1) == 0
            halo_in = jnp.concatenate([jnp.where(even, got, mate), jnp.where(even, mate, got)], axis=0)
        else:
            halo_in = swap(sent, "ctx", 1)
        halo_seg = swap(halo_of(seg_own, c, rim), "ctx", 1)
    else:
        ahead = [(i, i + 1) for i in range(n_c - 1)]
        behind = [(i + 1, i) for i in range(n_c - 1)]

        def both(value):
            return jnp.concatenate(
                [
                    lax.ppermute(value[rows - rim :], "ctx", ahead),
                    lax.ppermute(value[:rim], "ctx", behind),
                ],
                axis=0,
            )

        halo_in = both(inputs)
        halo_seg = both(seg_own + 1) - 1
        halo_seg = jnp.where(halo_seg < 0, NO_ID, halo_seg)
    w_qkv = whole_a[:, : 3 * local]
    bias = jnp.concatenate([b_query, jnp.zeros_like(b_query), b_value]).astype(high)
    own_qkv = (nn(inputs, w_qkv) + bias).astype(low)
    halo_kv = (nn(halo_in, w_qkv[:, local:]) + bias[local:]).astype(low)
    queries = own_qkv[:, :local]
    keys = jnp.concatenate([own_qkv[:, local : 2 * local], halo_kv[:, :local]], axis=0)
    values = jnp.concatenate([own_qkv[:, 2 * local :], halo_kv[:, local:]], axis=0)
    seg_all = jnp.concatenate([seg_own, halo_seg])
    lane = jnp.arange(IDS)
    near_id = seg_all[:, None] == lane
    mask_k = (near_id | ((lane >= LSE_LANE) & (lane < LSE_LANE + 3))).astype(low)
    mask_q = jnp.where(near_id[:rows] | ((lane >= LSE_LANE) & (lane < LSE_LANE + 3)), 0.0, FAR).astype(low)
    here = t.reshape(1)
    attended, full, asks, keys_wide = attend(
        here, seg_own, seg_all, queries, keys, values, mask_q, mask_k, n_t
    )

    w_o = whole_a[:, 3 * local :]
    w_o_near = [w_o] + [swap(w_o, "tp", r) for r in range(1, n_t)]
    w_o_all = jnp.concatenate(w_o_near, axis=1)
    att = jnp.concatenate([attended[0]] + [swap(attended[r], "tp", r) for r in range(1, n_t)], axis=1)
    gain_one_f, shift_one_f, gain_two_f, shift_two_f = (
        v.astype(high) for v in (gain_one, shift_one, gain_two, shift_two)
    )
    first_row = t * tokens
    branch = nt(att, w_o_all) + b_out.astype(high)
    hat_one, inverse_one = norm_parts(take(inputs, first_row, tokens).astype(high) + branch)
    normed = hat_one * gain_one_f + shift_one_f
    normed_low = normed.astype(low)
    acts, slopes = [], []
    outer = b_outer.astype(high)
    for r in range(n_t):
        act, slope = gelu_parts(nn(normed_low, w_in[r]) + b_in[r])
        acts.append(act.astype(low))
        slopes.append(slope)
        outer = outer + nt(acts[r], w_ot[r])
    hat_two, inverse_two = norm_parts(normed + outer)
    output = (hat_two * gain_two_f + shift_two_f).astype(low)
    grad = take(grad_output, first_row, tokens).astype(high)
    g_gain_two = jnp.sum(grad * hat_two, axis=0)
    g_shift_two = jnp.sum(grad, axis=0)
    g_two = norm_back(grad, hat_two, inverse_two, gain_two_f)
    g_outer = g_two.astype(low)
    g_b_outer = jnp.sum(g_outer.astype(high), axis=0)
    g_normed = g_two
    g_inner = []
    for r in range(n_t):
        g_inner.append((nn(g_outer, w_ot[r]) * slopes[r]).astype(low))
        g_normed = g_normed + nt(g_inner[r], w_in[r])
    g_gain_one = jnp.sum(g_normed * hat_one, axis=0)
    g_shift_one = jnp.sum(g_normed, axis=0)
    g_one = norm_back(g_normed, hat_one, inverse_one, gain_one_f)
    g_branch = g_one.astype(low)
    g_b_out = jnp.sum(g_branch.astype(high), axis=0)
    g_att = nn(g_branch, w_o_all).astype(low)
    g_b_inner = [jnp.sum(g.astype(high), axis=0) for g in g_inner]

    g_att_heads = jnp.stack(
        [g_att[:, :local]]
        + [swap(g_att[:, r * local : (r + 1) * local], "tp", r) for r in range(1, n_t)]
    )

    def blocks(r):
        return jnp.concatenate([g_inner[r], acts[r], att[:, r * local : (r + 1) * local]], axis=1)

    def weight_grads(norm, g_out, g_br, wide):
        return jnp.concatenate(
            [
                tn(norm, wide[:, :hidden]),
                tn(g_out, wide[:, hidden : 2 * hidden]),
                tn(g_br, wide[:, 2 * hidden :]),
            ],
            axis=1,
        )

    rows_own = jnp.concatenate([normed_low, g_outer, g_branch], axis=1)
    if quick:
        rows_mate = swap(rows_own, "tp", 1)
        grads_f = []
        for r in (0, 2):
            mate = swap(blocks(r + 1), "tp", 1)
            mine = blocks(r)
            parts = []
            for i in range(3):
                cols = slice(i * width, (i + 1) * width)
                units = slice(min(i * hidden, 2 * hidden), (i + 1) * hidden if i < 2 else 2 * hidden + local)
                parts.append(
                    tn(rows_own[:, cols], mine[:, units]) + tn(rows_mate[:, cols], mate[:, units])
                )
            grads_f.append(jnp.concatenate(parts, axis=1).astype(low))
        near_g, far_g = grads_f
        wide = near_g.shape[1]
        mid = width // 2
        quarters = mid // piece
        part_a = near_g[:mid] + swap(far_g[:mid], "tp", 2)
        both_b = jnp.stack([near_g[mid:], far_g[mid:]]).reshape(2, quarters, 2, half, wide)
        keep_b = lax.dynamic_index_in_dim(both_b, c, 2, keepdims=False)
        send_b = lax.dynamic_index_in_dim(both_b, 1 - c, 2, keepdims=False)
        both_b = keep_b + swap(send_b, "ctx", 1)
        part_a = part_a.reshape(quarters, 2, half, wide)
        keep_a = lax.dynamic_index_in_dim(part_a, c, 1, keepdims=False)
        send_a = lax.dynamic_index_in_dim(part_a, 1 - c, 1, keepdims=False)
        part_a = keep_a + swap(send_a, "ctx", 1)
        part_b = both_b[0] + swap(both_b[1], "tp", 2)
        all_z = jnp.concatenate([part_a, part_b], axis=0)
        total = lax.dynamic_index_in_dim(all_z, f, 0, keepdims=False).astype(high)
        for s in range(1, n_f):
            total = total + shift(
                lax.dynamic_index_in_dim(all_z, (f + s) % n_f, 0, keepdims=False), "fsdp", s
            ).astype(high)
        total = total.astype(low)
        other = swap(total, "ctx", 1)
        even = c == 0
        shard_f = jnp.concatenate(
            [jnp.where(even, total, other), jnp.where(even, other, total)], axis=0
        ).astype(high)
    else:
        stacked = jnp.stack(
            [weight_grads(normed_low, g_outer, g_branch, blocks(r)) for r in range(n_t)]
        )
        ordered = jnp.stack([lax.dynamic_index_in_dim(stacked, i, 0, keepdims=False) for i in flip])
        mine = lax.psum_scatter(ordered, "tp", scatter_dimension=0, tiled=False)
        mine = lax.psum(mine, ("fsdp", "ctx"))
        shard_f = take(mine, f * piece, piece)

    g_q, g_k, g_v = attend_back(here, seg_own, seg_all, g_att_heads, full, asks, keys_wide, values)
    edge_kv = jnp.concatenate([g_k[rows:], g_v[rows:]], axis=1)
    g_kv = jnp.concatenate([g_k[:rows], g_v[:rows]], axis=1).astype(high)

    def add_edge(first, got):
        return place(g_kv, take(g_kv, first, rim) + got.astype(high), first)

    if n_c == 2:
        g_kv = add_edge((1 - c) * (rows - rim), swap(edge_kv, "ctx", 1))
    else:
        g_kv = add_edge(0, lax.ppermute(edge_kv[rim:], "ctx", ahead))
        g_kv = add_edge(rows - rim, lax.ppermute(edge_kv[:rim], "ctx", behind))
    g_qkv = jnp.concatenate([g_q, g_kv.astype(low)], axis=1)
    g_b_qkv = jnp.sum(g_qkv.astype(high), axis=0)
    g_in_part = nt(g_qkv, w_qkv).astype(low)
    grad_a = tn(inputs, g_qkv)

    if quick:
        pairs = g_in_part.reshape(n_t, tokens, width)
        first_sum = [
            lax.dynamic_index_in_dim(pairs, flip[r], 0, keepdims=False)
            + swap(lax.dynamic_index_in_dim(pairs, flip[r ^ 1], 0, keepdims=False), "tp", 1)
            for r in (0, 2)
        ]
        mine_in = first_sum[0].astype(high) + swap(first_sum[1], "tp", 2).astype(high) + g_one
        mine_in = mine_in.astype(low)
        small_a = grad_a.astype(low).reshape(n_f, 2, half, 3 * local)
        keep = lax.dynamic_index_in_dim(small_a, c, 1, keepdims=False)
        keep = keep + swap(lax.dynamic_index_in_dim(small_a, 1 - c, 1, keepdims=False), "ctx", 1)
        total = lax.dynamic_index_in_dim(keep, f, 0, keepdims=False).astype(high)
        for s in range(1, n_f):
            total = total + shift(
                lax.dynamic_index_in_dim(keep, (f + s) % n_f, 0, keepdims=False), "fsdp", s
            ).astype(high)
        total = total.astype(low)
        other = swap(total, "ctx", 1)
        shard_a = jnp.concatenate(
            [jnp.where(even, total, other), jnp.where(even, other, total)], axis=0
        ).astype(high)

        def everyone(value):
            far_value = swap(value, "tp", 2)
            duo = jnp.stack([value, far_value])
            mates = swap(duo, "tp", 1)
            result = jnp.zeros((n_t,) + value.shape, value.dtype)
            for r, v in enumerate((duo[0], mates[0], duo[1], mates[1])):
                result = lax.dynamic_update_index_in_dim(result, v, flip[r], 0)
            return result.reshape((n_t * value.shape[0],) + value.shape[1:])

        output = everyone(output)
        grad_inputs = everyone(mine_in).astype(high)
    else:
        mine_in = lax.psum_scatter(
            g_in_part.astype(high).reshape(n_t, tokens, width), "tp", scatter_dimension=0, tiled=False
        )
        grad_inputs = lax.all_gather((mine_in + g_one).astype(low), "tp", axis=0, tiled=True).astype(high)
        output = lax.all_gather(output, "tp", axis=0, tiled=True)
        shard_a = take(lax.psum(grad_a, ("fsdp", "ctx")), f * piece, piece)

    shared = jnp.stack([g_b_out, g_gain_one, g_shift_one, g_b_outer, g_gain_two, g_shift_two])
    stacked = jnp.stack(g_b_inner)
    if quick:
        pair = jnp.concatenate([shared, stacked[0:1], stacked[2:3]], axis=0)
        away = jnp.concatenate([shared, stacked[1:2], stacked[3:4]], axis=0)
        pair = pair + swap(away, "tp", 1)
        away = jnp.concatenate([pair[:6], pair[7:8]], axis=0)
        pair = pair[:7] + swap(away, "tp", 2)
        qv = jnp.pad(g_b_qkv[None], ((0, 0), (0, width - 3 * local)))
        pair = jnp.concatenate([pair, qv], axis=0)
        pair = pair + swap(pair, "ctx", 1)
        pair = pair + swap(pair, "fsdp", 1)
        pair = pair + swap(pair, "fsdp", 2)
        shared, s_b_inner, s_qkv = pair[:6], pair[6], pair[7, : 3 * local]
    else:
        ordered = jnp.stack([lax.dynamic_index_in_dim(stacked, i, 0, keepdims=False) for i in flip])
        s_b_inner = lax.psum(lax.psum_scatter(ordered, "tp", scatter_dimension=0, tiled=False), ("fsdp", "ctx"))
        shared = lax.psum(shared, ("fsdp", "ctx", "tp"))
        s_qkv = lax.psum(g_b_qkv, ("fsdp", "ctx"))
    return (
        output,
        grad_inputs,
        shard_a[:, :local],
        s_qkv[:local],
        shard_a[:, local : 2 * local],
        shard_a[:, 2 * local :],
        s_qkv[2 * local :],
        shard_f[:, 2 * hidden :].T,
        shared[0],
        shared[1],
        shared[2],
        shard_f[:, :hidden],
        s_b_inner,
        shard_f[:, hidden : 2 * hidden].T,
        shared[3],
        shared[4],
        shared[5],
    )


def solution(mesh):
    rows = P(("fsdp", "ctx"), None)
    down, flat, across = P("fsdp", "tp"), P("tp"), P("tp", "fsdp")
    return jax.shard_map(
        shards,
        mesh=mesh,
        in_specs=(
            rows, P("fsdp", "ctx"), down, flat, down, down, flat, across, P(), P(), P(), down, flat,
            across, P(), P(), P(), rows,
        ),
        out_specs=(
            rows, rows, down, flat, down, down, flat, across, P(), P(), P(), down, flat, across,
            P(), P(), P(),
        ),
        check_vma=False,
    )
```

```python
import math

import jax
import jax.numpy as jnp
from jax import lax
from jax.experimental import pallas as pl
from jax.experimental.pallas import tpu as pltpu
from jax.sharding import PartitionSpec as P

HEAD_DIM = 64
MOST = 512
IDS = 64
NO_ID = 63
LSE_LANE = 60
FAR = -1e30

layer_eps = 1e-12
low = jnp.bfloat16
high = jnp.float32


def nn(left, right):
    return jnp.dot(left, right, preferred_element_type=high)


def nt(left, right):
    return lax.dot_general(left, right, (((1,), (1,)), ((), ())), preferred_element_type=high)


def tn(left, right):
    return lax.dot_general(left, right, (((0,), (0,)), ((), ())), preferred_element_type=high)


def swap(value, axis, bit):
    count = lax.axis_size(axis)
    return lax.ppermute(value, axis, [(i, i ^ bit) for i in range(count)])


def shift(value, axis, step):
    count = lax.axis_size(axis)
    return lax.ppermute(value, axis, [(i, (i + step) % count) for i in range(count)])


def place(whole, part, first):
    return lax.dynamic_update_slice_in_dim(whole, part, first, 0)


def take(whole, first, count):
    return lax.dynamic_slice_in_dim(whole, first, count, 0)


def norm_parts(hidden):
    average = jnp.mean(hidden, axis=-1, keepdims=True)
    centred = hidden - average
    variance = jnp.mean(centred * centred, axis=-1, keepdims=True)
    inverse = lax.rsqrt(variance + layer_eps)
    return centred * inverse, inverse


def norm_back(grad, hat, inverse, gain):
    scaled = grad * gain
    first = jnp.mean(scaled, axis=-1, keepdims=True)
    second = jnp.mean(scaled * hat, axis=-1, keepdims=True)
    return inverse * (scaled - first - hat * second)


def gelu_parts(inner):
    half = 0.5 * (1.0 + lax.erf(inner * 0.7071067811865476))
    slope = half + inner * (jnp.exp(-0.5 * inner * inner) * 0.3989422804014327)
    return inner * half, slope


def three(value):
    first = value.astype(low)
    rest = value - first.astype(high)
    second = rest.astype(low)
    third = (rest - second.astype(high)).astype(low)
    return first, second, third


def meets(seg_q, first_q, size_q, seg_k, first_k, size_k):
    return (seg_q[first_q + size_q - 1] >= seg_k[first_k]) & (
        seg_q[first_q] <= seg_k[first_k + size_k - 1]
    )


def score_part(r, q_ref, q_row, first_q, seg_q, seg_k, ka_ref, vt_ref, acc_ref, top_ref, width):
    heads, keys = ka_ref.shape[0], ka_ref.shape[1]
    block = acc_ref.shape[2]
    acc_ref[...] = jnp.zeros_like(acc_ref)
    top_ref[...] = jnp.full_like(top_ref, 2 * FAR)

    def one_block(b, carry):
        first_k = b * width

        @pl.when(meets(seg_q, first_q, block, seg_k, first_k, width))
        def _():
            for h in range(heads):
                scores = nt(ka_ref[h, pl.ds(first_k, width), :], q_ref[h, q_row])
                top = top_ref[h]
                peak = jnp.maximum(top, jnp.max(scores, axis=0, keepdims=True))
                weights = jnp.exp(scores - peak).astype(low)
                acc_ref[h] = acc_ref[h] * jnp.exp(top - peak) + nn(
                    vt_ref[h, :, pl.ds(first_k, width)], weights
                )
                top_ref[h] = peak

        return carry

    lax.fori_loop(0, keys // width, one_block, 0)
    outs = []
    lane = lax.broadcasted_iota(jnp.int32, (block, HEAD_DIM), 1)
    for h in range(heads):
        acc = acc_ref[h]
        total = acc[HEAD_DIM : HEAD_DIM + 1]
        lse = top_ref[h] + jnp.log(total)
        joined = jnp.concatenate(
            [acc[:HEAD_DIM] / total, jnp.broadcast_to(lse, (HEAD_DIM, block))], axis=0
        )
        turned = joined.T
        outs.append(turned[:, :HEAD_DIM])
        minus = three(-turned[:, HEAD_DIM:])
        mask = q_ref[h, q_row, :, HEAD_DIM:].astype(high)
        for i in range(3):
            mask = jnp.where(lane == LSE_LANE + i, minus[i].astype(high), mask)
        q_ref[h, q_row, :, HEAD_DIM:] = mask.astype(low)
    return jnp.concatenate(outs, axis=1)


def attend_far_kernel(*refs, block, width, heads, marks):
    pieces = len(marks)
    here, seg_q, seg_k, x_ref, halo_ref, bias_ref, mq_ref, mk_ref = refs[:8]
    w_refs = refs[8 : 8 + pieces]
    (out_2, out_3, full_ref, q_near, q_far, ka_ref, v_ref, vt_ref, w_ref) = refs[8 + pieces : 17 + pieces]
    acc_ref, top_ref, sems = refs[17 + pieces :]
    keys = v_ref.shape[0]
    rows = x_ref.shape[0]
    local = heads * HEAD_DIM
    scale = 1.0 / math.sqrt(HEAD_DIM)
    mine, f, c = here[0], here[1], here[2]
    copies = []
    for i, mark in enumerate(marks):
        first, count = mark(f, c)
        copies.append(
            pltpu.make_async_copy(w_refs[i], w_ref.at[pl.ds(first, count)], sems.at[i])
        )
        copies[-1].start()
    vt_ref[:, HEAD_DIM:, :] = jnp.ones((heads, vt_ref.shape[1] - HEAD_DIM, keys), low)
    for copy in copies:
        copy.wait()
    weights_all = w_ref[...].reshape(-1, w_ref.shape[2])

    def keep(first, count, mask, kv):
        span = pl.ds(first, count)
        for h in range(heads):
            cols = slice(h * HEAD_DIM, (h + 1) * HEAD_DIM)
            tail = slice(local + h * HEAD_DIM, local + (h + 1) * HEAD_DIM)
            ka_ref[h, span, :] = jnp.concatenate([kv[:, cols], mask], axis=1)
            vt_ref[h, :HEAD_DIM, span] = kv[:, tail].T
        v_ref[span, :] = kv[:, local:]

    for q_ref, base in ((q_near, 0), (q_far, 2)):

        def project(i, carry, q_ref=q_ref, base=base):
            first = pl.multiple_of((mine ^ (base + i)) * block, block)
            span = pl.ds(first, block)
            both = (nn(x_ref[span, :], weights_all) + bias_ref[...]).astype(low)
            for h in range(heads):
                cols = slice(h * HEAD_DIM, (h + 1) * HEAD_DIM)
                q_ref[h, i] = jnp.concatenate(
                    [both[:, cols] * jnp.array(scale, low), mq_ref[span, :]], axis=1
                )
            keep(first, block, mk_ref[span, :], both[:, local:])
            return carry

        lax.fori_loop(0, 2, project, 0)
    step = min(512, keys - rows)
    for first in range(rows, keys, step):
        span = slice(first - rows, first - rows + step)
        kv = (nn(halo_ref[span, :], weights_all[:, local:]) + bias_ref[:, local:]).astype(low)
        keep(first, step, mk_ref[first : first + step, :], kv)
    for i, out_ref in enumerate((out_2, out_3)):
        joined = score_part(
            2 + i, q_far, i, (mine ^ (2 + i)) * block, seg_q, seg_k, ka_ref, vt_ref, acc_ref, top_ref, width
        )
        full_ref[i] = joined
        out_ref[...] = joined.astype(low)


def attend_near_kernel(
    here, seg_q, seg_k, q_in, ka_ref, vt_ref, out_0, out_1, full_ref, q_ref, acc_ref, top_ref, *, block, width
):
    mine = here[0]
    q_ref[...] = q_in[...]
    for i, out_ref in enumerate((out_0, out_1)):
        joined = score_part(
            i, q_ref, i, (mine ^ i) * block, seg_q, seg_k, ka_ref, vt_ref, acc_ref, top_ref, width
        )
        full_ref[i] = joined
        out_ref[...] = joined.astype(low)


VMEM = pl.BlockSpec(memory_space=pltpu.VMEM)
SMEM = pl.BlockSpec(memory_space=pltpu.SMEM)
ANY = pl.BlockSpec(memory_space=pl.ANY)
HBM = pl.BlockSpec(memory_space=pltpu.HBM)


def shape(*dims, kind=low):
    return jax.ShapeDtypeStruct(dims, kind)


def cost(flops, size, transcendentals=0):
    return pl.CostEstimate(flops=flops, transcendentals=transcendentals, bytes_accessed=flops if flops == 1 else size)


def attend_far(here, seg_q, seg_k, x, halo, bias, mask_q, mask_k, pieces, marks, blocks, block):
    rows = x.shape[0]
    local = bias.shape[1] // 3
    count = rows + halo.shape[0]
    heads = local // HEAD_DIM
    wide = 2 * HEAD_DIM
    return pl.pallas_call(
        lambda *refs: attend_far_kernel(*refs, block=block, width=256, heads=heads, marks=marks),
        name="attend_far",
        out_shape=(
            shape(block, local),
            shape(block, local),
            shape(2, block, local, kind=high),
            shape(heads, 2, block, wide),
            shape(heads, 2, block, wide),
            shape(heads, count, wide),
            shape(count, local),
            shape(heads, HEAD_DIM + 16, count),
            shape(*blocks, 3 * local),
        ),
        in_specs=[SMEM] * 3 + [VMEM] * 5 + [ANY] * len(pieces),
        out_specs=(VMEM,) * 9,
        scratch_shapes=[
            pltpu.VMEM((heads, HEAD_DIM + 16, block), high),
            pltpu.VMEM((heads, 1, block), high),
            pltpu.SemaphoreType.DMA((len(pieces),)),
        ],
        cost_estimate=cost(FAR_COST, 8 << 20),
    )(here, seg_q, seg_k, x, halo, bias, mask_q, mask_k, *pieces)


def attend_near(here, seg_q, seg_k, q_near, keys_wide, values_t):
    heads, _, block, wide = q_near.shape
    local = heads * HEAD_DIM
    return pl.pallas_call(
        lambda *refs: attend_near_kernel(*refs, block=block, width=256),
        name="attend_near",
        out_shape=(
            shape(block, local),
            shape(block, local),
            shape(2, block, local, kind=high),
            shape(heads, 2, block, wide),
        ),
        in_specs=[SMEM] * 3 + [VMEM] * 3,
        out_specs=(VMEM,) * 4,
        scratch_shapes=[
            pltpu.VMEM((heads, HEAD_DIM + 16, block), high),
            pltpu.VMEM((heads, 1, block), high),
        ],
        cost_estimate=cost(NEAR_COST, 8 << 20),
    )(here, seg_q, seg_k, q_near, keys_wide, values_t)


FAR_COST = 1
NEAR_COST = 1
FEED_COST = 1
UNIT_COST = 1
BACK_COST = 1
LAST_COST = 1
SMALL_COST = 1


def feed_kernel(*refs, plan, hidden, local):
    count = len(plan)
    here, x_all, g_all, att_0, att_1, att_2, att_3, vec_ref = refs[:8]
    w_refs = refs[8 : 8 + count]
    (out_ref, one_ref, stat_ref, ga_0, ga_1, ga_2, ga_3, rows_hbm, keep_hbm, send_hbm) = refs[8 + count : 18 + count]
    (w_ref, b_ref, x_ref, g_ref, att_ref, hat_ref, inv_ref, norm_ref, acc_ref, slope_ref, gl_ref,
     rows_ref, keep_ref, send_ref, sems, out_sems) = refs[18 + count :]
    puts = []

    def put(src, dst):
        puts.append(pltpu.make_async_copy(src, dst, out_sems.at[len(puts)]))
        puts[-1].start()

    tokens, width = x_ref.shape
    mine, f, c = here[0], here[1], here[2]
    copies = []

    def begin(src, dst):
        copies.append(pltpu.make_async_copy(src, dst, sems.at[len(copies)]))
        copies[-1].start()

    first = pl.multiple_of(mine * tokens, tokens)
    begin(x_all.at[pl.ds(first, tokens)], x_ref)
    begin(g_all.at[pl.ds(first, tokens)], g_ref)
    for r, att in enumerate((att_0, att_1, att_2, att_3)):
        begin(att, att_ref.at[r])
    for i, (kind, r, mark) in enumerate(plan):
        start, size = mark(f, c)
        if kind == "own":
            begin(w_refs[i].at[pl.ds(0, size)], w_ref.at[r, pl.ds(start, size)])
            begin(w_refs[i].at[pl.ds(size, 8)], b_ref.at[r])
        else:
            begin(w_refs[i], w_ref.at[r, pl.ds(start, size)])
    for copy in copies:
        copy.wait()
    b_out, gain_one, shift_one, b_outer, gain_two, shift_two = (
        vec_ref[i : i + 1, :].astype(high) for i in range(6)
    )

    def weights(r, first, last):
        return w_ref[r, :, first:last]

    acc_ref[...] = nt(att_ref[0], weights(0, 2 * hidden, 2 * hidden + local))
    for r in range(1, 4):
        acc_ref[...] += nt(att_ref[r], weights(r, 2 * hidden, 2 * hidden + local))
    step = 64
    chunks = tokens // step

    def first_norm(i, carry):
        span = pl.ds(pl.multiple_of(i * step, step), step)
        hat, inverse = norm_parts(x_ref[span, :].astype(high) + (acc_ref[span, :] + b_out))
        hat_ref[span, :] = hat
        inv_ref[span, :] = inverse
        normed = hat * gain_one + shift_one
        norm_ref[span, :] = normed.astype(low)
        acc_ref[span, :] = normed + b_outer
        return carry

    lax.fori_loop(0, chunks, first_norm, 0)
    part = 256
    for k, side in enumerate((keep_ref, send_ref)):
        for x in range(2):
            side[x, :, 2 * hidden :] = att_ref[2 * x + k]

        def up(x, carry, k=k, side=side):
            r = 2 * x + k
            for j in range(0, hidden, part):
                inner = nn(norm_ref[...], weights(r, j, j + part))
                inner = inner + b_ref[r, 0:1, j : j + part].astype(high)
                act, slope = gelu_parts(inner)
                side[x, :, hidden + j : hidden + j + part] = act.astype(low)
                slope_ref[r, :, j : j + part] = slope
            acc_ref[...] += nt(side[x, :, hidden : 2 * hidden], weights(r, hidden, 2 * hidden))
            return carry

        lax.fori_loop(0, 2, up, 0)

    zero = jnp.zeros((1, width), high)

    def second_norm(i, sums):
        span = pl.ds(pl.multiple_of(i * step, step), step)
        hat, inverse = norm_parts(acc_ref[span, :])
        out_ref[span, :] = (hat * gain_two + shift_two).astype(low)
        grad = g_ref[span, :].astype(high)
        two = norm_back(grad, hat, inverse, gain_two)
        acc_ref[span, :] = two
        two_low = two.astype(low)
        gl_ref[span, :] = two_low
        terms = (two_low.astype(high), grad * hat, grad)
        return tuple(s + jnp.sum(v, axis=0, keepdims=True) for s, v in zip(sums, terms))

    sums_two = lax.fori_loop(0, chunks, second_norm, (zero,) * 3)
    rows_ref[0] = norm_ref[...].T
    rows_ref[1] = gl_ref[...].T
    put(rows_ref.at[pl.ds(0, 2)], rows_hbm.at[pl.ds(0, 2)])
    for k, side in ((1, send_ref), (0, keep_ref)):

        def down(x, carry, k=k, side=side):
            r = 2 * x + k
            for j in range(0, hidden, part):
                grad = nn(gl_ref[...], weights(r, hidden + j, hidden + j + part))
                grad = (grad * slope_ref[r, :, j : j + part]).astype(low)
                side[x, :, j : j + part] = grad
                stat_ref[8 + r, 0:1, j : j + part] = jnp.sum(grad.astype(high), axis=0, keepdims=True)
            acc_ref[...] += nt(side[x, :, :hidden], weights(r, 0, hidden))
            return carry

        lax.fori_loop(0, 2, down, 0)
        put(side, send_hbm if k else keep_hbm)

    def first_back(i, sums):
        span = pl.ds(pl.multiple_of(i * step, step), step)
        grad = acc_ref[span, :]
        hat = hat_ref[span, :]
        one = norm_back(grad, hat, inv_ref[span, :], gain_one)
        one_ref[span, :] = one
        one_low = one.astype(low)
        gl_ref[span, :] = one_low
        terms = (one_low.astype(high), grad * hat, grad)
        return tuple(s + jnp.sum(v, axis=0, keepdims=True) for s, v in zip(sums, terms))

    sums_one = lax.fori_loop(0, chunks, first_back, (zero,) * 3)
    for i, value in enumerate(sums_one + sums_two):
        stat_ref[i, 0:1, :] = value
    rows_ref[2] = gl_ref[...].T
    put(rows_ref.at[2], rows_hbm.at[2])
    for r, ga in enumerate((ga_0, ga_1, ga_2, ga_3)):
        ga[...] = nn(gl_ref[...], weights(r, 2 * hidden, 2 * hidden + local)).astype(low)
    for copy in puts:
        copy.wait()


def feed(here, x, grad, att, vectors, pieces, plan, tokens, hidden, local):
    width = x.shape[1]
    wide = 2 * hidden + local
    copies = 6 + len(pieces) + sum(kind == "own" for kind, _, _ in plan)
    return pl.pallas_call(
        lambda *refs: feed_kernel(*refs, plan=plan, hidden=hidden, local=local),
        name="feed",
        out_shape=(
            shape(tokens, width),
            shape(tokens, width, kind=high),
            shape(12, 1, width, kind=high),
            shape(tokens, local),
            shape(tokens, local),
            shape(tokens, local),
            shape(tokens, local),
            shape(3, width, tokens),
            shape(2, tokens, wide),
            shape(2, tokens, wide),
        ),
        in_specs=[SMEM] + [ANY] * 6 + [VMEM] + [ANY] * len(pieces),
        out_specs=(VMEM,) * 7 + (HBM,) * 3,
        scratch_shapes=[
            pltpu.VMEM((4, width, wide), low),
            pltpu.VMEM((4, 8, wide), low),
            pltpu.VMEM((tokens, width), low),
            pltpu.VMEM((tokens, width), low),
            pltpu.VMEM((4, tokens, local), low),
            pltpu.VMEM((tokens, width), high),
            pltpu.VMEM((tokens, 1), high),
            pltpu.VMEM((tokens, width), low),
            pltpu.VMEM((tokens, width), high),
            pltpu.VMEM((4, tokens, hidden), high),
            pltpu.VMEM((tokens, width), low),
            pltpu.VMEM((3, width, tokens), low),
            pltpu.VMEM((2, tokens, wide), low),
            pltpu.VMEM((2, tokens, wide), low),
            pltpu.SemaphoreType.DMA((copies,)),
            pltpu.SemaphoreType.DMA((4,)),
        ],
        cost_estimate=cost(FEED_COST, 24 << 20),
    )(here, x, grad, *att, vectors, *pieces)


def unit_kernel(here, rows_own, rows_mate, wide_own, wide_mate, *refs, hidden):
    ak_ref, as_ref, bk_ref, bs_ref, rows_ref, wide_ref, sems = refs
    c = here[2]
    tokens = rows_own.shape[2]
    wide = wide_own.shape[2]
    half = ak_ref.shape[1]
    mid = rows_own.shape[1] // 2
    copies = [
        pltpu.make_async_copy(rows_own, rows_ref.at[:, :, pl.ds(0, tokens)], sems.at[0]),
        pltpu.make_async_copy(wide_own, wide_ref.at[:, pl.ds(0, tokens)], sems.at[1]),
        pltpu.make_async_copy(rows_mate, rows_ref.at[:, :, pl.ds(tokens, tokens)], sems.at[2]),
        pltpu.make_async_copy(wide_mate, wide_ref.at[:, pl.ds(tokens, tokens)], sems.at[3]),
    ]
    for copy in copies:
        copy.start()
    for copy in copies:
        copy.wait()
    spans = ((0, 0, hidden), (1, hidden, 2 * hidden), (2, 2 * hidden, wide))
    for x in range(2):
        for i, first, last in spans:
            for top in range(2):
                part = slice(top * mid, (top + 1) * mid)
                got = nn(rows_ref[i, part, :], wide_ref[x, :, first:last]).astype(low)
                if top == 0:
                    side = ak_ref if x == 0 else as_ref
                    side[:, :, first:last] = got.reshape(-1, half, last - first)
                else:
                    got = got.reshape(-1, 2, half, last - first)
                    for z in range(got.shape[0]):

                        @pl.when(c == 0)
                        def _():
                            bk_ref[x, z, :, first:last] = got[z, 0]
                            bs_ref[x, z, :, first:last] = got[z, 1]

                        @pl.when(c != 0)
                        def _():
                            bk_ref[x, z, :, first:last] = got[z, 1]
                            bs_ref[x, z, :, first:last] = got[z, 0]


def unit_grads(here, rows, mate_rows, keep, mate, half, hidden):
    wide = keep.shape[2]
    tokens = rows.shape[2]
    width = rows.shape[1]
    quarters = width // 4 // half
    return pl.pallas_call(
        lambda *refs: unit_kernel(*refs, hidden=hidden),
        name="unit_grads",
        out_shape=(
            shape(2 * quarters, half, wide),
            shape(2 * quarters, half, wide),
            shape(2, quarters, half, wide),
            shape(2, quarters, half, wide),
        ),
        in_specs=[SMEM] + [ANY] * 4,
        out_specs=(VMEM,) * 4,
        scratch_shapes=[
            pltpu.VMEM((3, width, 2 * tokens), low),
            pltpu.VMEM((2, 2 * tokens, wide), low),
            pltpu.SemaphoreType.DMA((4,)),
        ],
        cost_estimate=cost(UNIT_COST, 14 << 20),
    )(here, rows, mate_rows, keep, mate)


def merge_one_kernel(here, ak, ga, bk, gb, a_keep, a_send, b_keep, b_send):
    c = here[2]
    for z in range(2):
        for side in range(2):
            i = 2 * z + side
            got = ak[i] + ga[i]

            @pl.when(c == side)
            def _():
                a_keep[z] = got

            @pl.when(c != side)
            def _():
                a_send[z] = got

    b_keep[...] = bk[0] + gb[0]
    b_send[...] = bk[1] + gb[1]


def merge_one(here, ak, ga, bk, gb):
    out = shape(*bk.shape[1:])
    return pl.pallas_call(
        merge_one_kernel,
        name="merge_one",
        out_shape=(out,) * 4,
        in_specs=[SMEM] + [VMEM] * 4,
        out_specs=(VMEM,) * 4,
        cost_estimate=cost(SMALL_COST, 8 << 20),
    )(here, ak, ga, bk, gb)


def merge_two_kernel(here, a_keep, a_got, b_keep, b_got, d_keep, d_got, *refs, start):
    outs, all_ref = refs[:4], refs[4]
    f = here[1]
    wide = a_keep.shape[2]
    for z in range(2):
        all_ref[z, :, :wide] = a_keep[z] + a_got[z]
        all_ref[2 + z, :, :wide] = b_keep[z] + b_got[z]
    all_ref[:, :, start:] = d_keep[...] + d_got[...]
    for s, out in enumerate(outs):
        out[...] = all_ref[(f + s) % 4]


def merge_two(here, a_keep, a_got, b_keep, b_got, d_keep, d_got, start):
    half = a_keep.shape[1]
    full = start + d_keep.shape[2]
    return pl.pallas_call(
        lambda *refs: merge_two_kernel(*refs, start=start),
        name="merge_two",
        out_shape=(shape(half, full),) * 4,
        in_specs=[SMEM] + [VMEM] * 6,
        out_specs=(VMEM,) * 4,
        scratch_shapes=[pltpu.VMEM((4, half, full), low)],
        cost_estimate=cost(SMALL_COST, 8 << 20),
    )(here, a_keep, a_got, b_keep, b_got, d_keep, d_got)


def merge_three_kernel(here, own, got_1, got_2, got_3, out, all_ref):
    f = here[1]
    for s, piece in enumerate((own, got_1, got_2, got_3)):
        all_ref[(f - s + 4) % 4] = piece[...]
    total = all_ref[0].astype(high)
    for z in range(1, 4):
        total = total + all_ref[z].astype(high)
    out[...] = total.astype(low)


def merge_three(here, pieces):
    return pl.pallas_call(
        merge_three_kernel,
        name="merge_three",
        out_shape=shape(*pieces[0].shape),
        in_specs=[SMEM] + [VMEM] * 4,
        out_specs=VMEM,
        scratch_shapes=[pltpu.VMEM((4,) + pieces[0].shape, low)],
        cost_estimate=cost(SMALL_COST, 4 << 20),
    )(here, *pieces)


def finish_kernel(here, own, got, inner, outer, out, query, key, value, bias, all_ref, *, start):
    c = here[2]
    hidden = inner.shape[1]
    local = query.shape[1]
    all_ref[c] = own[...]
    all_ref[1 - c] = got[...]
    half, full = own.shape

    def cols(first, last):
        return all_ref[:, :, first:last].reshape(2 * half, last - first).astype(high)

    inner[...] = cols(0, hidden)
    outer[...] = cols(hidden, 2 * hidden).T
    out[...] = cols(2 * hidden, 2 * hidden + local).T
    rest = cols(start, full)
    query[...] = rest[:, :local]
    key[...] = rest[:, local : 2 * local]
    value[...] = rest[:, 2 * local : 3 * local]
    bias[...] = own[:16, start + 3 * local :].astype(high)


def finish(here, own, got, start, hidden, local):
    half, full = own.shape
    piece = 2 * half
    return pl.pallas_call(
        lambda *refs: finish_kernel(*refs, start=start),
        name="finish",
        out_shape=(
            shape(piece, hidden, kind=high),
            shape(hidden, piece, kind=high),
            shape(local, piece, kind=high),
            shape(piece, local, kind=high),
            shape(piece, local, kind=high),
            shape(piece, local, kind=high),
            shape(16, full - start - 3 * local, kind=high),
        ),
        in_specs=[SMEM] + [VMEM] * 2,
        out_specs=(VMEM,) * 7,
        scratch_shapes=[pltpu.VMEM((2, half, full), low)],
        cost_estimate=cost(SMALL_COST, 4 << 20),
    )(here, own, got)


def spread_kernel(here, p_0, p_1, p_2, p_3, out):
    tokens = p_0.shape[0]
    for r, piece in enumerate((p_0, p_1, p_2, p_3)):
        first = pl.multiple_of((here[0] ^ r) * tokens, tokens)
        out[pl.ds(first, tokens), :] = piece[...].astype(out.dtype)


def spread(here, pieces, kind):
    tokens, width = pieces[0].shape
    return pl.pallas_call(
        spread_kernel,
        name="spread",
        out_shape=shape(4 * tokens, width, kind=kind),
        in_specs=[SMEM] + [VMEM] * 4,
        out_specs=VMEM,
        cost_estimate=cost(SMALL_COST, 8 << 20),
    )(here, *pieces)


def project_back_kernel(here, g_ref, edge_ref, x_ref, w_ref, keep, send, d_keep, d_send, all_ref, *, local):
    mine, c = here[0], here[2]
    rows = g_ref.shape[0]
    rim = edge_ref.shape[0]
    tokens = keep.shape[1]
    half = d_keep.shape[1]
    pad = d_keep.shape[2] - 3 * local
    all_ref[...] = g_ref[...]
    edge = pl.ds(pl.multiple_of((1 - c) * (rows - rim), rim), rim)
    all_ref[edge, local:] = (
        g_ref[edge, local:].astype(high) + edge_ref[...].astype(high)
    ).astype(low)
    for k, side in ((1, send), (0, keep)):
        for x in range(2):
            first = pl.multiple_of((mine ^ (2 * x + k)) * tokens, tokens)
            side[x] = nt(all_ref[pl.ds(first, tokens), :], w_ref[...]).astype(low)
    sums = jnp.zeros((1, 3 * local), high)
    for i in range(rows // tokens):
        part = all_ref[i * tokens : (i + 1) * tokens, :].astype(high)
        sums = sums + jnp.sum(part, axis=0, keepdims=True)
    row = lax.broadcasted_iota(jnp.int32, (half, pad), 0)
    extra = jnp.zeros((half, pad), high)
    for j in range(3 * local // pad):
        extra = jnp.where(row == j, sums[:, j * pad : (j + 1) * pad], extra)
    extra = extra.astype(low)
    got = tn(x_ref[...], all_ref[...]).astype(low).reshape(-1, 2, half, 3 * local)
    for z in range(got.shape[0]):
        d_keep[z, :, 3 * local :] = extra
        d_send[z, :, 3 * local :] = extra
        for side in range(2):

            @pl.when(c == side)
            def _():
                d_keep[z, :, : 3 * local] = got[z, side]

            @pl.when(c != side)
            def _():
                d_send[z, :, : 3 * local] = got[z, side]


def project_back(here, grads, edge, x, weights, tokens, half):
    rows, width = x.shape
    local = grads.shape[1] // 3
    pad = HEAD_DIM
    return pl.pallas_call(
        lambda *refs: project_back_kernel(*refs, local=local),
        name="project_back",
        out_shape=(
            shape(2, tokens, width),
            shape(2, tokens, width),
            shape(width // half // 2, half, 3 * local + pad),
            shape(width // half // 2, half, 3 * local + pad),
        ),
        in_specs=[SMEM] + [VMEM] * 4,
        out_specs=(VMEM,) * 4,
        scratch_shapes=[pltpu.VMEM(grads.shape, low)],
        cost_estimate=cost(LAST_COST, 8 << 20),
    )(here, grads, edge, x, weights)


def attend_back_kernel(
    here, seg_q, seg_k, g_0, g_1, g_2, g_3, full_near, full_far, q_near, q_far, ka_ref, v_ref, own_ref, rim_ref,
    g_ref, kt_ref, va_ref, ga_ref, dka_ref, dva_ref, dqa_ref, sems, *, block, width, heads
):
    copies = [
        pltpu.make_async_copy(g, g_ref.at[r], sems.at[r]) for r, g in enumerate((g_0, g_1, g_2, g_3))
    ]
    for copy in copies:
        copy.start()
    keys = v_ref.shape[0]
    rows = own_ref.shape[0]
    local = heads * HEAD_DIM
    scale = 1.0 / math.sqrt(HEAD_DIM)
    mine = here[0]
    for h in range(heads):
        cols = slice(h * HEAD_DIM, (h + 1) * HEAD_DIM)
        kt_ref[h] = ka_ref[h, :, :HEAD_DIM].T
        va_ref[h] = jnp.concatenate([v_ref[:, cols], jnp.ones((keys, HEAD_DIM), low)], axis=1)
    dka_ref[...] = jnp.zeros_like(dka_ref)
    dva_ref[...] = jnp.zeros_like(dva_ref)
    for copy in copies:
        copy.wait()

    for base, q_ref, full_ref in ((0, q_near, full_near), (2, q_far, full_far)):

        def one_part(i, carry, base=base, q_ref=q_ref, full_ref=full_ref):
            first_q = pl.multiple_of((mine ^ (base + i)) * block, block)
            for h in range(heads):
                cols = slice(h * HEAD_DIM, (h + 1) * HEAD_DIM)
                grad = g_ref[base + i, :, cols]
                delta = jnp.sum(grad.astype(high) * full_ref[i, :, cols], axis=1, keepdims=True)
                lane = lax.broadcasted_iota(jnp.int32, (block, HEAD_DIM), 1)
                extra = jnp.zeros((block, HEAD_DIM), high)
                for j, piece in enumerate(three(-delta)):
                    extra = jnp.where(lane == j, piece.astype(high), extra)
                ga_ref[h] = jnp.concatenate([grad, extra.astype(low)], axis=1)
            dqa_ref[...] = jnp.zeros_like(dqa_ref)

            def one_block(b, carry):
                first_k = b * width

                @pl.when(meets(seg_q, first_q, block, seg_k, first_k, width))
                def _():
                    for h in range(heads):
                        span = pl.ds(first_k, width)
                        asks = q_ref[h, i]
                        probs = jnp.exp(nt(ka_ref[h, span, :], asks))
                        slopes = (probs * nt(va_ref[h, span, :], ga_ref[h])).astype(low)
                        dva_ref[h, span, :] += nn(probs.astype(low), ga_ref[h, :, :HEAD_DIM])
                        dka_ref[h, span, :] += nn(slopes, asks[:, :HEAD_DIM])
                        dqa_ref[h] += nn(kt_ref[h, :, span], slopes)

                return carry

            lax.fori_loop(0, keys // width, one_block, 0)
            own_ref[pl.ds(first_q, block), :local] = jnp.concatenate(
                [(dqa_ref[h] * scale).T for h in range(heads)], axis=1
            ).astype(low)
            return carry

        lax.fori_loop(0, 2, one_part, 0)
    for j, part in enumerate((dka_ref, dva_ref)):
        wide = jnp.concatenate([part[h] for h in range(heads)], axis=1).astype(low)
        own_ref[:, (1 + j) * local : (2 + j) * local] = wide[:rows]
        rim_ref[:, j * local : (j + 1) * local] = wide[rows:]


def attend_back(here, seg_q, seg_k, grads, full_near, full_far, q_near, q_far, keys, values):
    parts = len(grads)
    block, local = grads[0].shape
    rows = parts * block
    count = values.shape[0]
    heads = local // HEAD_DIM
    return pl.pallas_call(
        lambda *refs: attend_back_kernel(*refs, block=block, width=256, heads=heads),
        name="attend_back",
        out_shape=(shape(rows, 3 * local), shape(count - rows, 2 * local)),
        in_specs=[SMEM] * 3 + [ANY] * 4 + [VMEM] * 6,
        out_specs=(VMEM,) * 2,
        scratch_shapes=[
            pltpu.VMEM((parts, block, local), low),
            pltpu.VMEM((heads, HEAD_DIM, count), low),
            pltpu.VMEM((heads, count, 2 * HEAD_DIM), low),
            pltpu.VMEM((heads, block, 2 * HEAD_DIM), low),
            pltpu.VMEM((heads, count, HEAD_DIM), high),
            pltpu.VMEM((heads, count, HEAD_DIM), high),
            pltpu.VMEM((heads, HEAD_DIM, block), high),
            pltpu.SemaphoreType.DMA((parts,)),
        ],
        cost_estimate=cost(BACK_COST, 8 << 20),
    )(here, seg_q, seg_k, *grads, full_near, full_far, q_near, q_far, keys, values)


def after(values, gate):
    return lax.optimization_barrier((tuple(values), gate))[0]


def halo_of(value, c, span):
    rows = value.shape[0]
    return take(value, (1 - c) * (rows - span), span)


def shards(
    inputs, segments, w_query, b_query, w_key, w_value, b_value, w_out, b_out, gain_one, shift_one,
    w_inner, b_inner, w_outer, b_outer, gain_two, shift_two, grad_output,
):
    rows, width = inputs.shape
    local = w_query.shape[1]
    hidden = w_inner.shape[1]
    n_f, n_c, n_t = (lax.axis_size(a) for a in ("fsdp", "ctx", "tp"))
    f, c, t = (lax.axis_index(a) for a in ("fsdp", "ctx", "tp"))
    tokens = rows // n_t
    rim = MOST
    quick = n_f == 4 and n_c == 2 and n_t == 4
    piece = width // n_f
    flip = [t ^ r for r in range(n_t)]

    half = piece // 2
    blocks = (2 * n_f, half)
    here = jnp.stack([t, f, c]).astype(jnp.int32)
    bundle_a = jnp.concatenate([w_query, w_key, w_value], axis=1)

    def spot(s, side):
        def mark(f, c):
            return (f - s + n_f) % n_f * 2 + (c if side == 0 else 1 - c), 1

        return mark

    def spot_own(f, c):
        return 2 * f, 2

    def spot_all(f, c):
        return 0, 2 * n_f

    def in_rows(mark):
        def rows_mark(f, c):
            first, count = mark(f, c)
            return (first if isinstance(first, int) else pl.multiple_of(first * half, half)), count * half

        return rows_mark

    seg_own = segments.reshape(rows)
    if quick:
        halves_a = bundle_a.reshape(2, half, -1)
        own_a = lax.dynamic_index_in_dim(halves_a, c, 0)
        pieces_a, marks_a = [halves_a], [spot_own]
        gots = [shift(own_a, "fsdp", s) for s in range(1, n_f)]
        for s, got in enumerate(gots, 1):
            pieces_a += [got, swap(got, "ctx", 1)]
            marks_a += [spot(s, 0), spot(s, 1)]
    else:
        whole_a = lax.all_gather(bundle_a, "fsdp", axis=0, tiled=True)
        pieces_a, marks_a = [whole_a.reshape(blocks + (-1,))], [spot_all]

    if n_c == 2:
        sent = halo_of(inputs, c, rim)
        if quick:
            part = rim // 2
            got = swap(take(sent, (t & 1) * part, part), "ctx", 1)
            mate = swap(got, "tp", 1)
            even = (t & 1) == 0
            halo_in = jnp.concatenate([jnp.where(even, got, mate), jnp.where(even, mate, got)], axis=0)
        else:
            halo_in = swap(sent, "ctx", 1)
        halo_seg = swap(halo_of(seg_own, c, rim), "ctx", 1)
    else:
        ahead = [(i, i + 1) for i in range(n_c - 1)]
        behind = [(i + 1, i) for i in range(n_c - 1)]

        def both(value):
            return jnp.concatenate(
                [
                    lax.ppermute(value[rows - rim :], "ctx", ahead),
                    lax.ppermute(value[:rim], "ctx", behind),
                ],
                axis=0,
            )

        halo_in = both(inputs)
        halo_seg = both(seg_own + 1) - 1
        halo_seg = jnp.where(halo_seg < 0, NO_ID, halo_seg)

    bias_row = jnp.pad(b_inner[None], ((0, 7), (0, hidden + local)))
    bundle_f = jnp.concatenate([w_inner, w_outer.T, w_out.T], axis=1)
    own_rows = jnp.concatenate([bundle_f, bias_row], axis=0)
    if quick:
        own_f = take(bundle_f, c * half, half)
        gots = [shift(own_f, "fsdp", s) for s in range(1, n_f)]
        far_rows = swap(own_rows, "tp", 2)

    bias = jnp.concatenate([b_query, jnp.zeros_like(b_query), b_value]).astype(high)[None]
    seg_all = jnp.concatenate([seg_own, halo_seg])
    lane = jnp.arange(IDS)
    near_id = seg_all[:, None] == lane
    mask_k = (near_id | ((lane >= LSE_LANE) & (lane < LSE_LANE + 3))).astype(low)
    mask_q = jnp.where(near_id[:rows] | ((lane >= LSE_LANE) & (lane < LSE_LANE + 3)), 0.0, FAR).astype(low)
    att_2, att_3, full_far, q_near, q_far, keys_wide, values, values_t, w_qkv = attend_far(
        here, seg_own, seg_all, inputs, halo_in, bias, mask_q, mask_k, pieces_a, marks_a, blocks, tokens
    )
    w_qkv = w_qkv.reshape(width, 3 * local)
    att_0, att_1, full_near, q_near = attend_near(here, seg_own, seg_all, q_near, keys_wide, values_t)
    att = [att_0, swap(att_1, "tp", 1), swap(att_2, "tp", 2), swap(att_3, "tp", 3)]

    if quick:
        pieces_f, plan = [], []

        def add(r, kind, value, mark):
            pieces_f.extend([value, swap(value, "tp", 1)])
            plan.extend([(kind, r, in_rows(mark)), (kind, r + 1, in_rows(mark))])

        add(0, "own", own_rows, spot_own)
        add(2, "own", far_rows, spot_own)
        for s, got in enumerate(gots, 1):
            if s > 1:
                (got,) = after([got], att_2)
            add(0, "part", got, spot(s, 0))
            add(0, "part", swap(got, "ctx", 1), spot(s, 1))
            add(2, "part", swap(got, "tp", 2), spot(s, 0))
            diag = lax.ppermute(
                got, ("ctx", "tp"), [(i, i ^ (n_t + 2)) for i in range(n_c * n_t)]
            )
            add(2, "part", diag, spot(s, 1))
    else:
        gathered = lax.all_gather(bundle_f, "fsdp", axis=0, tiled=True)
        gathered = jnp.concatenate([gathered, bias_row], axis=0)
        gathered = lax.all_gather(gathered, "tp", axis=0)
        pieces_f = [lax.dynamic_index_in_dim(gathered, i, 0, keepdims=False) for i in flip]
        plan = [("own", r, in_rows(spot_all)) for r in range(n_t)]

    vectors = jnp.stack([b_out, gain_one, shift_one, b_outer, gain_two, shift_two, b_out, b_out])
    output, g_one, stats, ga_0, ga_1, ga_2, ga_3, rows_t, keep, send = feed(
        here, inputs, grad_output, att, vectors, pieces_f, plan, tokens, hidden, local
    )
    g_att = [ga_0, swap(ga_1, "tp", 1), swap(ga_2, "tp", 2), swap(ga_3, "tp", 3)]
    stats = stats[:, 0]

    if quick:
        mate_rows = swap(rows_t, "tp", 1)
        mate = swap(send, "tp", 1)
        pair = jnp.concatenate([stats[:6], stats[8:9], stats[10:11]], axis=0)
        away = jnp.concatenate([stats[:6], stats[9:10], stats[11:12]], axis=0)
        pair = pair + swap(away, "tp", 1)
        away = jnp.concatenate([pair[:6], pair[7:8], pair[7:8]], axis=0)
        pair = pair + swap(away, "tp", 2)
        pair = pair + swap(pair, "ctx", 1)
        keep_a, send_a, keep_b, send_b = unit_grads(here, rows_t, mate_rows, keep, mate, half, hidden)
        got_a = swap(send_a, "tp", 2)
        got_b = swap(send_b, "ctx", 1)
        *g_att, keep_a, keep_b = lax.optimization_barrier((*g_att, keep_a, keep_b))
    else:
        ordered = []
        for r in range(n_t):
            wide = (keep, send)[r % 2][r // 2]
            ordered.append(
                jnp.concatenate(
                    [
                        nn(rows_t[0], wide[:, :hidden]),
                        nn(rows_t[1], wide[:, hidden : 2 * hidden]),
                        nn(rows_t[2], wide[:, 2 * hidden :]),
                    ],
                    axis=1,
                )
            )
        stacked = jnp.stack(ordered)
        ordered = jnp.stack([lax.dynamic_index_in_dim(stacked, i, 0, keepdims=False) for i in flip])
        mine = lax.psum_scatter(ordered, "tp", scatter_dimension=0, tiled=False)
        mine = lax.psum(mine, ("fsdp", "ctx"))
        shard_f = take(mine, f * piece, piece)

    g_own, g_rim = attend_back(
        here, seg_own, seg_all, g_att, full_near, full_far, q_near, q_far, keys_wide, values
    )
    if quick:
        edge = swap(g_rim, "ctx", 1)
        got_a, got_b = after([got_a, got_b], g_own)
        keep_a, send_a, keep_b, send_b = merge_one(here, keep_a, got_a, keep_b, got_b)
        got_a = swap(send_a, "ctx", 1)
        got_b = swap(send_b, "tp", 2)
        dx_keep, dx_send, d_keep, d_send = project_back(here, g_own, edge, inputs, w_qkv, tokens, half)
        dx_got = swap(dx_send, "tp", 1)
        d_got = swap(d_send, "ctx", 1)
        near_dx = dx_keep[0] + dx_got[0]
        far_dx = dx_keep[1] + dx_got[1]
        far_got = swap(far_dx, "tp", 2)
        start = (2 * hidden + local + 127) // 128 * 128
        outs = merge_two(here, keep_a, got_a, keep_b, got_b, d_keep, d_got, start)
        totals = [outs[0]] + [shift(outs[s], "fsdp", s) for s in range(1, n_f)]
        mine = (near_dx.astype(high) + far_got.astype(high) + g_one).astype(low)

        def everyone(value, kind):
            far_value = swap(value, "tp", 2)
            return spread(here, [value, swap(value, "tp", 1), far_value, swap(far_value, "tp", 1)], kind)

        output = everyone(output, low)
        grad_inputs = everyone(mine, high)
        total = merge_three(here, totals)
        s_inner, s_outer, s_out, s_query, s_key, s_value, s_bias = finish(
            here, total, swap(total, "ctx", 1), start, hidden, local
        )
        s_qkv = s_bias.reshape(-1)[: 3 * local]
        pair = pair + swap(pair, "fsdp", 1)
        pair = pair + swap(pair, "fsdp", 2)
        shared, s_b_inner = pair[:6], pair[6]
    else:
        edge_got = []
        if n_c == 2:
            edge_got.append(((1 - c) * (rows - rim), swap(g_rim, "ctx", 1)))
        else:
            edge_got.append((0, lax.ppermute(g_rim[rim:], "ctx", ahead)))
            edge_got.append((rows - rim, lax.ppermute(g_rim[:rim], "ctx", behind)))
        g_all = g_own.astype(high)
        for first, got in edge_got:
            got = jnp.pad(got.astype(high), ((0, 0), (local, 0)))
            g_all = place(g_all, take(g_all, first, rim) + got, first)
        g_all = g_all.astype(low)
        part = nt(g_all, w_qkv).reshape(n_t, tokens, width)
        mine = lax.psum_scatter(part, "tp", scatter_dimension=0, tiled=False)
        grad_inputs = lax.all_gather((mine + g_one).astype(low), "tp", axis=0, tiled=True).astype(high)
        output = lax.all_gather(output, "tp", axis=0, tiled=True)
        shard_a = take(lax.psum(tn(inputs, g_all), ("fsdp", "ctx")), f * piece, piece)
        s_query, s_key, s_value = (shard_a[:, i * local : (i + 1) * local] for i in range(3))
        s_qkv = lax.psum(jnp.sum(g_all.astype(high), axis=0), ("fsdp", "ctx"))
        s_inner, s_outer, s_out = shard_f[:, :hidden], shard_f[:, hidden : 2 * hidden].T, shard_f[:, 2 * hidden :].T
        ordered = jnp.stack([lax.dynamic_index_in_dim(stats[8:], i, 0, keepdims=False) for i in flip])
        s_b_inner = lax.psum(
            lax.psum_scatter(ordered, "tp", scatter_dimension=0, tiled=False), ("fsdp", "ctx")
        )
        shared = lax.psum(stats[:6], ("fsdp", "ctx", "tp"))
    return (
        output,
        grad_inputs,
        s_query,
        s_qkv[:local],
        s_key,
        s_value,
        s_qkv[2 * local :],
        s_out,
        shared[0],
        shared[1],
        shared[2],
        s_inner,
        s_b_inner,
        s_outer,
        shared[3],
        shared[4],
        shared[5],
    )


def solution(mesh):
    rows = P(("fsdp", "ctx"), None)
    down, flat, across = P("fsdp", "tp"), P("tp"), P("tp", "fsdp")
    return jax.shard_map(
        shards,
        mesh=mesh,
        in_specs=(
            rows, P("fsdp", "ctx"), down, flat, down, down, flat, across, P(), P(), P(), down, flat,
            across, P(), P(), P(), rows,
        ),
        out_specs=(
            rows, rows, down, flat, down, down, flat, across, P(), P(), P(), down, flat, across,
            P(), P(), P(),
        ),
        check_vma=False,
    )
```

```python
import math

import jax
import jax.numpy as jnp
from jax import lax
from jax.experimental import pallas as pl
from jax.experimental.pallas import tpu as pltpu
from jax.sharding import PartitionSpec as P

HEAD_DIM = 64
MOST = 512
IDS = 64
NO_ID = 63
LSE_LANE = 60
FAR = -1e30

layer_eps = 1e-12
low = jnp.bfloat16
high = jnp.float32


def nn(left, right):
    return jnp.dot(left, right, preferred_element_type=high)


def nt(left, right):
    return lax.dot_general(left, right, (((1,), (1,)), ((), ())), preferred_element_type=high)


def tn(left, right):
    return lax.dot_general(left, right, (((0,), (0,)), ((), ())), preferred_element_type=high)


def swap(value, axis, bit):
    count = lax.axis_size(axis)
    return lax.ppermute(value, axis, [(i, i ^ bit) for i in range(count)])


def shift(value, axis, step):
    count = lax.axis_size(axis)
    return lax.ppermute(value, axis, [(i, (i + step) % count) for i in range(count)])


def place(whole, part, first):
    return lax.dynamic_update_slice_in_dim(whole, part, first, 0)


def take(whole, first, count):
    return lax.dynamic_slice_in_dim(whole, first, count, 0)


def norm_parts(hidden):
    average = jnp.mean(hidden, axis=-1, keepdims=True)
    centred = hidden - average
    variance = jnp.mean(centred * centred, axis=-1, keepdims=True)
    inverse = lax.rsqrt(variance + layer_eps)
    return centred * inverse, inverse


def norm_back(grad, hat, inverse, gain):
    scaled = grad * gain
    first = jnp.mean(scaled, axis=-1, keepdims=True)
    second = jnp.mean(scaled * hat, axis=-1, keepdims=True)
    return inverse * (scaled - first - hat * second)


def gelu_parts(inner):
    half = 0.5 * (1.0 + lax.erf(inner * 0.7071067811865476))
    slope = half + inner * (jnp.exp(-0.5 * inner * inner) * 0.3989422804014327)
    return inner * half, slope


def three(value):
    first = value.astype(low)
    rest = value - first.astype(high)
    second = rest.astype(low)
    third = (rest - second.astype(high)).astype(low)
    return first, second, third


def meets(seg_q, first_q, size_q, seg_k, first_k, size_k):
    return (seg_q[first_q + size_q - 1] >= seg_k[first_k]) & (
        seg_q[first_q] <= seg_k[first_k + size_k - 1]
    )


def score_part(r, q_ref, q_row, first_q, seg_q, seg_k, ka_ref, vt_ref, acc_ref, top_ref, width):
    heads, keys = ka_ref.shape[0], ka_ref.shape[1]
    block = acc_ref.shape[2]
    acc_ref[...] = jnp.zeros_like(acc_ref)
    top_ref[...] = jnp.full_like(top_ref, 2 * FAR)

    def one_block(b, carry):
        first_k = b * width

        @pl.when(meets(seg_q, first_q, block, seg_k, first_k, width))
        def _():
            for h in range(heads):
                scores = nt(ka_ref[h, pl.ds(first_k, width), :], q_ref[h, q_row])
                top = top_ref[h]
                peak = jnp.maximum(top, jnp.max(scores, axis=0, keepdims=True))
                weights = jnp.exp(scores - peak).astype(low)
                acc_ref[h] = acc_ref[h] * jnp.exp(top - peak) + nn(
                    vt_ref[h, :, pl.ds(first_k, width)], weights
                )
                top_ref[h] = peak

        return carry

    lax.fori_loop(0, keys // width, one_block, 0)
    outs = []
    lane = lax.broadcasted_iota(jnp.int32, (block, HEAD_DIM), 1)
    for h in range(heads):
        acc = acc_ref[h]
        total = acc[HEAD_DIM : HEAD_DIM + 1]
        lse = top_ref[h] + jnp.log(total)
        joined = jnp.concatenate(
            [acc[:HEAD_DIM] / total, jnp.broadcast_to(lse, (HEAD_DIM, block))], axis=0
        )
        turned = joined.T
        outs.append(turned[:, :HEAD_DIM])
        minus = three(-turned[:, HEAD_DIM:])
        mask = q_ref[h, q_row, :, HEAD_DIM:].astype(high)
        for i in range(3):
            mask = jnp.where(lane == LSE_LANE + i, minus[i].astype(high), mask)
        q_ref[h, q_row, :, HEAD_DIM:] = mask.astype(low)
    return jnp.concatenate(outs, axis=1)


def attend_far_kernel(*refs, block, width, heads, marks):
    pieces = len(marks)
    here, seg_q, seg_k, x_ref, halo_ref, bias_ref, mq_ref, mk_ref = refs[:8]
    w_refs = refs[8 : 8 + pieces]
    (out_2, out_3, full_ref, q_near, q_far, ka_ref, v_ref, vt_ref, w_ref) = refs[8 + pieces : 17 + pieces]
    acc_ref, top_ref, sems = refs[17 + pieces :]
    keys = v_ref.shape[0]
    rows = x_ref.shape[0]
    local = heads * HEAD_DIM
    scale = 1.0 / math.sqrt(HEAD_DIM)
    mine, f, c = here[0], here[1], here[2]
    copies = []
    for i, mark in enumerate(marks):
        first, count = mark(f, c)
        copies.append(
            pltpu.make_async_copy(w_refs[i], w_ref.at[pl.ds(first, count)], sems.at[i])
        )
        copies[-1].start()
    vt_ref[:, HEAD_DIM:, :] = jnp.ones((heads, vt_ref.shape[1] - HEAD_DIM, keys), low)
    for copy in copies:
        copy.wait()
    weights_all = w_ref[...].reshape(-1, w_ref.shape[2])

    def keep(first, count, mask, kv):
        span = pl.ds(first, count)
        for h in range(heads):
            cols = slice(h * HEAD_DIM, (h + 1) * HEAD_DIM)
            tail = slice(local + h * HEAD_DIM, local + (h + 1) * HEAD_DIM)
            ka_ref[h, span, :] = jnp.concatenate([kv[:, cols], mask], axis=1)
            vt_ref[h, :HEAD_DIM, span] = kv[:, tail].T
        v_ref[span, :] = kv[:, local:]

    for q_ref, base in ((q_near, 0), (q_far, 2)):

        def project(i, carry, q_ref=q_ref, base=base):
            first = pl.multiple_of((mine ^ (base + i)) * block, block)
            span = pl.ds(first, block)
            both = (nn(x_ref[span, :], weights_all) + bias_ref[...]).astype(low)
            for h in range(heads):
                cols = slice(h * HEAD_DIM, (h + 1) * HEAD_DIM)
                q_ref[h, i] = jnp.concatenate(
                    [both[:, cols] * jnp.array(scale, low), mq_ref[span, :]], axis=1
                )
            keep(first, block, mk_ref[span, :], both[:, local:])
            return carry

        lax.fori_loop(0, 2, project, 0)
    step = min(512, keys - rows)
    for first in range(rows, keys, step):
        span = slice(first - rows, first - rows + step)
        kv = (nn(halo_ref[span, :], weights_all[:, local:]) + bias_ref[:, local:]).astype(low)
        keep(first, step, mk_ref[first : first + step, :], kv)
    for i, out_ref in enumerate((out_2, out_3)):
        joined = score_part(
            2 + i, q_far, i, (mine ^ (2 + i)) * block, seg_q, seg_k, ka_ref, vt_ref, acc_ref, top_ref, width
        )
        full_ref[i] = joined
        out_ref[...] = joined.astype(low)


def attend_near_kernel(
    here, seg_q, seg_k, q_in, ka_ref, vt_ref, out_0, out_1, full_ref, q_ref, acc_ref, top_ref, *, block, width
):
    mine = here[0]
    q_ref[...] = q_in[...]
    for i, out_ref in enumerate((out_0, out_1)):
        joined = score_part(
            i, q_ref, i, (mine ^ i) * block, seg_q, seg_k, ka_ref, vt_ref, acc_ref, top_ref, width
        )
        full_ref[i] = joined
        out_ref[...] = joined.astype(low)


VMEM = pl.BlockSpec(memory_space=pltpu.VMEM)
SMEM = pl.BlockSpec(memory_space=pltpu.SMEM)
ANY = pl.BlockSpec(memory_space=pl.ANY)
HBM = pl.BlockSpec(memory_space=pltpu.HBM)


def shape(*dims, kind=low):
    return jax.ShapeDtypeStruct(dims, kind)


def cost(flops, size, transcendentals=0):
    return pl.CostEstimate(flops=flops, transcendentals=transcendentals, bytes_accessed=size)


def attend_far(here, seg_q, seg_k, x, halo, bias, mask_q, mask_k, pieces, marks, blocks, block):
    rows = x.shape[0]
    local = bias.shape[1] // 3
    count = rows + halo.shape[0]
    heads = local // HEAD_DIM
    wide = 2 * HEAD_DIM
    return pl.pallas_call(
        lambda *refs: attend_far_kernel(*refs, block=block, width=256, heads=heads, marks=marks),
        name="attend_far",
        out_shape=(
            shape(block, local),
            shape(block, local),
            shape(2, block, local, kind=high),
            shape(heads, 2, block, wide),
            shape(heads, 2, block, wide),
            shape(heads, count, wide),
            shape(count, local),
            shape(heads, HEAD_DIM + 16, count),
            shape(*blocks, 3 * local),
        ),
        in_specs=[SMEM] * 3 + [VMEM] * 5 + [ANY] * len(pieces),
        out_specs=(VMEM,) * 9,
        scratch_shapes=[
            pltpu.VMEM((heads, HEAD_DIM + 16, block), high),
            pltpu.VMEM((heads, 1, block), high),
            pltpu.SemaphoreType.DMA((len(pieces),)),
        ],
        cost_estimate=cost(FAR_COST, 8 << 20),
    )(here, seg_q, seg_k, x, halo, bias, mask_q, mask_k, *pieces)


def attend_near(here, seg_q, seg_k, q_near, keys_wide, values_t):
    heads, _, block, wide = q_near.shape
    local = heads * HEAD_DIM
    return pl.pallas_call(
        lambda *refs: attend_near_kernel(*refs, block=block, width=256),
        name="attend_near",
        out_shape=(
            shape(block, local),
            shape(block, local),
            shape(2, block, local, kind=high),
            shape(heads, 2, block, wide),
        ),
        in_specs=[SMEM] * 3 + [VMEM] * 3,
        out_specs=(VMEM,) * 4,
        scratch_shapes=[
            pltpu.VMEM((heads, HEAD_DIM + 16, block), high),
            pltpu.VMEM((heads, 1, block), high),
        ],
        cost_estimate=cost(NEAR_COST, 8 << 20),
    )(here, seg_q, seg_k, q_near, keys_wide, values_t)


FAR_COST = 20 * 10**9
NEAR_COST = 12 * 10**9
FEED_COST = 26 * 10**9
UNIT_COST = 12 * 10**9
BACK_COST = 24 * 10**9
LAST_COST = 9 * 10**9
SMALL_COST = 3 * 10**9


def feed_kernel(*refs, plan, count, hidden, local):
    here, x_all, g_all, att_0, att_1, att_2, att_3, vec_ref = refs[:8]
    w_refs = refs[8 : 8 + count]
    (out_ref, one_ref, stat_ref, ga_0, ga_1, ga_2, ga_3, rows_hbm, keep_hbm, send_hbm) = refs[8 + count : 18 + count]
    (w_ref, b_ref, x_ref, g_ref, att_ref, hat_ref, inv_ref, norm_ref, acc_ref, slope_ref, gl_ref,
     rows_ref, keep_ref, send_ref, sems, out_sems) = refs[18 + count :]
    puts = []

    def put(src, dst):
        puts.append(pltpu.make_async_copy(src, dst, out_sems.at[len(puts)]))
        puts[-1].start()

    tokens, width = x_ref.shape
    mine, f, c = here[0], here[1], here[2]
    wide = 2 * hidden + local
    copies = []

    def begin(src, dst):
        copies.append(pltpu.make_async_copy(src, dst, sems.at[len(copies)]))
        copies[-1].start()

    first = pl.multiple_of(mine * tokens, tokens)
    begin(x_all.at[pl.ds(first, tokens)], x_ref)
    begin(g_all.at[pl.ds(first, tokens)], g_ref)
    for r, att in enumerate((att_0, att_1, att_2, att_3)):
        begin(att, att_ref.at[r])
    for i, offset, r, mark in plan:
        if mark is None:
            begin(w_refs[i].at[pl.ds(offset, 8)], b_ref.at[r])
        else:
            start, size = mark(f, c)
            begin(w_refs[i].at[pl.ds(offset, size)], w_ref.at[r, pl.ds(start, size)])
    for copy in copies:
        copy.wait()
    b_out, gain_one, shift_one, b_outer, gain_two, shift_two = (
        vec_ref[i : i + 1, :].astype(high) for i in range(6)
    )

    def weights(r, first, last):
        return w_ref[r, :, first:last]

    acc_ref[...] = nt(att_ref[0], weights(0, 2 * hidden, 2 * hidden + local))
    for r in range(1, 4):
        acc_ref[...] += nt(att_ref[r], weights(r, 2 * hidden, 2 * hidden + local))
    step = 64
    chunks = tokens // step

    def first_norm(i, carry):
        span = pl.ds(pl.multiple_of(i * step, step), step)
        hat, inverse = norm_parts(x_ref[span, :].astype(high) + (acc_ref[span, :] + b_out))
        hat_ref[span, :] = hat
        inv_ref[span, :] = inverse
        normed = hat * gain_one + shift_one
        norm_ref[span, :] = normed.astype(low)
        acc_ref[span, :] = normed + b_outer
        return carry

    lax.fori_loop(0, chunks, first_norm, 0)
    part = 256
    for k, side in enumerate((keep_ref, send_ref)):
        for x in range(2):
            side[x, :, 2 * hidden : wide] = att_ref[2 * x + k]
            side[x, :, wide:] = jnp.zeros((tokens, side.shape[2] - wide), low)

        def up(x, carry, k=k, side=side):
            r = 2 * x + k
            for j in range(0, hidden, part):
                inner = nn(norm_ref[...], weights(r, j, j + part))
                inner = inner + b_ref[r, 0:1, j : j + part].astype(high)
                act, slope = gelu_parts(inner)
                side[x, :, hidden + j : hidden + j + part] = act.astype(low)
                slope_ref[r, :, j : j + part] = slope
            acc_ref[...] += nt(side[x, :, hidden : 2 * hidden], weights(r, hidden, 2 * hidden))
            return carry

        lax.fori_loop(0, 2, up, 0)

    zero = jnp.zeros((1, width), high)

    def second_norm(i, sums):
        span = pl.ds(pl.multiple_of(i * step, step), step)
        hat, inverse = norm_parts(acc_ref[span, :])
        out_ref[span, :] = (hat * gain_two + shift_two).astype(low)
        grad = g_ref[span, :].astype(high)
        two = norm_back(grad, hat, inverse, gain_two)
        acc_ref[span, :] = two
        two_low = two.astype(low)
        gl_ref[span, :] = two_low
        terms = (two_low.astype(high), grad * hat, grad)
        return tuple(s + jnp.sum(v, axis=0, keepdims=True) for s, v in zip(sums, terms))

    sums_two = lax.fori_loop(0, chunks, second_norm, (zero,) * 3)
    rows_ref[0] = norm_ref[...].T
    rows_ref[1] = gl_ref[...].T
    put(rows_ref.at[pl.ds(0, 2)], rows_hbm.at[pl.ds(0, 2)])
    for k, side in ((1, send_ref), (0, keep_ref)):

        def down(x, carry, k=k, side=side):
            r = 2 * x + k
            for j in range(0, hidden, part):
                grad = nn(gl_ref[...], weights(r, hidden + j, hidden + j + part))
                grad = (grad * slope_ref[r, :, j : j + part]).astype(low)
                side[x, :, j : j + part] = grad
                stat_ref[8 + r, 0:1, j : j + part] = jnp.sum(grad.astype(high), axis=0, keepdims=True)
            acc_ref[...] += nt(side[x, :, :hidden], weights(r, 0, hidden))
            return carry

        lax.fori_loop(0, 2, down, 0)
        put(side, send_hbm if k else keep_hbm)

    def first_back(i, sums):
        span = pl.ds(pl.multiple_of(i * step, step), step)
        grad = acc_ref[span, :]
        hat = hat_ref[span, :]
        one = norm_back(grad, hat, inv_ref[span, :], gain_one)
        one_ref[span, :] = one
        one_low = one.astype(low)
        gl_ref[span, :] = one_low
        terms = (one_low.astype(high), grad * hat, grad)
        return tuple(s + jnp.sum(v, axis=0, keepdims=True) for s, v in zip(sums, terms))

    sums_one = lax.fori_loop(0, chunks, first_back, (zero,) * 3)
    for i, value in enumerate(sums_one + sums_two):
        stat_ref[i, 0:1, :] = value
    rows_ref[2] = gl_ref[...].T
    put(rows_ref.at[2], rows_hbm.at[2])
    for r, ga in enumerate((ga_0, ga_1, ga_2, ga_3)):
        ga[...] = nn(gl_ref[...], weights(r, 2 * hidden, 2 * hidden + local)).astype(low)
    for copy in puts:
        copy.wait()


def feed(here, x, grad, att, vectors, pieces, plan, tokens, hidden, local):
    width = x.shape[1]
    wide = 2 * hidden + local
    padded = (wide + 127) // 128 * 128
    copies = 6 + len(plan)
    return pl.pallas_call(
        lambda *refs: feed_kernel(*refs, plan=plan, count=len(pieces), hidden=hidden, local=local),
        name="feed",
        out_shape=(
            shape(tokens, width),
            shape(tokens, width, kind=high),
            shape(12, 1, width, kind=high),
            shape(tokens, local),
            shape(tokens, local),
            shape(tokens, local),
            shape(tokens, local),
            shape(3, width, tokens),
            shape(2, tokens, padded),
            shape(2, tokens, padded),
        ),
        in_specs=[SMEM] + [ANY] * 6 + [VMEM] + [ANY] * len(pieces),
        out_specs=(VMEM,) * 7 + (HBM,) * 3,
        scratch_shapes=[
            pltpu.VMEM((4, width, wide), low),
            pltpu.VMEM((4, 8, wide), low),
            pltpu.VMEM((tokens, width), low),
            pltpu.VMEM((tokens, width), low),
            pltpu.VMEM((4, tokens, local), low),
            pltpu.VMEM((tokens, width), high),
            pltpu.VMEM((tokens, 1), high),
            pltpu.VMEM((tokens, width), low),
            pltpu.VMEM((tokens, width), high),
            pltpu.VMEM((4, tokens, hidden), high),
            pltpu.VMEM((tokens, width), low),
            pltpu.VMEM((3, width, tokens), low),
            pltpu.VMEM((2, tokens, padded), low),
            pltpu.VMEM((2, tokens, padded), low),
            pltpu.SemaphoreType.DMA((copies,)),
            pltpu.SemaphoreType.DMA((4,)),
        ],
        cost_estimate=cost(FEED_COST, 24 << 20),
    )(here, x, grad, *att, vectors, *pieces)


def unit_kernel(here, rows_own, rows_mate, wide_own, wide_mate, *refs, hidden):
    ak_ref, as_ref, bk_ref, bs_ref, rows_ref, wide_ref, sems = refs
    c = here[2]
    tokens = rows_own.shape[2]
    wide = ak_ref.shape[2]
    half = ak_ref.shape[1]
    mid = rows_own.shape[1] // 2
    copies = [
        pltpu.make_async_copy(rows_own, rows_ref.at[:, :, pl.ds(0, tokens)], sems.at[0]),
        pltpu.make_async_copy(wide_own, wide_ref.at[:, pl.ds(0, tokens)], sems.at[1]),
        pltpu.make_async_copy(rows_mate, rows_ref.at[:, :, pl.ds(tokens, tokens)], sems.at[2]),
        pltpu.make_async_copy(wide_mate, wide_ref.at[:, pl.ds(tokens, tokens)], sems.at[3]),
    ]
    for copy in copies:
        copy.start()
    for copy in copies:
        copy.wait()
    spans = ((0, 0, hidden), (1, hidden, 2 * hidden), (2, 2 * hidden, wide))
    for x in range(2):
        for i, first, last in spans:
            for top in range(2):
                part = slice(top * mid, (top + 1) * mid)
                got = nn(rows_ref[i, part, :], wide_ref[x, :, first:last]).astype(low)
                if top == 0:
                    side = ak_ref if x == 0 else as_ref
                    side[:, :, first:last] = got.reshape(-1, half, last - first)
                else:
                    got = got.reshape(-1, 2, half, last - first)
                    for z in range(got.shape[0]):

                        @pl.when(c == 0)
                        def _():
                            bk_ref[x, z, :, first:last] = got[z, 0]
                            bs_ref[x, z, :, first:last] = got[z, 1]

                        @pl.when(c != 0)
                        def _():
                            bk_ref[x, z, :, first:last] = got[z, 1]
                            bs_ref[x, z, :, first:last] = got[z, 0]


def unit_grads(here, rows, mate_rows, keep, mate, half, hidden, local):
    wide = 2 * hidden + local
    tokens = rows.shape[2]
    width = rows.shape[1]
    quarters = width // 4 // half
    return pl.pallas_call(
        lambda *refs: unit_kernel(*refs, hidden=hidden),
        name="unit_grads",
        out_shape=(
            shape(2 * quarters, half, wide),
            shape(2 * quarters, half, wide),
            shape(2, quarters, half, wide),
            shape(2, quarters, half, wide),
        ),
        in_specs=[SMEM] + [ANY] * 4,
        out_specs=(VMEM,) * 4,
        scratch_shapes=[
            pltpu.VMEM((3, width, 2 * tokens), low),
            pltpu.VMEM((2, 2 * tokens, keep.shape[2]), low),
            pltpu.SemaphoreType.DMA((4,)),
        ],
        cost_estimate=cost(UNIT_COST, 14 << 20),
    )(here, rows, mate_rows, keep, mate)


def merge_one_kernel(here, ak, ga, bk, gb, a_keep, a_send, b_keep, b_send):
    c = here[2]
    for z in range(2):
        for side in range(2):
            i = 2 * z + side
            got = ak[i] + ga[i]

            @pl.when(c == side)
            def _():
                a_keep[z] = got

            @pl.when(c != side)
            def _():
                a_send[z] = got

    b_keep[...] = bk[0] + gb[0]
    b_send[...] = bk[1] + gb[1]


def merge_one(here, ak, ga, bk, gb):
    out = shape(*bk.shape[1:])
    return pl.pallas_call(
        merge_one_kernel,
        name="merge_one",
        out_shape=(out,) * 4,
        in_specs=[SMEM] + [VMEM] * 4,
        out_specs=(VMEM,) * 4,
        cost_estimate=cost(SMALL_COST, 8 << 20),
    )(here, ak, ga, bk, gb)


def merge_two_kernel(here, a_keep, a_got, b_keep, b_got, d_keep, d_got, *refs, start):
    outs, all_ref = refs[:4], refs[4]
    f = here[1]
    wide = a_keep.shape[2]
    for z in range(2):
        all_ref[z, :, :wide] = a_keep[z] + a_got[z]
        all_ref[2 + z, :, :wide] = b_keep[z] + b_got[z]
    all_ref[:, :, start:] = d_keep[...] + d_got[...]
    for s, out in enumerate(outs):
        out[...] = all_ref[(f + s) % 4]


def merge_two(here, a_keep, a_got, b_keep, b_got, d_keep, d_got, start):
    half = a_keep.shape[1]
    full = start + d_keep.shape[2]
    return pl.pallas_call(
        lambda *refs: merge_two_kernel(*refs, start=start),
        name="merge_two",
        out_shape=(shape(half, full),) * 4,
        in_specs=[SMEM] + [VMEM] * 6,
        out_specs=(VMEM,) * 4,
        scratch_shapes=[pltpu.VMEM((4, half, full), low)],
        cost_estimate=cost(SMALL_COST, 8 << 20),
    )(here, a_keep, a_got, b_keep, b_got, d_keep, d_got)


def merge_three_kernel(here, own, got_1, got_2, got_3, out, all_ref):
    f = here[1]
    for s, piece in enumerate((own, got_1, got_2, got_3)):
        all_ref[(f - s + 4) % 4] = piece[...]
    total = all_ref[0].astype(high)
    for z in range(1, 4):
        total = total + all_ref[z].astype(high)
    out[...] = total.astype(low)


def merge_three(here, pieces):
    return pl.pallas_call(
        merge_three_kernel,
        name="merge_three",
        out_shape=shape(*pieces[0].shape),
        in_specs=[SMEM] + [VMEM] * 4,
        out_specs=VMEM,
        scratch_shapes=[pltpu.VMEM((4,) + pieces[0].shape, low)],
        cost_estimate=cost(SMALL_COST, 4 << 20),
    )(here, *pieces)


def finish_kernel(here, own, got, inner, outer, out, query, key, value, bias, all_ref, *, start):
    c = here[2]
    hidden = inner.shape[1]
    local = query.shape[1]
    all_ref[c] = own[...]
    all_ref[1 - c] = got[...]
    half, full = own.shape

    def cols(first, last):
        return all_ref[:, :, first:last].reshape(2 * half, last - first).astype(high)

    inner[...] = cols(0, hidden)
    outer[...] = cols(hidden, 2 * hidden)
    out[...] = cols(2 * hidden, 2 * hidden + local).T
    rest = cols(start, full)
    query[...] = rest[:, :local]
    key[...] = rest[:, local : 2 * local]
    value[...] = rest[:, 2 * local : 3 * local]
    bias[...] = own[:16, start + 3 * local :].astype(high)


def finish(here, own, got, start, hidden, local):
    half, full = own.shape
    piece = 2 * half
    return pl.pallas_call(
        lambda *refs: finish_kernel(*refs, start=start),
        name="finish",
        out_shape=(
            shape(piece, hidden, kind=high),
            shape(piece, hidden, kind=high),
            shape(local, piece, kind=high),
            shape(piece, local, kind=high),
            shape(piece, local, kind=high),
            shape(piece, local, kind=high),
            shape(16, full - start - 3 * local, kind=high),
        ),
        in_specs=[SMEM] + [VMEM] * 2,
        out_specs=(VMEM,) * 7,
        scratch_shapes=[pltpu.VMEM((2, half, full), low)],
        cost_estimate=cost(SMALL_COST, 4 << 20),
    )(here, own, got)


def spread_kernel(here, p_0, p_1, p_2, p_3, out):
    tokens = p_0.shape[0]
    for r, piece in enumerate((p_0, p_1, p_2, p_3)):
        first = pl.multiple_of((here[0] ^ r) * tokens, tokens)
        out[pl.ds(first, tokens), :] = piece[...].astype(out.dtype)


def spread(here, pieces, kind):
    tokens, width = pieces[0].shape
    return pl.pallas_call(
        spread_kernel,
        name="spread",
        out_shape=shape(4 * tokens, width, kind=kind),
        in_specs=[SMEM] + [VMEM] * 4,
        out_specs=VMEM,
        cost_estimate=cost(SMALL_COST, 8 << 20),
    )(here, *pieces)


def project_back_kernel(here, g_ref, edge_ref, x_ref, w_ref, keep, send, d_keep, d_send, all_ref, *, local):
    mine, c = here[0], here[2]
    rows = g_ref.shape[0]
    rim = edge_ref.shape[0]
    tokens = keep.shape[1]
    half = d_keep.shape[1]
    pad = d_keep.shape[2] - 3 * local
    all_ref[...] = g_ref[...]
    edge = pl.ds(pl.multiple_of((1 - c) * (rows - rim), rim), rim)
    all_ref[edge, local:] = (
        g_ref[edge, local:].astype(high) + edge_ref[...].astype(high)
    ).astype(low)
    for k, side in ((1, send), (0, keep)):
        for x in range(2):
            first = pl.multiple_of((mine ^ (2 * x + k)) * tokens, tokens)
            side[x] = nt(all_ref[pl.ds(first, tokens), :], w_ref[...]).astype(low)
    sums = jnp.zeros((1, 3 * local), high)
    for i in range(rows // tokens):
        part = all_ref[i * tokens : (i + 1) * tokens, :].astype(high)
        sums = sums + jnp.sum(part, axis=0, keepdims=True)
    row = lax.broadcasted_iota(jnp.int32, (half, pad), 0)
    extra = jnp.zeros((half, pad), high)
    for j in range(3 * local // pad):
        extra = jnp.where(row == j, sums[:, j * pad : (j + 1) * pad], extra)
    extra = extra.astype(low)
    got = tn(x_ref[...], all_ref[...]).astype(low).reshape(-1, 2, half, 3 * local)
    for z in range(got.shape[0]):
        d_keep[z, :, 3 * local :] = extra
        d_send[z, :, 3 * local :] = extra
        for side in range(2):

            @pl.when(c == side)
            def _():
                d_keep[z, :, : 3 * local] = got[z, side]

            @pl.when(c != side)
            def _():
                d_send[z, :, : 3 * local] = got[z, side]


def project_back(here, grads, edge, x, weights, tokens, half):
    rows, width = x.shape
    local = grads.shape[1] // 3
    pad = HEAD_DIM
    return pl.pallas_call(
        lambda *refs: project_back_kernel(*refs, local=local),
        name="project_back",
        out_shape=(
            shape(2, tokens, width),
            shape(2, tokens, width),
            shape(width // half // 2, half, 3 * local + pad),
            shape(width // half // 2, half, 3 * local + pad),
        ),
        in_specs=[SMEM] + [VMEM] * 4,
        out_specs=(VMEM,) * 4,
        scratch_shapes=[pltpu.VMEM(grads.shape, low)],
        cost_estimate=cost(LAST_COST, 8 << 20),
    )(here, grads, edge, x, weights)


def attend_back_kernel(
    here, seg_q, seg_k, g_0, g_1, g_2, g_3, full_near, full_far, q_near, q_far, ka_ref, v_ref, own_ref, rim_ref,
    g_ref, kt_ref, va_ref, ga_ref, dka_ref, dva_ref, dqa_ref, sems, *, block, width, heads
):
    copies = [
        pltpu.make_async_copy(g, g_ref.at[r], sems.at[r]) for r, g in enumerate((g_0, g_1, g_2, g_3))
    ]
    for copy in copies:
        copy.start()
    keys = v_ref.shape[0]
    rows = own_ref.shape[0]
    local = heads * HEAD_DIM
    scale = 1.0 / math.sqrt(HEAD_DIM)
    mine = here[0]
    for h in range(heads):
        cols = slice(h * HEAD_DIM, (h + 1) * HEAD_DIM)
        kt_ref[h] = ka_ref[h, :, :HEAD_DIM].T
        va_ref[h] = jnp.concatenate([v_ref[:, cols], jnp.ones((keys, HEAD_DIM), low)], axis=1)
    dka_ref[...] = jnp.zeros_like(dka_ref)
    dva_ref[...] = jnp.zeros_like(dva_ref)
    for copy in copies:
        copy.wait()

    for base, q_ref, full_ref in ((0, q_near, full_near), (2, q_far, full_far)):

        def one_part(i, carry, base=base, q_ref=q_ref, full_ref=full_ref):
            first_q = pl.multiple_of((mine ^ (base + i)) * block, block)
            for h in range(heads):
                cols = slice(h * HEAD_DIM, (h + 1) * HEAD_DIM)
                grad = g_ref[base + i, :, cols]
                delta = jnp.sum(grad.astype(high) * full_ref[i, :, cols], axis=1, keepdims=True)
                lane = lax.broadcasted_iota(jnp.int32, (block, HEAD_DIM), 1)
                extra = jnp.zeros((block, HEAD_DIM), high)
                for j, piece in enumerate(three(-delta)):
                    extra = jnp.where(lane == j, piece.astype(high), extra)
                ga_ref[h] = jnp.concatenate([grad, extra.astype(low)], axis=1)
            dqa_ref[...] = jnp.zeros_like(dqa_ref)

            def one_block(b, carry):
                first_k = b * width

                @pl.when(meets(seg_q, first_q, block, seg_k, first_k, width))
                def _():
                    for h in range(heads):
                        span = pl.ds(first_k, width)
                        asks = q_ref[h, i]
                        probs = jnp.exp(nt(ka_ref[h, span, :], asks))
                        slopes = (probs * nt(va_ref[h, span, :], ga_ref[h])).astype(low)
                        dva_ref[h, span, :] += nn(probs.astype(low), ga_ref[h, :, :HEAD_DIM])
                        dka_ref[h, span, :] += nn(slopes, asks[:, :HEAD_DIM])
                        dqa_ref[h] += nn(kt_ref[h, :, span], slopes)

                return carry

            lax.fori_loop(0, keys // width, one_block, 0)
            own_ref[pl.ds(first_q, block), :local] = jnp.concatenate(
                [(dqa_ref[h] * scale).T for h in range(heads)], axis=1
            ).astype(low)
            return carry

        lax.fori_loop(0, 2, one_part, 0)
    for j, part in enumerate((dka_ref, dva_ref)):
        wide = jnp.concatenate([part[h] for h in range(heads)], axis=1).astype(low)
        own_ref[:, (1 + j) * local : (2 + j) * local] = wide[:rows]
        rim_ref[:, j * local : (j + 1) * local] = wide[rows:]


def attend_back(here, seg_q, seg_k, grads, full_near, full_far, q_near, q_far, keys, values):
    parts = len(grads)
    block, local = grads[0].shape
    rows = parts * block
    count = values.shape[0]
    heads = local // HEAD_DIM
    return pl.pallas_call(
        lambda *refs: attend_back_kernel(*refs, block=block, width=256, heads=heads),
        name="attend_back",
        out_shape=(shape(rows, 3 * local), shape(count - rows, 2 * local)),
        in_specs=[SMEM] * 3 + [ANY] * 4 + [VMEM] * 6,
        out_specs=(VMEM,) * 2,
        scratch_shapes=[
            pltpu.VMEM((parts, block, local), low),
            pltpu.VMEM((heads, HEAD_DIM, count), low),
            pltpu.VMEM((heads, count, 2 * HEAD_DIM), low),
            pltpu.VMEM((heads, block, 2 * HEAD_DIM), low),
            pltpu.VMEM((heads, count, HEAD_DIM), high),
            pltpu.VMEM((heads, count, HEAD_DIM), high),
            pltpu.VMEM((heads, HEAD_DIM, block), high),
            pltpu.SemaphoreType.DMA((parts,)),
        ],
        cost_estimate=cost(BACK_COST, 8 << 20),
    )(here, seg_q, seg_k, *grads, full_near, full_far, q_near, q_far, keys, values)


def after(values, gate):
    return lax.optimization_barrier((tuple(values), gate))[0]


def halo_of(value, c, span):
    rows = value.shape[0]
    return take(value, (1 - c) * (rows - span), span)


def shards(
    inputs, segments, w_query, b_query, w_key, w_value, b_value, w_out, b_out, gain_one, shift_one,
    w_inner, b_inner, w_outer, b_outer, gain_two, shift_two, grad_output,
):
    rows, width = inputs.shape
    local = w_query.shape[1]
    hidden = w_inner.shape[1]
    n_f, n_c, n_t = (lax.axis_size(a) for a in ("fsdp", "ctx", "tp"))
    f, c, t = (lax.axis_index(a) for a in ("fsdp", "ctx", "tp"))
    tokens = rows // n_t
    rim = MOST
    quick = n_f == 4 and n_c == 2 and n_t == 4
    piece = width // n_f
    flip = [t ^ r for r in range(n_t)]

    half = piece // 2
    blocks = (2 * n_f, half)
    here = jnp.stack([t, f, c]).astype(jnp.int32)
    bundle_a = jnp.concatenate([w_query, w_key, w_value], axis=1)

    def spot(s, side):
        def mark(f, c):
            return (f - s + n_f) % n_f * 2 + (c if side == 0 else 1 - c), 1

        return mark

    def spot_from(s):
        return lambda f, c: ((f - s + n_f) % n_f * 2, 2)

    def spot_all(f, c):
        return 0, 2 * n_f

    def in_rows(mark):
        def rows_mark(f, c):
            first, count = mark(f, c)
            return (first if isinstance(first, int) else pl.multiple_of(first * half, half)), count * half

        return rows_mark

    seg_own = segments.reshape(rows)
    if quick:
        halves_a = bundle_a.reshape(2, half, -1)
        pieces_a = [halves_a] + [shift(halves_a, "fsdp", s) for s in range(1, n_f)]
        marks_a = [spot_from(s) for s in range(n_f)]
    else:
        whole_a = lax.all_gather(bundle_a, "fsdp", axis=0, tiled=True)
        pieces_a, marks_a = [whole_a.reshape(blocks + (-1,))], [spot_all]

    if n_c == 2:
        sent = halo_of(inputs, c, rim)
        if quick:
            part = rim // 2
            got = swap(take(sent, (t & 1) * part, part), "ctx", 1)
            mate = swap(got, "tp", 1)
            even = (t & 1) == 0
            halo_in = jnp.concatenate([jnp.where(even, got, mate), jnp.where(even, mate, got)], axis=0)
        else:
            halo_in = swap(sent, "ctx", 1)
        halo_seg = swap(halo_of(seg_own, c, rim), "ctx", 1)
    else:
        ahead = [(i, i + 1) for i in range(n_c - 1)]
        behind = [(i + 1, i) for i in range(n_c - 1)]

        def both(value):
            return jnp.concatenate(
                [
                    lax.ppermute(value[rows - rim :], "ctx", ahead),
                    lax.ppermute(value[:rim], "ctx", behind),
                ],
                axis=0,
            )

        halo_in = both(inputs)
        halo_seg = both(seg_own + 1) - 1
        halo_seg = jnp.where(halo_seg < 0, NO_ID, halo_seg)

    bias_row = jnp.pad(b_inner[None], ((0, 7), (0, hidden + local)))
    bundle_f = jnp.concatenate([w_inner, w_outer.T, w_out.T], axis=1)
    own_rows = jnp.concatenate([bundle_f, bias_row], axis=0)
    if quick:
        far_rows = swap(own_rows, "tp", 2)
        own_f = take(bundle_f, c * half, half)
        gots = [shift(own_f, "fsdp", s) for s in range(1, n_f)]
        halo_in, far_rows = lax.optimization_barrier((halo_in, far_rows))
        far_f = take(far_rows, (1 - c) * half, half)

    bias = jnp.concatenate([b_query, jnp.zeros_like(b_query), b_value]).astype(high)[None]
    seg_all = jnp.concatenate([seg_own, halo_seg])
    lane = jnp.arange(IDS)
    near_id = seg_all[:, None] == lane
    mask_k = (near_id | ((lane >= LSE_LANE) & (lane < LSE_LANE + 3))).astype(low)
    mask_q = jnp.where(near_id[:rows] | ((lane >= LSE_LANE) & (lane < LSE_LANE + 3)), 0.0, FAR).astype(low)
    att_2, att_3, full_far, q_near, q_far, keys_wide, values, values_t, w_qkv = attend_far(
        here, seg_own, seg_all, inputs, halo_in, bias, mask_q, mask_k, pieces_a, marks_a, blocks, tokens
    )
    w_qkv = w_qkv.reshape(width, 3 * local)
    att_0, att_1, full_near, q_near = attend_near(here, seg_own, seg_all, q_near, keys_wide, values_t)
    att = [att_0, swap(att_1, "tp", 1), swap(att_2, "tp", 2), swap(att_3, "tp", 3)]

    if quick:
        pieces_f, plan = [], []

        def add(r, value, marks, gate=None, bias=False):
            twin = value
            if gate is not None:
                (twin,) = after([value], gate)
            for r, piece in ((r, value), (r + 1, swap(twin, "tp", 1))):
                offset = 0
                for mark in marks:
                    plan.append((len(pieces_f), offset, r, in_rows(mark)))
                    offset += half
                if bias:
                    plan.append((len(pieces_f), piece_rows, r, None))
                pieces_f.append(piece)

        piece_rows = piece
        add(0, own_rows, [spot_from(0)], att_2, bias=True)
        add(2, far_rows, [spot_from(0)], att_2, bias=True)
        near = []
        for s, got in enumerate(gots, 1):
            near += after([got], att_2)
            add(0, got, [spot(s, 0)], att_2)
        near = jnp.concatenate(near, axis=0)
        steps = range(1, n_f)
        add(2, swap(near, "tp", 2), [spot(s, 0) for s in steps], att_0)
        add(0, swap(near, "ctx", 1), [spot(s, 1) for s in steps], att_0)
        for s in steps:
            add(2, shift(far_f, "fsdp", s), [spot(s, 1)], att_0)
    else:
        gathered = lax.all_gather(bundle_f, "fsdp", axis=0, tiled=True)
        gathered = jnp.concatenate([gathered, bias_row], axis=0)
        gathered = lax.all_gather(gathered, "tp", axis=0)
        pieces_f = [lax.dynamic_index_in_dim(gathered, i, 0, keepdims=False) for i in flip]
        plan = [(r, 0, r, in_rows(spot_all)) for r in range(n_t)]
        plan += [(r, width, r, None) for r in range(n_t)]

    vectors = jnp.stack([b_out, gain_one, shift_one, b_outer, gain_two, shift_two, b_out, b_out])
    output, g_one, stats, ga_0, ga_1, ga_2, ga_3, rows_t, keep, send = feed(
        here, inputs, grad_output, att, vectors, pieces_f, plan, tokens, hidden, local
    )
    g_att = [ga_0, swap(ga_1, "tp", 1), swap(ga_2, "tp", 2), swap(ga_3, "tp", 3)]
    stats = stats[:, 0]

    if quick:
        mate_rows = swap(rows_t, "tp", 1)
        mate = swap(send, "tp", 1)
        pair = jnp.concatenate([stats[:6], stats[8:9], stats[10:11]], axis=0)
        away = jnp.concatenate([stats[:6], stats[9:10], stats[11:12]], axis=0)
        pair = pair + swap(away, "tp", 1)
        away = jnp.concatenate([pair[:6], pair[7:8], pair[7:8]], axis=0)
        pair = pair + swap(away, "tp", 2)
        pair = pair + swap(pair, "ctx", 1)
        keep_a, send_a, keep_b, send_b = unit_grads(here, rows_t, mate_rows, keep, mate, half, hidden, local)
        send_a, send_b, pair = lax.optimization_barrier((send_a, send_b, pair))
        got_a = swap(send_a, "tp", 2)
        got_b = swap(send_b, "ctx", 1)
        pair = pair + swap(pair, "fsdp", 1)
        *g_att, keep_a, keep_b = lax.optimization_barrier((*g_att, keep_a, keep_b))
    else:
        ordered = []
        for r in range(n_t):
            wide = (keep, send)[r % 2][r // 2]
            ordered.append(
                jnp.concatenate(
                    [
                        nn(rows_t[0], wide[:, :hidden]),
                        nn(rows_t[1], wide[:, hidden : 2 * hidden]),
                        nn(rows_t[2], wide[:, 2 * hidden : 2 * hidden + local]),
                    ],
                    axis=1,
                )
            )
        stacked = jnp.stack(ordered)
        ordered = jnp.stack([lax.dynamic_index_in_dim(stacked, i, 0, keepdims=False) for i in flip])
        mine = lax.psum_scatter(ordered, "tp", scatter_dimension=0, tiled=False)
        mine = lax.psum(mine, ("fsdp", "ctx"))
        shard_f = take(mine, f * piece, piece)

    g_own, g_rim = attend_back(
        here, seg_own, seg_all, g_att, full_near, full_far, q_near, q_far, keys_wide, values
    )
    if quick:
        got_a, got_b = after([got_a, got_b], g_own)
        (rim_out,) = after([g_rim], (got_a, got_b, pair))
        pair = pair + swap(pair, "fsdp", 2)
        edge = swap(rim_out, "ctx", 1)
        keep_a, send_a, keep_b, send_b = merge_one(here, keep_a, got_a, keep_b, got_b)
        got_a = swap(send_a, "ctx", 1)
        got_b = swap(send_b, "tp", 2)
        dx_keep, dx_send, d_keep, d_send = project_back(here, g_own, edge, inputs, w_qkv, tokens, half)
        dx_got = swap(dx_send, "tp", 1)
        d_got = swap(d_send, "ctx", 1)
        near_dx = dx_keep[0] + dx_got[0]
        far_dx = dx_keep[1] + dx_got[1]
        far_got = swap(far_dx, "tp", 2)
        start = (2 * hidden + local + 127) // 128 * 128
        keep_a, pair = lax.optimization_barrier((keep_a, pair))
        outs = merge_two(here, keep_a, got_a, keep_b, got_b, d_keep, d_got, start)
        totals = [outs[0]] + [shift(outs[s], "fsdp", s) for s in range(1, n_f)]
        mine = (near_dx.astype(high) + far_got.astype(high) + g_one).astype(low)

        def everyone(value, kind):
            far_value = swap(value, "tp", 2)
            return spread(here, [value, swap(value, "tp", 1), far_value, swap(far_value, "tp", 1)], kind)

        output = everyone(output, low)
        grad_inputs = everyone(mine, high)
        total = merge_three(here, totals)
        s_inner, s_outer, s_out, s_query, s_key, s_value, s_bias = finish(
            here, total, swap(total, "ctx", 1), start, hidden, local
        )
        s_outer = s_outer.T
        s_qkv = s_bias.reshape(-1)[: 3 * local]
        shared, s_b_inner = pair[:6], pair[6]
    else:
        edge_got = []
        if n_c == 2:
            edge_got.append(((1 - c) * (rows - rim), swap(g_rim, "ctx", 1)))
        else:
            edge_got.append((0, lax.ppermute(g_rim[rim:], "ctx", ahead)))
            edge_got.append((rows - rim, lax.ppermute(g_rim[:rim], "ctx", behind)))
        g_all = g_own.astype(high)
        for first, got in edge_got:
            got = jnp.pad(got.astype(high), ((0, 0), (local, 0)))
            g_all = place(g_all, take(g_all, first, rim) + got, first)
        g_all = g_all.astype(low)
        part = nt(g_all, w_qkv).reshape(n_t, tokens, width)
        mine = lax.psum_scatter(part, "tp", scatter_dimension=0, tiled=False)
        grad_inputs = lax.all_gather((mine + g_one).astype(low), "tp", axis=0, tiled=True).astype(high)
        output = lax.all_gather(output, "tp", axis=0, tiled=True)
        shard_a = take(lax.psum(tn(inputs, g_all), ("fsdp", "ctx")), f * piece, piece)
        s_query, s_key, s_value = (shard_a[:, i * local : (i + 1) * local] for i in range(3))
        s_qkv = lax.psum(jnp.sum(g_all.astype(high), axis=0), ("fsdp", "ctx"))
        s_inner, s_outer, s_out = shard_f[:, :hidden], shard_f[:, hidden : 2 * hidden].T, shard_f[:, 2 * hidden :].T
        ordered = jnp.stack([lax.dynamic_index_in_dim(stats[8:], i, 0, keepdims=False) for i in flip])
        s_b_inner = lax.psum(
            lax.psum_scatter(ordered, "tp", scatter_dimension=0, tiled=False), ("fsdp", "ctx")
        )
        shared = lax.psum(stats[:6], ("fsdp", "ctx", "tp"))
    return (
        output,
        grad_inputs,
        s_query,
        s_qkv[:local],
        s_key,
        s_value,
        s_qkv[2 * local :],
        s_out,
        shared[0],
        shared[1],
        shared[2],
        s_inner,
        s_b_inner,
        s_outer,
        shared[3],
        shared[4],
        shared[5],
    )


def solution(mesh):
    rows = P(("fsdp", "ctx"), None)
    down, flat, across = P("fsdp", "tp"), P("tp"), P("tp", "fsdp")
    return jax.shard_map(
        shards,
        mesh=mesh,
        in_specs=(
            rows, P("fsdp", "ctx"), down, flat, down, down, flat, across, P(), P(), P(), down, flat,
            across, P(), P(), P(), rows,
        ),
        out_specs=(
            rows, rows, down, flat, down, down, flat, across, P(), P(), P(), down, flat, across,
            P(), P(), P(),
        ),
        check_vma=False,
    )
```

```python
import math

import jax
import jax.numpy as jnp
from jax import lax
from jax.experimental import pallas as pl
from jax.experimental.pallas import tpu as pltpu
from jax.sharding import PartitionSpec as P

HEAD_DIM = 64
MOST = 512
IDS = 64
NO_ID = 63
LSE_LANE = 60
FAR = -1e30

layer_eps = 1e-12
low = jnp.bfloat16
high = jnp.float32


def nn(left, right):
    return jnp.dot(left, right, preferred_element_type=high)


def nt(left, right):
    return lax.dot_general(left, right, (((1,), (1,)), ((), ())), preferred_element_type=high)


def tn(left, right):
    return lax.dot_general(left, right, (((0,), (0,)), ((), ())), preferred_element_type=high)


def swap(value, axis, bit):
    count = lax.axis_size(axis)
    return lax.ppermute(value, axis, [(i, i ^ bit) for i in range(count)])


def shift(value, axis, step):
    count = lax.axis_size(axis)
    return lax.ppermute(value, axis, [(i, (i + step) % count) for i in range(count)])


def place(whole, part, first):
    return lax.dynamic_update_slice_in_dim(whole, part, first, 0)


def take(whole, first, count):
    return lax.dynamic_slice_in_dim(whole, first, count, 0)


def norm_parts(hidden):
    average = jnp.mean(hidden, axis=-1, keepdims=True)
    centred = hidden - average
    variance = jnp.mean(centred * centred, axis=-1, keepdims=True)
    inverse = lax.rsqrt(variance + layer_eps)
    return centred * inverse, inverse


def norm_back(grad, hat, inverse, gain):
    scaled = grad * gain
    first = jnp.mean(scaled, axis=-1, keepdims=True)
    second = jnp.mean(scaled * hat, axis=-1, keepdims=True)
    return inverse * (scaled - first - hat * second)


def gelu_parts(inner):
    half = 0.5 * (1.0 + lax.erf(inner * 0.7071067811865476))
    slope = half + inner * (jnp.exp(-0.5 * inner * inner) * 0.3989422804014327)
    return inner * half, slope


def three(value):
    first = value.astype(low)
    rest = value - first.astype(high)
    second = rest.astype(low)
    third = (rest - second.astype(high)).astype(low)
    return first, second, third


def meets(seg_q, first_q, size_q, seg_k, first_k, size_k):
    return (seg_q[first_q + size_q - 1] >= seg_k[first_k]) & (
        seg_q[first_q] <= seg_k[first_k + size_k - 1]
    )


def score_part(r, q_ref, q_row, first_q, seg_q, seg_k, ka_ref, vt_ref, acc_ref, top_ref, width):
    heads, keys = ka_ref.shape[0], ka_ref.shape[1]
    block = acc_ref.shape[2]
    acc_ref[...] = jnp.zeros_like(acc_ref)
    top_ref[...] = jnp.full_like(top_ref, 2 * FAR)

    def one_block(b, carry):
        first_k = b * width

        @pl.when(meets(seg_q, first_q, block, seg_k, first_k, width))
        def _():
            for h in range(heads):
                scores = nt(ka_ref[h, pl.ds(first_k, width), :], q_ref[h, q_row])
                top = top_ref[h]
                peak = jnp.maximum(top, jnp.max(scores, axis=0, keepdims=True))
                weights = jnp.exp(scores - peak).astype(low)
                acc_ref[h] = acc_ref[h] * jnp.exp(top - peak) + nn(
                    vt_ref[h, :, pl.ds(first_k, width)], weights
                )
                top_ref[h] = peak

        return carry

    lax.fori_loop(0, keys // width, one_block, 0)
    outs = []
    lane = lax.broadcasted_iota(jnp.int32, (block, HEAD_DIM), 1)
    for h in range(heads):
        acc = acc_ref[h]
        total = acc[HEAD_DIM : HEAD_DIM + 1]
        lse = top_ref[h] + jnp.log(total)
        joined = jnp.concatenate(
            [acc[:HEAD_DIM] / total, jnp.broadcast_to(lse, (HEAD_DIM, block))], axis=0
        )
        turned = joined.T
        outs.append(turned[:, :HEAD_DIM])
        minus = three(-turned[:, HEAD_DIM:])
        mask = q_ref[h, q_row, :, HEAD_DIM:].astype(high)
        for i in range(3):
            mask = jnp.where(lane == LSE_LANE + i, minus[i].astype(high), mask)
        q_ref[h, q_row, :, HEAD_DIM:] = mask.astype(low)
    return jnp.concatenate(outs, axis=1)


def attend_far_kernel(*refs, block, width, heads, marks):
    pieces = len(marks)
    here, seg_q, seg_k, x_ref, halo_ref, bias_ref, mq_ref, mk_ref = refs[:8]
    w_refs = refs[8 : 8 + pieces]
    (out_2, out_3, full_ref, q_near, q_far, ka_ref, v_ref, vt_ref, w_ref) = refs[8 + pieces : 17 + pieces]
    acc_ref, top_ref, sems = refs[17 + pieces :]
    keys = v_ref.shape[0]
    rows = x_ref.shape[0]
    local = heads * HEAD_DIM
    scale = 1.0 / math.sqrt(HEAD_DIM)
    mine, f, c = here[0], here[1], here[2]
    copies = []
    for i, mark in enumerate(marks):
        first, count = mark(f, c)
        copies.append(
            pltpu.make_async_copy(w_refs[i], w_ref.at[pl.ds(first, count)], sems.at[i])
        )
        copies[-1].start()
    vt_ref[:, HEAD_DIM:, :] = jnp.ones((heads, vt_ref.shape[1] - HEAD_DIM, keys), low)
    for copy in copies:
        copy.wait()
    weights_all = w_ref[...].reshape(-1, w_ref.shape[2])

    def keep(first, count, mask, kv):
        span = pl.ds(first, count)
        for h in range(heads):
            cols = slice(h * HEAD_DIM, (h + 1) * HEAD_DIM)
            tail = slice(local + h * HEAD_DIM, local + (h + 1) * HEAD_DIM)
            ka_ref[h, span, :] = jnp.concatenate([kv[:, cols], mask], axis=1)
            vt_ref[h, :HEAD_DIM, span] = kv[:, tail].T
        v_ref[span, :] = kv[:, local:]

    for q_ref, base in ((q_near, 0), (q_far, 2)):

        def project(i, carry, q_ref=q_ref, base=base):
            first = pl.multiple_of((mine ^ (base + i)) * block, block)
            span = pl.ds(first, block)
            both = (nn(x_ref[span, :], weights_all) + bias_ref[...]).astype(low)
            for h in range(heads):
                cols = slice(h * HEAD_DIM, (h + 1) * HEAD_DIM)
                q_ref[h, i] = jnp.concatenate(
                    [both[:, cols] * jnp.array(scale, low), mq_ref[span, :]], axis=1
                )
            keep(first, block, mk_ref[span, :], both[:, local:])
            return carry

        lax.fori_loop(0, 2, project, 0)
    step = min(512, keys - rows)
    for first in range(rows, keys, step):
        span = slice(first - rows, first - rows + step)
        kv = (nn(halo_ref[span, :], weights_all[:, local:]) + bias_ref[:, local:]).astype(low)
        keep(first, step, mk_ref[first : first + step, :], kv)
    for i, out_ref in enumerate((out_2, out_3)):
        joined = score_part(
            2 + i, q_far, i, (mine ^ (2 + i)) * block, seg_q, seg_k, ka_ref, vt_ref, acc_ref, top_ref, width
        )
        full_ref[i] = joined
        out_ref[...] = joined.astype(low)


def attend_near_kernel(
    here, seg_q, seg_k, q_in, ka_ref, vt_ref, out_0, out_1, full_ref, q_ref, acc_ref, top_ref, *, block, width
):
    mine = here[0]
    q_ref[...] = q_in[...]
    for i, out_ref in enumerate((out_0, out_1)):
        joined = score_part(
            i, q_ref, i, (mine ^ i) * block, seg_q, seg_k, ka_ref, vt_ref, acc_ref, top_ref, width
        )
        full_ref[i] = joined
        out_ref[...] = joined.astype(low)


VMEM = pl.BlockSpec(memory_space=pltpu.VMEM)
SMEM = pl.BlockSpec(memory_space=pltpu.SMEM)
ANY = pl.BlockSpec(memory_space=pl.ANY)
HBM = pl.BlockSpec(memory_space=pltpu.HBM)


def shape(*dims, kind=low):
    return jax.ShapeDtypeStruct(dims, kind)


def cost(flops, size, transcendentals=0):
    return pl.CostEstimate(flops=flops, transcendentals=transcendentals, bytes_accessed=size)


def attend_far(here, seg_q, seg_k, x, halo, bias, mask_q, mask_k, pieces, marks, blocks, block):
    rows = x.shape[0]
    local = bias.shape[1] // 3
    count = rows + halo.shape[0]
    heads = local // HEAD_DIM
    wide = 2 * HEAD_DIM
    return pl.pallas_call(
        lambda *refs: attend_far_kernel(*refs, block=block, width=256, heads=heads, marks=marks),
        name="attend_far",
        out_shape=(
            shape(block, local),
            shape(block, local),
            shape(2, block, local, kind=high),
            shape(heads, 2, block, wide),
            shape(heads, 2, block, wide),
            shape(heads, count, wide),
            shape(count, local),
            shape(heads, HEAD_DIM + 16, count),
            shape(*blocks, 3 * local),
        ),
        in_specs=[SMEM] * 3 + [VMEM] * 5 + [ANY] * len(pieces),
        out_specs=(VMEM,) * 9,
        scratch_shapes=[
            pltpu.VMEM((heads, HEAD_DIM + 16, block), high),
            pltpu.VMEM((heads, 1, block), high),
            pltpu.SemaphoreType.DMA((len(pieces),)),
        ],
        cost_estimate=cost(FAR_COST, 8 << 20),
    )(here, seg_q, seg_k, x, halo, bias, mask_q, mask_k, *pieces)


def attend_near(here, seg_q, seg_k, q_near, keys_wide, values_t):
    heads, _, block, wide = q_near.shape
    local = heads * HEAD_DIM
    return pl.pallas_call(
        lambda *refs: attend_near_kernel(*refs, block=block, width=256),
        name="attend_near",
        out_shape=(
            shape(block, local),
            shape(block, local),
            shape(2, block, local, kind=high),
            shape(heads, 2, block, wide),
        ),
        in_specs=[SMEM] * 3 + [VMEM] * 3,
        out_specs=(VMEM,) * 4,
        scratch_shapes=[
            pltpu.VMEM((heads, HEAD_DIM + 16, block), high),
            pltpu.VMEM((heads, 1, block), high),
        ],
        cost_estimate=cost(NEAR_COST, 8 << 20),
    )(here, seg_q, seg_k, q_near, keys_wide, values_t)


FAR_COST = 20 * 10**9
NEAR_COST = 12 * 10**9
FEED_COST = 26 * 10**9
UNIT_COST = 12 * 10**9
BACK_COST = 24 * 10**9
LAST_COST = 9 * 10**9
SMALL_COST = 3 * 10**9


def feed_kernel(*refs, plan, count, hidden, local):
    here, x_all, g_all, att_0, att_1, att_2, att_3, vec_ref = refs[:8]
    w_refs = refs[8 : 8 + count]
    (out_ref, one_ref, stat_ref, ga_0, ga_1, ga_2, ga_3, rows_hbm, keep_hbm, send_hbm) = refs[8 + count : 18 + count]
    (w_ref, b_ref, x_ref, g_ref, att_ref, hat_ref, inv_ref, norm_ref, acc_ref, slope_ref, gl_ref,
     rows_ref, keep_ref, send_ref, sems, out_sems) = refs[18 + count :]
    puts = []

    def put(src, dst):
        puts.append(pltpu.make_async_copy(src, dst, out_sems.at[len(puts)]))
        puts[-1].start()

    tokens, width = x_ref.shape
    mine, f, c = here[0], here[1], here[2]
    wide = 2 * hidden + local
    copies = []

    def begin(src, dst):
        copies.append(pltpu.make_async_copy(src, dst, sems.at[len(copies)]))
        copies[-1].start()

    first = pl.multiple_of(mine * tokens, tokens)
    begin(x_all.at[pl.ds(first, tokens)], x_ref)
    begin(g_all.at[pl.ds(first, tokens)], g_ref)
    for r, att in enumerate((att_0, att_1, att_2, att_3)):
        begin(att, att_ref.at[r])
    for i, offset, r, mark in plan:
        if mark is None:
            begin(w_refs[i].at[pl.ds(offset, 8)], b_ref.at[r])
        else:
            start, size = mark(f, c)
            begin(w_refs[i].at[pl.ds(offset, size)], w_ref.at[r, pl.ds(start, size)])
    for copy in copies:
        copy.wait()
    b_out, gain_one, shift_one, b_outer, gain_two, shift_two = (
        vec_ref[i : i + 1, :].astype(high) for i in range(6)
    )

    def weights(r, first, last):
        return w_ref[r, :, first:last]

    acc_ref[...] = nt(att_ref[0], weights(0, 2 * hidden, 2 * hidden + local))
    for r in range(1, 4):
        acc_ref[...] += nt(att_ref[r], weights(r, 2 * hidden, 2 * hidden + local))
    step = 64
    chunks = tokens // step

    def first_norm(i, carry):
        span = pl.ds(pl.multiple_of(i * step, step), step)
        hat, inverse = norm_parts(x_ref[span, :].astype(high) + (acc_ref[span, :] + b_out))
        hat_ref[span, :] = hat
        inv_ref[span, :] = inverse
        normed = hat * gain_one + shift_one
        norm_ref[span, :] = normed.astype(low)
        acc_ref[span, :] = normed + b_outer
        return carry

    lax.fori_loop(0, chunks, first_norm, 0)
    part = 256
    for k, side in enumerate((keep_ref, send_ref)):
        for x in range(2):
            side[x, :, 2 * hidden : wide] = att_ref[2 * x + k]
            side[x, :, wide:] = jnp.zeros((tokens, side.shape[2] - wide), low)

        def up(x, carry, k=k, side=side):
            r = 2 * x + k
            for j in range(0, hidden, part):
                inner = nn(norm_ref[...], weights(r, j, j + part))
                inner = inner + b_ref[r, 0:1, j : j + part].astype(high)
                act, slope = gelu_parts(inner)
                side[x, :, hidden + j : hidden + j + part] = act.astype(low)
                slope_ref[r, :, j : j + part] = slope
            acc_ref[...] += nt(side[x, :, hidden : 2 * hidden], weights(r, hidden, 2 * hidden))
            return carry

        lax.fori_loop(0, 2, up, 0)

    zero = jnp.zeros((1, width), high)

    def second_norm(i, sums):
        span = pl.ds(pl.multiple_of(i * step, step), step)
        hat, inverse = norm_parts(acc_ref[span, :])
        out_ref[span, :] = (hat * gain_two + shift_two).astype(low)
        grad = g_ref[span, :].astype(high)
        two = norm_back(grad, hat, inverse, gain_two)
        acc_ref[span, :] = two
        two_low = two.astype(low)
        gl_ref[span, :] = two_low
        terms = (two_low.astype(high), grad * hat, grad)
        return tuple(s + jnp.sum(v, axis=0, keepdims=True) for s, v in zip(sums, terms))

    sums_two = lax.fori_loop(0, chunks, second_norm, (zero,) * 3)
    rows_ref[0] = norm_ref[...].T
    rows_ref[1] = gl_ref[...].T
    put(rows_ref.at[pl.ds(0, 2)], rows_hbm.at[pl.ds(0, 2)])
    for k, side in ((1, send_ref), (0, keep_ref)):

        def down(x, carry, k=k, side=side):
            r = 2 * x + k
            for j in range(0, hidden, part):
                grad = nn(gl_ref[...], weights(r, hidden + j, hidden + j + part))
                grad = (grad * slope_ref[r, :, j : j + part]).astype(low)
                side[x, :, j : j + part] = grad
                stat_ref[8 + r, 0:1, j : j + part] = jnp.sum(grad.astype(high), axis=0, keepdims=True)
            acc_ref[...] += nt(side[x, :, :hidden], weights(r, 0, hidden))
            return carry

        lax.fori_loop(0, 2, down, 0)
        put(side, send_hbm if k else keep_hbm)

    def first_back(i, sums):
        span = pl.ds(pl.multiple_of(i * step, step), step)
        grad = acc_ref[span, :]
        hat = hat_ref[span, :]
        one = norm_back(grad, hat, inv_ref[span, :], gain_one)
        one_ref[span, :] = one
        one_low = one.astype(low)
        gl_ref[span, :] = one_low
        terms = (one_low.astype(high), grad * hat, grad)
        return tuple(s + jnp.sum(v, axis=0, keepdims=True) for s, v in zip(sums, terms))

    sums_one = lax.fori_loop(0, chunks, first_back, (zero,) * 3)
    for i, value in enumerate(sums_one + sums_two):
        stat_ref[i, 0:1, :] = value
    rows_ref[2] = gl_ref[...].T
    put(rows_ref.at[2], rows_hbm.at[2])
    for r, ga in enumerate((ga_0, ga_1, ga_2, ga_3)):
        ga[...] = nn(gl_ref[...], weights(r, 2 * hidden, 2 * hidden + local)).astype(low)
    for copy in puts:
        copy.wait()


def feed(here, x, grad, att, vectors, pieces, plan, tokens, hidden, local):
    width = x.shape[1]
    wide = 2 * hidden + local
    padded = (wide + 127) // 128 * 128
    copies = 6 + len(plan)
    return pl.pallas_call(
        lambda *refs: feed_kernel(*refs, plan=plan, count=len(pieces), hidden=hidden, local=local),
        name="feed",
        out_shape=(
            shape(tokens, width),
            shape(tokens, width, kind=high),
            shape(12, 1, width, kind=high),
            shape(tokens, local),
            shape(tokens, local),
            shape(tokens, local),
            shape(tokens, local),
            shape(3, width, tokens),
            shape(2, tokens, padded),
            shape(2, tokens, padded),
        ),
        in_specs=[SMEM] + [ANY] * 6 + [VMEM] + [ANY] * len(pieces),
        out_specs=(VMEM,) * 7 + (HBM,) * 3,
        scratch_shapes=[
            pltpu.VMEM((4, width, wide), low),
            pltpu.VMEM((4, 8, wide), low),
            pltpu.VMEM((tokens, width), low),
            pltpu.VMEM((tokens, width), low),
            pltpu.VMEM((4, tokens, local), low),
            pltpu.VMEM((tokens, width), high),
            pltpu.VMEM((tokens, 1), high),
            pltpu.VMEM((tokens, width), low),
            pltpu.VMEM((tokens, width), high),
            pltpu.VMEM((4, tokens, hidden), high),
            pltpu.VMEM((tokens, width), low),
            pltpu.VMEM((3, width, tokens), low),
            pltpu.VMEM((2, tokens, padded), low),
            pltpu.VMEM((2, tokens, padded), low),
            pltpu.SemaphoreType.DMA((copies,)),
            pltpu.SemaphoreType.DMA((4,)),
        ],
        cost_estimate=cost(FEED_COST, 24 << 20),
    )(here, x, grad, *att, vectors, *pieces)


def unit_kernel(here, rows_own, rows_mate, wide_own, wide_mate, *refs, hidden):
    ak_ref, as_ref, bk_ref, bs_ref, rows_ref, wide_ref, sems = refs
    c = here[2]
    tokens = rows_own.shape[2]
    wide = ak_ref.shape[2]
    half = ak_ref.shape[1]
    mid = rows_own.shape[1] // 2
    copies = [
        pltpu.make_async_copy(rows_own, rows_ref.at[:, :, pl.ds(0, tokens)], sems.at[0]),
        pltpu.make_async_copy(wide_own, wide_ref.at[:, pl.ds(0, tokens)], sems.at[1]),
        pltpu.make_async_copy(rows_mate, rows_ref.at[:, :, pl.ds(tokens, tokens)], sems.at[2]),
        pltpu.make_async_copy(wide_mate, wide_ref.at[:, pl.ds(tokens, tokens)], sems.at[3]),
    ]
    for copy in copies:
        copy.start()
    for copy in copies:
        copy.wait()
    spans = ((0, 0, hidden), (1, hidden, 2 * hidden), (2, 2 * hidden, wide))
    for x in range(2):
        for i, first, last in spans:
            for top in range(2):
                part = slice(top * mid, (top + 1) * mid)
                got = nn(rows_ref[i, part, :], wide_ref[x, :, first:last]).astype(low)
                if top == 0:
                    side = ak_ref if x == 0 else as_ref
                    side[:, :, first:last] = got.reshape(-1, half, last - first)
                else:
                    got = got.reshape(-1, 2, half, last - first)
                    for z in range(got.shape[0]):

                        @pl.when(c == 0)
                        def _():
                            bk_ref[x, z, :, first:last] = got[z, 0]
                            bs_ref[x, z, :, first:last] = got[z, 1]

                        @pl.when(c != 0)
                        def _():
                            bk_ref[x, z, :, first:last] = got[z, 1]
                            bs_ref[x, z, :, first:last] = got[z, 0]


def unit_grads(here, rows, mate_rows, keep, mate, half, hidden, local):
    wide = 2 * hidden + local
    tokens = rows.shape[2]
    width = rows.shape[1]
    quarters = width // 4 // half
    return pl.pallas_call(
        lambda *refs: unit_kernel(*refs, hidden=hidden),
        name="unit_grads",
        out_shape=(
            shape(2 * quarters, half, wide),
            shape(2 * quarters, half, wide),
            shape(2, quarters, half, wide),
            shape(2, quarters, half, wide),
        ),
        in_specs=[SMEM] + [ANY] * 4,
        out_specs=(VMEM,) * 4,
        scratch_shapes=[
            pltpu.VMEM((3, width, 2 * tokens), low),
            pltpu.VMEM((2, 2 * tokens, keep.shape[2]), low),
            pltpu.SemaphoreType.DMA((4,)),
        ],
        cost_estimate=cost(UNIT_COST, 14 << 20),
    )(here, rows, mate_rows, keep, mate)


def merge_one_kernel(here, ak, ga, bk, gb, a_keep, a_send, b_keep, b_send):
    c = here[2]
    for z in range(2):
        for side in range(2):
            i = 2 * z + side
            got = ak[i] + ga[i]

            @pl.when(c == side)
            def _():
                a_keep[z] = got

            @pl.when(c != side)
            def _():
                a_send[z] = got

    b_keep[...] = bk[0] + gb[0]
    b_send[...] = bk[1] + gb[1]


def merge_one(here, ak, ga, bk, gb):
    out = shape(*bk.shape[1:])
    return pl.pallas_call(
        merge_one_kernel,
        name="merge_one",
        out_shape=(out,) * 4,
        in_specs=[SMEM] + [VMEM] * 4,
        out_specs=(VMEM,) * 4,
        cost_estimate=cost(SMALL_COST, 8 << 20),
    )(here, ak, ga, bk, gb)


def merge_two_kernel(here, a_keep, a_got, b_keep, b_got, d_keep, d_got, *refs, start):
    outs, all_ref = refs[:4], refs[4]
    f = here[1]
    wide = a_keep.shape[2]
    for z in range(2):
        all_ref[z, :, :wide] = a_keep[z] + a_got[z]
        all_ref[2 + z, :, :wide] = b_keep[z] + b_got[z]
    all_ref[:, :, start:] = d_keep[...] + d_got[...]
    for s, out in enumerate(outs):
        out[...] = all_ref[(f + s) % 4]


def merge_two(here, a_keep, a_got, b_keep, b_got, d_keep, d_got, start):
    half = a_keep.shape[1]
    full = start + d_keep.shape[2]
    return pl.pallas_call(
        lambda *refs: merge_two_kernel(*refs, start=start),
        name="merge_two",
        out_shape=(shape(half, full),) * 4,
        in_specs=[SMEM] + [VMEM] * 6,
        out_specs=(VMEM,) * 4,
        scratch_shapes=[pltpu.VMEM((4, half, full), low)],
        cost_estimate=cost(SMALL_COST, 8 << 20),
    )(here, a_keep, a_got, b_keep, b_got, d_keep, d_got)


def merge_three_kernel(here, own, got_1, got_2, got_3, out, all_ref):
    f = here[1]
    for s, piece in enumerate((own, got_1, got_2, got_3)):
        all_ref[(f - s + 4) % 4] = piece[...]
    total = all_ref[0].astype(high)
    for z in range(1, 4):
        total = total + all_ref[z].astype(high)
    out[...] = total.astype(low)


def merge_three(here, pieces):
    return pl.pallas_call(
        merge_three_kernel,
        name="merge_three",
        out_shape=shape(*pieces[0].shape),
        in_specs=[SMEM] + [VMEM] * 4,
        out_specs=VMEM,
        scratch_shapes=[pltpu.VMEM((4,) + pieces[0].shape, low)],
        cost_estimate=cost(SMALL_COST, 4 << 20),
    )(here, *pieces)


def finish_kernel(here, own, got, inner, outer, out, query, key, value, bias, all_ref, *, start):
    c = here[2]
    hidden = inner.shape[1]
    local = query.shape[1]
    all_ref[c] = own[...]
    all_ref[1 - c] = got[...]
    half, full = own.shape

    def cols(first, last):
        return all_ref[:, :, first:last].reshape(2 * half, last - first).astype(high)

    inner[...] = cols(0, hidden)
    outer[...] = cols(hidden, 2 * hidden)
    out[...] = cols(2 * hidden, 2 * hidden + local).T
    rest = cols(start, full)
    query[...] = rest[:, :local]
    key[...] = rest[:, local : 2 * local]
    value[...] = rest[:, 2 * local : 3 * local]
    bias[...] = own[:16, start + 3 * local :].astype(high)


def finish(here, own, got, start, hidden, local):
    half, full = own.shape
    piece = 2 * half
    return pl.pallas_call(
        lambda *refs: finish_kernel(*refs, start=start),
        name="finish",
        out_shape=(
            shape(piece, hidden, kind=high),
            shape(piece, hidden, kind=high),
            shape(local, piece, kind=high),
            shape(piece, local, kind=high),
            shape(piece, local, kind=high),
            shape(piece, local, kind=high),
            shape(16, full - start - 3 * local, kind=high),
        ),
        in_specs=[SMEM] + [VMEM] * 2,
        out_specs=(VMEM,) * 7,
        scratch_shapes=[pltpu.VMEM((2, half, full), low)],
        cost_estimate=cost(SMALL_COST, 4 << 20),
    )(here, own, got)


def spread_kernel(here, p_0, p_1, p_2, p_3, out):
    tokens = p_0.shape[0]
    for r, piece in enumerate((p_0, p_1, p_2, p_3)):
        first = pl.multiple_of((here[0] ^ r) * tokens, tokens)
        out[pl.ds(first, tokens), :] = piece[...].astype(out.dtype)


def spread(here, pieces, kind):
    tokens, width = pieces[0].shape
    return pl.pallas_call(
        spread_kernel,
        name="spread",
        out_shape=shape(4 * tokens, width, kind=kind),
        in_specs=[SMEM] + [VMEM] * 4,
        out_specs=VMEM,
        cost_estimate=cost(SMALL_COST, 8 << 20),
    )(here, *pieces)


def project_back_kernel(here, g_ref, edge_ref, x_ref, w_ref, keep, send, d_keep, d_send, all_ref, *, local):
    mine, c = here[0], here[2]
    rows = g_ref.shape[0]
    rim = edge_ref.shape[0]
    tokens = keep.shape[1]
    half = d_keep.shape[1]
    pad = d_keep.shape[2] - 3 * local
    all_ref[...] = g_ref[...]
    edge = pl.ds(pl.multiple_of((1 - c) * (rows - rim), rim), rim)
    all_ref[edge, local:] = (
        g_ref[edge, local:].astype(high) + edge_ref[...].astype(high)
    ).astype(low)
    for k, side in ((1, send), (0, keep)):
        for x in range(2):
            first = pl.multiple_of((mine ^ (2 * x + k)) * tokens, tokens)
            side[x] = nt(all_ref[pl.ds(first, tokens), :], w_ref[...]).astype(low)
    sums = jnp.zeros((1, 3 * local), high)
    for i in range(rows // tokens):
        part = all_ref[i * tokens : (i + 1) * tokens, :].astype(high)
        sums = sums + jnp.sum(part, axis=0, keepdims=True)
    row = lax.broadcasted_iota(jnp.int32, (half, pad), 0)
    extra = jnp.zeros((half, pad), high)
    for j in range(3 * local // pad):
        extra = jnp.where(row == j, sums[:, j * pad : (j + 1) * pad], extra)
    extra = extra.astype(low)
    got = tn(x_ref[...], all_ref[...]).astype(low).reshape(-1, 2, half, 3 * local)
    for z in range(got.shape[0]):
        d_keep[z, :, 3 * local :] = extra
        d_send[z, :, 3 * local :] = extra
        for side in range(2):

            @pl.when(c == side)
            def _():
                d_keep[z, :, : 3 * local] = got[z, side]

            @pl.when(c != side)
            def _():
                d_send[z, :, : 3 * local] = got[z, side]


def project_back(here, grads, edge, x, weights, tokens, half):
    rows, width = x.shape
    local = grads.shape[1] // 3
    pad = HEAD_DIM
    return pl.pallas_call(
        lambda *refs: project_back_kernel(*refs, local=local),
        name="project_back",
        out_shape=(
            shape(2, tokens, width),
            shape(2, tokens, width),
            shape(width // half // 2, half, 3 * local + pad),
            shape(width // half // 2, half, 3 * local + pad),
        ),
        in_specs=[SMEM] + [VMEM] * 4,
        out_specs=(VMEM,) * 4,
        scratch_shapes=[pltpu.VMEM(grads.shape, low)],
        cost_estimate=cost(LAST_COST, 8 << 20),
    )(here, grads, edge, x, weights)


def attend_back_kernel(
    here, seg_q, seg_k, g_0, g_1, g_2, g_3, full_near, full_far, q_near, q_far, ka_ref, v_ref, own_ref, rim_ref,
    g_ref, full_ref, q_ref, kt_ref, va_ref, ga_ref, dka_ref, dva_ref, dqa_ref, sems, *, block, width, heads
):
    copies = [
        pltpu.make_async_copy(g, g_ref.at[r], sems.at[r]) for r, g in enumerate((g_0, g_1, g_2, g_3))
    ]
    for i, (q_part, full_part) in enumerate(((q_near, full_near), (q_far, full_far))):
        span = pl.ds(2 * i, 2)
        copies.append(pltpu.make_async_copy(q_part, q_ref.at[:, span], sems.at[4 + 2 * i]))
        copies.append(pltpu.make_async_copy(full_part, full_ref.at[span], sems.at[5 + 2 * i]))
    for copy in copies:
        copy.start()
    keys = v_ref.shape[0]
    rows = own_ref.shape[0]
    local = heads * HEAD_DIM
    scale = 1.0 / math.sqrt(HEAD_DIM)
    mine = here[0]
    for h in range(heads):
        cols = slice(h * HEAD_DIM, (h + 1) * HEAD_DIM)
        kt_ref[h] = ka_ref[h, :, :HEAD_DIM].T
        va_ref[h] = jnp.concatenate([v_ref[:, cols], jnp.ones((keys, HEAD_DIM), low)], axis=1)
    dka_ref[...] = jnp.zeros_like(dka_ref)
    dva_ref[...] = jnp.zeros_like(dva_ref)
    for copy in copies:
        copy.wait()

    def one_part(i, carry):
        first_q = pl.multiple_of((mine ^ i) * block, block)
        for h in range(heads):
            cols = slice(h * HEAD_DIM, (h + 1) * HEAD_DIM)
            grad = g_ref[i, :, cols]
            delta = jnp.sum(grad.astype(high) * full_ref[i, :, cols], axis=1, keepdims=True)
            lane = lax.broadcasted_iota(jnp.int32, (block, HEAD_DIM), 1)
            extra = jnp.zeros((block, HEAD_DIM), high)
            for j, piece in enumerate(three(-delta)):
                extra = jnp.where(lane == j, piece.astype(high), extra)
            ga_ref[h] = jnp.concatenate([grad, extra.astype(low)], axis=1)
        dqa_ref[...] = jnp.zeros_like(dqa_ref)

        def one_block(b, carry):
            first_k = b * width

            @pl.when(meets(seg_q, first_q, block, seg_k, first_k, width))
            def _():
                for h in range(heads):
                    span = pl.ds(first_k, width)
                    asks = q_ref[h, i]
                    probs = jnp.exp(nt(ka_ref[h, span, :], asks))
                    slopes = (probs * nt(va_ref[h, span, :], ga_ref[h])).astype(low)
                    dva_ref[h, span, :] += nn(probs.astype(low), ga_ref[h, :, :HEAD_DIM])
                    dka_ref[h, span, :] += nn(slopes, asks[:, :HEAD_DIM])
                    dqa_ref[h] += nn(kt_ref[h, :, span], slopes)

            return carry

        lax.fori_loop(0, keys // width, one_block, 0)
        own_ref[pl.ds(first_q, block), :local] = jnp.concatenate(
            [(dqa_ref[h] * scale).T for h in range(heads)], axis=1
        ).astype(low)
        return carry

    lax.fori_loop(0, 4, one_part, 0)
    for j, part in enumerate((dka_ref, dva_ref)):
        wide = jnp.concatenate([part[h] for h in range(heads)], axis=1).astype(low)
        own_ref[:, (1 + j) * local : (2 + j) * local] = wide[:rows]
        rim_ref[:, j * local : (j + 1) * local] = wide[rows:]


def attend_back(here, seg_q, seg_k, grads, full_near, full_far, q_near, q_far, keys, values):
    parts = len(grads)
    block, local = grads[0].shape
    rows = parts * block
    count = values.shape[0]
    heads = local // HEAD_DIM
    return pl.pallas_call(
        lambda *refs: attend_back_kernel(*refs, block=block, width=256, heads=heads),
        name="attend_back",
        out_shape=(shape(rows, 3 * local), shape(count - rows, 2 * local)),
        in_specs=[SMEM] * 3 + [ANY] * 8 + [VMEM] * 2,
        out_specs=(VMEM,) * 2,
        scratch_shapes=[
            pltpu.VMEM((parts, block, local), low),
            pltpu.VMEM((parts, block, local), high),
            pltpu.VMEM((heads, parts, block, 2 * HEAD_DIM), low),
            pltpu.VMEM((heads, HEAD_DIM, count), low),
            pltpu.VMEM((heads, count, 2 * HEAD_DIM), low),
            pltpu.VMEM((heads, block, 2 * HEAD_DIM), low),
            pltpu.VMEM((heads, count, HEAD_DIM), high),
            pltpu.VMEM((heads, count, HEAD_DIM), high),
            pltpu.VMEM((heads, HEAD_DIM, block), high),
            pltpu.SemaphoreType.DMA((parts + 4,)),
        ],
        cost_estimate=cost(BACK_COST, 8 << 20),
    )(here, seg_q, seg_k, *grads, full_near, full_far, q_near, q_far, keys, values)


def after(values, gate):
    return lax.optimization_barrier((tuple(values), gate))[0]


def halo_of(value, c, span):
    rows = value.shape[0]
    return take(value, (1 - c) * (rows - span), span)


def shards(
    inputs, segments, w_query, b_query, w_key, w_value, b_value, w_out, b_out, gain_one, shift_one,
    w_inner, b_inner, w_outer, b_outer, gain_two, shift_two, grad_output,
):
    rows, width = inputs.shape
    local = w_query.shape[1]
    hidden = w_inner.shape[1]
    n_f, n_c, n_t = (lax.axis_size(a) for a in ("fsdp", "ctx", "tp"))
    f, c, t = (lax.axis_index(a) for a in ("fsdp", "ctx", "tp"))
    tokens = rows // n_t
    rim = MOST
    quick = n_f == 4 and n_c == 2 and n_t == 4
    piece = width // n_f
    flip = [t ^ r for r in range(n_t)]

    half = piece // 2
    blocks = (2 * n_f, half)
    here = jnp.stack([t, f, c]).astype(jnp.int32)
    bundle_a = jnp.concatenate([w_query, w_key, w_value], axis=1)

    def spot(s, side):
        def mark(f, c):
            return (f - s + n_f) % n_f * 2 + (c if side == 0 else 1 - c), 1

        return mark

    def spot_from(s):
        return lambda f, c: ((f - s + n_f) % n_f * 2, 2)

    def spot_all(f, c):
        return 0, 2 * n_f

    def in_rows(mark):
        def rows_mark(f, c):
            first, count = mark(f, c)
            return (first if isinstance(first, int) else pl.multiple_of(first * half, half)), count * half

        return rows_mark

    seg_own = segments.reshape(rows)
    if quick:
        halves_a = bundle_a.reshape(2, half, -1)
        pieces_a = [halves_a] + [shift(halves_a, "fsdp", s) for s in range(1, n_f)]
        marks_a = [spot_from(s) for s in range(n_f)]
    else:
        whole_a = lax.all_gather(bundle_a, "fsdp", axis=0, tiled=True)
        pieces_a, marks_a = [whole_a.reshape(blocks + (-1,))], [spot_all]

    if n_c == 2:
        sent = halo_of(inputs, c, rim)
        if quick:
            part = rim // 2
            ids = halo_of(seg_own, c, rim).astype(low).reshape(2, part)
            ids = jnp.pad(ids, ((0, 14), (0, width - part)))
            got = swap(jnp.concatenate([take(sent, (t & 1) * part, part), ids], axis=0), "ctx", 1)
            halo_seg = got[part : part + 2, :part].astype(jnp.int32).reshape(rim)
            got = got[:part]
            mate = swap(got, "tp", 1)
            even = (t & 1) == 0
            halo_in = jnp.concatenate([jnp.where(even, got, mate), jnp.where(even, mate, got)], axis=0)
        else:
            halo_in = swap(sent, "ctx", 1)
            halo_seg = swap(halo_of(seg_own, c, rim), "ctx", 1)
    else:
        ahead = [(i, i + 1) for i in range(n_c - 1)]
        behind = [(i + 1, i) for i in range(n_c - 1)]

        def both(value):
            return jnp.concatenate(
                [
                    lax.ppermute(value[rows - rim :], "ctx", ahead),
                    lax.ppermute(value[:rim], "ctx", behind),
                ],
                axis=0,
            )

        halo_in = both(inputs)
        halo_seg = both(seg_own + 1) - 1
        halo_seg = jnp.where(halo_seg < 0, NO_ID, halo_seg)

    bias_row = jnp.pad(b_inner[None], ((0, 7), (0, hidden + local)))
    bundle_f = jnp.concatenate([w_inner, w_outer.T, w_out.T], axis=1)
    own_rows = jnp.concatenate([bundle_f, bias_row], axis=0)
    if quick:
        far_rows = swap(own_rows, "tp", 2)
        own_f = take(bundle_f, c * half, half)
        (own_1,) = after([own_f], (pieces_a[1], pieces_a[3]))
        gots = {s: shift(own_1, "fsdp", s) for s in (1, 3)}
        halo_in, far_rows = lax.optimization_barrier((halo_in, far_rows))
        far_f = take(far_rows, (1 - c) * half, half)
        corners = {s: shift(far_f, "fsdp", s) for s in (1, 3)}

    bias = jnp.concatenate([b_query, jnp.zeros_like(b_query), b_value]).astype(high)[None]
    seg_all = jnp.concatenate([seg_own, halo_seg])
    lane = jnp.arange(IDS)
    near_id = seg_all[:, None] == lane
    mask_k = (near_id | ((lane >= LSE_LANE) & (lane < LSE_LANE + 3))).astype(low)
    mask_q = jnp.where(near_id[:rows] | ((lane >= LSE_LANE) & (lane < LSE_LANE + 3)), 0.0, FAR).astype(low)
    att_2, att_3, full_far, q_near, q_far, keys_wide, values, values_t, w_qkv = attend_far(
        here, seg_own, seg_all, inputs, halo_in, bias, mask_q, mask_k, pieces_a, marks_a, blocks, tokens
    )
    w_qkv = w_qkv.reshape(width, 3 * local)

    if quick:
        (own_2,) = after([own_f], att_2)
        gots[2] = shift(own_2, "fsdp", 2)
        *near, corners[1], corners[3] = after([gots[1], gots[3], corners[1], corners[3]], att_2)
        (q_near,) = after([q_near], (*near, corners[1], corners[3]))
    att_0, att_1, full_near, q_near = attend_near(here, seg_own, seg_all, q_near, keys_wide, values_t)
    if quick:
        pieces_f, plan = [], []

        def add(r, value, marks, gate=None, bias=False):
            twin = value
            if gate is not None:
                (twin,) = after([value], gate)
            for r, piece in ((r, value), (r + 1, swap(twin, "tp", 1))):
                offset = 0
                for mark in marks:
                    plan.append((len(pieces_f), offset, r, in_rows(mark)))
                    offset += half
                if bias:
                    plan.append((len(pieces_f), piece_rows, r, None))
                pieces_f.append(piece)

        piece_rows = piece
        add(0, own_rows, [spot_from(0)], att_0, bias=True)
        add(2, far_rows, [spot_from(0)], att_0, bias=True)
        for s, got in zip((1, 3), near):
            add(0, got, [spot(s, 0)], att_0)
            add(2, corners[s], [spot(s, 1)], att_0)
        near = jnp.concatenate(near, axis=0)
        near_x, near_y = swap(near, "tp", 2), swap(near, "ctx", 1)
        last, near_x, near_y, *att = lax.optimization_barrier((gots[2], near_x, near_y, att_0, att_1, att_2, att_3))
        att_0, att_1, att_2, att_3 = att
        att = [att_0, swap(att_1, "tp", 1), swap(att_2, "tp", 2), swap(att_3, "tp", 3)]
        add(2, near_x, [spot(1, 0), spot(3, 0)])
        add(0, near_y, [spot(1, 1), spot(3, 1)])
        add(0, last, [spot(2, 0)])
        add(2, swap(last, "tp", 2), [spot(2, 0)])
        add(0, swap(last, "ctx", 1), [spot(2, 1)])
        corner = lax.ppermute(last, ("ctx", "tp"), [(i, i ^ (n_t + 2)) for i in range(n_c * n_t)])
        add(2, corner, [spot(2, 1)])
    else:
        gathered = lax.all_gather(bundle_f, "fsdp", axis=0, tiled=True)
        gathered = jnp.concatenate([gathered, bias_row], axis=0)
        gathered = lax.all_gather(gathered, "tp", axis=0)
        pieces_f = [lax.dynamic_index_in_dim(gathered, i, 0, keepdims=False) for i in flip]
        plan = [(r, 0, r, in_rows(spot_all)) for r in range(n_t)]
        plan += [(r, width, r, None) for r in range(n_t)]

    if not quick:
        att = [att_0, swap(att_1, "tp", 1), swap(att_2, "tp", 2), swap(att_3, "tp", 3)]

    vectors = jnp.stack([b_out, gain_one, shift_one, b_outer, gain_two, shift_two, b_out, b_out])
    output, g_one, stats, ga_0, ga_1, ga_2, ga_3, rows_t, keep, send = feed(
        here, inputs, grad_output, att, vectors, pieces_f, plan, tokens, hidden, local
    )
    g_att = [ga_0, swap(ga_1, "tp", 1), swap(ga_2, "tp", 2), swap(ga_3, "tp", 3)]
    stats = stats[:, 0]

    if quick:
        mate_rows = swap(rows_t, "tp", 1)
        mate = swap(send, "tp", 1)
        near_sums = jnp.concatenate([stats[:6], stats[8:9], stats[10:11]], axis=0)
        away = jnp.concatenate([stats[:6], stats[9:10], stats[11:12]], axis=0)
        keep_a, send_a, keep_b, send_b = unit_grads(here, rows_t, mate_rows, keep, mate, half, hidden, local)
        got_a = swap(send_a, "tp", 2)
        got_b = swap(send_b, "ctx", 1)
        *g_att, keep_a, keep_b = lax.optimization_barrier((*g_att, keep_a, keep_b))
    else:
        ordered = []
        for r in range(n_t):
            wide = (keep, send)[r % 2][r // 2]
            ordered.append(
                jnp.concatenate(
                    [
                        nn(rows_t[0], wide[:, :hidden]),
                        nn(rows_t[1], wide[:, hidden : 2 * hidden]),
                        nn(rows_t[2], wide[:, 2 * hidden : 2 * hidden + local]),
                    ],
                    axis=1,
                )
            )
        stacked = jnp.stack(ordered)
        ordered = jnp.stack([lax.dynamic_index_in_dim(stacked, i, 0, keepdims=False) for i in flip])
        mine = lax.psum_scatter(ordered, "tp", scatter_dimension=0, tiled=False)
        mine = lax.psum(mine, ("fsdp", "ctx"))
        shard_f = take(mine, f * piece, piece)

    g_own, g_rim = attend_back(
        here, seg_own, seg_all, g_att, full_near, full_far, q_near, q_far, keys_wide, values
    )
    if quick:
        got_a, got_b = after([got_a, got_b], g_own)
        (rim_out,) = after([g_rim], (got_a, got_b))
        (away,) = after([away], g_own)
        pair = near_sums + swap(away, "tp", 1)
        edge = swap(rim_out, "ctx", 1)
        keep_a, send_a, keep_b, send_b = merge_one(here, keep_a, got_a, keep_b, got_b)
        got_a = swap(send_a, "ctx", 1)
        got_b = swap(send_b, "tp", 2)
        (edge,) = after([edge], (send_a, send_b, pair))
        away = jnp.concatenate([pair[:6], pair[7:8], pair[7:8]], axis=0)
        pair = pair + swap(away, "tp", 2)
        dx_keep, dx_send, d_keep, d_send = project_back(here, g_own, edge, inputs, w_qkv, tokens, half)
        (dx_send,) = after([dx_send], (got_a, got_b))
        dx_got = swap(dx_send, "tp", 1)
        d_got = swap(d_send, "ctx", 1)
        near_dx = dx_keep[0] + dx_got[0]
        far_dx = dx_keep[1] + dx_got[1]
        far_got = swap(far_dx, "tp", 2)
        start = (2 * hidden + local + 127) // 128 * 128
        pair = pair + swap(pair, "ctx", 1)
        keep_a, pair = lax.optimization_barrier((keep_a, pair))
        outs = merge_two(here, keep_a, got_a, keep_b, got_b, d_keep, d_got, start)
        (output,) = after([output], outs[0])
        pair = pair + swap(pair, "fsdp", 1)
        totals = [outs[0]] + [shift(outs[s], "fsdp", s) for s in range(1, n_f)]
        mine = (near_dx.astype(high) + far_got.astype(high) + g_one).astype(low)

        def everyone(value, kind):
            far_value = swap(value, "tp", 2)
            return spread(here, [value, swap(value, "tp", 1), far_value, swap(far_value, "tp", 1)], kind)

        output = everyone(output, low)
        grad_inputs = everyone(mine, high)
        totals[1], pair = lax.optimization_barrier((totals[1], pair))
        total = merge_three(here, totals)
        pair = pair + swap(pair, "fsdp", 2)
        got = swap(total, "ctx", 1)
        got, output, grad_inputs = lax.optimization_barrier((got, output, grad_inputs))
        s_inner, s_outer, s_out, s_query, s_key, s_value, s_bias = finish(
            here, total, got, start, hidden, local
        )
        s_outer = s_outer.T
        s_qkv = s_bias.reshape(-1)[: 3 * local]
        shared, s_b_inner = pair[:6], pair[6]
    else:
        edge_got = []
        if n_c == 2:
            edge_got.append(((1 - c) * (rows - rim), swap(g_rim, "ctx", 1)))
        else:
            edge_got.append((0, lax.ppermute(g_rim[rim:], "ctx", ahead)))
            edge_got.append((rows - rim, lax.ppermute(g_rim[:rim], "ctx", behind)))
        g_all = g_own.astype(high)
        for first, got in edge_got:
            got = jnp.pad(got.astype(high), ((0, 0), (local, 0)))
            g_all = place(g_all, take(g_all, first, rim) + got, first)
        g_all = g_all.astype(low)
        part = nt(g_all, w_qkv).reshape(n_t, tokens, width)
        mine = lax.psum_scatter(part, "tp", scatter_dimension=0, tiled=False)
        grad_inputs = lax.all_gather((mine + g_one).astype(low), "tp", axis=0, tiled=True).astype(high)
        output = lax.all_gather(output, "tp", axis=0, tiled=True)
        shard_a = take(lax.psum(tn(inputs, g_all), ("fsdp", "ctx")), f * piece, piece)
        s_query, s_key, s_value = (shard_a[:, i * local : (i + 1) * local] for i in range(3))
        s_qkv = lax.psum(jnp.sum(g_all.astype(high), axis=0), ("fsdp", "ctx"))
        s_inner, s_outer, s_out = shard_f[:, :hidden], shard_f[:, hidden : 2 * hidden].T, shard_f[:, 2 * hidden :].T
        ordered = jnp.stack([lax.dynamic_index_in_dim(stats[8:], i, 0, keepdims=False) for i in flip])
        s_b_inner = lax.psum(
            lax.psum_scatter(ordered, "tp", scatter_dimension=0, tiled=False), ("fsdp", "ctx")
        )
        shared = lax.psum(stats[:6], ("fsdp", "ctx", "tp"))
    return (
        output,
        grad_inputs,
        s_query,
        s_qkv[:local],
        s_key,
        s_value,
        s_qkv[2 * local :],
        s_out,
        shared[0],
        shared[1],
        shared[2],
        s_inner,
        s_b_inner,
        s_outer,
        shared[3],
        shared[4],
        shared[5],
    )


def solution(mesh):
    rows = P(("fsdp", "ctx"), None)
    down, flat, across = P("fsdp", "tp"), P("tp"), P("tp", "fsdp")
    return jax.shard_map(
        shards,
        mesh=mesh,
        in_specs=(
            rows, P("fsdp", "ctx"), down, flat, down, down, flat, across, P(), P(), P(), down, flat,
            across, P(), P(), P(), rows,
        ),
        out_specs=(
            rows, rows, down, flat, down, down, flat, across, P(), P(), P(), down, flat, across,
            P(), P(), P(),
        ),
        check_vma=False,
    )
```

```python
import math

import jax
import jax.numpy as jnp
from jax import lax
from jax.experimental import pallas as pl
from jax.experimental.pallas import tpu as pltpu
from jax.sharding import PartitionSpec as P

HEAD_DIM = 64
MOST = 512
IDS = 64
NO_ID = 63
LSE_LANE = 60
FAR = -1e30

layer_eps = 1e-12
low = jnp.bfloat16
high = jnp.float32


def nn(left, right):
    return jnp.dot(left, right, preferred_element_type=high)


def nt(left, right):
    return lax.dot_general(left, right, (((1,), (1,)), ((), ())), preferred_element_type=high)


def tn(left, right):
    return lax.dot_general(left, right, (((0,), (0,)), ((), ())), preferred_element_type=high)


def swap(value, axis, bit):
    count = lax.axis_size(axis)
    return lax.ppermute(value, axis, [(i, i ^ bit) for i in range(count)])


def shift(value, axis, step):
    count = lax.axis_size(axis)
    return lax.ppermute(value, axis, [(i, (i + step) % count) for i in range(count)])


def place(whole, part, first):
    return lax.dynamic_update_slice_in_dim(whole, part, first, 0)


def take(whole, first, count):
    return lax.dynamic_slice_in_dim(whole, first, count, 0)


def norm_parts(hidden):
    average = jnp.mean(hidden, axis=-1, keepdims=True)
    centred = hidden - average
    variance = jnp.mean(centred * centred, axis=-1, keepdims=True)
    inverse = lax.rsqrt(variance + layer_eps)
    return centred * inverse, inverse


def norm_back(grad, hat, inverse, gain):
    scaled = grad * gain
    first = jnp.mean(scaled, axis=-1, keepdims=True)
    second = jnp.mean(scaled * hat, axis=-1, keepdims=True)
    return inverse * (scaled - first - hat * second)


def gelu_parts(inner):
    half = 0.5 * (1.0 + lax.erf(inner * 0.7071067811865476))
    slope = half + inner * (jnp.exp(-0.5 * inner * inner) * 0.3989422804014327)
    return inner * half, slope


def three(value):
    first = value.astype(low)
    rest = value - first.astype(high)
    second = rest.astype(low)
    third = (rest - second.astype(high)).astype(low)
    return first, second, third


def meets(seg_q, first_q, size_q, seg_k, first_k, size_k):
    return (seg_q[first_q + size_q - 1] >= seg_k[first_k]) & (
        seg_q[first_q] <= seg_k[first_k + size_k - 1]
    )


def score_part(r, q_ref, q_row, first_q, seg_q, seg_k, ka_ref, vt_ref, acc_ref, top_ref, width):
    heads, keys = ka_ref.shape[0], ka_ref.shape[1]
    block = acc_ref.shape[2]
    acc_ref[...] = jnp.zeros_like(acc_ref)
    top_ref[...] = jnp.full_like(top_ref, 2 * FAR)

    def one_block(b, carry):
        first_k = b * width

        @pl.when(meets(seg_q, first_q, block, seg_k, first_k, width))
        def _():
            for h in range(heads):
                scores = nt(ka_ref[h, pl.ds(first_k, width), :], q_ref[h, q_row])
                top = top_ref[h]
                peak = jnp.maximum(top, jnp.max(scores, axis=0, keepdims=True))
                weights = jnp.exp(scores - peak).astype(low)
                acc_ref[h] = acc_ref[h] * jnp.exp(top - peak) + nn(
                    vt_ref[h, :, pl.ds(first_k, width)], weights
                )
                top_ref[h] = peak

        return carry

    lax.fori_loop(0, keys // width, one_block, 0)
    outs = []
    lane = lax.broadcasted_iota(jnp.int32, (block, HEAD_DIM), 1)
    for h in range(heads):
        acc = acc_ref[h]
        total = acc[HEAD_DIM : HEAD_DIM + 1]
        lse = top_ref[h] + jnp.log(total)
        joined = jnp.concatenate(
            [acc[:HEAD_DIM] / total, jnp.broadcast_to(lse, (HEAD_DIM, block))], axis=0
        )
        turned = joined.T
        outs.append(turned[:, :HEAD_DIM])
        minus = three(-turned[:, HEAD_DIM:])
        mask = q_ref[h, q_row, :, HEAD_DIM:].astype(high)
        for i in range(3):
            mask = jnp.where(lane == LSE_LANE + i, minus[i].astype(high), mask)
        q_ref[h, q_row, :, HEAD_DIM:] = mask.astype(low)
    return jnp.concatenate(outs, axis=1)


def attend_far_kernel(*refs, block, width, heads, marks):
    pieces = len(marks)
    here, seg_q, seg_k, x_ref, halo_ref, bias_ref, mq_ref, mk_ref = refs[:8]
    w_refs = refs[8 : 8 + pieces]
    (out_2, out_3, full_ref, q_near, q_far, ka_ref, v_ref, vt_ref, w_ref) = refs[8 + pieces : 17 + pieces]
    acc_ref, top_ref, sems = refs[17 + pieces :]
    keys = v_ref.shape[0]
    rows = x_ref.shape[0]
    local = heads * HEAD_DIM
    scale = 1.0 / math.sqrt(HEAD_DIM)
    mine, f, c = here[0], here[1], here[2]
    copies = []
    for i, spots in enumerate(marks):
        offset = 0
        for mark in spots:
            first, count = mark(f, c)
            src = w_refs[i].at[pl.ds(offset, count)]
            copies.append(
                pltpu.make_async_copy(src, w_ref.at[pl.ds(first, count)], sems.at[len(copies)])
            )
            copies[-1].start()
            offset += count
    vt_ref[:, HEAD_DIM:, :] = jnp.ones((heads, vt_ref.shape[1] - HEAD_DIM, keys), low)
    for copy in copies:
        copy.wait()
    weights_all = w_ref[...].reshape(-1, w_ref.shape[2])

    def keep(first, count, mask, kv):
        span = pl.ds(first, count)
        for h in range(heads):
            cols = slice(h * HEAD_DIM, (h + 1) * HEAD_DIM)
            tail = slice(local + h * HEAD_DIM, local + (h + 1) * HEAD_DIM)
            ka_ref[h, span, :] = jnp.concatenate([kv[:, cols], mask], axis=1)
            vt_ref[h, :HEAD_DIM, span] = kv[:, tail].T
        v_ref[span, :] = kv[:, local:]

    for q_ref, base in ((q_near, 0), (q_far, 2)):

        def project(i, carry, q_ref=q_ref, base=base):
            first = pl.multiple_of((mine ^ (base + i)) * block, block)
            span = pl.ds(first, block)
            both = (nn(x_ref[span, :], weights_all) + bias_ref[...]).astype(low)
            for h in range(heads):
                cols = slice(h * HEAD_DIM, (h + 1) * HEAD_DIM)
                q_ref[h, i] = jnp.concatenate(
                    [both[:, cols] * jnp.array(scale, low), mq_ref[span, :]], axis=1
                )
            keep(first, block, mk_ref[span, :], both[:, local:])
            return carry

        lax.fori_loop(0, 2, project, 0)
    step = min(512, keys - rows)
    for first in range(rows, keys, step):
        span = slice(first - rows, first - rows + step)
        kv = (nn(halo_ref[span, :], weights_all[:, local:]) + bias_ref[:, local:]).astype(low)
        keep(first, step, mk_ref[first : first + step, :], kv)
    for i, out_ref in enumerate((out_2, out_3)):
        joined = score_part(
            2 + i, q_far, i, (mine ^ (2 + i)) * block, seg_q, seg_k, ka_ref, vt_ref, acc_ref, top_ref, width
        )
        full_ref[i] = joined
        out_ref[...] = joined.astype(low)


def attend_near_kernel(
    here, seg_q, seg_k, q_in, ka_ref, vt_ref, out_0, out_1, full_ref, q_ref, acc_ref, top_ref, *, block, width
):
    mine = here[0]
    q_ref[...] = q_in[...]
    for i, out_ref in enumerate((out_0, out_1)):
        joined = score_part(
            i, q_ref, i, (mine ^ i) * block, seg_q, seg_k, ka_ref, vt_ref, acc_ref, top_ref, width
        )
        full_ref[i] = joined
        out_ref[...] = joined.astype(low)


VMEM = pl.BlockSpec(memory_space=pltpu.VMEM)
SMEM = pl.BlockSpec(memory_space=pltpu.SMEM)
ANY = pl.BlockSpec(memory_space=pl.ANY)
HBM = pl.BlockSpec(memory_space=pltpu.HBM)


def shape(*dims, kind=low):
    return jax.ShapeDtypeStruct(dims, kind)


def cost(flops, size, transcendentals=0):
    return pl.CostEstimate(flops=flops, transcendentals=transcendentals, bytes_accessed=size)


def attend_far(here, seg_q, seg_k, x, halo, bias, mask_q, mask_k, pieces, marks, blocks, block):
    rows = x.shape[0]
    local = bias.shape[1] // 3
    count = rows + halo.shape[0]
    heads = local // HEAD_DIM
    wide = 2 * HEAD_DIM
    return pl.pallas_call(
        lambda *refs: attend_far_kernel(*refs, block=block, width=256, heads=heads, marks=marks),
        name="attend_far",
        out_shape=(
            shape(block, local),
            shape(block, local),
            shape(2, block, local, kind=high),
            shape(heads, 2, block, wide),
            shape(heads, 2, block, wide),
            shape(heads, count, wide),
            shape(count, local),
            shape(heads, HEAD_DIM + 16, count),
            shape(*blocks, 3 * local),
        ),
        in_specs=[SMEM] * 3 + [VMEM] * 5 + [ANY] * len(pieces),
        out_specs=(VMEM,) * 9,
        scratch_shapes=[
            pltpu.VMEM((heads, HEAD_DIM + 16, block), high),
            pltpu.VMEM((heads, 1, block), high),
            pltpu.SemaphoreType.DMA((sum(map(len, marks)),)),
        ],
        cost_estimate=cost(FAR_COST, 8 << 20),
    )(here, seg_q, seg_k, x, halo, bias, mask_q, mask_k, *pieces)


def attend_near(here, seg_q, seg_k, q_near, keys_wide, values_t):
    heads, _, block, wide = q_near.shape
    local = heads * HEAD_DIM
    return pl.pallas_call(
        lambda *refs: attend_near_kernel(*refs, block=block, width=256),
        name="attend_near",
        out_shape=(
            shape(block, local),
            shape(block, local),
            shape(2, block, local, kind=high),
            shape(heads, 2, block, wide),
        ),
        in_specs=[SMEM] * 3 + [VMEM] * 3,
        out_specs=(VMEM,) * 4,
        scratch_shapes=[
            pltpu.VMEM((heads, HEAD_DIM + 16, block), high),
            pltpu.VMEM((heads, 1, block), high),
        ],
        cost_estimate=cost(NEAR_COST, 8 << 20),
    )(here, seg_q, seg_k, q_near, keys_wide, values_t)


FAR_COST = 20 * 10**9
NEAR_COST = 12 * 10**9
FEED_COST = 26 * 10**9
UNIT_COST = 12 * 10**9
BACK_COST = 24 * 10**9
LAST_COST = 9 * 10**9
SMALL_COST = 3 * 10**9


def feed_kernel(*refs, plan, count, hidden, local):
    here, x_all, g_all, att_0, att_1, att_2, att_3, vec_ref = refs[:8]
    w_refs = refs[8 : 8 + count]
    (out_ref, one_ref, stat_ref, ga_0, ga_1, ga_2, ga_3, rows_hbm, keep_hbm, send_hbm) = refs[8 + count : 18 + count]
    (w_ref, b_ref, x_ref, g_ref, att_ref, hat_ref, inv_ref, norm_ref, acc_ref, slope_ref, gl_ref,
     rows_ref, keep_ref, send_ref, sems, out_sems) = refs[18 + count :]
    puts = []

    def put(src, dst):
        puts.append(pltpu.make_async_copy(src, dst, out_sems.at[len(puts)]))
        puts[-1].start()

    tokens, width = x_ref.shape
    mine, f, c = here[0], here[1], here[2]
    wide = 2 * hidden + local
    copies = []

    def begin(src, dst):
        copies.append(pltpu.make_async_copy(src, dst, sems.at[len(copies)]))
        copies[-1].start()

    first = pl.multiple_of(mine * tokens, tokens)
    begin(x_all.at[pl.ds(first, tokens)], x_ref)
    begin(g_all.at[pl.ds(first, tokens)], g_ref)
    for r, att in enumerate((att_0, att_1, att_2, att_3)):
        begin(att, att_ref.at[r])
    for i, offset, r, mark in plan:
        if mark is None:
            begin(w_refs[i].at[pl.ds(offset, 8)], b_ref.at[r])
        else:
            start, size = mark(f, c)
            begin(
                w_refs[i].at[pl.ds(offset, size), pl.ds(2 * hidden, local)],
                w_ref.at[r, pl.ds(start, size), pl.ds(2 * hidden, local)],
            )
    first_copies = len(copies)
    for i, offset, r, mark in plan:
        if mark is not None:
            start, size = mark(f, c)
            begin(
                w_refs[i].at[pl.ds(offset, size), pl.ds(0, 2 * hidden)],
                w_ref.at[r, pl.ds(start, size), pl.ds(0, 2 * hidden)],
            )
    for copy in copies[:first_copies]:
        copy.wait()
    b_out, gain_one, shift_one, b_outer, gain_two, shift_two = (
        vec_ref[i : i + 1, :].astype(high) for i in range(6)
    )

    def weights(r, first, last):
        return w_ref[r, :, first:last]

    acc_ref[...] = nt(att_ref[0], weights(0, 2 * hidden, 2 * hidden + local))
    for r in range(1, 4):
        acc_ref[...] += nt(att_ref[r], weights(r, 2 * hidden, 2 * hidden + local))
    step = 64
    chunks = tokens // step

    def first_norm(i, carry):
        span = pl.ds(pl.multiple_of(i * step, step), step)
        hat, inverse = norm_parts(x_ref[span, :].astype(high) + (acc_ref[span, :] + b_out))
        hat_ref[span, :] = hat
        inv_ref[span, :] = inverse
        normed = hat * gain_one + shift_one
        norm_ref[span, :] = normed.astype(low)
        acc_ref[span, :] = normed + b_outer
        return carry

    lax.fori_loop(0, chunks, first_norm, 0)
    for copy in copies[first_copies:]:
        copy.wait()
    part = 256
    for k, side in enumerate((keep_ref, send_ref)):
        for x in range(2):
            side[x, :, 2 * hidden : wide] = att_ref[2 * x + k]
            side[x, :, wide:] = jnp.zeros((tokens, side.shape[2] - wide), low)

        def up(x, carry, k=k, side=side):
            r = 2 * x + k
            for j in range(0, hidden, part):
                inner = nn(norm_ref[...], weights(r, j, j + part))
                inner = inner + b_ref[r, 0:1, j : j + part].astype(high)
                act, slope = gelu_parts(inner)
                side[x, :, hidden + j : hidden + j + part] = act.astype(low)
                slope_ref[r, :, j : j + part] = slope
            acc_ref[...] += nt(side[x, :, hidden : 2 * hidden], weights(r, hidden, 2 * hidden))
            return carry

        lax.fori_loop(0, 2, up, 0)

    zero = jnp.zeros((1, width), high)

    def second_norm(i, sums):
        span = pl.ds(pl.multiple_of(i * step, step), step)
        hat, inverse = norm_parts(acc_ref[span, :])
        out_ref[span, :] = (hat * gain_two + shift_two).astype(low)
        grad = g_ref[span, :].astype(high)
        two = norm_back(grad, hat, inverse, gain_two)
        acc_ref[span, :] = two
        two_low = two.astype(low)
        gl_ref[span, :] = two_low
        terms = (two_low.astype(high), grad * hat, grad)
        return tuple(s + jnp.sum(v, axis=0, keepdims=True) for s, v in zip(sums, terms))

    sums_two = lax.fori_loop(0, chunks, second_norm, (zero,) * 3)
    rows_ref[0] = norm_ref[...].T
    rows_ref[1] = gl_ref[...].T
    put(rows_ref.at[pl.ds(0, 2)], rows_hbm.at[pl.ds(0, 2)])
    for k, side in ((1, send_ref), (0, keep_ref)):

        def down(x, carry, k=k, side=side):
            r = 2 * x + k
            for j in range(0, hidden, part):
                grad = nn(gl_ref[...], weights(r, hidden + j, hidden + j + part))
                grad = (grad * slope_ref[r, :, j : j + part]).astype(low)
                side[x, :, j : j + part] = grad
                stat_ref[8 + r, 0:1, j : j + part] = jnp.sum(grad.astype(high), axis=0, keepdims=True)
            acc_ref[...] += nt(side[x, :, :hidden], weights(r, 0, hidden))
            return carry

        lax.fori_loop(0, 2, down, 0)
        put(side, send_hbm if k else keep_hbm)

    def first_back(i, sums):
        span = pl.ds(pl.multiple_of(i * step, step), step)
        grad = acc_ref[span, :]
        hat = hat_ref[span, :]
        one = norm_back(grad, hat, inv_ref[span, :], gain_one)
        one_ref[span, :] = one
        one_low = one.astype(low)
        gl_ref[span, :] = one_low
        terms = (one_low.astype(high), grad * hat, grad)
        return tuple(s + jnp.sum(v, axis=0, keepdims=True) for s, v in zip(sums, terms))

    sums_one = lax.fori_loop(0, chunks, first_back, (zero,) * 3)
    for i, value in enumerate(sums_one + sums_two):
        stat_ref[i, 0:1, :] = value
    rows_ref[2] = gl_ref[...].T
    put(rows_ref.at[2], rows_hbm.at[2])
    for r, ga in enumerate((ga_0, ga_1, ga_2, ga_3)):
        ga[...] = nn(gl_ref[...], weights(r, 2 * hidden, 2 * hidden + local)).astype(low)
    for copy in puts:
        copy.wait()


def feed(here, x, grad, att, vectors, pieces, plan, tokens, hidden, local):
    width = x.shape[1]
    wide = 2 * hidden + local
    padded = (wide + 127) // 128 * 128
    copies = 6 + len(plan) + sum(mark is not None for _, _, _, mark in plan)
    return pl.pallas_call(
        lambda *refs: feed_kernel(*refs, plan=plan, count=len(pieces), hidden=hidden, local=local),
        name="feed",
        out_shape=(
            shape(tokens, width),
            shape(tokens, width, kind=high),
            shape(12, 1, width, kind=high),
            shape(tokens, local),
            shape(tokens, local),
            shape(tokens, local),
            shape(tokens, local),
            shape(3, width, tokens),
            shape(2, tokens, padded),
            shape(2, tokens, padded),
        ),
        in_specs=[SMEM] + [ANY] * 6 + [VMEM] + [ANY] * len(pieces),
        out_specs=(VMEM,) * 7 + (HBM,) * 3,
        scratch_shapes=[
            pltpu.VMEM((4, width, wide), low),
            pltpu.VMEM((4, 8, wide), low),
            pltpu.VMEM((tokens, width), low),
            pltpu.VMEM((tokens, width), low),
            pltpu.VMEM((4, tokens, local), low),
            pltpu.VMEM((tokens, width), high),
            pltpu.VMEM((tokens, 1), high),
            pltpu.VMEM((tokens, width), low),
            pltpu.VMEM((tokens, width), high),
            pltpu.VMEM((4, tokens, hidden), high),
            pltpu.VMEM((tokens, width), low),
            pltpu.VMEM((3, width, tokens), low),
            pltpu.VMEM((2, tokens, padded), low),
            pltpu.VMEM((2, tokens, padded), low),
            pltpu.SemaphoreType.DMA((copies,)),
            pltpu.SemaphoreType.DMA((4,)),
        ],
        cost_estimate=cost(FEED_COST, 24 << 20),
    )(here, x, grad, *att, vectors, *pieces)


def unit_kernel(here, rows_own, rows_mate, wide_own, wide_mate, *refs, hidden):
    ak_ref, as_ref, bk_ref, bs_ref, rows_ref, wide_ref, sems = refs
    c = here[2]
    tokens = rows_own.shape[2]
    wide = ak_ref.shape[2]
    half = ak_ref.shape[1]
    mid = rows_own.shape[1] // 2
    copies = [
        pltpu.make_async_copy(rows_own, rows_ref.at[:, :, pl.ds(0, tokens)], sems.at[0]),
        pltpu.make_async_copy(wide_own, wide_ref.at[:, pl.ds(0, tokens)], sems.at[1]),
        pltpu.make_async_copy(rows_mate, rows_ref.at[:, :, pl.ds(tokens, tokens)], sems.at[2]),
        pltpu.make_async_copy(wide_mate, wide_ref.at[:, pl.ds(tokens, tokens)], sems.at[3]),
    ]
    for copy in copies:
        copy.start()
    for copy in copies:
        copy.wait()
    spans = ((0, 0, hidden), (1, hidden, 2 * hidden), (2, 2 * hidden, wide))
    for x in range(2):
        for i, first, last in spans:
            for top in range(2):
                part = slice(top * mid, (top + 1) * mid)
                got = nn(rows_ref[i, part, :], wide_ref[x, :, first:last]).astype(low)
                if top == 0:
                    side = ak_ref if x == 0 else as_ref
                    side[:, :, first:last] = got.reshape(-1, half, last - first)
                else:
                    got = got.reshape(-1, 2, half, last - first)
                    for z in range(got.shape[0]):

                        @pl.when(c == 0)
                        def _():
                            bk_ref[x, z, :, first:last] = got[z, 0]
                            bs_ref[x, z, :, first:last] = got[z, 1]

                        @pl.when(c != 0)
                        def _():
                            bk_ref[x, z, :, first:last] = got[z, 1]
                            bs_ref[x, z, :, first:last] = got[z, 0]


def unit_grads(here, rows, mate_rows, keep, mate, half, hidden, local):
    wide = 2 * hidden + local
    tokens = rows.shape[2]
    width = rows.shape[1]
    quarters = width // 4 // half
    return pl.pallas_call(
        lambda *refs: unit_kernel(*refs, hidden=hidden),
        name="unit_grads",
        out_shape=(
            shape(2 * quarters, half, wide),
            shape(2 * quarters, half, wide),
            shape(2, quarters, half, wide),
            shape(2, quarters, half, wide),
        ),
        in_specs=[SMEM] + [ANY] * 4,
        out_specs=(VMEM,) * 4,
        scratch_shapes=[
            pltpu.VMEM((3, width, 2 * tokens), low),
            pltpu.VMEM((2, 2 * tokens, keep.shape[2]), low),
            pltpu.SemaphoreType.DMA((4,)),
        ],
        cost_estimate=cost(UNIT_COST, 14 << 20),
    )(here, rows, mate_rows, keep, mate)


def merge_one_kernel(here, ak, ga, bk, gb, a_keep, a_send, b_keep, b_send):
    c = here[2]
    for z in range(2):
        for side in range(2):
            i = 2 * z + side
            got = ak[i] + ga[i]

            @pl.when(c == side)
            def _():
                a_keep[z] = got

            @pl.when(c != side)
            def _():
                a_send[z] = got

    b_keep[...] = bk[0] + gb[0]
    b_send[...] = bk[1] + gb[1]


def merge_one(here, ak, ga, bk, gb):
    out = shape(*bk.shape[1:])
    return pl.pallas_call(
        merge_one_kernel,
        name="merge_one",
        out_shape=(out,) * 4,
        in_specs=[SMEM] + [VMEM] * 4,
        out_specs=(VMEM,) * 4,
        cost_estimate=cost(SMALL_COST, 8 << 20),
    )(here, ak, ga, bk, gb)


def merge_two_kernel(here, a_keep, a_got, b_keep, b_got, d_keep, d_got, *refs, start):
    outs, all_ref = refs[:4], refs[4]
    f = here[1]
    wide = a_keep.shape[2]
    for z in range(2):
        all_ref[z, :, :wide] = a_keep[z] + a_got[z]
        all_ref[2 + z, :, :wide] = b_keep[z] + b_got[z]
    all_ref[:, :, start:] = d_keep[...] + d_got[...]
    for s, out in enumerate(outs):
        out[...] = all_ref[(f + s) % 4]


def merge_two(here, a_keep, a_got, b_keep, b_got, d_keep, d_got, start):
    half = a_keep.shape[1]
    full = start + d_keep.shape[2]
    return pl.pallas_call(
        lambda *refs: merge_two_kernel(*refs, start=start),
        name="merge_two",
        out_shape=(shape(half, full),) * 4,
        in_specs=[SMEM] + [VMEM] * 6,
        out_specs=(VMEM,) * 4,
        scratch_shapes=[pltpu.VMEM((4, half, full), low)],
        cost_estimate=cost(SMALL_COST, 8 << 20),
    )(here, a_keep, a_got, b_keep, b_got, d_keep, d_got)


def merge_three_kernel(here, own, got_1, got_2, got_3, out, all_ref):
    f = here[1]
    for s, piece in enumerate((own, got_1, got_2, got_3)):
        all_ref[(f - s + 4) % 4] = piece[...]
    total = all_ref[0].astype(high)
    for z in range(1, 4):
        total = total + all_ref[z].astype(high)
    out[...] = total.astype(low)


def merge_three(here, pieces):
    return pl.pallas_call(
        merge_three_kernel,
        name="merge_three",
        out_shape=shape(*pieces[0].shape),
        in_specs=[SMEM] + [VMEM] * 4,
        out_specs=VMEM,
        scratch_shapes=[pltpu.VMEM((4,) + pieces[0].shape, low)],
        cost_estimate=cost(SMALL_COST, 4 << 20),
    )(here, *pieces)


def finish_kernel(here, own, got, inner, outer, out, query, key, value, bias, all_ref, *, start):
    c = here[2]
    hidden = inner.shape[1]
    local = query.shape[1]
    all_ref[c] = own[...]
    all_ref[1 - c] = got[...]
    half, full = own.shape

    def cols(first, last):
        return all_ref[:, :, first:last].reshape(2 * half, last - first).astype(high)

    inner[...] = cols(0, hidden)
    outer[...] = cols(hidden, 2 * hidden)
    out[...] = cols(2 * hidden, 2 * hidden + local).T
    rest = cols(start, full)
    query[...] = rest[:, :local]
    key[...] = rest[:, local : 2 * local]
    value[...] = rest[:, 2 * local : 3 * local]
    bias[...] = own[:16, start + 3 * local :].astype(high)


def finish(here, own, got, start, hidden, local):
    half, full = own.shape
    piece = 2 * half
    return pl.pallas_call(
        lambda *refs: finish_kernel(*refs, start=start),
        name="finish",
        out_shape=(
            shape(piece, hidden, kind=high),
            shape(piece, hidden, kind=high),
            shape(local, piece, kind=high),
            shape(piece, local, kind=high),
            shape(piece, local, kind=high),
            shape(piece, local, kind=high),
            shape(16, full - start - 3 * local, kind=high),
        ),
        in_specs=[SMEM] + [VMEM] * 2,
        out_specs=(VMEM,) * 7,
        scratch_shapes=[pltpu.VMEM((2, half, full), low)],
        cost_estimate=cost(SMALL_COST, 4 << 20),
    )(here, own, got)


def spread_kernel(here, p_0, p_1, p_2, p_3, out):
    tokens = p_0.shape[0]
    for r, piece in enumerate((p_0, p_1, p_2, p_3)):
        first = pl.multiple_of((here[0] ^ r) * tokens, tokens)
        out[pl.ds(first, tokens), :] = piece[...].astype(out.dtype)


def spread(here, pieces, kind):
    tokens, width = pieces[0].shape
    return pl.pallas_call(
        spread_kernel,
        name="spread",
        out_shape=shape(4 * tokens, width, kind=kind),
        in_specs=[SMEM] + [VMEM] * 4,
        out_specs=VMEM,
        cost_estimate=cost(SMALL_COST, 8 << 20),
    )(here, *pieces)


def project_back_kernel(here, g_ref, edge_ref, x_ref, w_ref, keep, send, d_keep, d_send, all_ref, *, local):
    mine, c = here[0], here[2]
    rows = g_ref.shape[0]
    rim = edge_ref.shape[0]
    tokens = keep.shape[1]
    half = d_keep.shape[1]
    pad = d_keep.shape[2] - 3 * local
    all_ref[...] = g_ref[...]
    edge = pl.ds(pl.multiple_of((1 - c) * (rows - rim), rim), rim)
    all_ref[edge, local:] = (
        g_ref[edge, local:].astype(high) + edge_ref[...].astype(high)
    ).astype(low)
    for k, side in ((1, send), (0, keep)):
        for x in range(2):
            first = pl.multiple_of((mine ^ (2 * x + k)) * tokens, tokens)
            side[x] = nt(all_ref[pl.ds(first, tokens), :], w_ref[...]).astype(low)
    sums = jnp.zeros((1, 3 * local), high)
    for i in range(rows // tokens):
        part = all_ref[i * tokens : (i + 1) * tokens, :].astype(high)
        sums = sums + jnp.sum(part, axis=0, keepdims=True)
    row = lax.broadcasted_iota(jnp.int32, (half, pad), 0)
    extra = jnp.zeros((half, pad), high)
    for j in range(3 * local // pad):
        extra = jnp.where(row == j, sums[:, j * pad : (j + 1) * pad], extra)
    extra = extra.astype(low)
    got = tn(x_ref[...], all_ref[...]).astype(low).reshape(-1, 2, half, 3 * local)
    for z in range(got.shape[0]):
        d_keep[z, :, 3 * local :] = extra
        d_send[z, :, 3 * local :] = extra
        for side in range(2):

            @pl.when(c == side)
            def _():
                d_keep[z, :, : 3 * local] = got[z, side]

            @pl.when(c != side)
            def _():
                d_send[z, :, : 3 * local] = got[z, side]


def project_back(here, grads, edge, x, weights, tokens, half):
    rows, width = x.shape
    local = grads.shape[1] // 3
    pad = HEAD_DIM
    return pl.pallas_call(
        lambda *refs: project_back_kernel(*refs, local=local),
        name="project_back",
        out_shape=(
            shape(2, tokens, width),
            shape(2, tokens, width),
            shape(width // half // 2, half, 3 * local + pad),
            shape(width // half // 2, half, 3 * local + pad),
        ),
        in_specs=[SMEM] + [VMEM] * 4,
        out_specs=(VMEM,) * 4,
        scratch_shapes=[pltpu.VMEM(grads.shape, low)],
        cost_estimate=cost(LAST_COST, 8 << 20),
    )(here, grads, edge, x, weights)


def attend_back_kernel(
    here, seg_q, seg_k, g_0, g_1, g_2, g_3, full_near, full_far, q_near, q_far, ka_ref, v_ref, own_ref, rim_ref,
    g_ref, full_ref, q_ref, kt_ref, va_ref, ga_ref, dka_ref, dva_ref, dqa_ref, sems, *, block, width, heads
):
    copies = [
        pltpu.make_async_copy(g, g_ref.at[r], sems.at[r]) for r, g in enumerate((g_0, g_1, g_2, g_3))
    ]
    for i, (q_part, full_part) in enumerate(((q_near, full_near), (q_far, full_far))):
        span = pl.ds(2 * i, 2)
        copies.append(pltpu.make_async_copy(q_part, q_ref.at[:, span], sems.at[4 + 2 * i]))
        copies.append(pltpu.make_async_copy(full_part, full_ref.at[span], sems.at[5 + 2 * i]))
    for copy in copies:
        copy.start()
    keys = v_ref.shape[0]
    rows = own_ref.shape[0]
    local = heads * HEAD_DIM
    scale = 1.0 / math.sqrt(HEAD_DIM)
    mine = here[0]
    for h in range(heads):
        cols = slice(h * HEAD_DIM, (h + 1) * HEAD_DIM)
        kt_ref[h] = ka_ref[h, :, :HEAD_DIM].T
        va_ref[h] = jnp.concatenate([v_ref[:, cols], jnp.ones((keys, HEAD_DIM), low)], axis=1)
    dka_ref[...] = jnp.zeros_like(dka_ref)
    dva_ref[...] = jnp.zeros_like(dva_ref)
    for copy in copies:
        copy.wait()

    def one_part(i, carry):
        first_q = pl.multiple_of((mine ^ i) * block, block)
        for h in range(heads):
            cols = slice(h * HEAD_DIM, (h + 1) * HEAD_DIM)
            grad = g_ref[i, :, cols]
            delta = jnp.sum(grad.astype(high) * full_ref[i, :, cols], axis=1, keepdims=True)
            lane = lax.broadcasted_iota(jnp.int32, (block, HEAD_DIM), 1)
            extra = jnp.zeros((block, HEAD_DIM), high)
            for j, piece in enumerate(three(-delta)):
                extra = jnp.where(lane == j, piece.astype(high), extra)
            ga_ref[h] = jnp.concatenate([grad, extra.astype(low)], axis=1)
        dqa_ref[...] = jnp.zeros_like(dqa_ref)

        def one_block(b, carry):
            first_k = b * width

            @pl.when(meets(seg_q, first_q, block, seg_k, first_k, width))
            def _():
                for h in range(heads):
                    span = pl.ds(first_k, width)
                    asks = q_ref[h, i]
                    probs = jnp.exp(nt(ka_ref[h, span, :], asks))
                    slopes = (probs * nt(va_ref[h, span, :], ga_ref[h])).astype(low)
                    dva_ref[h, span, :] += nn(probs.astype(low), ga_ref[h, :, :HEAD_DIM])
                    dka_ref[h, span, :] += nn(slopes, asks[:, :HEAD_DIM])
                    dqa_ref[h] += nn(kt_ref[h, :, span], slopes)

            return carry

        lax.fori_loop(0, keys // width, one_block, 0)
        own_ref[pl.ds(first_q, block), :local] = jnp.concatenate(
            [(dqa_ref[h] * scale).T for h in range(heads)], axis=1
        ).astype(low)
        return carry

    lax.fori_loop(0, 4, one_part, 0)
    for j, part in enumerate((dka_ref, dva_ref)):
        wide = jnp.concatenate([part[h] for h in range(heads)], axis=1).astype(low)
        own_ref[:, (1 + j) * local : (2 + j) * local] = wide[:rows]
        rim_ref[:, j * local : (j + 1) * local] = wide[rows:]


def attend_back(here, seg_q, seg_k, grads, full_near, full_far, q_near, q_far, keys, values):
    parts = len(grads)
    block, local = grads[0].shape
    rows = parts * block
    count = values.shape[0]
    heads = local // HEAD_DIM
    return pl.pallas_call(
        lambda *refs: attend_back_kernel(*refs, block=block, width=256, heads=heads),
        name="attend_back",
        out_shape=(shape(rows, 3 * local), shape(count - rows, 2 * local)),
        in_specs=[SMEM] * 3 + [ANY] * 8 + [VMEM] * 2,
        out_specs=(VMEM,) * 2,
        scratch_shapes=[
            pltpu.VMEM((parts, block, local), low),
            pltpu.VMEM((parts, block, local), high),
            pltpu.VMEM((heads, parts, block, 2 * HEAD_DIM), low),
            pltpu.VMEM((heads, HEAD_DIM, count), low),
            pltpu.VMEM((heads, count, 2 * HEAD_DIM), low),
            pltpu.VMEM((heads, block, 2 * HEAD_DIM), low),
            pltpu.VMEM((heads, count, HEAD_DIM), high),
            pltpu.VMEM((heads, count, HEAD_DIM), high),
            pltpu.VMEM((heads, HEAD_DIM, block), high),
            pltpu.SemaphoreType.DMA((parts + 4,)),
        ],
        cost_estimate=cost(BACK_COST, 8 << 20),
    )(here, seg_q, seg_k, *grads, full_near, full_far, q_near, q_far, keys, values)


def after(values, gate):
    return lax.optimization_barrier((tuple(values), gate))[0]


def halo_of(value, c, span):
    rows = value.shape[0]
    return take(value, (1 - c) * (rows - span), span)


def shards(
    inputs, segments, w_query, b_query, w_key, w_value, b_value, w_out, b_out, gain_one, shift_one,
    w_inner, b_inner, w_outer, b_outer, gain_two, shift_two, grad_output,
):
    rows, width = inputs.shape
    local = w_query.shape[1]
    hidden = w_inner.shape[1]
    n_f, n_c, n_t = (lax.axis_size(a) for a in ("fsdp", "ctx", "tp"))
    f, c, t = (lax.axis_index(a) for a in ("fsdp", "ctx", "tp"))
    tokens = rows // n_t
    rim = MOST
    quick = n_f == 4 and n_c == 2 and n_t == 4
    piece = width // n_f
    flip = [t ^ r for r in range(n_t)]

    half = piece // 2
    blocks = (2 * n_f, half)
    here = jnp.stack([t, f, c]).astype(jnp.int32)
    bundle_a = jnp.concatenate([w_query, w_key, w_value], axis=1)

    def spot(s, side):
        def mark(f, c):
            return (f - s + n_f) % n_f * 2 + (c if side == 0 else 1 - c), 1

        return mark

    def spot_from(s):
        return lambda f, c: ((f - s + n_f) % n_f * 2, 2)

    def spot_all(f, c):
        return 0, 2 * n_f

    def in_rows(mark):
        def rows_mark(f, c):
            first, count = mark(f, c)
            return (first if isinstance(first, int) else pl.multiple_of(first * half, half)), count * half

        return rows_mark

    seg_own = segments.reshape(rows)
    if quick:
        halves_a = bundle_a.reshape(2, half, -1)
        own_a = lax.dynamic_index_in_dim(halves_a, c, 0)
        gots_a = [shift(own_a, "fsdp", s) for s in range(1, n_f)]
        joined = jnp.concatenate(gots_a, axis=0)
        mates_a = swap(joined, "ctx", 1)
        pieces_a = [halves_a, joined, mates_a]
        marks_a = [[spot_from(0)]]
        marks_a += [[spot(s, side) for s in range(1, n_f)] for side in range(2)]
    else:
        whole_a = lax.all_gather(bundle_a, "fsdp", axis=0, tiled=True)
        pieces_a, marks_a = [whole_a.reshape(blocks + (-1,))], [[spot_all]]

    if n_c == 2:
        sent = halo_of(inputs, c, rim)
        if quick:
            part = rim // 2
            ids = halo_of(seg_own, c, rim).astype(low).reshape(2, part)
            ids = jnp.pad(ids, ((0, 14), (0, width - part)))
            got = swap(jnp.concatenate([take(sent, (t & 1) * part, part), ids], axis=0), "ctx", 1)
            halo_seg = got[part : part + 2, :part].astype(jnp.int32).reshape(rim)
            got = got[:part]
            mate = swap(got, "tp", 1)
            even = (t & 1) == 0
            halo_in = jnp.concatenate([jnp.where(even, got, mate), jnp.where(even, mate, got)], axis=0)
        else:
            halo_in = swap(sent, "ctx", 1)
            halo_seg = swap(halo_of(seg_own, c, rim), "ctx", 1)
    else:
        ahead = [(i, i + 1) for i in range(n_c - 1)]
        behind = [(i + 1, i) for i in range(n_c - 1)]

        def both(value):
            return jnp.concatenate(
                [
                    lax.ppermute(value[rows - rim :], "ctx", ahead),
                    lax.ppermute(value[:rim], "ctx", behind),
                ],
                axis=0,
            )

        halo_in = both(inputs)
        halo_seg = both(seg_own + 1) - 1
        halo_seg = jnp.where(halo_seg < 0, NO_ID, halo_seg)

    bias_row = jnp.pad(b_inner[None], ((0, 7), (0, hidden + local)))
    bundle_f = jnp.concatenate([w_inner, w_outer.T, w_out.T], axis=1)
    own_rows = jnp.concatenate([bundle_f, bias_row], axis=0)
    if quick:
        far_rows = swap(own_rows, "tp", 2)
        own_f = take(bundle_f, c * half, half)
        (own_1,) = after([own_f], joined)
        gots = {s: shift(own_1, "fsdp", s) for s in (1, 3)}
        halo_in, far_rows = lax.optimization_barrier((halo_in, far_rows))
        far_f = take(far_rows, (1 - c) * half, half)
        corners = {s: shift(far_f, "fsdp", s) for s in (1, 3)}

    bias = jnp.concatenate([b_query, jnp.zeros_like(b_query), b_value]).astype(high)[None]
    seg_all = jnp.concatenate([seg_own, halo_seg])
    lane = jnp.arange(IDS)
    near_id = seg_all[:, None] == lane
    mask_k = (near_id | ((lane >= LSE_LANE) & (lane < LSE_LANE + 3))).astype(low)
    mask_q = jnp.where(near_id[:rows] | ((lane >= LSE_LANE) & (lane < LSE_LANE + 3)), 0.0, FAR).astype(low)
    att_2, att_3, full_far, q_near, q_far, keys_wide, values, values_t, w_qkv = attend_far(
        here, seg_own, seg_all, inputs, halo_in, bias, mask_q, mask_k, pieces_a, marks_a, blocks, tokens
    )
    w_qkv = w_qkv.reshape(width, 3 * local)

    if quick:
        (own_2,) = after([own_f], att_2)
        gots[2] = shift(own_2, "fsdp", 2)
        (far_2,) = after([far_f], att_2)
        corners[2] = shift(far_2, "fsdp", 2)
        *near, corners[1], corners[3] = after([gots[1], gots[3], corners[1], corners[3]], att_2)
        (q_near,) = after([q_near], (*near, corners[1], corners[3]))
    att_0, att_1, full_near, q_near = attend_near(here, seg_own, seg_all, q_near, keys_wide, values_t)
    if quick:
        pieces_f, plan = [], []

        def add(r, value, marks, gate=None, bias=False):
            twin = value
            if gate is not None:
                (twin,) = after([value], gate)
            for r, piece in ((r, value), (r + 1, swap(twin, "tp", 1))):
                offset = 0
                for mark in marks:
                    plan.append((len(pieces_f), offset, r, in_rows(mark)))
                    offset += half
                if bias:
                    plan.append((len(pieces_f), piece_rows, r, None))
                pieces_f.append(piece)

        piece_rows = piece
        add(0, own_rows, [spot_from(0)], att_0, bias=True)
        add(2, far_rows, [spot_from(0)], att_0, bias=True)
        near = jnp.concatenate(near, axis=0)
        add(0, near, [spot(1, 0), spot(3, 0)], att_0)
        for s in (1, 3):
            add(2, corners[s], [spot(s, 1)], att_0)
        near_x, near_y = swap(near, "tp", 2), swap(near, "ctx", 1)
        last, corner, near_x, near_y, *att = lax.optimization_barrier(
            (gots[2], corners[2], near_x, near_y, att_0, att_1, att_2, att_3)
        )
        att_0, att_1, att_2, att_3 = att
        att = [att_0, swap(att_1, "tp", 1), swap(att_2, "tp", 2), swap(att_3, "tp", 3)]
        add(2, near_x, [spot(1, 0), spot(3, 0)])
        add(0, near_y, [spot(1, 1), spot(3, 1)])
        add(0, last, [spot(2, 0)])
        add(2, swap(last, "tp", 2), [spot(2, 0)])
        add(0, swap(last, "ctx", 1), [spot(2, 1)])
        add(2, corner, [spot(2, 1)])
    else:
        gathered = lax.all_gather(bundle_f, "fsdp", axis=0, tiled=True)
        gathered = jnp.concatenate([gathered, bias_row], axis=0)
        gathered = lax.all_gather(gathered, "tp", axis=0)
        pieces_f = [lax.dynamic_index_in_dim(gathered, i, 0, keepdims=False) for i in flip]
        plan = [(r, 0, r, in_rows(spot_all)) for r in range(n_t)]
        plan += [(r, width, r, None) for r in range(n_t)]

    if not quick:
        att = [att_0, swap(att_1, "tp", 1), swap(att_2, "tp", 2), swap(att_3, "tp", 3)]

    vectors = jnp.stack([b_out, gain_one, shift_one, b_outer, gain_two, shift_two, b_out, b_out])
    output, g_one, stats, ga_0, ga_1, ga_2, ga_3, rows_t, keep, send = feed(
        here, inputs, grad_output, att, vectors, pieces_f, plan, tokens, hidden, local
    )
    g_att = [ga_0, swap(ga_1, "tp", 1), swap(ga_2, "tp", 2), swap(ga_3, "tp", 3)]
    stats = stats[:, 0]

    if quick:
        mate_rows = swap(rows_t, "tp", 1)
        mate = swap(send, "tp", 1)
        near_sums = jnp.concatenate([stats[:6], stats[8:9], stats[10:11]], axis=0)
        away = jnp.concatenate([stats[:6], stats[9:10], stats[11:12]], axis=0)
        keep_a, send_a, keep_b, send_b = unit_grads(here, rows_t, mate_rows, keep, mate, half, hidden, local)
        got_a = swap(send_a, "tp", 2)
        got_b = swap(send_b, "ctx", 1)
        (away,) = after([away], keep_a)
        away = swap(away, "tp", 1)
        *g_att, keep_a, keep_b = lax.optimization_barrier((*g_att, keep_a, keep_b))
    else:
        ordered = []
        for r in range(n_t):
            wide = (keep, send)[r % 2][r // 2]
            ordered.append(
                jnp.concatenate(
                    [
                        nn(rows_t[0], wide[:, :hidden]),
                        nn(rows_t[1], wide[:, hidden : 2 * hidden]),
                        nn(rows_t[2], wide[:, 2 * hidden : 2 * hidden + local]),
                    ],
                    axis=1,
                )
            )
        stacked = jnp.stack(ordered)
        ordered = jnp.stack([lax.dynamic_index_in_dim(stacked, i, 0, keepdims=False) for i in flip])
        mine = lax.psum_scatter(ordered, "tp", scatter_dimension=0, tiled=False)
        mine = lax.psum(mine, ("fsdp", "ctx"))
        shard_f = take(mine, f * piece, piece)

    g_own, g_rim = attend_back(
        here, seg_own, seg_all, g_att, full_near, full_far, q_near, q_far, keys_wide, values
    )
    if quick:
        got_a, got_b = after([got_a, got_b], g_own)
        (away,) = after([away], g_own)
        pair = near_sums + away
        (rim_out,) = after([g_rim], (got_a, got_b, pair))
        away = jnp.concatenate([pair[:6], pair[7:8], pair[7:8]], axis=0)
        away = swap(away, "tp", 2)
        edge = swap(rim_out, "ctx", 1)
        keep_a, send_a, keep_b, send_b = merge_one(here, keep_a, got_a, keep_b, got_b)
        got_a = swap(send_a, "ctx", 1)
        got_b = swap(send_b, "tp", 2)
        edge, away = after([edge, away], (send_a, send_b))
        pair = pair + away
        pair = pair + swap(pair, "ctx", 1)
        dx_keep, dx_send, d_keep, d_send = project_back(here, g_own, edge, inputs, w_qkv, tokens, half)
        (dx_send,) = after([dx_send], (got_a, got_b, pair))
        pair = pair + swap(pair, "fsdp", 1)
        dx_got = swap(dx_send, "tp", 1)
        d_got = swap(d_send, "ctx", 1)
        near_dx = dx_keep[0] + dx_got[0]
        far_dx = dx_keep[1] + dx_got[1]
        far_got = swap(far_dx, "tp", 2)
        start = (2 * hidden + local + 127) // 128 * 128
        keep_a, pair = lax.optimization_barrier((keep_a, pair))
        outs = merge_two(here, keep_a, got_a, keep_b, got_b, d_keep, d_got, start)
        (output,) = after([output], outs[0])
        pair = pair + swap(pair, "fsdp", 2)
        totals = [outs[0]] + [shift(outs[s], "fsdp", s) for s in range(1, n_f)]
        mine = (near_dx.astype(high) + far_got.astype(high) + g_one).astype(low)

        def everyone(value, kind):
            far_value = swap(value, "tp", 2)
            return spread(here, [value, swap(value, "tp", 1), far_value, swap(far_value, "tp", 1)], kind)

        output = everyone(output, low)
        grad_inputs = everyone(mine, high)
        totals[1], pair = lax.optimization_barrier((totals[1], pair))
        total = merge_three(here, totals)
        got = swap(total, "ctx", 1)
        got, output, grad_inputs = lax.optimization_barrier((got, output, grad_inputs))
        s_inner, s_outer, s_out, s_query, s_key, s_value, s_bias = finish(
            here, total, got, start, hidden, local
        )
        s_outer = s_outer.T
        s_qkv = s_bias.reshape(-1)[: 3 * local]
        shared, s_b_inner = pair[:6], pair[6]
    else:
        edge_got = []
        if n_c == 2:
            edge_got.append(((1 - c) * (rows - rim), swap(g_rim, "ctx", 1)))
        else:
            edge_got.append((0, lax.ppermute(g_rim[rim:], "ctx", ahead)))
            edge_got.append((rows - rim, lax.ppermute(g_rim[:rim], "ctx", behind)))
        g_all = g_own.astype(high)
        for first, got in edge_got:
            got = jnp.pad(got.astype(high), ((0, 0), (local, 0)))
            g_all = place(g_all, take(g_all, first, rim) + got, first)
        g_all = g_all.astype(low)
        part = nt(g_all, w_qkv).reshape(n_t, tokens, width)
        mine = lax.psum_scatter(part, "tp", scatter_dimension=0, tiled=False)
        grad_inputs = lax.all_gather((mine + g_one).astype(low), "tp", axis=0, tiled=True).astype(high)
        output = lax.all_gather(output, "tp", axis=0, tiled=True)
        shard_a = take(lax.psum(tn(inputs, g_all), ("fsdp", "ctx")), f * piece, piece)
        s_query, s_key, s_value = (shard_a[:, i * local : (i + 1) * local] for i in range(3))
        s_qkv = lax.psum(jnp.sum(g_all.astype(high), axis=0), ("fsdp", "ctx"))
        s_inner, s_outer, s_out = shard_f[:, :hidden], shard_f[:, hidden : 2 * hidden].T, shard_f[:, 2 * hidden :].T
        ordered = jnp.stack([lax.dynamic_index_in_dim(stats[8:], i, 0, keepdims=False) for i in flip])
        s_b_inner = lax.psum(
            lax.psum_scatter(ordered, "tp", scatter_dimension=0, tiled=False), ("fsdp", "ctx")
        )
        shared = lax.psum(stats[:6], ("fsdp", "ctx", "tp"))
    return (
        output,
        grad_inputs,
        s_query,
        s_qkv[:local],
        s_key,
        s_value,
        s_qkv[2 * local :],
        s_out,
        shared[0],
        shared[1],
        shared[2],
        s_inner,
        s_b_inner,
        s_outer,
        shared[3],
        shared[4],
        shared[5],
    )


def solution(mesh):
    rows = P(("fsdp", "ctx"), None)
    down, flat, across = P("fsdp", "tp"), P("tp"), P("tp", "fsdp")
    return jax.shard_map(
        shards,
        mesh=mesh,
        in_specs=(
            rows, P("fsdp", "ctx"), down, flat, down, down, flat, across, P(), P(), P(), down, flat,
            across, P(), P(), P(), rows,
        ),
        out_specs=(
            rows, rows, down, flat, down, down, flat, across, P(), P(), P(), down, flat, across,
            P(), P(), P(),
        ),
        check_vma=False,
    )
```

```python
import math

import jax
import jax.numpy as jnp
from jax import lax
from jax.experimental import pallas as pl
from jax.experimental.pallas import tpu as pltpu
from jax.sharding import PartitionSpec as P

HEAD_DIM = 64
MOST = 512
IDS = 64
NO_ID = 63
LSE_LANE = 60
FAR = -1e30

layer_eps = 1e-12
low = jnp.bfloat16
high = jnp.float32


def nn(left, right):
    return jnp.dot(left, right, preferred_element_type=high)


def nt(left, right):
    return lax.dot_general(left, right, (((1,), (1,)), ((), ())), preferred_element_type=high)


def tn(left, right):
    return lax.dot_general(left, right, (((0,), (0,)), ((), ())), preferred_element_type=high)


def swap(value, axis, bit):
    count = lax.axis_size(axis)
    return lax.ppermute(value, axis, [(i, i ^ bit) for i in range(count)])


def shift(value, axis, step):
    count = lax.axis_size(axis)
    return lax.ppermute(value, axis, [(i, (i + step) % count) for i in range(count)])


def place(whole, part, first):
    return lax.dynamic_update_slice_in_dim(whole, part, first, 0)


def take(whole, first, count):
    return lax.dynamic_slice_in_dim(whole, first, count, 0)


def norm_parts(hidden):
    average = jnp.mean(hidden, axis=-1, keepdims=True)
    centred = hidden - average
    variance = jnp.mean(centred * centred, axis=-1, keepdims=True)
    inverse = lax.rsqrt(variance + layer_eps)
    return centred * inverse, inverse


def norm_back(grad, hat, inverse, gain):
    scaled = grad * gain
    first = jnp.mean(scaled, axis=-1, keepdims=True)
    second = jnp.mean(scaled * hat, axis=-1, keepdims=True)
    return inverse * (scaled - first - hat * second)


def gelu_parts(inner):
    half = 0.5 * (1.0 + lax.erf(inner * 0.7071067811865476))
    slope = half + inner * (jnp.exp(-0.5 * inner * inner) * 0.3989422804014327)
    return inner * half, slope


def three(value):
    first = value.astype(low)
    rest = value - first.astype(high)
    second = rest.astype(low)
    third = (rest - second.astype(high)).astype(low)
    return first, second, third


def meets(seg_q, first_q, size_q, seg_k, first_k, size_k):
    return (seg_q[first_q + size_q - 1] >= seg_k[first_k]) & (
        seg_q[first_q] <= seg_k[first_k + size_k - 1]
    )


def score_part(r, q_ref, q_row, first_q, seg_q, seg_k, ka_ref, vt_ref, acc_ref, top_ref, width):
    heads, keys = ka_ref.shape[0], ka_ref.shape[1]
    block = acc_ref.shape[2]
    acc_ref[...] = jnp.zeros_like(acc_ref)
    top_ref[...] = jnp.full_like(top_ref, 2 * FAR)

    def one_block(b, carry):
        first_k = b * width

        @pl.when(meets(seg_q, first_q, block, seg_k, first_k, width))
        def _():
            for h in range(heads):
                scores = nt(ka_ref[h, pl.ds(first_k, width), :], q_ref[h, q_row])
                top = top_ref[h]
                peak = jnp.maximum(top, jnp.max(scores, axis=0, keepdims=True))
                weights = jnp.exp(scores - peak).astype(low)
                acc_ref[h] = acc_ref[h] * jnp.exp(top - peak) + nn(
                    vt_ref[h, :, pl.ds(first_k, width)], weights
                )
                top_ref[h] = peak

        return carry

    lax.fori_loop(0, keys // width, one_block, 0)
    outs = []
    lane = lax.broadcasted_iota(jnp.int32, (block, HEAD_DIM), 1)
    for h in range(heads):
        acc = acc_ref[h]
        total = acc[HEAD_DIM : HEAD_DIM + 1]
        lse = top_ref[h] + jnp.log(total)
        joined = jnp.concatenate(
            [acc[:HEAD_DIM] / total, jnp.broadcast_to(lse, (HEAD_DIM, block))], axis=0
        )
        turned = joined.T
        outs.append(turned[:, :HEAD_DIM])
        minus = three(-turned[:, HEAD_DIM:])
        mask = q_ref[h, q_row, :, HEAD_DIM:].astype(high)
        for i in range(3):
            mask = jnp.where(lane == LSE_LANE + i, minus[i].astype(high), mask)
        q_ref[h, q_row, :, HEAD_DIM:] = mask.astype(low)
    return jnp.concatenate(outs, axis=1)


def attend_far_kernel(*refs, block, width, heads, marks):
    pieces = len(marks)
    here, seg_q, seg_k, x_ref, halo_ref, bias_ref, mq_ref, mk_ref = refs[:8]
    w_refs = refs[8 : 8 + pieces]
    (out_2, out_3, full_ref, q_near, q_far, ka_ref, v_ref, vt_ref, w_ref) = refs[8 + pieces : 17 + pieces]
    acc_ref, top_ref, sems = refs[17 + pieces :]
    keys = v_ref.shape[0]
    rows = x_ref.shape[0]
    local = heads * HEAD_DIM
    scale = 1.0 / math.sqrt(HEAD_DIM)
    mine, f, c = here[0], here[1], here[2]
    copies = []
    for i, spots in enumerate(marks):
        offset = 0
        for mark in spots:
            first, count = mark(f, c)
            src = w_refs[i].at[pl.ds(offset, count)]
            copies.append(
                pltpu.make_async_copy(src, w_ref.at[pl.ds(first, count)], sems.at[len(copies)])
            )
            copies[-1].start()
            offset += count
    vt_ref[:, HEAD_DIM:, :] = jnp.ones((heads, vt_ref.shape[1] - HEAD_DIM, keys), low)
    for copy in copies:
        copy.wait()
    weights_all = w_ref[...].reshape(-1, w_ref.shape[2])

    def keep(first, count, mask, kv):
        span = pl.ds(first, count)
        for h in range(heads):
            cols = slice(h * HEAD_DIM, (h + 1) * HEAD_DIM)
            tail = slice(local + h * HEAD_DIM, local + (h + 1) * HEAD_DIM)
            ka_ref[h, span, :] = jnp.concatenate([kv[:, cols], mask], axis=1)
            vt_ref[h, :HEAD_DIM, span] = kv[:, tail].T
        v_ref[span, :] = kv[:, local:]

    for q_ref, base in ((q_near, 0), (q_far, 2)):

        def project(i, carry, q_ref=q_ref, base=base):
            first = pl.multiple_of((mine ^ (base + i)) * block, block)
            span = pl.ds(first, block)
            both = (nn(x_ref[span, :], weights_all) + bias_ref[...]).astype(low)
            for h in range(heads):
                cols = slice(h * HEAD_DIM, (h + 1) * HEAD_DIM)
                q_ref[h, i] = jnp.concatenate(
                    [both[:, cols] * jnp.array(scale, low), mq_ref[span, :]], axis=1
                )
            keep(first, block, mk_ref[span, :], both[:, local:])
            return carry

        lax.fori_loop(0, 2, project, 0)
    step = min(512, keys - rows)
    for first in range(rows, keys, step):
        span = slice(first - rows, first - rows + step)
        kv = (nn(halo_ref[span, :], weights_all[:, local:]) + bias_ref[:, local:]).astype(low)
        keep(first, step, mk_ref[first : first + step, :], kv)
    for i, out_ref in enumerate((out_2, out_3)):
        joined = score_part(
            2 + i, q_far, i, (mine ^ (2 + i)) * block, seg_q, seg_k, ka_ref, vt_ref, acc_ref, top_ref, width
        )
        full_ref[i] = joined
        out_ref[...] = joined.astype(low)


def attend_near_kernel(
    here, seg_q, seg_k, q_in, ka_ref, vt_ref, out_0, out_1, full_ref, q_ref, acc_ref, top_ref, *, block, width
):
    mine = here[0]
    q_ref[...] = q_in[...]
    for i, out_ref in enumerate((out_0, out_1)):
        joined = score_part(
            i, q_ref, i, (mine ^ i) * block, seg_q, seg_k, ka_ref, vt_ref, acc_ref, top_ref, width
        )
        full_ref[i] = joined
        out_ref[...] = joined.astype(low)


VMEM = pl.BlockSpec(memory_space=pltpu.VMEM)
SMEM = pl.BlockSpec(memory_space=pltpu.SMEM)
ANY = pl.BlockSpec(memory_space=pl.ANY)
HBM = pl.BlockSpec(memory_space=pltpu.HBM)


def shape(*dims, kind=low):
    return jax.ShapeDtypeStruct(dims, kind)


def cost(flops, size, transcendentals=0):
    return pl.CostEstimate(flops=flops, transcendentals=transcendentals, bytes_accessed=size)


def attend_far(here, seg_q, seg_k, x, halo, bias, mask_q, mask_k, pieces, marks, blocks, block):
    rows = x.shape[0]
    local = bias.shape[1] // 3
    count = rows + halo.shape[0]
    heads = local // HEAD_DIM
    wide = 2 * HEAD_DIM
    return pl.pallas_call(
        lambda *refs: attend_far_kernel(*refs, block=block, width=256, heads=heads, marks=marks),
        name="attend_far",
        out_shape=(
            shape(block, local),
            shape(block, local),
            shape(2, block, local, kind=high),
            shape(heads, 2, block, wide),
            shape(heads, 2, block, wide),
            shape(heads, count, wide),
            shape(count, local),
            shape(heads, HEAD_DIM + 16, count),
            shape(*blocks, 3 * local),
        ),
        in_specs=[SMEM] * 3 + [VMEM] * 5 + [ANY] * len(pieces),
        out_specs=(VMEM,) * 9,
        scratch_shapes=[
            pltpu.VMEM((heads, HEAD_DIM + 16, block), high),
            pltpu.VMEM((heads, 1, block), high),
            pltpu.SemaphoreType.DMA((sum(map(len, marks)),)),
        ],
        cost_estimate=cost(FAR_COST, 8 << 20),
    )(here, seg_q, seg_k, x, halo, bias, mask_q, mask_k, *pieces)


def attend_near(here, seg_q, seg_k, q_near, keys_wide, values_t):
    heads, _, block, wide = q_near.shape
    local = heads * HEAD_DIM
    return pl.pallas_call(
        lambda *refs: attend_near_kernel(*refs, block=block, width=256),
        name="attend_near",
        out_shape=(
            shape(block, local),
            shape(block, local),
            shape(2, block, local, kind=high),
            shape(heads, 2, block, wide),
        ),
        in_specs=[SMEM] * 3 + [VMEM] * 3,
        out_specs=(VMEM,) * 4,
        scratch_shapes=[
            pltpu.VMEM((heads, HEAD_DIM + 16, block), high),
            pltpu.VMEM((heads, 1, block), high),
        ],
        cost_estimate=cost(NEAR_COST, 8 << 20),
    )(here, seg_q, seg_k, q_near, keys_wide, values_t)


FAR_COST = 20 * 10**9
NEAR_COST = 12 * 10**9
FEED_COST = 26 * 10**9
UNIT_COST = 12 * 10**9
BACK_COST = 24 * 10**9
LAST_COST = 9 * 10**9
SMALL_COST = 3 * 10**9


def feed_kernel(*refs, plan, count, hidden, local):
    here, x_all, g_all, att_0, att_1, att_2, att_3, vec_ref = refs[:8]
    w_refs = refs[8 : 8 + count]
    (out_ref, one_ref, stat_ref, ga_0, ga_1, ga_2, ga_3, rows_hbm, keep_hbm, send_hbm) = refs[8 + count : 18 + count]
    (w_ref, b_ref, x_ref, g_ref, att_ref, hat_ref, inv_ref, norm_ref, acc_ref, slope_ref, gl_ref,
     rows_ref, keep_ref, send_ref, sems, out_sems) = refs[18 + count :]
    puts = []

    def put(src, dst):
        puts.append(pltpu.make_async_copy(src, dst, out_sems.at[len(puts)]))
        puts[-1].start()

    tokens, width = x_ref.shape
    mine, f, c = here[0], here[1], here[2]
    wide = 2 * hidden + local
    copies = []

    def begin(src, dst):
        copies.append(pltpu.make_async_copy(src, dst, sems.at[len(copies)]))
        copies[-1].start()

    first = pl.multiple_of(mine * tokens, tokens)
    begin(x_all.at[pl.ds(first, tokens)], x_ref)
    begin(g_all.at[pl.ds(first, tokens)], g_ref)
    for r, att in enumerate((att_0, att_1, att_2, att_3)):
        begin(att, att_ref.at[r])
    for i, offset, r, mark in plan:
        if mark is None:
            begin(w_refs[i].at[pl.ds(offset, 8)], b_ref.at[r])
        else:
            start, size = mark(f, c)
            begin(
                w_refs[i].at[pl.ds(offset, size), pl.ds(2 * hidden, local)],
                w_ref.at[r, pl.ds(start, size), pl.ds(2 * hidden, local)],
            )
    first_copies = len(copies)
    for i, offset, r, mark in plan:
        if mark is not None:
            start, size = mark(f, c)
            begin(
                w_refs[i].at[pl.ds(offset, size), pl.ds(0, 2 * hidden)],
                w_ref.at[r, pl.ds(start, size), pl.ds(0, 2 * hidden)],
            )
    for copy in copies[:first_copies]:
        copy.wait()
    b_out, gain_one, shift_one, b_outer, gain_two, shift_two = (
        vec_ref[i : i + 1, :].astype(high) for i in range(6)
    )

    def weights(r, first, last):
        return w_ref[r, :, first:last]

    acc_ref[...] = nt(att_ref[0], weights(0, 2 * hidden, 2 * hidden + local))
    for r in range(1, 4):
        acc_ref[...] += nt(att_ref[r], weights(r, 2 * hidden, 2 * hidden + local))
    step = 64
    chunks = tokens // step

    def first_norm(i, carry):
        span = pl.ds(pl.multiple_of(i * step, step), step)
        hat, inverse = norm_parts(x_ref[span, :].astype(high) + (acc_ref[span, :] + b_out))
        hat_ref[span, :] = hat
        inv_ref[span, :] = inverse
        normed = hat * gain_one + shift_one
        norm_ref[span, :] = normed.astype(low)
        acc_ref[span, :] = normed + b_outer
        return carry

    lax.fori_loop(0, chunks, first_norm, 0)
    for copy in copies[first_copies:]:
        copy.wait()
    part = 256
    for k, side in enumerate((keep_ref, send_ref)):
        for x in range(2):
            side[x, :, 2 * hidden : wide] = att_ref[2 * x + k]
            side[x, :, wide:] = jnp.zeros((tokens, side.shape[2] - wide), low)

        def up(x, carry, k=k, side=side):
            r = 2 * x + k
            for j in range(0, hidden, part):
                inner = nn(norm_ref[...], weights(r, j, j + part))
                inner = inner + b_ref[r, 0:1, j : j + part].astype(high)
                act, slope = gelu_parts(inner)
                side[x, :, hidden + j : hidden + j + part] = act.astype(low)
                slope_ref[r, :, j : j + part] = slope
            acc_ref[...] += nt(side[x, :, hidden : 2 * hidden], weights(r, hidden, 2 * hidden))
            return carry

        lax.fori_loop(0, 2, up, 0)

    zero = jnp.zeros((1, width), high)

    def second_norm(i, sums):
        span = pl.ds(pl.multiple_of(i * step, step), step)
        hat, inverse = norm_parts(acc_ref[span, :])
        out_ref[span, :] = (hat * gain_two + shift_two).astype(low)
        grad = g_ref[span, :].astype(high)
        two = norm_back(grad, hat, inverse, gain_two)
        acc_ref[span, :] = two
        two_low = two.astype(low)
        gl_ref[span, :] = two_low
        terms = (two_low.astype(high), grad * hat, grad)
        return tuple(s + jnp.sum(v, axis=0, keepdims=True) for s, v in zip(sums, terms))

    sums_two = lax.fori_loop(0, chunks, second_norm, (zero,) * 3)
    rows_ref[0] = norm_ref[...].T
    rows_ref[1] = gl_ref[...].T
    put(rows_ref.at[pl.ds(0, 2)], rows_hbm.at[pl.ds(0, 2)])
    for k, side in ((1, send_ref), (0, keep_ref)):

        def down(x, carry, k=k, side=side):
            r = 2 * x + k
            for j in range(0, hidden, part):
                grad = nn(gl_ref[...], weights(r, hidden + j, hidden + j + part))
                grad = (grad * slope_ref[r, :, j : j + part]).astype(low)
                side[x, :, j : j + part] = grad
                stat_ref[8 + r, 0:1, j : j + part] = jnp.sum(grad.astype(high), axis=0, keepdims=True)
            acc_ref[...] += nt(side[x, :, :hidden], weights(r, 0, hidden))
            return carry

        lax.fori_loop(0, 2, down, 0)
        put(side, send_hbm if k else keep_hbm)

    def first_back(i, sums):
        span = pl.ds(pl.multiple_of(i * step, step), step)
        grad = acc_ref[span, :]
        hat = hat_ref[span, :]
        one = norm_back(grad, hat, inv_ref[span, :], gain_one)
        one_ref[span, :] = one
        one_low = one.astype(low)
        gl_ref[span, :] = one_low
        terms = (one_low.astype(high), grad * hat, grad)
        return tuple(s + jnp.sum(v, axis=0, keepdims=True) for s, v in zip(sums, terms))

    sums_one = lax.fori_loop(0, chunks, first_back, (zero,) * 3)
    for i, value in enumerate(sums_one + sums_two):
        stat_ref[i, 0:1, :] = value
    rows_ref[2] = gl_ref[...].T
    put(rows_ref.at[2], rows_hbm.at[2])
    for r, ga in enumerate((ga_0, ga_1, ga_2, ga_3)):
        ga[...] = nn(gl_ref[...], weights(r, 2 * hidden, 2 * hidden + local)).astype(low)
    for copy in puts:
        copy.wait()


def feed(here, x, grad, att, vectors, pieces, plan, tokens, hidden, local):
    width = x.shape[1]
    wide = 2 * hidden + local
    padded = (wide + 127) // 128 * 128
    copies = 6 + len(plan) + sum(mark is not None for _, _, _, mark in plan)
    return pl.pallas_call(
        lambda *refs: feed_kernel(*refs, plan=plan, count=len(pieces), hidden=hidden, local=local),
        name="feed",
        out_shape=(
            shape(tokens, width),
            shape(tokens, width, kind=high),
            shape(12, 1, width, kind=high),
            shape(tokens, local),
            shape(tokens, local),
            shape(tokens, local),
            shape(tokens, local),
            shape(3, width, tokens),
            shape(2, tokens, padded),
            shape(2, tokens, padded),
        ),
        in_specs=[SMEM] + [ANY] * 6 + [VMEM] + [ANY] * len(pieces),
        out_specs=(VMEM,) * 7 + (HBM,) * 3,
        scratch_shapes=[
            pltpu.VMEM((4, width, wide), low),
            pltpu.VMEM((4, 8, wide), low),
            pltpu.VMEM((tokens, width), low),
            pltpu.VMEM((tokens, width), low),
            pltpu.VMEM((4, tokens, local), low),
            pltpu.VMEM((tokens, width), high),
            pltpu.VMEM((tokens, 1), high),
            pltpu.VMEM((tokens, width), low),
            pltpu.VMEM((tokens, width), high),
            pltpu.VMEM((4, tokens, hidden), high),
            pltpu.VMEM((tokens, width), low),
            pltpu.VMEM((3, width, tokens), low),
            pltpu.VMEM((2, tokens, padded), low),
            pltpu.VMEM((2, tokens, padded), low),
            pltpu.SemaphoreType.DMA((copies,)),
            pltpu.SemaphoreType.DMA((4,)),
        ],
        cost_estimate=cost(FEED_COST, 24 << 20),
    )(here, x, grad, *att, vectors, *pieces)


def unit_kernel(here, rows_own, rows_mate, wide_own, wide_mate, *refs, hidden):
    ak_ref, as_ref, bk_ref, bs_ref, rows_ref, wide_ref, sems = refs
    c = here[2]
    tokens = rows_own.shape[2]
    wide = ak_ref.shape[2]
    half = ak_ref.shape[1]
    mid = rows_own.shape[1] // 2
    copies = [
        pltpu.make_async_copy(rows_own, rows_ref.at[:, :, pl.ds(0, tokens)], sems.at[0]),
        pltpu.make_async_copy(wide_own, wide_ref.at[:, pl.ds(0, tokens)], sems.at[1]),
        pltpu.make_async_copy(rows_mate, rows_ref.at[:, :, pl.ds(tokens, tokens)], sems.at[2]),
        pltpu.make_async_copy(wide_mate, wide_ref.at[:, pl.ds(tokens, tokens)], sems.at[3]),
    ]
    for copy in copies:
        copy.start()
    for copy in copies:
        copy.wait()
    spans = ((0, 0, hidden), (1, hidden, 2 * hidden), (2, 2 * hidden, wide))
    for i, first, last in spans:
        for x, side in enumerate((ak_ref, as_ref)):
            got = nn(rows_ref[i, :mid, :], wide_ref[x, :, first:last]).astype(low)
            side[:, :, first:last] = got.reshape(-1, half, last - first)

        def lower(x, carry, i=i, first=first, last=last):
            got = nn(rows_ref[i, mid:, :], wide_ref[x, :, first:last]).astype(low)
            got = got.reshape(-1, 2, half, last - first)
            for z in range(got.shape[0]):

                @pl.when(c == 0)
                def _():
                    bk_ref[x, z, :, first:last] = got[z, 0]
                    bs_ref[x, z, :, first:last] = got[z, 1]

                @pl.when(c != 0)
                def _():
                    bk_ref[x, z, :, first:last] = got[z, 1]
                    bs_ref[x, z, :, first:last] = got[z, 0]

            return carry

        lax.fori_loop(0, 2, lower, 0)


def unit_grads(here, rows, mate_rows, keep, mate, half, hidden, local):
    wide = 2 * hidden + local
    tokens = rows.shape[2]
    width = rows.shape[1]
    quarters = width // 4 // half
    return pl.pallas_call(
        lambda *refs: unit_kernel(*refs, hidden=hidden),
        name="unit_grads",
        out_shape=(
            shape(2 * quarters, half, wide),
            shape(2 * quarters, half, wide),
            shape(2, quarters, half, wide),
            shape(2, quarters, half, wide),
        ),
        in_specs=[SMEM] + [ANY] * 4,
        out_specs=(VMEM,) * 4,
        scratch_shapes=[
            pltpu.VMEM((3, width, 2 * tokens), low),
            pltpu.VMEM((2, 2 * tokens, keep.shape[2]), low),
            pltpu.SemaphoreType.DMA((4,)),
        ],
        cost_estimate=cost(UNIT_COST, 14 << 20),
    )(here, rows, mate_rows, keep, mate)


def merge_one_kernel(here, ak, ga, bk, gb, a_keep, a_send, b_keep, b_send):
    c = here[2]
    for z in range(2):
        for side in range(2):
            i = 2 * z + side
            got = ak[i] + ga[i]

            @pl.when(c == side)
            def _():
                a_keep[z] = got

            @pl.when(c != side)
            def _():
                a_send[z] = got

    b_keep[...] = bk[0] + gb[0]
    b_send[...] = bk[1] + gb[1]


def merge_one(here, ak, ga, bk, gb):
    out = shape(*bk.shape[1:])
    return pl.pallas_call(
        merge_one_kernel,
        name="merge_one",
        out_shape=(out,) * 4,
        in_specs=[SMEM] + [VMEM] * 4,
        out_specs=(VMEM,) * 4,
        cost_estimate=cost(SMALL_COST, 8 << 20),
    )(here, ak, ga, bk, gb)


def merge_two_kernel(here, *refs, pairs):
    ins, outs, all_ref = refs[: 2 * pairs], refs[2 * pairs : -1], refs[-1]
    f = here[1]
    count = 4 // pairs
    for i in range(pairs):
        all_ref[i * count : (i + 1) * count] = ins[2 * i][...] + ins[2 * i + 1][...]
    for s, out in enumerate(outs):
        out[...] = all_ref[(f + s) % 4]


def merge_two(here, *parts):
    piece = parts[0].shape[1:]
    return pl.pallas_call(
        lambda *refs: merge_two_kernel(*refs, pairs=len(parts) // 2),
        name="merge_two",
        out_shape=(shape(*piece),) * 4,
        in_specs=[SMEM] + [VMEM] * len(parts),
        out_specs=(VMEM,) * 4,
        scratch_shapes=[pltpu.VMEM((4,) + piece, low)],
        cost_estimate=cost(SMALL_COST, 8 << 20),
    )(here, *parts)


def merge_three_kernel(here, own, got_1, got_2, got_3, out, all_ref):
    f = here[1]
    for s, piece in enumerate((own, got_1, got_2, got_3)):
        all_ref[(f - s + 4) % 4] = piece[...]
    total = all_ref[0].astype(high)
    for z in range(1, 4):
        total = total + all_ref[z].astype(high)
    out[...] = total.astype(low)


def merge_three(here, pieces):
    return pl.pallas_call(
        merge_three_kernel,
        name="merge_three",
        out_shape=shape(*pieces[0].shape),
        in_specs=[SMEM] + [VMEM] * 4,
        out_specs=VMEM,
        scratch_shapes=[pltpu.VMEM((4,) + pieces[0].shape, low)],
        cost_estimate=cost(SMALL_COST, 4 << 20),
    )(here, *pieces)


def finish_kernel(here, own, got, d_own, d_got, inner, outer, out, query, key, value, bias, all_ref, d_ref):
    c = here[2]
    hidden = inner.shape[1]
    local = query.shape[1]
    all_ref[c] = own[...]
    all_ref[1 - c] = got[...]
    d_ref[c] = d_own[...]
    d_ref[1 - c] = d_got[...]
    half = own.shape[0]

    def cols(ref, first, last):
        return ref[:, :, first:last].reshape(2 * half, last - first).astype(high)

    inner[...] = cols(all_ref, 0, hidden)
    outer[...] = cols(all_ref, hidden, 2 * hidden)
    out[...] = cols(all_ref, 2 * hidden, 2 * hidden + local).T
    rest = cols(d_ref, 0, 3 * local)
    query[...] = rest[:, :local]
    key[...] = rest[:, local : 2 * local]
    value[...] = rest[:, 2 * local : 3 * local]
    bias[...] = d_own[:16, 3 * local :].astype(high)


def finish(here, own, got, d_own, d_got, hidden, local):
    half, wide = own.shape
    full = d_own.shape[1]
    piece = 2 * half
    return pl.pallas_call(
        finish_kernel,
        name="finish",
        out_shape=(
            shape(piece, hidden, kind=high),
            shape(piece, hidden, kind=high),
            shape(local, piece, kind=high),
            shape(piece, local, kind=high),
            shape(piece, local, kind=high),
            shape(piece, local, kind=high),
            shape(16, full - 3 * local, kind=high),
        ),
        in_specs=[SMEM] + [VMEM] * 4,
        out_specs=(VMEM,) * 7,
        scratch_shapes=[pltpu.VMEM((2, half, wide), low), pltpu.VMEM((2, half, full), low)],
        cost_estimate=cost(SMALL_COST, 4 << 20),
    )(here, own, got, d_own, d_got)


def spread_kernel(here, p_0, p_1, p_2, p_3, out):
    tokens = p_0.shape[0]
    for r, piece in enumerate((p_0, p_1, p_2, p_3)):
        first = pl.multiple_of((here[0] ^ r) * tokens, tokens)
        out[pl.ds(first, tokens), :] = piece[...].astype(out.dtype)


def spread(here, pieces, kind):
    tokens, width = pieces[0].shape
    return pl.pallas_call(
        spread_kernel,
        name="spread",
        out_shape=shape(4 * tokens, width, kind=kind),
        in_specs=[SMEM] + [VMEM] * 4,
        out_specs=VMEM,
        cost_estimate=cost(SMALL_COST, 8 << 20),
    )(here, *pieces)


def project_back_kernel(here, g_ref, edge_ref, x_ref, w_ref, keep, send, d_keep, d_send, all_ref, *, local):
    mine, c = here[0], here[2]
    rows = g_ref.shape[0]
    rim = edge_ref.shape[0]
    tokens = keep.shape[1]
    half = d_keep.shape[1]
    pad = d_keep.shape[2] - 3 * local
    all_ref[...] = g_ref[...]
    edge = pl.ds(pl.multiple_of((1 - c) * (rows - rim), rim), rim)
    all_ref[edge, local:] = (
        g_ref[edge, local:].astype(high) + edge_ref[...].astype(high)
    ).astype(low)
    for k, side in ((1, send), (0, keep)):

        def back(x, carry, k=k, side=side):
            first = pl.multiple_of((mine ^ (2 * x + k)) * tokens, tokens)
            side[x] = nt(all_ref[pl.ds(first, tokens), :], w_ref[...]).astype(low)
            return carry

        lax.fori_loop(0, 2, back, 0)
    sums = jnp.zeros((1, 3 * local), high)
    for i in range(rows // tokens):
        part = all_ref[i * tokens : (i + 1) * tokens, :].astype(high)
        sums = sums + jnp.sum(part, axis=0, keepdims=True)
    row = lax.broadcasted_iota(jnp.int32, (half, pad), 0)
    extra = jnp.zeros((half, pad), high)
    for j in range(3 * local // pad):
        extra = jnp.where(row == j, sums[:, j * pad : (j + 1) * pad], extra)
    extra = extra.astype(low)
    got = tn(x_ref[...], all_ref[...]).astype(low).reshape(-1, 2, half, 3 * local)
    for z in range(got.shape[0]):
        d_keep[z, :, 3 * local :] = extra
        d_send[z, :, 3 * local :] = extra
        for side in range(2):

            @pl.when(c == side)
            def _():
                d_keep[z, :, : 3 * local] = got[z, side]

            @pl.when(c != side)
            def _():
                d_send[z, :, : 3 * local] = got[z, side]


def project_back(here, grads, edge, x, weights, tokens, half):
    rows, width = x.shape
    local = grads.shape[1] // 3
    pad = HEAD_DIM
    return pl.pallas_call(
        lambda *refs: project_back_kernel(*refs, local=local),
        name="project_back",
        out_shape=(
            shape(2, tokens, width),
            shape(2, tokens, width),
            shape(width // half // 2, half, 3 * local + pad),
            shape(width // half // 2, half, 3 * local + pad),
        ),
        in_specs=[SMEM] + [VMEM] * 4,
        out_specs=(VMEM,) * 4,
        scratch_shapes=[pltpu.VMEM(grads.shape, low)],
        cost_estimate=cost(LAST_COST, 8 << 20),
    )(here, grads, edge, x, weights)


def attend_back_kernel(
    here, seg_q, seg_k, g_0, g_1, g_2, g_3, full_near, full_far, q_near, q_far, ka_ref, v_ref, own_ref, rim_ref,
    g_ref, full_ref, q_ref, kt_ref, va_ref, ga_ref, dka_ref, dva_ref, dqa_ref, sems, *, block, width, heads
):
    copies = [
        pltpu.make_async_copy(g, g_ref.at[r], sems.at[r]) for r, g in enumerate((g_0, g_1, g_2, g_3))
    ]
    for i, (q_part, full_part) in enumerate(((q_near, full_near), (q_far, full_far))):
        span = pl.ds(2 * i, 2)
        copies.append(pltpu.make_async_copy(q_part, q_ref.at[:, span], sems.at[4 + 2 * i]))
        copies.append(pltpu.make_async_copy(full_part, full_ref.at[span], sems.at[5 + 2 * i]))
    for copy in copies:
        copy.start()
    keys = v_ref.shape[0]
    rows = own_ref.shape[0]
    local = heads * HEAD_DIM
    scale = 1.0 / math.sqrt(HEAD_DIM)
    mine = here[0]
    for h in range(heads):
        cols = slice(h * HEAD_DIM, (h + 1) * HEAD_DIM)
        kt_ref[h] = ka_ref[h, :, :HEAD_DIM].T
        va_ref[h] = jnp.concatenate([v_ref[:, cols], jnp.ones((keys, HEAD_DIM), low)], axis=1)
    dka_ref[...] = jnp.zeros_like(dka_ref)
    dva_ref[...] = jnp.zeros_like(dva_ref)
    for copy in copies:
        copy.wait()

    def one_part(i, carry):
        first_q = pl.multiple_of((mine ^ i) * block, block)
        for h in range(heads):
            cols = slice(h * HEAD_DIM, (h + 1) * HEAD_DIM)
            grad = g_ref[i, :, cols]
            delta = jnp.sum(grad.astype(high) * full_ref[i, :, cols], axis=1, keepdims=True)
            lane = lax.broadcasted_iota(jnp.int32, (block, HEAD_DIM), 1)
            extra = jnp.zeros((block, HEAD_DIM), high)
            for j, piece in enumerate(three(-delta)):
                extra = jnp.where(lane == j, piece.astype(high), extra)
            ga_ref[h] = jnp.concatenate([grad, extra.astype(low)], axis=1)
        dqa_ref[...] = jnp.zeros_like(dqa_ref)

        def one_block(b, carry):
            first_k = b * width

            @pl.when(meets(seg_q, first_q, block, seg_k, first_k, width))
            def _():
                for h in range(heads):
                    span = pl.ds(first_k, width)
                    asks = q_ref[h, i]
                    probs = jnp.exp(nt(ka_ref[h, span, :], asks))
                    slopes = (probs * nt(va_ref[h, span, :], ga_ref[h])).astype(low)
                    dva_ref[h, span, :] += nn(probs.astype(low), ga_ref[h, :, :HEAD_DIM])
                    dka_ref[h, span, :] += nn(slopes, asks[:, :HEAD_DIM])
                    dqa_ref[h] += nn(kt_ref[h, :, span], slopes)

            return carry

        lax.fori_loop(0, keys // width, one_block, 0)
        own_ref[pl.ds(first_q, block), :local] = jnp.concatenate(
            [(dqa_ref[h] * scale).T for h in range(heads)], axis=1
        ).astype(low)
        return carry

    lax.fori_loop(0, 4, one_part, 0)
    for j, part in enumerate((dka_ref, dva_ref)):
        wide = jnp.concatenate([part[h] for h in range(heads)], axis=1).astype(low)
        own_ref[:, (1 + j) * local : (2 + j) * local] = wide[:rows]
        rim_ref[:, j * local : (j + 1) * local] = wide[rows:]


def attend_back(here, seg_q, seg_k, grads, full_near, full_far, q_near, q_far, keys, values):
    parts = len(grads)
    block, local = grads[0].shape
    rows = parts * block
    count = values.shape[0]
    heads = local // HEAD_DIM
    return pl.pallas_call(
        lambda *refs: attend_back_kernel(*refs, block=block, width=256, heads=heads),
        name="attend_back",
        out_shape=(shape(rows, 3 * local), shape(count - rows, 2 * local)),
        in_specs=[SMEM] * 3 + [ANY] * 8 + [VMEM] * 2,
        out_specs=(VMEM,) * 2,
        scratch_shapes=[
            pltpu.VMEM((parts, block, local), low),
            pltpu.VMEM((parts, block, local), high),
            pltpu.VMEM((heads, parts, block, 2 * HEAD_DIM), low),
            pltpu.VMEM((heads, HEAD_DIM, count), low),
            pltpu.VMEM((heads, count, 2 * HEAD_DIM), low),
            pltpu.VMEM((heads, block, 2 * HEAD_DIM), low),
            pltpu.VMEM((heads, count, HEAD_DIM), high),
            pltpu.VMEM((heads, count, HEAD_DIM), high),
            pltpu.VMEM((heads, HEAD_DIM, block), high),
            pltpu.SemaphoreType.DMA((parts + 4,)),
        ],
        cost_estimate=cost(BACK_COST, 8 << 20),
    )(here, seg_q, seg_k, *grads, full_near, full_far, q_near, q_far, keys, values)


def after(values, gate):
    return lax.optimization_barrier((tuple(values), gate))[0]


def add_many(pieces, plan, value, spots, in_rows):
    offset = 0
    for r, mark in spots:
        mark = None if mark is None else in_rows(mark)
        plan.append((len(pieces), offset, r, mark))
        offset += 8 if mark is None else mark(0, 0)[1]
    pieces.append(value)


def halo_of(value, c, span):
    rows = value.shape[0]
    return take(value, (1 - c) * (rows - span), span)


def shards(
    inputs, segments, w_query, b_query, w_key, w_value, b_value, w_out, b_out, gain_one, shift_one,
    w_inner, b_inner, w_outer, b_outer, gain_two, shift_two, grad_output,
):
    rows, width = inputs.shape
    local = w_query.shape[1]
    hidden = w_inner.shape[1]
    n_f, n_c, n_t = (lax.axis_size(a) for a in ("fsdp", "ctx", "tp"))
    f, c, t = (lax.axis_index(a) for a in ("fsdp", "ctx", "tp"))
    tokens = rows // n_t
    rim = MOST
    quick = n_f == 4 and n_c == 2 and n_t == 4
    piece = width // n_f
    flip = [t ^ r for r in range(n_t)]

    half = piece // 2
    blocks = (2 * n_f, half)
    here = jnp.stack([t, f, c]).astype(jnp.int32)
    bundle_a = jnp.concatenate([w_query, w_key, w_value], axis=1)

    def spot(s, side):
        def mark(f, c):
            return (f - s + n_f) % n_f * 2 + (c if side == 0 else 1 - c), 1

        return mark

    def spot_from(s):
        return lambda f, c: ((f - s + n_f) % n_f * 2, 2)

    def spot_all(f, c):
        return 0, 2 * n_f

    def in_rows(mark):
        def rows_mark(f, c):
            first, count = mark(f, c)
            return (first if isinstance(first, int) else pl.multiple_of(first * half, half)), count * half

        return rows_mark

    seg_own = segments.reshape(rows)
    if quick:
        halves_a = bundle_a.reshape(2, half, -1)
        own_a = lax.dynamic_index_in_dim(halves_a, c, 0)
        gots_a = [shift(own_a, "fsdp", s) for s in range(1, n_f)]
        joined = jnp.concatenate(gots_a, axis=0)
        mates_a = swap(joined, "ctx", 1)
        pieces_a = [halves_a, joined, mates_a]
        marks_a = [[spot_from(0)]]
        marks_a += [[spot(s, side) for s in range(1, n_f)] for side in range(2)]
    else:
        whole_a = lax.all_gather(bundle_a, "fsdp", axis=0, tiled=True)
        pieces_a, marks_a = [whole_a.reshape(blocks + (-1,))], [[spot_all]]

    if n_c == 2:
        sent = halo_of(inputs, c, rim)
        if quick:
            part = rim // 2
            ids = halo_of(seg_own, c, rim).astype(low).reshape(2, part)
            ids = jnp.pad(ids, ((0, 14), (0, width - part)))
            got = swap(jnp.concatenate([take(sent, (t & 1) * part, part), ids], axis=0), "ctx", 1)
            halo_seg = got[part : part + 2, :part].astype(jnp.int32).reshape(rim)
            got = got[:part]
            mate = swap(got, "tp", 1)
            even = (t & 1) == 0
            halo_in = jnp.concatenate([jnp.where(even, got, mate), jnp.where(even, mate, got)], axis=0)
        else:
            halo_in = swap(sent, "ctx", 1)
            halo_seg = swap(halo_of(seg_own, c, rim), "ctx", 1)
    else:
        ahead = [(i, i + 1) for i in range(n_c - 1)]
        behind = [(i + 1, i) for i in range(n_c - 1)]

        def both(value):
            return jnp.concatenate(
                [
                    lax.ppermute(value[rows - rim :], "ctx", ahead),
                    lax.ppermute(value[:rim], "ctx", behind),
                ],
                axis=0,
            )

        halo_in = both(inputs)
        halo_seg = both(seg_own + 1) - 1
        halo_seg = jnp.where(halo_seg < 0, NO_ID, halo_seg)

    bias_row = jnp.pad(b_inner[None], ((0, 7), (0, hidden + local)))
    bundle_f = jnp.concatenate([w_inner, w_outer.T, w_out.T], axis=1)
    own_rows = jnp.concatenate([bundle_f, bias_row], axis=0)
    if quick:
        far_rows = swap(own_rows, "tp", 2)
        own_f = take(bundle_f, c * half, half)
        (own_1,) = after([own_f], joined)
        gots = {s: shift(own_1, "fsdp", s) for s in (1, 3)}
        halo_in, far_rows = lax.optimization_barrier((halo_in, far_rows))
        home_mate = swap(jnp.concatenate([own_rows, far_rows], axis=0), "tp", 1)
        far_f = take(far_rows, (1 - c) * half, half)
        corners = {s: shift(far_f, "fsdp", s) for s in (1, 3)}

    bias = jnp.concatenate([b_query, jnp.zeros_like(b_query), b_value]).astype(high)[None]
    seg_all = jnp.concatenate([seg_own, halo_seg])
    lane = jnp.arange(IDS)
    near_id = seg_all[:, None] == lane
    mask_k = (near_id | ((lane >= LSE_LANE) & (lane < LSE_LANE + 3))).astype(low)
    mask_q = jnp.where(near_id[:rows] | ((lane >= LSE_LANE) & (lane < LSE_LANE + 3)), 0.0, FAR).astype(low)
    att_2, att_3, full_far, q_near, q_far, keys_wide, values, values_t, w_qkv = attend_far(
        here, seg_own, seg_all, inputs, halo_in, bias, mask_q, mask_k, pieces_a, marks_a, blocks, tokens
    )
    w_qkv = w_qkv.reshape(width, 3 * local)

    if quick:
        (own_2,) = after([own_f], att_2)
        gots[2] = shift(own_2, "fsdp", 2)
        (far_2,) = after([far_f], att_2)
        corners[2] = shift(far_2, "fsdp", 2)
        *near, corners[1], corners[3] = after([gots[1], gots[3], corners[1], corners[3]], att_2)
        near = jnp.concatenate(near, axis=0)
        home_mate, q_near = lax.optimization_barrier((home_mate, q_near))
        (q_near,) = after([q_near], (near, corners[1], corners[3]))
    att_0, att_1, full_near, q_near = attend_near(here, seg_own, seg_all, q_near, keys_wide, values_t)
    if quick:
        pieces_f, plan = [], []

        def add(r, value, marks):
            offset = 0
            for mark in marks:
                if mark is None:
                    plan.append((len(pieces_f), offset, r, None))
                    offset += 8
                else:
                    mark = in_rows(mark)
                    plan.append((len(pieces_f), offset, r, mark))
                    offset += mark(0, 0)[1]
            pieces_f.append(value)

        def add_both(r, value, marks):
            add(r, value, marks)
            add(r + 1, swap(value, "tp", 1), marks)

        for r, value in ((0, own_rows), (2, far_rows)):
            add(r, value, [spot_from(0), None])
        add_many(pieces_f, plan, home_mate, ((1, spot_from(0)), (1, None), (3, spot_from(0)), (3, None)), in_rows)
        near_x, near_y = swap(near, "tp", 2), swap(near, "ctx", 1)
        last, near_x, near_y, *att = lax.optimization_barrier(
            (gots[2], near_x, near_y, att_0, att_1, att_2, att_3)
        )
        att_0, att_1, att_2, att_3 = att
        att = [att_0, swap(att_1, "tp", 1), swap(att_2, "tp", 2), swap(att_3, "tp", 3)]
        near, corners[1], corners[3] = after([near, corners[1], corners[3]], att_0)
        add_both(0, near, [spot(1, 0), spot(3, 0)])
        add_both(2, corners[1], [spot(1, 1)])
        add_both(2, corners[3], [spot(3, 1)])
        add_both(2, near_x, [spot(1, 0), spot(3, 0)])
        add_both(0, near_y, [spot(1, 1), spot(3, 1)])
        add_both(0, last, [spot(2, 0)])
        add_both(2, swap(last, "tp", 2), [spot(2, 0)])
        add_both(0, swap(last, "ctx", 1), [spot(2, 1)])
        (corner,) = after([corners[2]], att_0)
        add_both(2, corner, [spot(2, 1)])
    else:
        gathered = lax.all_gather(bundle_f, "fsdp", axis=0, tiled=True)
        gathered = jnp.concatenate([gathered, bias_row], axis=0)
        gathered = lax.all_gather(gathered, "tp", axis=0)
        pieces_f = [lax.dynamic_index_in_dim(gathered, i, 0, keepdims=False) for i in flip]
        plan = [(r, 0, r, in_rows(spot_all)) for r in range(n_t)]
        plan += [(r, width, r, None) for r in range(n_t)]

    if not quick:
        att = [att_0, swap(att_1, "tp", 1), swap(att_2, "tp", 2), swap(att_3, "tp", 3)]

    vectors = jnp.stack([b_out, gain_one, shift_one, b_outer, gain_two, shift_two, b_out, b_out])
    output, g_one, stats, ga_0, ga_1, ga_2, ga_3, rows_t, keep, send = feed(
        here, inputs, grad_output, att, vectors, pieces_f, plan, tokens, hidden, local
    )
    g_att = [ga_0, swap(ga_1, "tp", 1), swap(ga_2, "tp", 2), swap(ga_3, "tp", 3)]
    stats = stats[:, 0]

    if quick:
        mate_rows = swap(rows_t, "tp", 1)
        mate = swap(send, "tp", 1)
        near_sums = jnp.concatenate([stats[:6], stats[8:9], stats[10:11]], axis=0)
        away = jnp.concatenate([stats[:6], stats[9:10], stats[11:12]], axis=0)
        (away,) = after([away], mate)
        away = swap(away, "tp", 1)
        keep_a, send_a, keep_b, send_b = unit_grads(here, rows_t, mate_rows, keep, mate, half, hidden, local)
        send_a, send_b, away, *g_att = lax.optimization_barrier((send_a, send_b, away, *g_att))
        got_a = swap(send_a, "tp", 2)
        got_b = swap(send_b, "ctx", 1)
        (away,) = after([away], keep_a)
        pair = near_sums + away
        away = jnp.concatenate([pair[:6], pair[7:8], pair[7:8]], axis=0)
        away = swap(away, "tp", 2)
        *g_att, keep_a, keep_b = lax.optimization_barrier((*g_att, keep_a, keep_b))

        def everyone(value, far_value, kind):
            return spread(here, [value, swap(value, "tp", 1), far_value, swap(far_value, "tp", 1)], kind)

    else:
        ordered = []
        for r in range(n_t):
            wide = (keep, send)[r % 2][r // 2]
            ordered.append(
                jnp.concatenate(
                    [
                        nn(rows_t[0], wide[:, :hidden]),
                        nn(rows_t[1], wide[:, hidden : 2 * hidden]),
                        nn(rows_t[2], wide[:, 2 * hidden : 2 * hidden + local]),
                    ],
                    axis=1,
                )
            )
        stacked = jnp.stack(ordered)
        ordered = jnp.stack([lax.dynamic_index_in_dim(stacked, i, 0, keepdims=False) for i in flip])
        mine = lax.psum_scatter(ordered, "tp", scatter_dimension=0, tiled=False)
        mine = lax.psum(mine, ("fsdp", "ctx"))
        shard_f = take(mine, f * piece, piece)

    g_own, g_rim = attend_back(
        here, seg_own, seg_all, g_att, full_near, full_far, q_near, q_far, keys_wide, values
    )
    if quick:
        got_a, got_b = after([got_a, got_b], g_own)
        (away,) = after([away], g_own)
        pair = pair + away
        (rim_out,) = after([g_rim], (got_a, got_b, pair))
        away = swap(pair, "ctx", 1)
        edge = swap(rim_out, "ctx", 1)
        keep_a, send_a, keep_b, send_b = merge_one(here, keep_a, got_a, keep_b, got_b)
        got_a = swap(send_a, "ctx", 1)
        got_b = swap(send_b, "tp", 2)
        edge, away = after([edge, away], (send_a, send_b))
        pair = pair + away
        pair = pair + swap(pair, "fsdp", 1)
        dx_keep, dx_send, d_keep, d_send = project_back(here, g_own, edge, inputs, w_qkv, tokens, half)
        (dx_send,) = after([dx_send], (got_a, got_b, pair))
        pair = pair + swap(pair, "fsdp", 2)
        dx_got = swap(dx_send, "tp", 1)
        d_got = swap(d_send, "ctx", 1)
        outs = merge_two(here, keep_a, got_a, keep_b, got_b)
        totals = [outs[0]] + [shift(outs[s], "fsdp", s) for s in range(1, n_f)]
        near_dx = dx_keep[0] + dx_got[0]
        far_dx = dx_keep[1] + dx_got[1]
        far_got = swap(far_dx, "tp", 2)
        (d_got,) = after([d_got], outs[0])
        outs = merge_two(here, d_keep, d_got)
        d_totals = [outs[0]] + [shift(outs[s], "fsdp", s) for s in range(1, n_f)]
        (output,) = after([output], d_totals[0])
        output = everyone(output, swap(output, "tp", 2), low)
        (far_got,) = after([far_got], (*totals, d_totals[0]))
        mine = (near_dx.astype(high) + far_got.astype(high) + g_one).astype(low)
        (far_mine,) = after([swap(mine, "tp", 2)], d_totals)
        grad_inputs = everyone(mine, far_mine, high)
        total = merge_three(here, totals)
        got = swap(total, "ctx", 1)
        d_total = merge_three(here, d_totals)
        d_got = swap(d_total, "ctx", 1)
        d_got, grad_inputs, output, pair = lax.optimization_barrier((d_got, grad_inputs, output, pair))
        s_inner, s_outer, s_out, s_query, s_key, s_value, s_bias = finish(
            here, total, got, d_total, d_got, hidden, local
        )
        s_outer = s_outer.T
        s_qkv = s_bias.reshape(-1)[: 3 * local]
        shared, s_b_inner = pair[:6], pair[6]
    else:
        edge_got = []
        if n_c == 2:
            edge_got.append(((1 - c) * (rows - rim), swap(g_rim, "ctx", 1)))
        else:
            edge_got.append((0, lax.ppermute(g_rim[rim:], "ctx", ahead)))
            edge_got.append((rows - rim, lax.ppermute(g_rim[:rim], "ctx", behind)))
        g_all = g_own.astype(high)
        for first, got in edge_got:
            got = jnp.pad(got.astype(high), ((0, 0), (local, 0)))
            g_all = place(g_all, take(g_all, first, rim) + got, first)
        g_all = g_all.astype(low)
        part = nt(g_all, w_qkv).reshape(n_t, tokens, width)
        mine = lax.psum_scatter(part, "tp", scatter_dimension=0, tiled=False)
        grad_inputs = lax.all_gather((mine + g_one).astype(low), "tp", axis=0, tiled=True).astype(high)
        output = lax.all_gather(output, "tp", axis=0, tiled=True)
        shard_a = take(lax.psum(tn(inputs, g_all), ("fsdp", "ctx")), f * piece, piece)
        s_query, s_key, s_value = (shard_a[:, i * local : (i + 1) * local] for i in range(3))
        s_qkv = lax.psum(jnp.sum(g_all.astype(high), axis=0), ("fsdp", "ctx"))
        s_inner, s_outer, s_out = shard_f[:, :hidden], shard_f[:, hidden : 2 * hidden].T, shard_f[:, 2 * hidden :].T
        ordered = jnp.stack([lax.dynamic_index_in_dim(stats[8:], i, 0, keepdims=False) for i in flip])
        s_b_inner = lax.psum(
            lax.psum_scatter(ordered, "tp", scatter_dimension=0, tiled=False), ("fsdp", "ctx")
        )
        shared = lax.psum(stats[:6], ("fsdp", "ctx", "tp"))
    return (
        output,
        grad_inputs,
        s_query,
        s_qkv[:local],
        s_key,
        s_value,
        s_qkv[2 * local :],
        s_out,
        shared[0],
        shared[1],
        shared[2],
        s_inner,
        s_b_inner,
        s_outer,
        shared[3],
        shared[4],
        shared[5],
    )


def solution(mesh):
    rows = P(("fsdp", "ctx"), None)
    down, flat, across = P("fsdp", "tp"), P("tp"), P("tp", "fsdp")
    return jax.shard_map(
        shards,
        mesh=mesh,
        in_specs=(
            rows, P("fsdp", "ctx"), down, flat, down, down, flat, across, P(), P(), P(), down, flat,
            across, P(), P(), P(), rows,
        ),
        out_specs=(
            rows, rows, down, flat, down, down, flat, across, P(), P(), P(), down, flat, across,
            P(), P(), P(),
        ),
        check_vma=False,
    )
```

```python
import math

import jax
import jax.numpy as jnp
from jax import lax
from jax.experimental import pallas as pl
from jax.experimental.pallas import tpu as pltpu
from jax.sharding import PartitionSpec as P

HEAD_DIM = 64
MOST = 512
IDS = 64
NO_ID = 63
LSE_LANE = 60
FAR = -1e30

layer_eps = 1e-12
low = jnp.bfloat16
high = jnp.float32


def nn(left, right):
    return jnp.dot(left, right, preferred_element_type=high)


def nt(left, right):
    return lax.dot_general(left, right, (((1,), (1,)), ((), ())), preferred_element_type=high)


def tn(left, right):
    return lax.dot_general(left, right, (((0,), (0,)), ((), ())), preferred_element_type=high)


def swap(value, axis, bit):
    count = lax.axis_size(axis)
    return lax.ppermute(value, axis, [(i, i ^ bit) for i in range(count)])


def shift(value, axis, step):
    count = lax.axis_size(axis)
    return lax.ppermute(value, axis, [(i, (i + step) % count) for i in range(count)])


def place(whole, part, first):
    return lax.dynamic_update_slice_in_dim(whole, part, first, 0)


def take(whole, first, count):
    return lax.dynamic_slice_in_dim(whole, first, count, 0)


def norm_parts(hidden):
    average = jnp.mean(hidden, axis=-1, keepdims=True)
    centred = hidden - average
    variance = jnp.mean(centred * centred, axis=-1, keepdims=True)
    inverse = lax.rsqrt(variance + layer_eps)
    return centred * inverse, inverse


def norm_back(grad, hat, inverse, gain):
    scaled = grad * gain
    first = jnp.mean(scaled, axis=-1, keepdims=True)
    second = jnp.mean(scaled * hat, axis=-1, keepdims=True)
    return inverse * (scaled - first - hat * second)


def gelu_parts(inner):
    half = 0.5 * (1.0 + lax.erf(inner * 0.7071067811865476))
    slope = half + inner * (jnp.exp(-0.5 * inner * inner) * 0.3989422804014327)
    return inner * half, slope


def three(value):
    first = value.astype(low)
    rest = value - first.astype(high)
    second = rest.astype(low)
    third = (rest - second.astype(high)).astype(low)
    return first, second, third


def meets(seg_q, first_q, size_q, seg_k, first_k, size_k):
    return (seg_q[first_q + size_q - 1] >= seg_k[first_k]) & (
        seg_q[first_q] <= seg_k[first_k + size_k - 1]
    )


def score_part(r, q_ref, q_row, first_q, seg_q, seg_k, ka_ref, vt_ref, acc_ref, top_ref, width):
    heads, keys = ka_ref.shape[0], ka_ref.shape[1]
    block = acc_ref.shape[2]
    acc_ref[...] = jnp.zeros_like(acc_ref)
    top_ref[...] = jnp.full_like(top_ref, 2 * FAR)

    def one_block(b, carry):
        first_k = b * width

        @pl.when(meets(seg_q, first_q, block, seg_k, first_k, width))
        def _():
            for h in range(heads):
                scores = nt(ka_ref[h, pl.ds(first_k, width), :], q_ref[h, q_row])
                top = top_ref[h]
                peak = jnp.maximum(top, jnp.max(scores, axis=0, keepdims=True))
                weights = jnp.exp(scores - peak).astype(low)
                acc_ref[h] = acc_ref[h] * jnp.exp(top - peak) + nn(
                    vt_ref[h, :, pl.ds(first_k, width)], weights
                )
                top_ref[h] = peak

        return carry

    lax.fori_loop(0, keys // width, one_block, 0)
    outs = []
    lane = lax.broadcasted_iota(jnp.int32, (block, HEAD_DIM), 1)
    for h in range(heads):
        acc = acc_ref[h]
        total = acc[HEAD_DIM : HEAD_DIM + 1]
        lse = top_ref[h] + jnp.log(total)
        joined = jnp.concatenate(
            [acc[:HEAD_DIM] / total, jnp.broadcast_to(lse, (HEAD_DIM, block))], axis=0
        )
        turned = joined.T
        outs.append(turned[:, :HEAD_DIM])
        minus = three(-turned[:, HEAD_DIM:])
        mask = q_ref[h, q_row, :, HEAD_DIM:].astype(high)
        for i in range(3):
            mask = jnp.where(lane == LSE_LANE + i, minus[i].astype(high), mask)
        q_ref[h, q_row, :, HEAD_DIM:] = mask.astype(low)
    return jnp.concatenate(outs, axis=1)


def attend_far_kernel(*refs, block, width, heads, marks):
    pieces = len(marks)
    here, seg_q, seg_k, x_ref, halo_ref, bias_ref, mq_ref, mk_ref = refs[:8]
    w_refs = refs[8 : 8 + pieces]
    (out_2, out_3, full_ref, q_near, q_far, ka_ref, v_ref, vt_ref, w_ref) = refs[8 + pieces : 17 + pieces]
    acc_ref, top_ref, sems = refs[17 + pieces :]
    keys = v_ref.shape[0]
    rows = x_ref.shape[0]
    local = heads * HEAD_DIM
    scale = 1.0 / math.sqrt(HEAD_DIM)
    mine, f, c = here[0], here[1], here[2]
    copies = []
    for i, spots in enumerate(marks):
        offset = 0
        for mark in spots:
            first, count = mark(f, c)
            src = w_refs[i].at[pl.ds(offset, count)]
            copies.append(
                pltpu.make_async_copy(src, w_ref.at[pl.ds(first, count)], sems.at[len(copies)])
            )
            copies[-1].start()
            offset += count
    vt_ref[:, HEAD_DIM:, :] = jnp.ones((heads, vt_ref.shape[1] - HEAD_DIM, keys), low)
    for copy in copies:
        copy.wait()
    weights_all = w_ref[...].reshape(-1, w_ref.shape[2])

    def keep(first, count, mask, kv):
        span = pl.ds(first, count)
        for h in range(heads):
            cols = slice(h * HEAD_DIM, (h + 1) * HEAD_DIM)
            tail = slice(local + h * HEAD_DIM, local + (h + 1) * HEAD_DIM)
            ka_ref[h, span, :] = jnp.concatenate([kv[:, cols], mask], axis=1)
            vt_ref[h, :HEAD_DIM, span] = kv[:, tail].T
        v_ref[span, :] = kv[:, local:]

    for q_ref, base in ((q_near, 0), (q_far, 2)):

        def project(i, carry, q_ref=q_ref, base=base):
            first = pl.multiple_of((mine ^ (base + i)) * block, block)
            span = pl.ds(first, block)
            both = (nn(x_ref[span, :], weights_all) + bias_ref[...]).astype(low)
            for h in range(heads):
                cols = slice(h * HEAD_DIM, (h + 1) * HEAD_DIM)
                q_ref[h, i] = jnp.concatenate(
                    [both[:, cols] * jnp.array(scale, low), mq_ref[span, :]], axis=1
                )
            keep(first, block, mk_ref[span, :], both[:, local:])
            return carry

        lax.fori_loop(0, 2, project, 0)
    step = min(512, keys - rows)
    for first in range(rows, keys, step):
        span = slice(first - rows, first - rows + step)
        kv = (nn(halo_ref[span, :], weights_all[:, local:]) + bias_ref[:, local:]).astype(low)
        keep(first, step, mk_ref[first : first + step, :], kv)
    for i, out_ref in enumerate((out_2, out_3)):
        joined = score_part(
            2 + i, q_far, i, (mine ^ (2 + i)) * block, seg_q, seg_k, ka_ref, vt_ref, acc_ref, top_ref, width
        )
        full_ref[i] = joined
        out_ref[...] = joined.astype(low)


def attend_near_kernel(
    here, seg_q, seg_k, q_in, ka_ref, vt_ref, out_0, out_1, full_ref, q_ref, acc_ref, top_ref, *, block, width
):
    mine = here[0]
    q_ref[...] = q_in[...]
    for i, out_ref in enumerate((out_0, out_1)):
        joined = score_part(
            i, q_ref, i, (mine ^ i) * block, seg_q, seg_k, ka_ref, vt_ref, acc_ref, top_ref, width
        )
        full_ref[i] = joined
        out_ref[...] = joined.astype(low)


VMEM = pl.BlockSpec(memory_space=pltpu.VMEM)
SMEM = pl.BlockSpec(memory_space=pltpu.SMEM)
ANY = pl.BlockSpec(memory_space=pl.ANY)
HBM = pl.BlockSpec(memory_space=pltpu.HBM)


def shape(*dims, kind=low):
    return jax.ShapeDtypeStruct(dims, kind)


def cost(flops, size, transcendentals=0):
    return pl.CostEstimate(flops=flops, transcendentals=transcendentals, bytes_accessed=size)


def attend_far(here, seg_q, seg_k, x, halo, bias, mask_q, mask_k, pieces, marks, blocks, block):
    rows = x.shape[0]
    local = bias.shape[1] // 3
    count = rows + halo.shape[0]
    heads = local // HEAD_DIM
    wide = 2 * HEAD_DIM
    return pl.pallas_call(
        lambda *refs: attend_far_kernel(*refs, block=block, width=256, heads=heads, marks=marks),
        name="attend_far",
        out_shape=(
            shape(block, local),
            shape(block, local),
            shape(2, block, local, kind=high),
            shape(heads, 2, block, wide),
            shape(heads, 2, block, wide),
            shape(heads, count, wide),
            shape(count, local),
            shape(heads, HEAD_DIM + 16, count),
            shape(*blocks, 3 * local),
        ),
        in_specs=[SMEM] * 3 + [VMEM] * 5 + [ANY] * len(pieces),
        out_specs=(VMEM,) * 9,
        scratch_shapes=[
            pltpu.VMEM((heads, HEAD_DIM + 16, block), high),
            pltpu.VMEM((heads, 1, block), high),
            pltpu.SemaphoreType.DMA((sum(map(len, marks)),)),
        ],
        cost_estimate=cost(FAR_COST, 8 << 20),
    )(here, seg_q, seg_k, x, halo, bias, mask_q, mask_k, *pieces)


def attend_near(here, seg_q, seg_k, q_near, keys_wide, values_t):
    heads, _, block, wide = q_near.shape
    local = heads * HEAD_DIM
    return pl.pallas_call(
        lambda *refs: attend_near_kernel(*refs, block=block, width=256),
        name="attend_near",
        out_shape=(
            shape(block, local),
            shape(block, local),
            shape(2, block, local, kind=high),
            shape(heads, 2, block, wide),
        ),
        in_specs=[SMEM] * 3 + [VMEM] * 3,
        out_specs=(VMEM,) * 4,
        scratch_shapes=[
            pltpu.VMEM((heads, HEAD_DIM + 16, block), high),
            pltpu.VMEM((heads, 1, block), high),
        ],
        cost_estimate=cost(NEAR_COST, 8 << 20),
    )(here, seg_q, seg_k, q_near, keys_wide, values_t)


FAR_COST = 20 * 10**9
NEAR_COST = 12 * 10**9
FEED_COST = 26 * 10**9
UNIT_COST = 12 * 10**9
BACK_COST = 24 * 10**9
LAST_COST = 9 * 10**9
SMALL_COST = 3 * 10**9


def feed_kernel(*refs, plan, count, hidden, local):
    here, x_all, g_all, att_0, att_1, att_2, att_3, vec_ref = refs[:8]
    w_refs = refs[8 : 8 + count]
    (out_ref, one_ref, stat_ref, ga_0, ga_1, ga_2, ga_3, rows_hbm, keep_hbm, send_hbm) = refs[8 + count : 18 + count]
    (w_ref, b_ref, x_ref, g_ref, att_ref, hat_ref, inv_ref, norm_ref, acc_ref, slope_ref, gl_ref,
     rows_ref, keep_ref, send_ref, sems, out_sems) = refs[18 + count :]
    puts = []

    def put(src, dst):
        puts.append(pltpu.make_async_copy(src, dst, out_sems.at[len(puts)]))
        puts[-1].start()

    tokens, width = x_ref.shape
    mine, f, c = here[0], here[1], here[2]
    wide = 2 * hidden + local
    copies = []

    def begin(src, dst):
        copies.append(pltpu.make_async_copy(src, dst, sems.at[len(copies)]))
        copies[-1].start()

    first = pl.multiple_of(mine * tokens, tokens)
    begin(x_all.at[pl.ds(first, tokens)], x_ref)
    begin(g_all.at[pl.ds(first, tokens)], g_ref)
    for r, att in enumerate((att_0, att_1, att_2, att_3)):
        begin(att, att_ref.at[r])
    for i, offset, r, mark in plan:
        if mark is None:
            begin(w_refs[i].at[pl.ds(offset, 8)], b_ref.at[r])
        else:
            start, size = mark(f, c)
            begin(
                w_refs[i].at[pl.ds(offset, size), pl.ds(2 * hidden, local)],
                w_ref.at[r, pl.ds(start, size), pl.ds(2 * hidden, local)],
            )
    first_copies = len(copies)
    for i, offset, r, mark in plan:
        if mark is not None:
            start, size = mark(f, c)
            begin(
                w_refs[i].at[pl.ds(offset, size), pl.ds(0, 2 * hidden)],
                w_ref.at[r, pl.ds(start, size), pl.ds(0, 2 * hidden)],
            )
    for copy in copies[:first_copies]:
        copy.wait()
    b_out, gain_one, shift_one, b_outer, gain_two, shift_two = (
        vec_ref[i : i + 1, :].astype(high) for i in range(6)
    )

    def weights(r, first, last):
        return w_ref[r, :, first:last]

    acc_ref[...] = nt(att_ref[0], weights(0, 2 * hidden, 2 * hidden + local))
    for r in range(1, 4):
        acc_ref[...] += nt(att_ref[r], weights(r, 2 * hidden, 2 * hidden + local))
    step = 64
    chunks = tokens // step

    def first_norm(i, carry):
        span = pl.ds(pl.multiple_of(i * step, step), step)
        hat, inverse = norm_parts(x_ref[span, :].astype(high) + (acc_ref[span, :] + b_out))
        hat_ref[span, :] = hat
        inv_ref[span, :] = inverse
        normed = hat * gain_one + shift_one
        norm_ref[span, :] = normed.astype(low)
        acc_ref[span, :] = normed + b_outer
        return carry

    lax.fori_loop(0, chunks, first_norm, 0)
    for copy in copies[first_copies:]:
        copy.wait()
    part = 256
    for k, side in enumerate((keep_ref, send_ref)):
        for x in range(2):
            side[x, :, 2 * hidden : wide] = att_ref[2 * x + k]
            side[x, :, wide:] = jnp.zeros((tokens, side.shape[2] - wide), low)

        def up(x, carry, k=k, side=side):
            r = 2 * x + k
            for j in range(0, hidden, part):
                inner = nn(norm_ref[...], weights(r, j, j + part))
                inner = inner + b_ref[r, 0:1, j : j + part].astype(high)
                act, slope = gelu_parts(inner)
                side[x, :, hidden + j : hidden + j + part] = act.astype(low)
                slope_ref[r, :, j : j + part] = slope
            acc_ref[...] += nt(side[x, :, hidden : 2 * hidden], weights(r, hidden, 2 * hidden))
            return carry

        lax.fori_loop(0, 2, up, 0)

    zero = jnp.zeros((1, width), high)

    def second_norm(i, sums):
        span = pl.ds(pl.multiple_of(i * step, step), step)
        hat, inverse = norm_parts(acc_ref[span, :])
        out_ref[span, :] = (hat * gain_two + shift_two).astype(low)
        grad = g_ref[span, :].astype(high)
        two = norm_back(grad, hat, inverse, gain_two)
        acc_ref[span, :] = two
        two_low = two.astype(low)
        gl_ref[span, :] = two_low
        terms = (two_low.astype(high), grad * hat, grad)
        return tuple(s + jnp.sum(v, axis=0, keepdims=True) for s, v in zip(sums, terms))

    sums_two = lax.fori_loop(0, chunks, second_norm, (zero,) * 3)
    rows_ref[0] = norm_ref[...].T
    rows_ref[1] = gl_ref[...].T
    put(rows_ref.at[pl.ds(0, 2)], rows_hbm.at[pl.ds(0, 2)])
    for k, side in ((1, send_ref), (0, keep_ref)):

        def down(x, carry, k=k, side=side):
            r = 2 * x + k
            for j in range(0, hidden, part):
                grad = nn(gl_ref[...], weights(r, hidden + j, hidden + j + part))
                grad = (grad * slope_ref[r, :, j : j + part]).astype(low)
                side[x, :, j : j + part] = grad
                stat_ref[8 + r, 0:1, j : j + part] = jnp.sum(grad.astype(high), axis=0, keepdims=True)
            acc_ref[...] += nt(side[x, :, :hidden], weights(r, 0, hidden))
            return carry

        lax.fori_loop(0, 2, down, 0)
        put(side, send_hbm if k else keep_hbm)

    def first_back(i, sums):
        span = pl.ds(pl.multiple_of(i * step, step), step)
        grad = acc_ref[span, :]
        hat = hat_ref[span, :]
        one = norm_back(grad, hat, inv_ref[span, :], gain_one)
        one_ref[span, :] = one
        one_low = one.astype(low)
        gl_ref[span, :] = one_low
        terms = (one_low.astype(high), grad * hat, grad)
        return tuple(s + jnp.sum(v, axis=0, keepdims=True) for s, v in zip(sums, terms))

    sums_one = lax.fori_loop(0, chunks, first_back, (zero,) * 3)
    for i, value in enumerate(sums_one + sums_two):
        stat_ref[i, 0:1, :] = value
    rows_ref[2] = gl_ref[...].T
    put(rows_ref.at[2], rows_hbm.at[2])
    for r, ga in enumerate((ga_0, ga_1, ga_2, ga_3)):
        ga[...] = nn(gl_ref[...], weights(r, 2 * hidden, 2 * hidden + local)).astype(low)
    for copy in puts:
        copy.wait()


def feed(here, x, grad, att, vectors, pieces, plan, tokens, hidden, local):
    width = x.shape[1]
    wide = 2 * hidden + local
    padded = (wide + 127) // 128 * 128
    copies = 6 + len(plan) + sum(mark is not None for _, _, _, mark in plan)
    return pl.pallas_call(
        lambda *refs: feed_kernel(*refs, plan=plan, count=len(pieces), hidden=hidden, local=local),
        name="feed",
        out_shape=(
            shape(tokens, width),
            shape(tokens, width, kind=high),
            shape(12, 1, width, kind=high),
            shape(tokens, local),
            shape(tokens, local),
            shape(tokens, local),
            shape(tokens, local),
            shape(3, width, tokens),
            shape(2, tokens, padded),
            shape(2, tokens, padded),
        ),
        in_specs=[SMEM] + [ANY] * 6 + [VMEM] + [ANY] * len(pieces),
        out_specs=(VMEM,) * 7 + (HBM,) * 3,
        scratch_shapes=[
            pltpu.VMEM((4, width, wide), low),
            pltpu.VMEM((4, 8, wide), low),
            pltpu.VMEM((tokens, width), low),
            pltpu.VMEM((tokens, width), low),
            pltpu.VMEM((4, tokens, local), low),
            pltpu.VMEM((tokens, width), high),
            pltpu.VMEM((tokens, 1), high),
            pltpu.VMEM((tokens, width), low),
            pltpu.VMEM((tokens, width), high),
            pltpu.VMEM((4, tokens, hidden), high),
            pltpu.VMEM((tokens, width), low),
            pltpu.VMEM((3, width, tokens), low),
            pltpu.VMEM((2, tokens, padded), low),
            pltpu.VMEM((2, tokens, padded), low),
            pltpu.SemaphoreType.DMA((copies,)),
            pltpu.SemaphoreType.DMA((4,)),
        ],
        cost_estimate=cost(FEED_COST, 24 << 20),
    )(here, x, grad, *att, vectors, *pieces)


def unit_kernel(here, rows_own, rows_mate, wide_own, wide_mate, *refs, hidden):
    ak_ref, as_ref, bk_ref, bs_ref, rows_ref, wide_ref, sems = refs
    c = here[2]
    tokens = rows_own.shape[2]
    wide = ak_ref.shape[2]
    half = ak_ref.shape[1]
    mid = rows_own.shape[1] // 2
    copies = [
        pltpu.make_async_copy(rows_own, rows_ref.at[:, :, pl.ds(0, tokens)], sems.at[0]),
        pltpu.make_async_copy(wide_own, wide_ref.at[:, pl.ds(0, tokens)], sems.at[1]),
        pltpu.make_async_copy(rows_mate, rows_ref.at[:, :, pl.ds(tokens, tokens)], sems.at[2]),
        pltpu.make_async_copy(wide_mate, wide_ref.at[:, pl.ds(tokens, tokens)], sems.at[3]),
    ]
    for copy in copies:
        copy.start()
    for copy in copies:
        copy.wait()
    spans = ((0, 0, hidden), (1, hidden, 2 * hidden), (2, 2 * hidden, wide))
    for i, first, last in spans:
        for x, side in enumerate((ak_ref, as_ref)):
            got = nn(rows_ref[i, :mid, :], wide_ref[x, :, first:last]).astype(low)
            side[:, :, first:last] = got.reshape(-1, half, last - first)

        def lower(x, carry, i=i, first=first, last=last):
            got = nn(rows_ref[i, mid:, :], wide_ref[x, :, first:last]).astype(low)
            got = got.reshape(-1, 2, half, last - first)
            for z in range(got.shape[0]):

                @pl.when(c == 0)
                def _():
                    bk_ref[x, z, :, first:last] = got[z, 0]
                    bs_ref[x, z, :, first:last] = got[z, 1]

                @pl.when(c != 0)
                def _():
                    bk_ref[x, z, :, first:last] = got[z, 1]
                    bs_ref[x, z, :, first:last] = got[z, 0]

            return carry

        lax.fori_loop(0, 2, lower, 0)


def unit_grads(here, rows, mate_rows, keep, mate, half, hidden, local):
    wide = 2 * hidden + local
    tokens = rows.shape[2]
    width = rows.shape[1]
    quarters = width // 4 // half
    return pl.pallas_call(
        lambda *refs: unit_kernel(*refs, hidden=hidden),
        name="unit_grads",
        out_shape=(
            shape(2 * quarters, half, wide),
            shape(2 * quarters, half, wide),
            shape(2, quarters, half, wide),
            shape(2, quarters, half, wide),
        ),
        in_specs=[SMEM] + [ANY] * 4,
        out_specs=(VMEM,) * 4,
        scratch_shapes=[
            pltpu.VMEM((3, width, 2 * tokens), low),
            pltpu.VMEM((2, 2 * tokens, keep.shape[2]), low),
            pltpu.SemaphoreType.DMA((4,)),
        ],
        cost_estimate=cost(UNIT_COST, 14 << 20),
    )(here, rows, mate_rows, keep, mate)


def merge_one_kernel(here, ak, ga, bk, gb, a_keep, a_send, b_keep, b_send):
    c = here[2]
    for z in range(2):
        for side in range(2):
            i = 2 * z + side
            got = ak[i] + ga[i]

            @pl.when(c == side)
            def _():
                a_keep[z] = got

            @pl.when(c != side)
            def _():
                a_send[z] = got

    b_keep[...] = bk[0] + gb[0]
    b_send[...] = bk[1] + gb[1]


def merge_one(here, ak, ga, bk, gb):
    out = shape(*bk.shape[1:])
    return pl.pallas_call(
        merge_one_kernel,
        name="merge_one",
        out_shape=(out,) * 4,
        in_specs=[SMEM] + [VMEM] * 4,
        out_specs=(VMEM,) * 4,
        cost_estimate=cost(SMALL_COST, 8 << 20),
    )(here, ak, ga, bk, gb)


def merge_two_kernel(here, *refs, pairs):
    ins, outs, all_ref = refs[: 2 * pairs], refs[2 * pairs : -1], refs[-1]
    f = here[1]
    count = 4 // pairs
    for i in range(pairs):
        all_ref[i * count : (i + 1) * count] = ins[2 * i][...] + ins[2 * i + 1][...]
    for s, out in enumerate(outs):
        out[...] = all_ref[(f + s) % 4]


def merge_two(here, *parts):
    piece = parts[0].shape[1:]
    return pl.pallas_call(
        lambda *refs: merge_two_kernel(*refs, pairs=len(parts) // 2),
        name="merge_two",
        out_shape=(shape(*piece),) * 4,
        in_specs=[SMEM] + [VMEM] * len(parts),
        out_specs=(VMEM,) * 4,
        scratch_shapes=[pltpu.VMEM((4,) + piece, low)],
        cost_estimate=cost(SMALL_COST, 8 << 20),
    )(here, *parts)


def merge_three_kernel(here, own, got_1, got_2, got_3, out, all_ref):
    f = here[1]
    for s, piece in enumerate((own, got_1, got_2, got_3)):
        all_ref[(f - s + 4) % 4] = piece[...]
    total = all_ref[0].astype(high)
    for z in range(1, 4):
        total = total + all_ref[z].astype(high)
    out[...] = total.astype(low)


def merge_three(here, pieces):
    return pl.pallas_call(
        merge_three_kernel,
        name="merge_three",
        out_shape=shape(*pieces[0].shape),
        in_specs=[SMEM] + [VMEM] * 4,
        out_specs=VMEM,
        scratch_shapes=[pltpu.VMEM((4,) + pieces[0].shape, low)],
        cost_estimate=cost(SMALL_COST, 4 << 20),
    )(here, *pieces)


def finish_kernel(here, own, got, d_own, d_got, inner, outer, out, query, key, value, bias, all_ref, d_ref):
    c = here[2]
    hidden = inner.shape[1]
    local = query.shape[1]
    all_ref[c] = own[...]
    all_ref[1 - c] = got[...]
    d_ref[c] = d_own[...]
    d_ref[1 - c] = d_got[...]
    half = own.shape[0]

    def cols(ref, first, last):
        return ref[:, :, first:last].reshape(2 * half, last - first).astype(high)

    inner[...] = cols(all_ref, 0, hidden)
    outer[...] = cols(all_ref, hidden, 2 * hidden)
    out[...] = cols(all_ref, 2 * hidden, 2 * hidden + local).T
    rest = cols(d_ref, 0, 3 * local)
    query[...] = rest[:, :local]
    key[...] = rest[:, local : 2 * local]
    value[...] = rest[:, 2 * local : 3 * local]
    bias[...] = d_own[:16, 3 * local :].astype(high)


def finish(here, own, got, d_own, d_got, hidden, local):
    half, wide = own.shape
    full = d_own.shape[1]
    piece = 2 * half
    return pl.pallas_call(
        finish_kernel,
        name="finish",
        out_shape=(
            shape(piece, hidden, kind=high),
            shape(piece, hidden, kind=high),
            shape(local, piece, kind=high),
            shape(piece, local, kind=high),
            shape(piece, local, kind=high),
            shape(piece, local, kind=high),
            shape(16, full - 3 * local, kind=high),
        ),
        in_specs=[SMEM] + [VMEM] * 4,
        out_specs=(VMEM,) * 7,
        scratch_shapes=[pltpu.VMEM((2, half, wide), low), pltpu.VMEM((2, half, full), low)],
        cost_estimate=cost(SMALL_COST, 4 << 20),
    )(here, own, got, d_own, d_got)


def spread_kernel(here, p_0, p_1, p_2, p_3, out):
    tokens = p_0.shape[0]
    for r, piece in enumerate((p_0, p_1, p_2, p_3)):
        first = pl.multiple_of((here[0] ^ r) * tokens, tokens)
        out[pl.ds(first, tokens), :] = piece[...].astype(out.dtype)


def spread(here, pieces, kind):
    tokens, width = pieces[0].shape
    return pl.pallas_call(
        spread_kernel,
        name="spread",
        out_shape=shape(4 * tokens, width, kind=kind),
        in_specs=[SMEM] + [VMEM] * 4,
        out_specs=VMEM,
        cost_estimate=cost(SMALL_COST, 8 << 20),
    )(here, *pieces)


def project_back_kernel(here, g_ref, edge_ref, x_ref, w_ref, keep, send, d_keep, d_send, all_ref, *, local):
    mine, c = here[0], here[2]
    rows = g_ref.shape[0]
    rim = edge_ref.shape[0]
    tokens = keep.shape[1]
    half = d_keep.shape[1]
    pad = d_keep.shape[2] - 3 * local
    all_ref[...] = g_ref[...]
    edge = pl.ds(pl.multiple_of((1 - c) * (rows - rim), rim), rim)
    all_ref[edge, local:] = (
        g_ref[edge, local:].astype(high) + edge_ref[...].astype(high)
    ).astype(low)
    for k, side in ((1, send), (0, keep)):

        def back(x, carry, k=k, side=side):
            first = pl.multiple_of((mine ^ (2 * x + k)) * tokens, tokens)
            side[x] = nt(all_ref[pl.ds(first, tokens), :], w_ref[...]).astype(low)
            return carry

        lax.fori_loop(0, 2, back, 0)
    sums = jnp.zeros((1, 3 * local), high)
    for i in range(rows // tokens):
        part = all_ref[i * tokens : (i + 1) * tokens, :].astype(high)
        sums = sums + jnp.sum(part, axis=0, keepdims=True)
    row = lax.broadcasted_iota(jnp.int32, (half, pad), 0)
    extra = jnp.zeros((half, pad), high)
    for j in range(3 * local // pad):
        extra = jnp.where(row == j, sums[:, j * pad : (j + 1) * pad], extra)
    extra = extra.astype(low)
    got = tn(x_ref[...], all_ref[...]).astype(low).reshape(-1, 2, half, 3 * local)
    for z in range(got.shape[0]):
        d_keep[z, :, 3 * local :] = extra
        d_send[z, :, 3 * local :] = extra
        for side in range(2):

            @pl.when(c == side)
            def _():
                d_keep[z, :, : 3 * local] = got[z, side]

            @pl.when(c != side)
            def _():
                d_send[z, :, : 3 * local] = got[z, side]


def project_back(here, grads, edge, x, weights, tokens, half):
    rows, width = x.shape
    local = grads.shape[1] // 3
    pad = HEAD_DIM
    return pl.pallas_call(
        lambda *refs: project_back_kernel(*refs, local=local),
        name="project_back",
        out_shape=(
            shape(2, tokens, width),
            shape(2, tokens, width),
            shape(width // half // 2, half, 3 * local + pad),
            shape(width // half // 2, half, 3 * local + pad),
        ),
        in_specs=[SMEM] + [VMEM] * 4,
        out_specs=(VMEM,) * 4,
        scratch_shapes=[pltpu.VMEM(grads.shape, low)],
        cost_estimate=cost(LAST_COST, 8 << 20),
    )(here, grads, edge, x, weights)


def attend_back_kernel(
    here, seg_q, seg_k, g_0, g_1, g_2, g_3, full_near, full_far, q_near, q_far, ka_ref, v_ref, own_ref, rim_ref,
    g_ref, full_ref, q_ref, kt_ref, va_ref, ga_ref, dka_ref, dva_ref, dqa_ref, sems, *, block, width, heads
):
    copies = [
        pltpu.make_async_copy(g, g_ref.at[r], sems.at[r]) for r, g in enumerate((g_0, g_1, g_2, g_3))
    ]
    for i, (q_part, full_part) in enumerate(((q_near, full_near), (q_far, full_far))):
        span = pl.ds(2 * i, 2)
        copies.append(pltpu.make_async_copy(q_part, q_ref.at[:, span], sems.at[4 + 2 * i]))
        copies.append(pltpu.make_async_copy(full_part, full_ref.at[span], sems.at[5 + 2 * i]))
    for copy in copies:
        copy.start()
    keys = v_ref.shape[0]
    rows = own_ref.shape[0]
    local = heads * HEAD_DIM
    scale = 1.0 / math.sqrt(HEAD_DIM)
    mine = here[0]
    for h in range(heads):
        cols = slice(h * HEAD_DIM, (h + 1) * HEAD_DIM)
        kt_ref[h] = ka_ref[h, :, :HEAD_DIM].T
        va_ref[h] = jnp.concatenate([v_ref[:, cols], jnp.ones((keys, HEAD_DIM), low)], axis=1)
    dka_ref[...] = jnp.zeros_like(dka_ref)
    dva_ref[...] = jnp.zeros_like(dva_ref)
    for copy in copies:
        copy.wait()

    def one_part(i, carry):
        first_q = pl.multiple_of((mine ^ i) * block, block)
        for h in range(heads):
            cols = slice(h * HEAD_DIM, (h + 1) * HEAD_DIM)
            grad = g_ref[i, :, cols]
            delta = jnp.sum(grad.astype(high) * full_ref[i, :, cols], axis=1, keepdims=True)
            lane = lax.broadcasted_iota(jnp.int32, (block, HEAD_DIM), 1)
            extra = jnp.zeros((block, HEAD_DIM), high)
            for j, piece in enumerate(three(-delta)):
                extra = jnp.where(lane == j, piece.astype(high), extra)
            ga_ref[h] = jnp.concatenate([grad, extra.astype(low)], axis=1)
        dqa_ref[...] = jnp.zeros_like(dqa_ref)

        def one_block(b, carry):
            first_k = b * width

            @pl.when(meets(seg_q, first_q, block, seg_k, first_k, width))
            def _():
                for h in range(heads):
                    span = pl.ds(first_k, width)
                    asks = q_ref[h, i]
                    probs = jnp.exp(nt(ka_ref[h, span, :], asks))
                    slopes = (probs * nt(va_ref[h, span, :], ga_ref[h])).astype(low)
                    dva_ref[h, span, :] += nn(probs.astype(low), ga_ref[h, :, :HEAD_DIM])
                    dka_ref[h, span, :] += nn(slopes, asks[:, :HEAD_DIM])
                    dqa_ref[h] += nn(kt_ref[h, :, span], slopes)

            return carry

        lax.fori_loop(0, keys // width, one_block, 0)
        own_ref[pl.ds(first_q, block), :local] = jnp.concatenate(
            [(dqa_ref[h] * scale).T for h in range(heads)], axis=1
        ).astype(low)
        return carry

    lax.fori_loop(0, 4, one_part, 0)
    for j, part in enumerate((dka_ref, dva_ref)):
        wide = jnp.concatenate([part[h] for h in range(heads)], axis=1).astype(low)
        own_ref[:, (1 + j) * local : (2 + j) * local] = wide[:rows]
        rim_ref[:, j * local : (j + 1) * local] = wide[rows:]


def attend_back(here, seg_q, seg_k, grads, full_near, full_far, q_near, q_far, keys, values):
    parts = len(grads)
    block, local = grads[0].shape
    rows = parts * block
    count = values.shape[0]
    heads = local // HEAD_DIM
    return pl.pallas_call(
        lambda *refs: attend_back_kernel(*refs, block=block, width=256, heads=heads),
        name="attend_back",
        out_shape=(shape(rows, 3 * local), shape(count - rows, 2 * local)),
        in_specs=[SMEM] * 3 + [ANY] * 8 + [VMEM] * 2,
        out_specs=(VMEM,) * 2,
        scratch_shapes=[
            pltpu.VMEM((parts, block, local), low),
            pltpu.VMEM((parts, block, local), high),
            pltpu.VMEM((heads, parts, block, 2 * HEAD_DIM), low),
            pltpu.VMEM((heads, HEAD_DIM, count), low),
            pltpu.VMEM((heads, count, 2 * HEAD_DIM), low),
            pltpu.VMEM((heads, block, 2 * HEAD_DIM), low),
            pltpu.VMEM((heads, count, HEAD_DIM), high),
            pltpu.VMEM((heads, count, HEAD_DIM), high),
            pltpu.VMEM((heads, HEAD_DIM, block), high),
            pltpu.SemaphoreType.DMA((parts + 4,)),
        ],
        cost_estimate=cost(BACK_COST, 8 << 20),
    )(here, seg_q, seg_k, *grads, full_near, full_far, q_near, q_far, keys, values)


def after(values, gate):
    return lax.optimization_barrier((tuple(values), gate))[0]


def add_many(pieces, plan, value, spots, in_rows):
    offset = 0
    for r, mark in spots:
        mark = None if mark is None else in_rows(mark)
        plan.append((len(pieces), offset, r, mark))
        offset += 8 if mark is None else mark(0, 0)[1]
    pieces.append(value)


def halo_of(value, c, span):
    rows = value.shape[0]
    return take(value, (1 - c) * (rows - span), span)


def shards(
    inputs, segments, w_query, b_query, w_key, w_value, b_value, w_out, b_out, gain_one, shift_one,
    w_inner, b_inner, w_outer, b_outer, gain_two, shift_two, grad_output,
):
    rows, width = inputs.shape
    local = w_query.shape[1]
    hidden = w_inner.shape[1]
    n_f, n_c, n_t = (lax.axis_size(a) for a in ("fsdp", "ctx", "tp"))
    f, c, t = (lax.axis_index(a) for a in ("fsdp", "ctx", "tp"))
    tokens = rows // n_t
    rim = MOST
    quick = n_f == 4 and n_c == 2 and n_t == 4
    piece = width // n_f
    flip = [t ^ r for r in range(n_t)]

    half = piece // 2
    blocks = (2 * n_f, half)
    here = jnp.stack([t, f, c]).astype(jnp.int32)
    bundle_a = jnp.concatenate([w_query, w_key, w_value], axis=1)

    def spot(s, side):
        def mark(f, c):
            return (f - s + n_f) % n_f * 2 + (c if side == 0 else 1 - c), 1

        return mark

    def spot_from(s):
        return lambda f, c: ((f - s + n_f) % n_f * 2, 2)

    def spot_all(f, c):
        return 0, 2 * n_f

    def in_rows(mark):
        def rows_mark(f, c):
            first, count = mark(f, c)
            return (first if isinstance(first, int) else pl.multiple_of(first * half, half)), count * half

        return rows_mark

    seg_own = segments.reshape(rows)
    if quick:
        halves_a = bundle_a.reshape(2, half, -1)
        own_a = lax.dynamic_index_in_dim(halves_a, c, 0)
        gots_a = [shift(own_a, "fsdp", s) for s in range(1, n_f)]
        joined = jnp.concatenate(gots_a, axis=0)
        mates_a = swap(joined, "ctx", 1)
        pieces_a = [halves_a, joined, mates_a]
        marks_a = [[spot_from(0)]]
        marks_a += [[spot(s, side) for s in range(1, n_f)] for side in range(2)]
    else:
        whole_a = lax.all_gather(bundle_a, "fsdp", axis=0, tiled=True)
        pieces_a, marks_a = [whole_a.reshape(blocks + (-1,))], [[spot_all]]

    if n_c == 2:
        sent = halo_of(inputs, c, rim)
        if quick:
            part = rim // 2
            ids = halo_of(seg_own, c, rim).astype(low).reshape(2, part)
            ids = jnp.pad(ids, ((0, 14), (0, width - part)))
            got = swap(jnp.concatenate([take(sent, (t & 1) * part, part), ids], axis=0), "ctx", 1)
            halo_seg = got[part : part + 2, :part].astype(jnp.int32).reshape(rim)
            got = got[:part]
            mate = swap(got, "tp", 1)
            even = (t & 1) == 0
            halo_in = jnp.concatenate([jnp.where(even, got, mate), jnp.where(even, mate, got)], axis=0)
        else:
            halo_in = swap(sent, "ctx", 1)
            halo_seg = swap(halo_of(seg_own, c, rim), "ctx", 1)
    else:
        ahead = [(i, i + 1) for i in range(n_c - 1)]
        behind = [(i + 1, i) for i in range(n_c - 1)]

        def both(value):
            return jnp.concatenate(
                [
                    lax.ppermute(value[rows - rim :], "ctx", ahead),
                    lax.ppermute(value[:rim], "ctx", behind),
                ],
                axis=0,
            )

        halo_in = both(inputs)
        halo_seg = both(seg_own + 1) - 1
        halo_seg = jnp.where(halo_seg < 0, NO_ID, halo_seg)

    bias_row = jnp.pad(b_inner[None], ((0, 7), (0, hidden + local)))
    bundle_f = jnp.concatenate([w_inner, w_outer.T, w_out.T], axis=1)
    own_rows = jnp.concatenate([bundle_f, bias_row], axis=0)
    if quick:
        far_rows = swap(own_rows, "tp", 2)
        own_f = take(bundle_f, c * half, half)
        (own_1,) = after([own_f], joined)
        gots = {s: shift(own_1, "fsdp", s) for s in (1, 3)}
        halo_in, far_rows = lax.optimization_barrier((halo_in, far_rows))
        home_mate = swap(jnp.concatenate([own_rows, far_rows], axis=0), "tp", 1)
        far_f = take(far_rows, (1 - c) * half, half)
        corners = {s: shift(far_f, "fsdp", s) for s in (1, 3)}

    bias = jnp.concatenate([b_query, jnp.zeros_like(b_query), b_value]).astype(high)[None]
    seg_all = jnp.concatenate([seg_own, halo_seg])
    lane = jnp.arange(IDS)
    near_id = seg_all[:, None] == lane
    mask_k = (near_id | ((lane >= LSE_LANE) & (lane < LSE_LANE + 3))).astype(low)
    mask_q = jnp.where(near_id[:rows] | ((lane >= LSE_LANE) & (lane < LSE_LANE + 3)), 0.0, FAR).astype(low)
    att_2, att_3, full_far, q_near, q_far, keys_wide, values, values_t, w_qkv = attend_far(
        here, seg_own, seg_all, inputs, halo_in, bias, mask_q, mask_k, pieces_a, marks_a, blocks, tokens
    )
    w_qkv = w_qkv.reshape(width, 3 * local)

    if quick:
        (own_2,) = after([own_f], att_2)
        gots[2] = shift(own_2, "fsdp", 2)
        (far_2,) = after([far_f], att_2)
        corners[2] = shift(far_2, "fsdp", 2)
        *near, corners[1], corners[3] = after([gots[1], gots[3], corners[1], corners[3]], att_2)
        near = jnp.concatenate(near, axis=0)
        home_mate, q_near = lax.optimization_barrier((home_mate, q_near))
        (q_near,) = after([q_near], (near, corners[1], corners[3]))
    att_0, att_1, full_near, q_near = attend_near(here, seg_own, seg_all, q_near, keys_wide, values_t)
    if quick:
        pieces_f, plan = [], []

        def add(r, value, marks):
            offset = 0
            for mark in marks:
                if mark is None:
                    plan.append((len(pieces_f), offset, r, None))
                    offset += 8
                else:
                    mark = in_rows(mark)
                    plan.append((len(pieces_f), offset, r, mark))
                    offset += mark(0, 0)[1]
            pieces_f.append(value)

        def add_both(r, value, marks):
            add(r, value, marks)
            add(r + 1, swap(value, "tp", 1), marks)

        for r, value in ((0, own_rows), (2, far_rows)):
            add(r, value, [spot_from(0), None])
        add_many(pieces_f, plan, home_mate, ((1, spot_from(0)), (1, None), (3, spot_from(0)), (3, None)), in_rows)
        near_x, near_y = swap(near, "tp", 2), swap(near, "ctx", 1)
        near_mate = swap(near, "tp", 1)
        near_mate, near_x, near_y, *att = lax.optimization_barrier(
            (near_mate, near_x, near_y, att_0, att_1, att_2, att_3)
        )
        att_0, att_1, att_2, att_3 = att
        att = [att_0, swap(att_1, "tp", 1), swap(att_2, "tp", 2), swap(att_3, "tp", 3)]
        (last,) = after([gots[2]], (near_x, near_y, att_0))
        last_x, last_y = swap(last, "tp", 2), swap(last, "ctx", 1)
        for r, value in ((0, near), (1, near_mate)):
            add(r, value, [spot(1, 0), spot(3, 0)])
        late = [corners[1], corners[3], near_x, near_y, last]
        corners[1], corners[3], near_x, near_y, last = after(late, tuple(att[1:]))
        add_both(2, corners[1], [spot(1, 1)])
        add_both(2, corners[3], [spot(3, 1)])
        add_both(2, near_x, [spot(1, 0), spot(3, 0)])
        add_both(0, near_y, [spot(1, 1), spot(3, 1)])
        add_both(0, last, [spot(2, 0)])
        add_both(2, last_x, [spot(2, 0)])
        add_both(0, last_y, [spot(2, 1)])
        (corner,) = after([corners[2]], tuple(att[1:]))
        add_both(2, corner, [spot(2, 1)])
    else:
        gathered = lax.all_gather(bundle_f, "fsdp", axis=0, tiled=True)
        gathered = jnp.concatenate([gathered, bias_row], axis=0)
        gathered = lax.all_gather(gathered, "tp", axis=0)
        pieces_f = [lax.dynamic_index_in_dim(gathered, i, 0, keepdims=False) for i in flip]
        plan = [(r, 0, r, in_rows(spot_all)) for r in range(n_t)]
        plan += [(r, width, r, None) for r in range(n_t)]

    if not quick:
        att = [att_0, swap(att_1, "tp", 1), swap(att_2, "tp", 2), swap(att_3, "tp", 3)]

    vectors = jnp.stack([b_out, gain_one, shift_one, b_outer, gain_two, shift_two, b_out, b_out])
    output, g_one, stats, ga_0, ga_1, ga_2, ga_3, rows_t, keep, send = feed(
        here, inputs, grad_output, att, vectors, pieces_f, plan, tokens, hidden, local
    )
    g_att = [ga_0, swap(ga_1, "tp", 1), swap(ga_2, "tp", 2), swap(ga_3, "tp", 3)]
    stats = stats[:, 0]

    if quick:
        mate_rows = swap(rows_t, "tp", 1)
        mate = swap(send, "tp", 1)
        near_sums = jnp.concatenate([stats[:6], stats[8:9], stats[10:11]], axis=0)
        away = jnp.concatenate([stats[:6], stats[9:10], stats[11:12]], axis=0)
        (away,) = after([away], mate)
        away = swap(away, "tp", 1)
        keep_a, send_a, keep_b, send_b = unit_grads(here, rows_t, mate_rows, keep, mate, half, hidden, local)
        send_a, send_b, away, *g_att = lax.optimization_barrier((send_a, send_b, away, *g_att))
        got_a = swap(send_a, "tp", 2)
        got_b = swap(send_b, "ctx", 1)
        (away,) = after([away], keep_a)
        pair = near_sums + away
        away = jnp.concatenate([pair[:6], pair[7:8], pair[7:8]], axis=0)
        away = swap(away, "tp", 2)
        *g_att, keep_a, keep_b = lax.optimization_barrier((*g_att, keep_a, keep_b))

        def everyone(value, far_value, kind):
            return spread(here, [value, swap(value, "tp", 1), far_value, swap(far_value, "tp", 1)], kind)

    else:
        ordered = []
        for r in range(n_t):
            wide = (keep, send)[r % 2][r // 2]
            ordered.append(
                jnp.concatenate(
                    [
                        nn(rows_t[0], wide[:, :hidden]),
                        nn(rows_t[1], wide[:, hidden : 2 * hidden]),
                        nn(rows_t[2], wide[:, 2 * hidden : 2 * hidden + local]),
                    ],
                    axis=1,
                )
            )
        stacked = jnp.stack(ordered)
        ordered = jnp.stack([lax.dynamic_index_in_dim(stacked, i, 0, keepdims=False) for i in flip])
        mine = lax.psum_scatter(ordered, "tp", scatter_dimension=0, tiled=False)
        mine = lax.psum(mine, ("fsdp", "ctx"))
        shard_f = take(mine, f * piece, piece)

    g_own, g_rim = attend_back(
        here, seg_own, seg_all, g_att, full_near, full_far, q_near, q_far, keys_wide, values
    )
    if quick:
        got_a, got_b = after([got_a, got_b], g_own)
        (away,) = after([away], g_own)
        pair = pair + away
        (rim_out,) = after([g_rim], (got_a, got_b, pair))
        away = swap(pair, "ctx", 1)
        edge = swap(rim_out, "ctx", 1)
        keep_a, send_a, keep_b, send_b = merge_one(here, keep_a, got_a, keep_b, got_b)
        got_a = swap(send_a, "ctx", 1)
        got_b = swap(send_b, "tp", 2)
        edge, away = after([edge, away], (send_a, send_b))
        pair = pair + away
        pair = pair + swap(pair, "fsdp", 1)
        dx_keep, dx_send, d_keep, d_send = project_back(here, g_own, edge, inputs, w_qkv, tokens, half)
        (dx_send,) = after([dx_send], (got_a, got_b, pair))
        pair = pair + swap(pair, "fsdp", 2)
        dx_got = swap(dx_send, "tp", 1)
        d_got = swap(d_send, "ctx", 1)
        outs = merge_two(here, keep_a, got_a, keep_b, got_b)
        totals = [outs[0]] + [shift(outs[s], "fsdp", s) for s in range(1, n_f)]
        near_dx = dx_keep[0] + dx_got[0]
        far_dx = dx_keep[1] + dx_got[1]
        far_got = swap(far_dx, "tp", 2)
        (d_got,) = after([d_got], outs[0])
        outs = merge_two(here, d_keep, d_got)
        d_totals = [outs[0]] + [shift(outs[s], "fsdp", s) for s in range(1, n_f)]
        (output,) = after([output], d_totals[0])
        output = everyone(output, swap(output, "tp", 2), low)
        (far_got,) = after([far_got], (*totals, d_totals[0]))
        mine = (near_dx.astype(high) + far_got.astype(high) + g_one).astype(low)
        (far_mine,) = after([swap(mine, "tp", 2)], d_totals)
        grad_inputs = everyone(mine, far_mine, high)
        total = merge_three(here, totals)
        got = swap(total, "ctx", 1)
        d_total = merge_three(here, d_totals)
        d_got = swap(d_total, "ctx", 1)
        d_got, grad_inputs, output, pair = lax.optimization_barrier((d_got, grad_inputs, output, pair))
        s_inner, s_outer, s_out, s_query, s_key, s_value, s_bias = finish(
            here, total, got, d_total, d_got, hidden, local
        )
        s_outer = s_outer.T
        s_qkv = s_bias.reshape(-1)[: 3 * local]
        shared, s_b_inner = pair[:6], pair[6]
    else:
        edge_got = []
        if n_c == 2:
            edge_got.append(((1 - c) * (rows - rim), swap(g_rim, "ctx", 1)))
        else:
            edge_got.append((0, lax.ppermute(g_rim[rim:], "ctx", ahead)))
            edge_got.append((rows - rim, lax.ppermute(g_rim[:rim], "ctx", behind)))
        g_all = g_own.astype(high)
        for first, got in edge_got:
            got = jnp.pad(got.astype(high), ((0, 0), (local, 0)))
            g_all = place(g_all, take(g_all, first, rim) + got, first)
        g_all = g_all.astype(low)
        part = nt(g_all, w_qkv).reshape(n_t, tokens, width)
        mine = lax.psum_scatter(part, "tp", scatter_dimension=0, tiled=False)
        grad_inputs = lax.all_gather((mine + g_one).astype(low), "tp", axis=0, tiled=True).astype(high)
        output = lax.all_gather(output, "tp", axis=0, tiled=True)
        shard_a = take(lax.psum(tn(inputs, g_all), ("fsdp", "ctx")), f * piece, piece)
        s_query, s_key, s_value = (shard_a[:, i * local : (i + 1) * local] for i in range(3))
        s_qkv = lax.psum(jnp.sum(g_all.astype(high), axis=0), ("fsdp", "ctx"))
        s_inner, s_outer, s_out = shard_f[:, :hidden], shard_f[:, hidden : 2 * hidden].T, shard_f[:, 2 * hidden :].T
        ordered = jnp.stack([lax.dynamic_index_in_dim(stats[8:], i, 0, keepdims=False) for i in flip])
        s_b_inner = lax.psum(
            lax.psum_scatter(ordered, "tp", scatter_dimension=0, tiled=False), ("fsdp", "ctx")
        )
        shared = lax.psum(stats[:6], ("fsdp", "ctx", "tp"))
    return (
        output,
        grad_inputs,
        s_query,
        s_qkv[:local],
        s_key,
        s_value,
        s_qkv[2 * local :],
        s_out,
        shared[0],
        shared[1],
        shared[2],
        s_inner,
        s_b_inner,
        s_outer,
        shared[3],
        shared[4],
        shared[5],
    )


def solution(mesh):
    rows = P(("fsdp", "ctx"), None)
    down, flat, across = P("fsdp", "tp"), P("tp"), P("tp", "fsdp")
    return jax.shard_map(
        shards,
        mesh=mesh,
        in_specs=(
            rows, P("fsdp", "ctx"), down, flat, down, down, flat, across, P(), P(), P(), down, flat,
            across, P(), P(), P(), rows,
        ),
        out_specs=(
            rows, rows, down, flat, down, down, flat, across, P(), P(), P(), down, flat, across,
            P(), P(), P(),
        ),
        check_vma=False,
    )
```

```python
import math

import jax
import jax.numpy as jnp
from jax import lax
from jax.experimental import pallas as pl
from jax.experimental.pallas import tpu as pltpu
from jax.sharding import PartitionSpec as P

HEAD_DIM = 64
MOST = 512
IDS = 64
NO_ID = 63
LSE_LANE = 60
FAR = -1e30

layer_eps = 1e-12
low = jnp.bfloat16
high = jnp.float32


def nn(left, right):
    return jnp.dot(left, right, preferred_element_type=high)


def nt(left, right):
    return lax.dot_general(left, right, (((1,), (1,)), ((), ())), preferred_element_type=high)


def tn(left, right):
    return lax.dot_general(left, right, (((0,), (0,)), ((), ())), preferred_element_type=high)


def swap(value, axis, bit):
    count = lax.axis_size(axis)
    return lax.ppermute(value, axis, [(i, i ^ bit) for i in range(count)])


def shift(value, axis, step):
    count = lax.axis_size(axis)
    return lax.ppermute(value, axis, [(i, (i + step) % count) for i in range(count)])


def place(whole, part, first):
    return lax.dynamic_update_slice_in_dim(whole, part, first, 0)


def take(whole, first, count):
    return lax.dynamic_slice_in_dim(whole, first, count, 0)


def norm_parts(hidden):
    average = jnp.mean(hidden, axis=-1, keepdims=True)
    centred = hidden - average
    variance = jnp.mean(centred * centred, axis=-1, keepdims=True)
    inverse = lax.rsqrt(variance + layer_eps)
    return centred * inverse, inverse


def norm_back(grad, hat, inverse, gain):
    scaled = grad * gain
    first = jnp.mean(scaled, axis=-1, keepdims=True)
    second = jnp.mean(scaled * hat, axis=-1, keepdims=True)
    return inverse * (scaled - first - hat * second)


def gelu_parts(inner):
    half = 0.5 * (1.0 + lax.erf(inner * 0.7071067811865476))
    slope = half + inner * (jnp.exp(-0.5 * inner * inner) * 0.3989422804014327)
    return inner * half, slope


def three(value):
    first = value.astype(low)
    rest = value - first.astype(high)
    second = rest.astype(low)
    third = (rest - second.astype(high)).astype(low)
    return first, second, third


def meets(seg_q, first_q, size_q, seg_k, first_k, size_k):
    return (seg_q[first_q + size_q - 1] >= seg_k[first_k]) & (
        seg_q[first_q] <= seg_k[first_k + size_k - 1]
    )


def score_part(r, q_ref, q_row, first_q, seg_q, seg_k, ka_ref, vt_ref, acc_ref, top_ref, width):
    heads, keys = ka_ref.shape[0], ka_ref.shape[1]
    block = acc_ref.shape[2]
    acc_ref[...] = jnp.zeros_like(acc_ref)
    top_ref[...] = jnp.full_like(top_ref, 2 * FAR)

    def one_block(b, carry):
        first_k = b * width

        @pl.when(meets(seg_q, first_q, block, seg_k, first_k, width))
        def _():
            for h in range(heads):
                scores = nt(ka_ref[h, pl.ds(first_k, width), :], q_ref[h, q_row])
                top = top_ref[h]
                peak = jnp.maximum(top, jnp.max(scores, axis=0, keepdims=True))
                weights = jnp.exp(scores - peak).astype(low)
                acc_ref[h] = acc_ref[h] * jnp.exp(top - peak) + nn(
                    vt_ref[h, :, pl.ds(first_k, width)], weights
                )
                top_ref[h] = peak

        return carry

    lax.fori_loop(0, keys // width, one_block, 0)
    outs = []
    lane = lax.broadcasted_iota(jnp.int32, (block, HEAD_DIM), 1)
    for h in range(heads):
        acc = acc_ref[h]
        total = acc[HEAD_DIM : HEAD_DIM + 1]
        lse = top_ref[h] + jnp.log(total)
        joined = jnp.concatenate(
            [acc[:HEAD_DIM] / total, jnp.broadcast_to(lse, (HEAD_DIM, block))], axis=0
        )
        turned = joined.T
        outs.append(turned[:, :HEAD_DIM])
        minus = three(-turned[:, HEAD_DIM:])
        mask = q_ref[h, q_row, :, HEAD_DIM:].astype(high)
        for i in range(3):
            mask = jnp.where(lane == LSE_LANE + i, minus[i].astype(high), mask)
        q_ref[h, q_row, :, HEAD_DIM:] = mask.astype(low)
    return jnp.concatenate(outs, axis=1)


def attend_far_kernel(*refs, block, width, heads, marks):
    pieces = len(marks)
    here, seg_q, seg_k, x_ref, halo_ref, bias_ref, mq_ref, mk_ref = refs[:8]
    w_refs = refs[8 : 8 + pieces]
    (out_2, out_3, full_ref, q_near, q_far, ka_ref, v_ref, vt_ref, w_ref) = refs[8 + pieces : 17 + pieces]
    acc_ref, top_ref, sems = refs[17 + pieces :]
    keys = v_ref.shape[0]
    rows = x_ref.shape[0]
    local = heads * HEAD_DIM
    scale = 1.0 / math.sqrt(HEAD_DIM)
    mine, f, c = here[0], here[1], here[2]
    copies = []
    for i, spots in enumerate(marks):
        offset = 0
        for mark in spots:
            first, count = mark(f, c)
            src = w_refs[i].at[pl.ds(offset, count)]
            copies.append(
                pltpu.make_async_copy(src, w_ref.at[pl.ds(first, count)], sems.at[len(copies)])
            )
            copies[-1].start()
            offset += count
    vt_ref[:, HEAD_DIM:, :] = jnp.ones((heads, vt_ref.shape[1] - HEAD_DIM, keys), low)
    for copy in copies:
        copy.wait()
    weights_all = w_ref[...].reshape(-1, w_ref.shape[2])

    def keep(first, count, mask, kv):
        span = pl.ds(first, count)
        for h in range(heads):
            cols = slice(h * HEAD_DIM, (h + 1) * HEAD_DIM)
            tail = slice(local + h * HEAD_DIM, local + (h + 1) * HEAD_DIM)
            ka_ref[h, span, :] = jnp.concatenate([kv[:, cols], mask], axis=1)
            vt_ref[h, :HEAD_DIM, span] = kv[:, tail].T
        v_ref[span, :] = kv[:, local:]

    for q_ref, base in ((q_near, 0), (q_far, 2)):

        def project(i, carry, q_ref=q_ref, base=base):
            first = pl.multiple_of((mine ^ (base + i)) * block, block)
            span = pl.ds(first, block)
            both = (nn(x_ref[span, :], weights_all) + bias_ref[...]).astype(low)
            for h in range(heads):
                cols = slice(h * HEAD_DIM, (h + 1) * HEAD_DIM)
                q_ref[h, i] = jnp.concatenate(
                    [both[:, cols] * jnp.array(scale, low), mq_ref[span, :]], axis=1
                )
            keep(first, block, mk_ref[span, :], both[:, local:])
            return carry

        lax.fori_loop(0, 2, project, 0)
    step = min(512, keys - rows)
    for first in range(rows, keys, step):
        span = slice(first - rows, first - rows + step)
        kv = (nn(halo_ref[span, :], weights_all[:, local:]) + bias_ref[:, local:]).astype(low)
        keep(first, step, mk_ref[first : first + step, :], kv)
    for i, out_ref in enumerate((out_2, out_3)):
        joined = score_part(
            2 + i, q_far, i, (mine ^ (2 + i)) * block, seg_q, seg_k, ka_ref, vt_ref, acc_ref, top_ref, width
        )
        full_ref[i] = joined
        out_ref[...] = joined.astype(low)


def attend_near_kernel(
    here, seg_q, seg_k, q_in, ka_ref, vt_ref, out_0, out_1, full_ref, q_ref, acc_ref, top_ref, *, block, width
):
    mine = here[0]
    q_ref[...] = q_in[...]
    for i, out_ref in enumerate((out_0, out_1)):
        joined = score_part(
            i, q_ref, i, (mine ^ i) * block, seg_q, seg_k, ka_ref, vt_ref, acc_ref, top_ref, width
        )
        full_ref[i] = joined
        out_ref[...] = joined.astype(low)


VMEM = pl.BlockSpec(memory_space=pltpu.VMEM)
SMEM = pl.BlockSpec(memory_space=pltpu.SMEM)
ANY = pl.BlockSpec(memory_space=pl.ANY)
HBM = pl.BlockSpec(memory_space=pltpu.HBM)


def shape(*dims, kind=low):
    return jax.ShapeDtypeStruct(dims, kind)


def cost(flops, size, transcendentals=0):
    return pl.CostEstimate(flops=flops, transcendentals=transcendentals, bytes_accessed=size)


def attend_far(here, seg_q, seg_k, x, halo, bias, mask_q, mask_k, pieces, marks, blocks, block):
    rows = x.shape[0]
    local = bias.shape[1] // 3
    count = rows + halo.shape[0]
    heads = local // HEAD_DIM
    wide = 2 * HEAD_DIM
    return pl.pallas_call(
        lambda *refs: attend_far_kernel(*refs, block=block, width=256, heads=heads, marks=marks),
        name="attend_far",
        out_shape=(
            shape(block, local),
            shape(block, local),
            shape(2, block, local, kind=high),
            shape(heads, 2, block, wide),
            shape(heads, 2, block, wide),
            shape(heads, count, wide),
            shape(count, local),
            shape(heads, HEAD_DIM + 16, count),
            shape(*blocks, 3 * local),
        ),
        in_specs=[SMEM] * 3 + [VMEM] * 5 + [ANY] * len(pieces),
        out_specs=(VMEM,) * 9,
        scratch_shapes=[
            pltpu.VMEM((heads, HEAD_DIM + 16, block), high),
            pltpu.VMEM((heads, 1, block), high),
            pltpu.SemaphoreType.DMA((sum(map(len, marks)),)),
        ],
        cost_estimate=cost(FAR_COST, 8 << 20),
    )(here, seg_q, seg_k, x, halo, bias, mask_q, mask_k, *pieces)


def attend_near(here, seg_q, seg_k, q_near, keys_wide, values_t):
    heads, _, block, wide = q_near.shape
    local = heads * HEAD_DIM
    return pl.pallas_call(
        lambda *refs: attend_near_kernel(*refs, block=block, width=256),
        name="attend_near",
        out_shape=(
            shape(block, local),
            shape(block, local),
            shape(2, block, local, kind=high),
            shape(heads, 2, block, wide),
        ),
        in_specs=[SMEM] * 3 + [VMEM] * 3,
        out_specs=(VMEM,) * 4,
        scratch_shapes=[
            pltpu.VMEM((heads, HEAD_DIM + 16, block), high),
            pltpu.VMEM((heads, 1, block), high),
        ],
        cost_estimate=cost(NEAR_COST, 8 << 20),
    )(here, seg_q, seg_k, q_near, keys_wide, values_t)


FAR_COST = 20 * 10**9
NEAR_COST = 12 * 10**9
FEED_COST = 26 * 10**9
UNIT_COST = 12 * 10**9
BACK_COST = 24 * 10**9
LAST_COST = 9 * 10**9
SMALL_COST = 3 * 10**9


def feed_kernel(*refs, plan, count, hidden, local):
    here, x_all, g_all, att_0, att_1, att_2, att_3, vec_ref = refs[:8]
    w_refs = refs[8 : 8 + count]
    (out_ref, one_ref, stat_ref, ga_0, ga_1, ga_2, ga_3, rows_hbm, keep_hbm, send_hbm) = refs[8 + count : 18 + count]
    (w_ref, b_ref, x_ref, g_ref, att_ref, hat_ref, inv_ref, norm_ref, acc_ref, slope_ref, gl_ref,
     rows_ref, keep_ref, send_ref, sems, out_sems) = refs[18 + count :]
    puts = []

    def put(src, dst):
        puts.append(pltpu.make_async_copy(src, dst, out_sems.at[len(puts)]))
        puts[-1].start()

    tokens, width = x_ref.shape
    mine, f, c = here[0], here[1], here[2]
    wide = 2 * hidden + local
    copies = []

    def begin(src, dst):
        copies.append(pltpu.make_async_copy(src, dst, sems.at[len(copies)]))
        copies[-1].start()

    first = pl.multiple_of(mine * tokens, tokens)
    begin(x_all.at[pl.ds(first, tokens)], x_ref)
    begin(g_all.at[pl.ds(first, tokens)], g_ref)
    for r, att in enumerate((att_0, att_1, att_2, att_3)):
        begin(att, att_ref.at[r])
    for i, offset, r, mark in plan:
        if mark is None:
            begin(w_refs[i].at[pl.ds(offset, 8)], b_ref.at[r])
        else:
            start, size = mark(f, c)
            begin(
                w_refs[i].at[pl.ds(offset, size), pl.ds(2 * hidden, local)],
                w_ref.at[r, pl.ds(start, size), pl.ds(2 * hidden, local)],
            )
    first_copies = len(copies)
    for i, offset, r, mark in plan:
        if mark is not None:
            start, size = mark(f, c)
            begin(
                w_refs[i].at[pl.ds(offset, size), pl.ds(0, 2 * hidden)],
                w_ref.at[r, pl.ds(start, size), pl.ds(0, 2 * hidden)],
            )
    for copy in copies[:first_copies]:
        copy.wait()
    b_out, gain_one, shift_one, b_outer, gain_two, shift_two = (
        vec_ref[i : i + 1, :].astype(high) for i in range(6)
    )

    def weights(r, first, last):
        return w_ref[r, :, first:last]

    acc_ref[...] = nt(att_ref[0], weights(0, 2 * hidden, 2 * hidden + local))
    for r in range(1, 4):
        acc_ref[...] += nt(att_ref[r], weights(r, 2 * hidden, 2 * hidden + local))
    step = 64
    chunks = tokens // step

    def first_norm(i, carry):
        span = pl.ds(pl.multiple_of(i * step, step), step)
        hat, inverse = norm_parts(x_ref[span, :].astype(high) + (acc_ref[span, :] + b_out))
        hat_ref[span, :] = hat
        inv_ref[span, :] = inverse
        normed = hat * gain_one + shift_one
        norm_ref[span, :] = normed.astype(low)
        acc_ref[span, :] = normed + b_outer
        return carry

    lax.fori_loop(0, chunks, first_norm, 0)
    for copy in copies[first_copies:]:
        copy.wait()
    part = 256
    for k, side in enumerate((keep_ref, send_ref)):
        for x in range(2):
            side[x, :, 2 * hidden : wide] = att_ref[2 * x + k]
            side[x, :, wide:] = jnp.zeros((tokens, side.shape[2] - wide), low)

        def up(x, carry, k=k, side=side):
            r = 2 * x + k
            for j in range(0, hidden, part):
                inner = nn(norm_ref[...], weights(r, j, j + part))
                inner = inner + b_ref[r, 0:1, j : j + part].astype(high)
                act, slope = gelu_parts(inner)
                side[x, :, hidden + j : hidden + j + part] = act.astype(low)
                slope_ref[r, :, j : j + part] = slope
            acc_ref[...] += nt(side[x, :, hidden : 2 * hidden], weights(r, hidden, 2 * hidden))
            return carry

        lax.fori_loop(0, 2, up, 0)

    zero = jnp.zeros((1, width), high)

    def second_norm(i, sums):
        span = pl.ds(pl.multiple_of(i * step, step), step)
        hat, inverse = norm_parts(acc_ref[span, :])
        out_ref[span, :] = (hat * gain_two + shift_two).astype(low)
        grad = g_ref[span, :].astype(high)
        two = norm_back(grad, hat, inverse, gain_two)
        acc_ref[span, :] = two
        two_low = two.astype(low)
        gl_ref[span, :] = two_low
        terms = (two_low.astype(high), grad * hat, grad)
        return tuple(s + jnp.sum(v, axis=0, keepdims=True) for s, v in zip(sums, terms))

    sums_two = lax.fori_loop(0, chunks, second_norm, (zero,) * 3)
    rows_ref[0] = norm_ref[...].T
    rows_ref[1] = gl_ref[...].T
    put(rows_ref.at[pl.ds(0, 2)], rows_hbm.at[pl.ds(0, 2)])
    for k, side in ((1, send_ref), (0, keep_ref)):

        def down(x, carry, k=k, side=side):
            r = 2 * x + k
            for j in range(0, hidden, part):
                grad = nn(gl_ref[...], weights(r, hidden + j, hidden + j + part))
                grad = (grad * slope_ref[r, :, j : j + part]).astype(low)
                side[x, :, j : j + part] = grad
                stat_ref[8 + r, 0:1, j : j + part] = jnp.sum(grad.astype(high), axis=0, keepdims=True)
            acc_ref[...] += nt(side[x, :, :hidden], weights(r, 0, hidden))
            return carry

        lax.fori_loop(0, 2, down, 0)
        put(side, send_hbm if k else keep_hbm)

    def first_back(i, sums):
        span = pl.ds(pl.multiple_of(i * step, step), step)
        grad = acc_ref[span, :]
        hat = hat_ref[span, :]
        one = norm_back(grad, hat, inv_ref[span, :], gain_one)
        one_ref[span, :] = one
        one_low = one.astype(low)
        gl_ref[span, :] = one_low
        terms = (one_low.astype(high), grad * hat, grad)
        return tuple(s + jnp.sum(v, axis=0, keepdims=True) for s, v in zip(sums, terms))

    sums_one = lax.fori_loop(0, chunks, first_back, (zero,) * 3)
    for i, value in enumerate(sums_one + sums_two):
        stat_ref[i, 0:1, :] = value
    rows_ref[2] = gl_ref[...].T
    put(rows_ref.at[2], rows_hbm.at[2])
    for r, ga in enumerate((ga_0, ga_1, ga_2, ga_3)):
        ga[...] = nn(gl_ref[...], weights(r, 2 * hidden, 2 * hidden + local)).astype(low)
    for copy in puts:
        copy.wait()


def feed(here, x, grad, att, vectors, pieces, plan, tokens, hidden, local):
    width = x.shape[1]
    wide = 2 * hidden + local
    padded = (wide + 127) // 128 * 128
    copies = 6 + len(plan) + sum(mark is not None for _, _, _, mark in plan)
    return pl.pallas_call(
        lambda *refs: feed_kernel(*refs, plan=plan, count=len(pieces), hidden=hidden, local=local),
        name="feed",
        out_shape=(
            shape(tokens, width),
            shape(tokens, width, kind=high),
            shape(12, 1, width, kind=high),
            shape(tokens, local),
            shape(tokens, local),
            shape(tokens, local),
            shape(tokens, local),
            shape(3, width, tokens),
            shape(2, tokens, padded),
            shape(2, tokens, padded),
        ),
        in_specs=[SMEM] + [ANY] * 6 + [VMEM] + [ANY] * len(pieces),
        out_specs=(VMEM,) * 7 + (HBM,) * 3,
        scratch_shapes=[
            pltpu.VMEM((4, width, wide), low),
            pltpu.VMEM((4, 8, wide), low),
            pltpu.VMEM((tokens, width), low),
            pltpu.VMEM((tokens, width), low),
            pltpu.VMEM((4, tokens, local), low),
            pltpu.VMEM((tokens, width), high),
            pltpu.VMEM((tokens, 1), high),
            pltpu.VMEM((tokens, width), low),
            pltpu.VMEM((tokens, width), high),
            pltpu.VMEM((4, tokens, hidden), high),
            pltpu.VMEM((tokens, width), low),
            pltpu.VMEM((3, width, tokens), low),
            pltpu.VMEM((2, tokens, padded), low),
            pltpu.VMEM((2, tokens, padded), low),
            pltpu.SemaphoreType.DMA((copies,)),
            pltpu.SemaphoreType.DMA((4,)),
        ],
        cost_estimate=cost(FEED_COST, 24 << 20),
    )(here, x, grad, *att, vectors, *pieces)


def unit_kernel(here, rows_own, rows_mate, wide_own, wide_mate, *refs, hidden):
    ak_ref, as_ref, bk_ref, bs_ref, rows_ref, wide_ref, sems = refs
    c = here[2]
    tokens = rows_own.shape[2]
    wide = ak_ref.shape[2]
    half = ak_ref.shape[1]
    mid = rows_own.shape[1] // 2
    copies = [
        pltpu.make_async_copy(rows_own, rows_ref.at[:, :, pl.ds(0, tokens)], sems.at[0]),
        pltpu.make_async_copy(wide_own, wide_ref.at[:, pl.ds(0, tokens)], sems.at[1]),
        pltpu.make_async_copy(rows_mate, rows_ref.at[:, :, pl.ds(tokens, tokens)], sems.at[2]),
        pltpu.make_async_copy(wide_mate, wide_ref.at[:, pl.ds(tokens, tokens)], sems.at[3]),
    ]
    for copy in copies:
        copy.start()
    for copy in copies:
        copy.wait()
    spans = ((0, 0, hidden), (1, hidden, 2 * hidden), (2, 2 * hidden, wide))
    for i, first, last in spans:
        for x, side in enumerate((ak_ref, as_ref)):
            got = nn(rows_ref[i, :mid, :], wide_ref[x, :, first:last]).astype(low)
            side[:, :, first:last] = got.reshape(-1, half, last - first)

        def lower(x, carry, i=i, first=first, last=last):
            got = nn(rows_ref[i, mid:, :], wide_ref[x, :, first:last]).astype(low)
            got = got.reshape(-1, 2, half, last - first)
            for z in range(got.shape[0]):

                @pl.when(c == 0)
                def _():
                    bk_ref[x, z, :, first:last] = got[z, 0]
                    bs_ref[x, z, :, first:last] = got[z, 1]

                @pl.when(c != 0)
                def _():
                    bk_ref[x, z, :, first:last] = got[z, 1]
                    bs_ref[x, z, :, first:last] = got[z, 0]

            return carry

        lax.fori_loop(0, 2, lower, 0)


def unit_grads(here, rows, mate_rows, keep, mate, half, hidden, local):
    wide = 2 * hidden + local
    tokens = rows.shape[2]
    width = rows.shape[1]
    quarters = width // 4 // half
    return pl.pallas_call(
        lambda *refs: unit_kernel(*refs, hidden=hidden),
        name="unit_grads",
        out_shape=(
            shape(2 * quarters, half, wide),
            shape(2 * quarters, half, wide),
            shape(2, quarters, half, wide),
            shape(2, quarters, half, wide),
        ),
        in_specs=[SMEM] + [ANY] * 4,
        out_specs=(VMEM,) * 4,
        scratch_shapes=[
            pltpu.VMEM((3, width, 2 * tokens), low),
            pltpu.VMEM((2, 2 * tokens, keep.shape[2]), low),
            pltpu.SemaphoreType.DMA((4,)),
        ],
        cost_estimate=cost(UNIT_COST, 14 << 20),
    )(here, rows, mate_rows, keep, mate)


def merge_one_kernel(here, ak, ga, bk, gb, a_keep, a_send, b_keep, b_send):
    c = here[2]
    for z in range(2):
        for side in range(2):
            i = 2 * z + side
            got = ak[i] + ga[i]

            @pl.when(c == side)
            def _():
                a_keep[z] = got

            @pl.when(c != side)
            def _():
                a_send[z] = got

    b_keep[...] = bk[0] + gb[0]
    b_send[...] = bk[1] + gb[1]


def merge_one(here, ak, ga, bk, gb):
    out = shape(*bk.shape[1:])
    return pl.pallas_call(
        merge_one_kernel,
        name="merge_one",
        out_shape=(out,) * 4,
        in_specs=[SMEM] + [VMEM] * 4,
        out_specs=(VMEM,) * 4,
        cost_estimate=cost(SMALL_COST, 8 << 20),
    )(here, ak, ga, bk, gb)


def merge_two_kernel(here, *refs, pairs):
    ins, outs, all_ref = refs[: 2 * pairs], refs[2 * pairs : -1], refs[-1]
    f = here[1]
    count = 4 // pairs
    for i in range(pairs):
        all_ref[i * count : (i + 1) * count] = ins[2 * i][...] + ins[2 * i + 1][...]
    for s, out in enumerate(outs):
        out[...] = all_ref[(f + s) % 4]


def merge_two(here, *parts):
    piece = parts[0].shape[1:]
    return pl.pallas_call(
        lambda *refs: merge_two_kernel(*refs, pairs=len(parts) // 2),
        name="merge_two",
        out_shape=(shape(*piece),) * 4,
        in_specs=[SMEM] + [VMEM] * len(parts),
        out_specs=(VMEM,) * 4,
        scratch_shapes=[pltpu.VMEM((4,) + piece, low)],
        cost_estimate=cost(SMALL_COST, 8 << 20),
    )(here, *parts)


def merge_three_kernel(here, own, got_1, got_2, got_3, out, all_ref):
    f = here[1]
    for s, piece in enumerate((own, got_1, got_2, got_3)):
        all_ref[(f - s + 4) % 4] = piece[...]
    total = all_ref[0].astype(high)
    for z in range(1, 4):
        total = total + all_ref[z].astype(high)
    out[...] = total.astype(low)


def merge_three(here, pieces):
    return pl.pallas_call(
        merge_three_kernel,
        name="merge_three",
        out_shape=shape(*pieces[0].shape),
        in_specs=[SMEM] + [VMEM] * 4,
        out_specs=VMEM,
        scratch_shapes=[pltpu.VMEM((4,) + pieces[0].shape, low)],
        cost_estimate=cost(SMALL_COST, 4 << 20),
    )(here, *pieces)


def finish_kernel(here, own, got, d_own, d_got, inner, outer, out, query, key, value, bias, all_ref, d_ref):
    c = here[2]
    hidden = inner.shape[1]
    local = query.shape[1]
    all_ref[c] = own[...]
    all_ref[1 - c] = got[...]
    d_ref[c] = d_own[...]
    d_ref[1 - c] = d_got[...]
    half = own.shape[0]

    def cols(ref, first, last):
        return ref[:, :, first:last].reshape(2 * half, last - first).astype(high)

    inner[...] = cols(all_ref, 0, hidden)
    outer[...] = cols(all_ref, hidden, 2 * hidden)
    out[...] = cols(all_ref, 2 * hidden, 2 * hidden + local).T
    rest = cols(d_ref, 0, 3 * local)
    query[...] = rest[:, :local]
    key[...] = rest[:, local : 2 * local]
    value[...] = rest[:, 2 * local : 3 * local]
    bias[...] = d_own[:16, 3 * local :].astype(high)


def finish(here, own, got, d_own, d_got, hidden, local):
    half, wide = own.shape
    full = d_own.shape[1]
    piece = 2 * half
    return pl.pallas_call(
        finish_kernel,
        name="finish",
        out_shape=(
            shape(piece, hidden, kind=high),
            shape(piece, hidden, kind=high),
            shape(local, piece, kind=high),
            shape(piece, local, kind=high),
            shape(piece, local, kind=high),
            shape(piece, local, kind=high),
            shape(16, full - 3 * local, kind=high),
        ),
        in_specs=[SMEM] + [VMEM] * 4,
        out_specs=(VMEM,) * 7,
        scratch_shapes=[pltpu.VMEM((2, half, wide), low), pltpu.VMEM((2, half, full), low)],
        cost_estimate=cost(SMALL_COST, 4 << 20),
    )(here, own, got, d_own, d_got)


def spread_kernel(here, p_0, p_1, p_2, p_3, out):
    tokens = p_0.shape[0]
    for r, piece in enumerate((p_0, p_1, p_2, p_3)):
        first = pl.multiple_of((here[0] ^ r) * tokens, tokens)
        out[pl.ds(first, tokens), :] = piece[...].astype(out.dtype)


def spread(here, pieces, kind):
    tokens, width = pieces[0].shape
    return pl.pallas_call(
        spread_kernel,
        name="spread",
        out_shape=shape(4 * tokens, width, kind=kind),
        in_specs=[SMEM] + [VMEM] * 4,
        out_specs=VMEM,
        cost_estimate=cost(SMALL_COST, 8 << 20),
    )(here, *pieces)


def project_back_kernel(here, g_ref, edge_ref, x_ref, w_ref, keep, send, d_keep, d_send, all_ref, *, local):
    mine, c = here[0], here[2]
    rows = g_ref.shape[0]
    rim = edge_ref.shape[0]
    tokens = keep.shape[1]
    half = d_keep.shape[1]
    pad = d_keep.shape[2] - 3 * local
    all_ref[...] = g_ref[...]
    edge = pl.ds(pl.multiple_of((1 - c) * (rows - rim), rim), rim)
    all_ref[edge, local:] = (
        g_ref[edge, local:].astype(high) + edge_ref[...].astype(high)
    ).astype(low)
    for k, side in ((1, send), (0, keep)):

        def back(x, carry, k=k, side=side):
            first = pl.multiple_of((mine ^ (2 * x + k)) * tokens, tokens)
            side[x] = nt(all_ref[pl.ds(first, tokens), :], w_ref[...]).astype(low)
            return carry

        lax.fori_loop(0, 2, back, 0)
    sums = jnp.zeros((1, 3 * local), high)
    for i in range(rows // tokens):
        part = all_ref[i * tokens : (i + 1) * tokens, :].astype(high)
        sums = sums + jnp.sum(part, axis=0, keepdims=True)
    row = lax.broadcasted_iota(jnp.int32, (half, pad), 0)
    extra = jnp.zeros((half, pad), high)
    for j in range(3 * local // pad):
        extra = jnp.where(row == j, sums[:, j * pad : (j + 1) * pad], extra)
    extra = extra.astype(low)
    got = tn(x_ref[...], all_ref[...]).astype(low).reshape(-1, 2, half, 3 * local)
    for z in range(got.shape[0]):
        d_keep[z, :, 3 * local :] = extra
        d_send[z, :, 3 * local :] = extra
        for side in range(2):

            @pl.when(c == side)
            def _():
                d_keep[z, :, : 3 * local] = got[z, side]

            @pl.when(c != side)
            def _():
                d_send[z, :, : 3 * local] = got[z, side]


def project_back(here, grads, edge, x, weights, tokens, half):
    rows, width = x.shape
    local = grads.shape[1] // 3
    pad = HEAD_DIM
    return pl.pallas_call(
        lambda *refs: project_back_kernel(*refs, local=local),
        name="project_back",
        out_shape=(
            shape(2, tokens, width),
            shape(2, tokens, width),
            shape(width // half // 2, half, 3 * local + pad),
            shape(width // half // 2, half, 3 * local + pad),
        ),
        in_specs=[SMEM] + [VMEM] * 4,
        out_specs=(VMEM,) * 4,
        scratch_shapes=[pltpu.VMEM(grads.shape, low)],
        cost_estimate=cost(LAST_COST, 8 << 20),
    )(here, grads, edge, x, weights)


def attend_back_kernel(
    here, seg_q, seg_k, g_0, g_1, g_2, g_3, full_near, full_far, q_near, q_far, ka_ref, v_ref, own_ref, rim_ref,
    g_ref, full_ref, q_ref, kt_ref, va_ref, ga_ref, dka_ref, dva_ref, dqa_ref, sems, *, block, width, heads
):
    copies = [
        pltpu.make_async_copy(g, g_ref.at[r], sems.at[r]) for r, g in enumerate((g_0, g_1, g_2, g_3))
    ]
    for i, (q_part, full_part) in enumerate(((q_near, full_near), (q_far, full_far))):
        span = pl.ds(2 * i, 2)
        copies.append(pltpu.make_async_copy(q_part, q_ref.at[:, span], sems.at[4 + 2 * i]))
        copies.append(pltpu.make_async_copy(full_part, full_ref.at[span], sems.at[5 + 2 * i]))
    for copy in copies:
        copy.start()
    keys = v_ref.shape[0]
    rows = own_ref.shape[0]
    local = heads * HEAD_DIM
    scale = 1.0 / math.sqrt(HEAD_DIM)
    mine = here[0]
    for h in range(heads):
        cols = slice(h * HEAD_DIM, (h + 1) * HEAD_DIM)
        kt_ref[h] = ka_ref[h, :, :HEAD_DIM].T
        va_ref[h] = jnp.concatenate([v_ref[:, cols], jnp.ones((keys, HEAD_DIM), low)], axis=1)
    dka_ref[...] = jnp.zeros_like(dka_ref)
    dva_ref[...] = jnp.zeros_like(dva_ref)
    for copy in copies:
        copy.wait()

    def one_part(i, carry):
        first_q = pl.multiple_of((mine ^ i) * block, block)
        for h in range(heads):
            cols = slice(h * HEAD_DIM, (h + 1) * HEAD_DIM)
            grad = g_ref[i, :, cols]
            delta = jnp.sum(grad.astype(high) * full_ref[i, :, cols], axis=1, keepdims=True)
            lane = lax.broadcasted_iota(jnp.int32, (block, HEAD_DIM), 1)
            extra = jnp.zeros((block, HEAD_DIM), high)
            for j, piece in enumerate(three(-delta)):
                extra = jnp.where(lane == j, piece.astype(high), extra)
            ga_ref[h] = jnp.concatenate([grad, extra.astype(low)], axis=1)
        dqa_ref[...] = jnp.zeros_like(dqa_ref)

        def one_block(b, carry):
            first_k = b * width

            @pl.when(meets(seg_q, first_q, block, seg_k, first_k, width))
            def _():
                for h in range(heads):
                    span = pl.ds(first_k, width)
                    asks = q_ref[h, i]
                    probs = jnp.exp(nt(ka_ref[h, span, :], asks))
                    slopes = (probs * nt(va_ref[h, span, :], ga_ref[h])).astype(low)
                    dva_ref[h, span, :] += nn(probs.astype(low), ga_ref[h, :, :HEAD_DIM])
                    dka_ref[h, span, :] += nn(slopes, asks[:, :HEAD_DIM])
                    dqa_ref[h] += nn(kt_ref[h, :, span], slopes)

            return carry

        lax.fori_loop(0, keys // width, one_block, 0)
        own_ref[pl.ds(first_q, block), :local] = jnp.concatenate(
            [(dqa_ref[h] * scale).T for h in range(heads)], axis=1
        ).astype(low)
        return carry

    lax.fori_loop(0, 4, one_part, 0)
    for j, part in enumerate((dka_ref, dva_ref)):
        wide = jnp.concatenate([part[h] for h in range(heads)], axis=1).astype(low)
        own_ref[:, (1 + j) * local : (2 + j) * local] = wide[:rows]
        rim_ref[:, j * local : (j + 1) * local] = wide[rows:]


def attend_back(here, seg_q, seg_k, grads, full_near, full_far, q_near, q_far, keys, values):
    parts = len(grads)
    block, local = grads[0].shape
    rows = parts * block
    count = values.shape[0]
    heads = local // HEAD_DIM
    return pl.pallas_call(
        lambda *refs: attend_back_kernel(*refs, block=block, width=256, heads=heads),
        name="attend_back",
        out_shape=(shape(rows, 3 * local), shape(count - rows, 2 * local)),
        in_specs=[SMEM] * 3 + [ANY] * 8 + [VMEM] * 2,
        out_specs=(VMEM,) * 2,
        scratch_shapes=[
            pltpu.VMEM((parts, block, local), low),
            pltpu.VMEM((parts, block, local), high),
            pltpu.VMEM((heads, parts, block, 2 * HEAD_DIM), low),
            pltpu.VMEM((heads, HEAD_DIM, count), low),
            pltpu.VMEM((heads, count, 2 * HEAD_DIM), low),
            pltpu.VMEM((heads, block, 2 * HEAD_DIM), low),
            pltpu.VMEM((heads, count, HEAD_DIM), high),
            pltpu.VMEM((heads, count, HEAD_DIM), high),
            pltpu.VMEM((heads, HEAD_DIM, block), high),
            pltpu.SemaphoreType.DMA((parts + 4,)),
        ],
        cost_estimate=cost(BACK_COST, 8 << 20),
    )(here, seg_q, seg_k, *grads, full_near, full_far, q_near, q_far, keys, values)


def after(values, gate):
    return lax.optimization_barrier((tuple(values), gate))[0]


def add_many(pieces, plan, value, spots, in_rows):
    offset = 0
    for r, mark in spots:
        mark = None if mark is None else in_rows(mark)
        plan.append((len(pieces), offset, r, mark))
        offset += 8 if mark is None else mark(0, 0)[1]
    pieces.append(value)


def halo_of(value, c, span):
    rows = value.shape[0]
    return take(value, (1 - c) * (rows - span), span)


def shards(
    inputs, segments, w_query, b_query, w_key, w_value, b_value, w_out, b_out, gain_one, shift_one,
    w_inner, b_inner, w_outer, b_outer, gain_two, shift_two, grad_output,
):
    rows, width = inputs.shape
    local = w_query.shape[1]
    hidden = w_inner.shape[1]
    n_f, n_c, n_t = (lax.axis_size(a) for a in ("fsdp", "ctx", "tp"))
    f, c, t = (lax.axis_index(a) for a in ("fsdp", "ctx", "tp"))
    tokens = rows // n_t
    rim = MOST
    quick = n_f == 4 and n_c == 2 and n_t == 4
    piece = width // n_f
    flip = [t ^ r for r in range(n_t)]

    half = piece // 2
    blocks = (2 * n_f, half)
    here = jnp.stack([t, f, c]).astype(jnp.int32)
    bundle_a = jnp.concatenate([w_query, w_key, w_value], axis=1)

    def spot(s, side):
        def mark(f, c):
            return (f - s + n_f) % n_f * 2 + (c if side == 0 else 1 - c), 1

        return mark

    def spot_from(s):
        return lambda f, c: ((f - s + n_f) % n_f * 2, 2)

    def spot_all(f, c):
        return 0, 2 * n_f

    def in_rows(mark):
        def rows_mark(f, c):
            first, count = mark(f, c)
            return (first if isinstance(first, int) else pl.multiple_of(first * half, half)), count * half

        return rows_mark

    seg_own = segments.reshape(rows)
    if quick:
        halves_a = bundle_a.reshape(2, half, -1)
        own_a = lax.dynamic_index_in_dim(halves_a, c, 0)
        gots_a = [shift(own_a, "fsdp", s) for s in range(1, n_f)]
        joined = jnp.concatenate(gots_a, axis=0)
        mates_a = swap(joined, "ctx", 1)
        pieces_a = [halves_a, joined, mates_a]
        marks_a = [[spot_from(0)]]
        marks_a += [[spot(s, side) for s in range(1, n_f)] for side in range(2)]
    else:
        whole_a = lax.all_gather(bundle_a, "fsdp", axis=0, tiled=True)
        pieces_a, marks_a = [whole_a.reshape(blocks + (-1,))], [[spot_all]]

    if n_c == 2:
        sent = halo_of(inputs, c, rim)
        if quick:
            part = rim // 2
            ids = halo_of(seg_own, c, rim).astype(low).reshape(2, part)
            ids = jnp.pad(ids, ((0, 14), (0, width - part)))
            got = swap(jnp.concatenate([take(sent, (t & 1) * part, part), ids], axis=0), "ctx", 1)
            halo_seg = got[part : part + 2, :part].astype(jnp.int32).reshape(rim)
            got = got[:part]
            mate = swap(got, "tp", 1)
            even = (t & 1) == 0
            halo_in = jnp.concatenate([jnp.where(even, got, mate), jnp.where(even, mate, got)], axis=0)
        else:
            halo_in = swap(sent, "ctx", 1)
            halo_seg = swap(halo_of(seg_own, c, rim), "ctx", 1)
    else:
        ahead = [(i, i + 1) for i in range(n_c - 1)]
        behind = [(i + 1, i) for i in range(n_c - 1)]

        def both(value):
            return jnp.concatenate(
                [
                    lax.ppermute(value[rows - rim :], "ctx", ahead),
                    lax.ppermute(value[:rim], "ctx", behind),
                ],
                axis=0,
            )

        halo_in = both(inputs)
        halo_seg = both(seg_own + 1) - 1
        halo_seg = jnp.where(halo_seg < 0, NO_ID, halo_seg)

    bias_row = jnp.pad(b_inner[None], ((0, 7), (0, hidden + local)))
    bundle_f = jnp.concatenate([w_inner, w_outer.T, w_out.T], axis=1)
    own_rows = jnp.concatenate([bundle_f, bias_row], axis=0)
    if quick:
        far_rows = swap(own_rows, "tp", 2)
        own_f = take(bundle_f, c * half, half)
        (own_1,) = after([own_f], joined)
        gots = {s: shift(own_1, "fsdp", s) for s in (1, 3)}
        halo_in, far_rows = lax.optimization_barrier((halo_in, far_rows))
        home_mate = swap(jnp.concatenate([own_rows, far_rows], axis=0), "tp", 1)
        far_f = take(far_rows, (1 - c) * half, half)
        corners = {s: shift(far_f, "fsdp", s) for s in (1, 3)}

    bias = jnp.concatenate([b_query, jnp.zeros_like(b_query), b_value]).astype(high)[None]
    seg_all = jnp.concatenate([seg_own, halo_seg])
    lane = jnp.arange(IDS)
    near_id = seg_all[:, None] == lane
    mask_k = (near_id | ((lane >= LSE_LANE) & (lane < LSE_LANE + 3))).astype(low)
    mask_q = jnp.where(near_id[:rows] | ((lane >= LSE_LANE) & (lane < LSE_LANE + 3)), 0.0, FAR).astype(low)
    att_2, att_3, full_far, q_near, q_far, keys_wide, values, values_t, w_qkv = attend_far(
        here, seg_own, seg_all, inputs, halo_in, bias, mask_q, mask_k, pieces_a, marks_a, blocks, tokens
    )
    w_qkv = w_qkv.reshape(width, 3 * local)

    if quick:
        (own_2,) = after([own_f], att_2)
        gots[2] = shift(own_2, "fsdp", 2)
        (far_2,) = after([far_f], att_2)
        corners[2] = shift(far_2, "fsdp", 2)
        *near, corners[1], corners[3] = after([gots[1], gots[3], corners[1], corners[3]], att_2)
        near = jnp.concatenate(near, axis=0)
        home_mate, q_near = lax.optimization_barrier((home_mate, q_near))
        (q_near,) = after([q_near], (near, corners[1], corners[3]))
    att_0, att_1, full_near, q_near = attend_near(here, seg_own, seg_all, q_near, keys_wide, values_t)
    if quick:
        pieces_f, plan = [], []

        def add(r, value, marks):
            offset = 0
            for mark in marks:
                if mark is None:
                    plan.append((len(pieces_f), offset, r, None))
                    offset += 8
                else:
                    mark = in_rows(mark)
                    plan.append((len(pieces_f), offset, r, mark))
                    offset += mark(0, 0)[1]
            pieces_f.append(value)

        def add_both(r, value, marks):
            add(r, value, marks)
            add(r + 1, swap(value, "tp", 1), marks)

        for r, value in ((0, own_rows), (2, far_rows)):
            add(r, value, [spot_from(0), None])
        add_many(pieces_f, plan, home_mate, ((1, spot_from(0)), (1, None), (3, spot_from(0)), (3, None)), in_rows)
        near_x, near_y = swap(near, "tp", 2), swap(near, "ctx", 1)
        near_mate = swap(near, "tp", 1)
        near_mate, near_x, near_y, *att = lax.optimization_barrier(
            (near_mate, near_x, near_y, att_0, att_1, att_2, att_3)
        )
        att_0, att_1, att_2, att_3 = att
        att = [att_0, swap(att_1, "tp", 1), swap(att_2, "tp", 2), swap(att_3, "tp", 3)]
        (last,) = after([gots[2]], (near_x, near_y, att_0))
        last_x, last_y = swap(last, "tp", 2), swap(last, "ctx", 1)
        for r, value in ((0, near), (1, near_mate)):
            add(r, value, [spot(1, 0), spot(3, 0)])
        late = [corners[1], corners[3], near_x, near_y, last]
        corners[1], corners[3], near_x, near_y, last = after(late, (last_y, att[1]))
        add_both(2, corners[1], [spot(1, 1)])
        add_both(2, corners[3], [spot(3, 1)])
        add_both(2, near_x, [spot(1, 0), spot(3, 0)])
        add_both(0, near_y, [spot(1, 1), spot(3, 1)])
        add_both(0, last, [spot(2, 0)])
        add_both(2, last_x, [spot(2, 0)])
        add_both(0, last_y, [spot(2, 1)])
        (corner,) = after([corners[2]], (last_y, att[1], att[2]))
        add_both(2, corner, [spot(2, 1)])
    else:
        gathered = lax.all_gather(bundle_f, "fsdp", axis=0, tiled=True)
        gathered = jnp.concatenate([gathered, bias_row], axis=0)
        gathered = lax.all_gather(gathered, "tp", axis=0)
        pieces_f = [lax.dynamic_index_in_dim(gathered, i, 0, keepdims=False) for i in flip]
        plan = [(r, 0, r, in_rows(spot_all)) for r in range(n_t)]
        plan += [(r, width, r, None) for r in range(n_t)]

    if not quick:
        att = [att_0, swap(att_1, "tp", 1), swap(att_2, "tp", 2), swap(att_3, "tp", 3)]

    vectors = jnp.stack([b_out, gain_one, shift_one, b_outer, gain_two, shift_two, b_out, b_out])
    output, g_one, stats, ga_0, ga_1, ga_2, ga_3, rows_t, keep, send = feed(
        here, inputs, grad_output, att, vectors, pieces_f, plan, tokens, hidden, local
    )
    g_att = [ga_0, swap(ga_1, "tp", 1), swap(ga_2, "tp", 2), swap(ga_3, "tp", 3)]
    stats = stats[:, 0]

    if quick:
        mate_rows = swap(rows_t, "tp", 1)
        mate = swap(send, "tp", 1)
        near_sums = jnp.concatenate([stats[:6], stats[8:9], stats[10:11]], axis=0)
        away = jnp.concatenate([stats[:6], stats[9:10], stats[11:12]], axis=0)
        (away,) = after([away], mate)
        away = swap(away, "tp", 1)
        keep_a, send_a, keep_b, send_b = unit_grads(here, rows_t, mate_rows, keep, mate, half, hidden, local)
        send_a, send_b, away, *g_att = lax.optimization_barrier((send_a, send_b, away, *g_att))
        got_a = swap(send_a, "tp", 2)
        got_b = swap(send_b, "ctx", 1)
        (away,) = after([away], keep_a)
        pair = near_sums + away
        away = jnp.concatenate([pair[:6], pair[7:8], pair[7:8]], axis=0)
        away = swap(away, "tp", 2)
        *g_att, keep_a, keep_b = lax.optimization_barrier((*g_att, keep_a, keep_b))

        def everyone(value, far_value, kind):
            return spread(here, [value, swap(value, "tp", 1), far_value, swap(far_value, "tp", 1)], kind)

    else:
        ordered = []
        for r in range(n_t):
            wide = (keep, send)[r % 2][r // 2]
            ordered.append(
                jnp.concatenate(
                    [
                        nn(rows_t[0], wide[:, :hidden]),
                        nn(rows_t[1], wide[:, hidden : 2 * hidden]),
                        nn(rows_t[2], wide[:, 2 * hidden : 2 * hidden + local]),
                    ],
                    axis=1,
                )
            )
        stacked = jnp.stack(ordered)
        ordered = jnp.stack([lax.dynamic_index_in_dim(stacked, i, 0, keepdims=False) for i in flip])
        mine = lax.psum_scatter(ordered, "tp", scatter_dimension=0, tiled=False)
        mine = lax.psum(mine, ("fsdp", "ctx"))
        shard_f = take(mine, f * piece, piece)

    g_own, g_rim = attend_back(
        here, seg_own, seg_all, g_att, full_near, full_far, q_near, q_far, keys_wide, values
    )
    if quick:
        got_a, got_b = after([got_a, got_b], g_own)
        (away,) = after([away], g_own)
        pair = pair + away
        (rim_out,) = after([g_rim], (got_a, got_b, pair))
        away = swap(pair, "ctx", 1)
        edge = swap(rim_out, "ctx", 1)
        keep_a, send_a, keep_b, send_b = merge_one(here, keep_a, got_a, keep_b, got_b)
        got_a = swap(send_a, "ctx", 1)
        got_b = swap(send_b, "tp", 2)
        edge, away = after([edge, away], (send_a, send_b))
        pair = pair + away
        pair = pair + swap(pair, "fsdp", 1)
        dx_keep, dx_send, d_keep, d_send = project_back(here, g_own, edge, inputs, w_qkv, tokens, half)
        (dx_send,) = after([dx_send], (got_a, got_b, pair))
        pair = pair + swap(pair, "fsdp", 2)
        dx_got = swap(dx_send, "tp", 1)
        d_got = swap(d_send, "ctx", 1)
        outs = merge_two(here, keep_a, got_a, keep_b, got_b)
        totals = [outs[0]] + [shift(outs[s], "fsdp", s) for s in range(1, n_f)]
        near_dx = dx_keep[0] + dx_got[0]
        far_dx = dx_keep[1] + dx_got[1]
        far_got = swap(far_dx, "tp", 2)
        (d_got,) = after([d_got], outs[0])
        outs = merge_two(here, d_keep, d_got)
        d_totals = [outs[0]] + [shift(outs[s], "fsdp", s) for s in range(1, n_f)]
        (output,) = after([output], d_totals[0])
        output = everyone(output, swap(output, "tp", 2), low)
        total = merge_three(here, totals)
        (far_got,) = after([far_got], (total, d_totals[0], pair))
        mine = (near_dx.astype(high) + far_got.astype(high) + g_one).astype(low)
        (far_mine,) = after([swap(mine, "tp", 2)], d_totals)
        grad_inputs = everyone(mine, far_mine, high)
        got = swap(total, "ctx", 1)
        d_total = merge_three(here, d_totals)
        d_got = swap(d_total, "ctx", 1)
        d_got, grad_inputs, output, pair = lax.optimization_barrier((d_got, grad_inputs, output, pair))
        s_inner, s_outer, s_out, s_query, s_key, s_value, s_bias = finish(
            here, total, got, d_total, d_got, hidden, local
        )
        s_outer = s_outer.T
        s_qkv = s_bias.reshape(-1)[: 3 * local]
        shared, s_b_inner = pair[:6], pair[6]
    else:
        edge_got = []
        if n_c == 2:
            edge_got.append(((1 - c) * (rows - rim), swap(g_rim, "ctx", 1)))
        else:
            edge_got.append((0, lax.ppermute(g_rim[rim:], "ctx", ahead)))
            edge_got.append((rows - rim, lax.ppermute(g_rim[:rim], "ctx", behind)))
        g_all = g_own.astype(high)
        for first, got in edge_got:
            got = jnp.pad(got.astype(high), ((0, 0), (local, 0)))
            g_all = place(g_all, take(g_all, first, rim) + got, first)
        g_all = g_all.astype(low)
        part = nt(g_all, w_qkv).reshape(n_t, tokens, width)
        mine = lax.psum_scatter(part, "tp", scatter_dimension=0, tiled=False)
        grad_inputs = lax.all_gather((mine + g_one).astype(low), "tp", axis=0, tiled=True).astype(high)
        output = lax.all_gather(output, "tp", axis=0, tiled=True)
        shard_a = take(lax.psum(tn(inputs, g_all), ("fsdp", "ctx")), f * piece, piece)
        s_query, s_key, s_value = (shard_a[:, i * local : (i + 1) * local] for i in range(3))
        s_qkv = lax.psum(jnp.sum(g_all.astype(high), axis=0), ("fsdp", "ctx"))
        s_inner, s_outer, s_out = shard_f[:, :hidden], shard_f[:, hidden : 2 * hidden].T, shard_f[:, 2 * hidden :].T
        ordered = jnp.stack([lax.dynamic_index_in_dim(stats[8:], i, 0, keepdims=False) for i in flip])
        s_b_inner = lax.psum(
            lax.psum_scatter(ordered, "tp", scatter_dimension=0, tiled=False), ("fsdp", "ctx")
        )
        shared = lax.psum(stats[:6], ("fsdp", "ctx", "tp"))
    return (
        output,
        grad_inputs,
        s_query,
        s_qkv[:local],
        s_key,
        s_value,
        s_qkv[2 * local :],
        s_out,
        shared[0],
        shared[1],
        shared[2],
        s_inner,
        s_b_inner,
        s_outer,
        shared[3],
        shared[4],
        shared[5],
    )


def solution(mesh):
    rows = P(("fsdp", "ctx"), None)
    down, flat, across = P("fsdp", "tp"), P("tp"), P("tp", "fsdp")
    return jax.shard_map(
        shards,
        mesh=mesh,
        in_specs=(
            rows, P("fsdp", "ctx"), down, flat, down, down, flat, across, P(), P(), P(), down, flat,
            across, P(), P(), P(), rows,
        ),
        out_specs=(
            rows, rows, down, flat, down, down, flat, across, P(), P(), P(), down, flat, across,
            P(), P(), P(),
        ),
        check_vma=False,
    )
```

```python
import math

import jax
import jax.numpy as jnp
from jax import lax
from jax.experimental import pallas as pl
from jax.experimental.pallas import tpu as pltpu
from jax.sharding import PartitionSpec as P

HEAD_DIM = 64
MOST = 512
IDS = 64
NO_ID = 63
LSE_LANE = 60
FAR = -1e30

layer_eps = 1e-12
low = jnp.bfloat16
high = jnp.float32


def nn(left, right):
    return jnp.dot(left, right, preferred_element_type=high)


def nt(left, right):
    return lax.dot_general(left, right, (((1,), (1,)), ((), ())), preferred_element_type=high)


def tn(left, right):
    return lax.dot_general(left, right, (((0,), (0,)), ((), ())), preferred_element_type=high)


def swap(value, axis, bit):
    count = lax.axis_size(axis)
    return lax.ppermute(value, axis, [(i, i ^ bit) for i in range(count)])


def shift(value, axis, step):
    count = lax.axis_size(axis)
    return lax.ppermute(value, axis, [(i, (i + step) % count) for i in range(count)])


def place(whole, part, first):
    return lax.dynamic_update_slice_in_dim(whole, part, first, 0)


def take(whole, first, count):
    return lax.dynamic_slice_in_dim(whole, first, count, 0)


def norm_parts(hidden):
    average = jnp.mean(hidden, axis=-1, keepdims=True)
    centred = hidden - average
    variance = jnp.mean(centred * centred, axis=-1, keepdims=True)
    inverse = lax.rsqrt(variance + layer_eps)
    return centred * inverse, inverse


def norm_back(grad, hat, inverse, gain):
    scaled = grad * gain
    first = jnp.mean(scaled, axis=-1, keepdims=True)
    second = jnp.mean(scaled * hat, axis=-1, keepdims=True)
    return inverse * (scaled - first - hat * second)


def gelu_parts(inner):
    half = 0.5 * (1.0 + lax.erf(inner * 0.7071067811865476))
    slope = half + inner * (jnp.exp(-0.5 * inner * inner) * 0.3989422804014327)
    return inner * half, slope


def three(value):
    first = value.astype(low)
    rest = value - first.astype(high)
    second = rest.astype(low)
    third = (rest - second.astype(high)).astype(low)
    return first, second, third


def meets(seg_q, first_q, size_q, seg_k, first_k, size_k):
    return (seg_q[first_q + size_q - 1] >= seg_k[first_k]) & (
        seg_q[first_q] <= seg_k[first_k + size_k - 1]
    )


def score_part(r, q_ref, q_row, first_q, seg_q, seg_k, ka_ref, vt_ref, acc_ref, top_ref, width):
    heads, keys = ka_ref.shape[0], ka_ref.shape[1]
    block = acc_ref.shape[2]
    acc_ref[...] = jnp.zeros_like(acc_ref)
    top_ref[...] = jnp.full_like(top_ref, 2 * FAR)

    def one_block(b, carry):
        first_k = b * width

        @pl.when(meets(seg_q, first_q, block, seg_k, first_k, width))
        def _():
            for h in range(heads):
                scores = nt(ka_ref[h, pl.ds(first_k, width), :], q_ref[h, q_row])
                top = top_ref[h]
                peak = jnp.maximum(top, jnp.max(scores, axis=0, keepdims=True))
                weights = jnp.exp(scores - peak).astype(low)
                acc_ref[h] = acc_ref[h] * jnp.exp(top - peak) + nn(
                    vt_ref[h, :, pl.ds(first_k, width)], weights
                )
                top_ref[h] = peak

        return carry

    lax.fori_loop(0, keys // width, one_block, 0)
    outs = []
    lane = lax.broadcasted_iota(jnp.int32, (block, HEAD_DIM), 1)
    for h in range(heads):
        acc = acc_ref[h]
        total = acc[HEAD_DIM : HEAD_DIM + 1]
        lse = top_ref[h] + jnp.log(total)
        joined = jnp.concatenate(
            [acc[:HEAD_DIM] / total, jnp.broadcast_to(lse, (HEAD_DIM, block))], axis=0
        )
        turned = joined.T
        outs.append(turned[:, :HEAD_DIM])
        minus = three(-turned[:, HEAD_DIM:])
        mask = q_ref[h, q_row, :, HEAD_DIM:].astype(high)
        for i in range(3):
            mask = jnp.where(lane == LSE_LANE + i, minus[i].astype(high), mask)
        q_ref[h, q_row, :, HEAD_DIM:] = mask.astype(low)
    return jnp.concatenate(outs, axis=1)


def attend_far_kernel(*refs, block, width, heads, marks):
    pieces = len(marks)
    here, seg_q, seg_k, x_ref, halo_ref, bias_ref, mq_ref, mk_ref = refs[:8]
    w_refs = refs[8 : 8 + pieces]
    (out_2, out_3, full_ref, q_near, q_far, ka_ref, v_ref, vt_ref, w_ref) = refs[8 + pieces : 17 + pieces]
    acc_ref, top_ref, sems = refs[17 + pieces :]
    keys = v_ref.shape[0]
    rows = x_ref.shape[0]
    local = heads * HEAD_DIM
    scale = 1.0 / math.sqrt(HEAD_DIM)
    mine, f, c = here[0], here[1], here[2]
    copies = []
    for i, spots in enumerate(marks):
        offset = 0
        for mark in spots:
            first, count = mark(f, c)
            src = w_refs[i].at[pl.ds(offset, count)]
            copies.append(
                pltpu.make_async_copy(src, w_ref.at[pl.ds(first, count)], sems.at[len(copies)])
            )
            copies[-1].start()
            offset += count
    vt_ref[:, HEAD_DIM:, :] = jnp.ones((heads, vt_ref.shape[1] - HEAD_DIM, keys), low)
    for copy in copies:
        copy.wait()
    weights_all = w_ref[...].reshape(-1, w_ref.shape[2])

    def keep(first, count, mask, kv):
        span = pl.ds(first, count)
        for h in range(heads):
            cols = slice(h * HEAD_DIM, (h + 1) * HEAD_DIM)
            tail = slice(local + h * HEAD_DIM, local + (h + 1) * HEAD_DIM)
            ka_ref[h, span, :] = jnp.concatenate([kv[:, cols], mask], axis=1)
            vt_ref[h, :HEAD_DIM, span] = kv[:, tail].T
        v_ref[span, :] = kv[:, local:]

    for q_ref, base in ((q_near, 0), (q_far, 2)):

        def project(i, carry, q_ref=q_ref, base=base):
            first = pl.multiple_of((mine ^ (base + i)) * block, block)
            span = pl.ds(first, block)
            both = (nn(x_ref[span, :], weights_all) + bias_ref[...]).astype(low)
            for h in range(heads):
                cols = slice(h * HEAD_DIM, (h + 1) * HEAD_DIM)
                q_ref[h, i] = jnp.concatenate(
                    [both[:, cols] * jnp.array(scale, low), mq_ref[span, :]], axis=1
                )
            keep(first, block, mk_ref[span, :], both[:, local:])
            return carry

        lax.fori_loop(0, 2, project, 0)
    step = min(512, keys - rows)
    for first in range(rows, keys, step):
        span = slice(first - rows, first - rows + step)
        kv = (nn(halo_ref[span, :], weights_all[:, local:]) + bias_ref[:, local:]).astype(low)
        keep(first, step, mk_ref[first : first + step, :], kv)
    for i, out_ref in enumerate((out_2, out_3)):
        joined = score_part(
            2 + i, q_far, i, (mine ^ (2 + i)) * block, seg_q, seg_k, ka_ref, vt_ref, acc_ref, top_ref, width
        )
        full_ref[i] = joined
        out_ref[...] = joined.astype(low)


def attend_near_kernel(
    here, seg_q, seg_k, q_in, ka_ref, vt_ref, out_0, out_1, full_ref, q_ref, acc_ref, top_ref, *, block, width
):
    mine = here[0]
    q_ref[...] = q_in[...]
    for i, out_ref in enumerate((out_0, out_1)):
        joined = score_part(
            i, q_ref, i, (mine ^ i) * block, seg_q, seg_k, ka_ref, vt_ref, acc_ref, top_ref, width
        )
        full_ref[i] = joined
        out_ref[...] = joined.astype(low)


VMEM = pl.BlockSpec(memory_space=pltpu.VMEM)
SMEM = pl.BlockSpec(memory_space=pltpu.SMEM)
ANY = pl.BlockSpec(memory_space=pl.ANY)
HBM = pl.BlockSpec(memory_space=pltpu.HBM)


def shape(*dims, kind=low):
    return jax.ShapeDtypeStruct(dims, kind)


def cost(flops, size, transcendentals=0):
    return pl.CostEstimate(flops=flops, transcendentals=transcendentals, bytes_accessed=size)


def attend_far(here, seg_q, seg_k, x, halo, bias, mask_q, mask_k, pieces, marks, blocks, block):
    rows = x.shape[0]
    local = bias.shape[1] // 3
    count = rows + halo.shape[0]
    heads = local // HEAD_DIM
    wide = 2 * HEAD_DIM
    return pl.pallas_call(
        lambda *refs: attend_far_kernel(*refs, block=block, width=256, heads=heads, marks=marks),
        name="attend_far",
        out_shape=(
            shape(block, local),
            shape(block, local),
            shape(2, block, local, kind=high),
            shape(heads, 2, block, wide),
            shape(heads, 2, block, wide),
            shape(heads, count, wide),
            shape(count, local),
            shape(heads, HEAD_DIM + 16, count),
            shape(*blocks, 3 * local),
        ),
        in_specs=[SMEM] * 3 + [VMEM] * 5 + [ANY] * len(pieces),
        out_specs=(VMEM,) * 9,
        scratch_shapes=[
            pltpu.VMEM((heads, HEAD_DIM + 16, block), high),
            pltpu.VMEM((heads, 1, block), high),
            pltpu.SemaphoreType.DMA((sum(map(len, marks)),)),
        ],
        cost_estimate=cost(FAR_COST, 8 << 20),
    )(here, seg_q, seg_k, x, halo, bias, mask_q, mask_k, *pieces)


def attend_near(here, seg_q, seg_k, q_near, keys_wide, values_t):
    heads, _, block, wide = q_near.shape
    local = heads * HEAD_DIM
    return pl.pallas_call(
        lambda *refs: attend_near_kernel(*refs, block=block, width=256),
        name="attend_near",
        out_shape=(
            shape(block, local),
            shape(block, local),
            shape(2, block, local, kind=high),
            shape(heads, 2, block, wide),
        ),
        in_specs=[SMEM] * 3 + [VMEM] * 3,
        out_specs=(VMEM,) * 4,
        scratch_shapes=[
            pltpu.VMEM((heads, HEAD_DIM + 16, block), high),
            pltpu.VMEM((heads, 1, block), high),
        ],
        cost_estimate=cost(NEAR_COST, 8 << 20),
    )(here, seg_q, seg_k, q_near, keys_wide, values_t)


FAR_COST = 20 * 10**9
NEAR_COST = 12 * 10**9
FEED_COST = 26 * 10**9
UNIT_COST = 12 * 10**9
BACK_COST = 24 * 10**9
LAST_COST = 9 * 10**9
SMALL_COST = 3 * 10**9


def feed_kernel(*refs, plan, count, hidden, local):
    here, x_all, g_all, att_0, att_1, att_2, att_3, vec_ref = refs[:8]
    w_refs = refs[8 : 8 + count]
    (out_ref, one_ref, stat_ref, ga_0, ga_1, ga_2, ga_3, rows_hbm, keep_hbm, send_hbm) = refs[8 + count : 18 + count]
    (w_ref, b_ref, x_ref, g_ref, att_ref, hat_ref, inv_ref, norm_ref, acc_ref, slope_ref, gl_ref,
     rows_ref, keep_ref, send_ref, sems, out_sems) = refs[18 + count :]
    puts = []

    def put(src, dst):
        puts.append(pltpu.make_async_copy(src, dst, out_sems.at[len(puts)]))
        puts[-1].start()

    tokens, width = x_ref.shape
    mine, f, c = here[0], here[1], here[2]
    wide = 2 * hidden + local
    copies = []

    def begin(src, dst):
        copies.append(pltpu.make_async_copy(src, dst, sems.at[len(copies)]))
        copies[-1].start()

    first = pl.multiple_of(mine * tokens, tokens)
    begin(x_all.at[pl.ds(first, tokens)], x_ref)
    begin(g_all.at[pl.ds(first, tokens)], g_ref)
    for r, att in enumerate((att_0, att_1, att_2, att_3)):
        begin(att, att_ref.at[r])
    for i, offset, r, mark in plan:
        if mark is None:
            begin(w_refs[i].at[pl.ds(offset, 8)], b_ref.at[r])
        else:
            start, size = mark(f, c)
            begin(
                w_refs[i].at[pl.ds(offset, size), pl.ds(2 * hidden, local)],
                w_ref.at[r, pl.ds(start, size), pl.ds(2 * hidden, local)],
            )
    first_copies = len(copies)
    for i, offset, r, mark in plan:
        if mark is not None:
            start, size = mark(f, c)
            begin(
                w_refs[i].at[pl.ds(offset, size), pl.ds(0, 2 * hidden)],
                w_ref.at[r, pl.ds(start, size), pl.ds(0, 2 * hidden)],
            )
    for copy in copies[:first_copies]:
        copy.wait()
    b_out, gain_one, shift_one, b_outer, gain_two, shift_two = (
        vec_ref[i : i + 1, :].astype(high) for i in range(6)
    )

    def weights(r, first, last):
        return w_ref[r, :, first:last]

    acc_ref[...] = nt(att_ref[0], weights(0, 2 * hidden, 2 * hidden + local))
    for r in range(1, 4):
        acc_ref[...] += nt(att_ref[r], weights(r, 2 * hidden, 2 * hidden + local))
    step = 64
    chunks = tokens // step

    def first_norm(i, carry):
        span = pl.ds(pl.multiple_of(i * step, step), step)
        hat, inverse = norm_parts(x_ref[span, :].astype(high) + (acc_ref[span, :] + b_out))
        hat_ref[span, :] = hat
        inv_ref[span, :] = inverse
        normed = hat * gain_one + shift_one
        norm_ref[span, :] = normed.astype(low)
        acc_ref[span, :] = normed + b_outer
        return carry

    lax.fori_loop(0, chunks, first_norm, 0)
    for copy in copies[first_copies:]:
        copy.wait()
    part = 256
    for k, side in enumerate((keep_ref, send_ref)):
        for x in range(2):
            side[x, :, 2 * hidden : wide] = att_ref[2 * x + k]
            side[x, :, wide:] = jnp.zeros((tokens, side.shape[2] - wide), low)

        def up(x, carry, k=k, side=side):
            r = 2 * x + k
            for j in range(0, hidden, part):
                inner = nn(norm_ref[...], weights(r, j, j + part))
                inner = inner + b_ref[r, 0:1, j : j + part].astype(high)
                act, slope = gelu_parts(inner)
                side[x, :, hidden + j : hidden + j + part] = act.astype(low)
                slope_ref[r, :, j : j + part] = slope
            acc_ref[...] += nt(side[x, :, hidden : 2 * hidden], weights(r, hidden, 2 * hidden))
            return carry

        lax.fori_loop(0, 2, up, 0)

    zero = jnp.zeros((1, width), high)

    def second_norm(i, sums):
        span = pl.ds(pl.multiple_of(i * step, step), step)
        hat, inverse = norm_parts(acc_ref[span, :])
        out_ref[span, :] = (hat * gain_two + shift_two).astype(low)
        grad = g_ref[span, :].astype(high)
        two = norm_back(grad, hat, inverse, gain_two)
        acc_ref[span, :] = two
        two_low = two.astype(low)
        gl_ref[span, :] = two_low
        terms = (two_low.astype(high), grad * hat, grad)
        return tuple(s + jnp.sum(v, axis=0, keepdims=True) for s, v in zip(sums, terms))

    sums_two = lax.fori_loop(0, chunks, second_norm, (zero,) * 3)
    rows_ref[0] = norm_ref[...].T
    rows_ref[1] = gl_ref[...].T
    put(rows_ref.at[pl.ds(0, 2)], rows_hbm.at[pl.ds(0, 2)])
    for k, side in ((1, send_ref), (0, keep_ref)):

        def down(x, carry, k=k, side=side):
            r = 2 * x + k
            for j in range(0, hidden, part):
                grad = nn(gl_ref[...], weights(r, hidden + j, hidden + j + part))
                grad = (grad * slope_ref[r, :, j : j + part]).astype(low)
                side[x, :, j : j + part] = grad
                stat_ref[8 + r, 0:1, j : j + part] = jnp.sum(grad.astype(high), axis=0, keepdims=True)
            acc_ref[...] += nt(side[x, :, :hidden], weights(r, 0, hidden))
            return carry

        lax.fori_loop(0, 2, down, 0)
        put(side, send_hbm if k else keep_hbm)

    def first_back(i, sums):
        span = pl.ds(pl.multiple_of(i * step, step), step)
        grad = acc_ref[span, :]
        hat = hat_ref[span, :]
        one = norm_back(grad, hat, inv_ref[span, :], gain_one)
        one_ref[span, :] = one
        one_low = one.astype(low)
        gl_ref[span, :] = one_low
        terms = (one_low.astype(high), grad * hat, grad)
        return tuple(s + jnp.sum(v, axis=0, keepdims=True) for s, v in zip(sums, terms))

    sums_one = lax.fori_loop(0, chunks, first_back, (zero,) * 3)
    for i, value in enumerate(sums_one + sums_two):
        stat_ref[i, 0:1, :] = value
    rows_ref[2] = gl_ref[...].T
    put(rows_ref.at[2], rows_hbm.at[2])
    for r, ga in enumerate((ga_0, ga_1, ga_2, ga_3)):
        ga[...] = nn(gl_ref[...], weights(r, 2 * hidden, 2 * hidden + local)).astype(low)
    for copy in puts:
        copy.wait()


def feed(here, x, grad, att, vectors, pieces, plan, tokens, hidden, local):
    width = x.shape[1]
    wide = 2 * hidden + local
    padded = (wide + 127) // 128 * 128
    copies = 6 + len(plan) + sum(mark is not None for _, _, _, mark in plan)
    return pl.pallas_call(
        lambda *refs: feed_kernel(*refs, plan=plan, count=len(pieces), hidden=hidden, local=local),
        name="feed",
        out_shape=(
            shape(tokens, width),
            shape(tokens, width, kind=high),
            shape(12, 1, width, kind=high),
            shape(tokens, local),
            shape(tokens, local),
            shape(tokens, local),
            shape(tokens, local),
            shape(3, width, tokens),
            shape(2, tokens, padded),
            shape(2, tokens, padded),
        ),
        in_specs=[SMEM] + [ANY] * 6 + [VMEM] + [ANY] * len(pieces),
        out_specs=(VMEM,) * 7 + (HBM,) * 3,
        scratch_shapes=[
            pltpu.VMEM((4, width, wide), low),
            pltpu.VMEM((4, 8, wide), low),
            pltpu.VMEM((tokens, width), low),
            pltpu.VMEM((tokens, width), low),
            pltpu.VMEM((4, tokens, local), low),
            pltpu.VMEM((tokens, width), high),
            pltpu.VMEM((tokens, 1), high),
            pltpu.VMEM((tokens, width), low),
            pltpu.VMEM((tokens, width), high),
            pltpu.VMEM((4, tokens, hidden), high),
            pltpu.VMEM((tokens, width), low),
            pltpu.VMEM((3, width, tokens), low),
            pltpu.VMEM((2, tokens, padded), low),
            pltpu.VMEM((2, tokens, padded), low),
            pltpu.SemaphoreType.DMA((copies,)),
            pltpu.SemaphoreType.DMA((4,)),
        ],
        cost_estimate=cost(FEED_COST, 24 << 20),
    )(here, x, grad, *att, vectors, *pieces)


def unit_kernel(here, rows_own, rows_mate, wide_own, wide_mate, *refs, hidden):
    ak_ref, as_ref, bk_ref, bs_ref, rows_ref, wide_ref, sems = refs
    c = here[2]
    tokens = rows_own.shape[2]
    wide = ak_ref.shape[2]
    half = ak_ref.shape[1]
    mid = rows_own.shape[1] // 2
    copies = [
        pltpu.make_async_copy(rows_own, rows_ref.at[:, :, pl.ds(0, tokens)], sems.at[0]),
        pltpu.make_async_copy(wide_own, wide_ref.at[:, pl.ds(0, tokens)], sems.at[1]),
        pltpu.make_async_copy(rows_mate, rows_ref.at[:, :, pl.ds(tokens, tokens)], sems.at[2]),
        pltpu.make_async_copy(wide_mate, wide_ref.at[:, pl.ds(tokens, tokens)], sems.at[3]),
    ]
    for copy in copies:
        copy.start()
    for copy in copies:
        copy.wait()
    spans = ((0, 0, hidden), (1, hidden, 2 * hidden), (2, 2 * hidden, wide))
    for i, first, last in spans:
        for x, side in enumerate((ak_ref, as_ref)):
            got = nn(rows_ref[i, :mid, :], wide_ref[x, :, first:last]).astype(low)
            side[:, :, first:last] = got.reshape(-1, half, last - first)

        def lower(x, carry, i=i, first=first, last=last):
            got = nn(rows_ref[i, mid:, :], wide_ref[x, :, first:last]).astype(low)
            got = got.reshape(-1, 2, half, last - first)
            for z in range(got.shape[0]):

                @pl.when(c == 0)
                def _():
                    bk_ref[x, z, :, first:last] = got[z, 0]
                    bs_ref[x, z, :, first:last] = got[z, 1]

                @pl.when(c != 0)
                def _():
                    bk_ref[x, z, :, first:last] = got[z, 1]
                    bs_ref[x, z, :, first:last] = got[z, 0]

            return carry

        lax.fori_loop(0, 2, lower, 0)


def unit_grads(here, rows, mate_rows, keep, mate, half, hidden, local):
    wide = 2 * hidden + local
    tokens = rows.shape[2]
    width = rows.shape[1]
    quarters = width // 4 // half
    return pl.pallas_call(
        lambda *refs: unit_kernel(*refs, hidden=hidden),
        name="unit_grads",
        out_shape=(
            shape(2 * quarters, half, wide),
            shape(2 * quarters, half, wide),
            shape(2, quarters, half, wide),
            shape(2, quarters, half, wide),
        ),
        in_specs=[SMEM] + [ANY] * 4,
        out_specs=(VMEM,) * 4,
        scratch_shapes=[
            pltpu.VMEM((3, width, 2 * tokens), low),
            pltpu.VMEM((2, 2 * tokens, keep.shape[2]), low),
            pltpu.SemaphoreType.DMA((4,)),
        ],
        cost_estimate=cost(UNIT_COST, 14 << 20),
    )(here, rows, mate_rows, keep, mate)


def merge_one_kernel(here, ak, ga, bk, gb, a_keep, a_send, b_keep, b_send):
    c = here[2]
    for z in range(2):
        for side in range(2):
            i = 2 * z + side
            got = ak[i] + ga[i]

            @pl.when(c == side)
            def _():
                a_keep[z] = got

            @pl.when(c != side)
            def _():
                a_send[z] = got

    b_keep[...] = bk[0] + gb[0]
    b_send[...] = bk[1] + gb[1]


def merge_one(here, ak, ga, bk, gb):
    out = shape(*bk.shape[1:])
    return pl.pallas_call(
        merge_one_kernel,
        name="merge_one",
        out_shape=(out,) * 4,
        in_specs=[SMEM] + [VMEM] * 4,
        out_specs=(VMEM,) * 4,
        cost_estimate=cost(SMALL_COST, 8 << 20),
    )(here, ak, ga, bk, gb)


def merge_two_kernel(here, *refs, pairs):
    ins, outs, all_ref = refs[: 2 * pairs], refs[2 * pairs : -1], refs[-1]
    f = here[1]
    count = 4 // pairs
    for i in range(pairs):
        all_ref[i * count : (i + 1) * count] = ins[2 * i][...] + ins[2 * i + 1][...]
    for s, out in enumerate(outs):
        out[...] = all_ref[(f + s) % 4]


def merge_two(here, *parts):
    piece = parts[0].shape[1:]
    return pl.pallas_call(
        lambda *refs: merge_two_kernel(*refs, pairs=len(parts) // 2),
        name="merge_two",
        out_shape=(shape(*piece),) * 4,
        in_specs=[SMEM] + [VMEM] * len(parts),
        out_specs=(VMEM,) * 4,
        scratch_shapes=[pltpu.VMEM((4,) + piece, low)],
        cost_estimate=cost(SMALL_COST, 8 << 20),
    )(here, *parts)


def merge_three_kernel(here, own, got_1, got_2, got_3, out, all_ref):
    f = here[1]
    for s, piece in enumerate((own, got_1, got_2, got_3)):
        all_ref[(f - s + 4) % 4] = piece[...]
    total = all_ref[0].astype(high)
    for z in range(1, 4):
        total = total + all_ref[z].astype(high)
    out[...] = total.astype(low)


def merge_three(here, pieces):
    return pl.pallas_call(
        merge_three_kernel,
        name="merge_three",
        out_shape=shape(*pieces[0].shape),
        in_specs=[SMEM] + [VMEM] * 4,
        out_specs=VMEM,
        scratch_shapes=[pltpu.VMEM((4,) + pieces[0].shape, low)],
        cost_estimate=cost(SMALL_COST, 4 << 20),
    )(here, *pieces)


def finish_kernel(here, own, got, d_own, d_got, inner, outer, out, query, key, value, bias, all_ref, d_ref):
    c = here[2]
    hidden = inner.shape[1]
    local = query.shape[1]
    all_ref[c] = own[...]
    all_ref[1 - c] = got[...]
    d_ref[c] = d_own[...]
    d_ref[1 - c] = d_got[...]
    half = own.shape[0]

    def cols(ref, first, last):
        return ref[:, :, first:last].reshape(2 * half, last - first).astype(high)

    inner[...] = cols(all_ref, 0, hidden)
    outer[...] = cols(all_ref, hidden, 2 * hidden)
    out[...] = cols(all_ref, 2 * hidden, 2 * hidden + local).T
    rest = cols(d_ref, 0, 3 * local)
    query[...] = rest[:, :local]
    key[...] = rest[:, local : 2 * local]
    value[...] = rest[:, 2 * local : 3 * local]
    bias[...] = d_own[:16, 3 * local :].astype(high)


def finish(here, own, got, d_own, d_got, hidden, local):
    half, wide = own.shape
    full = d_own.shape[1]
    piece = 2 * half
    return pl.pallas_call(
        finish_kernel,
        name="finish",
        out_shape=(
            shape(piece, hidden, kind=high),
            shape(piece, hidden, kind=high),
            shape(local, piece, kind=high),
            shape(piece, local, kind=high),
            shape(piece, local, kind=high),
            shape(piece, local, kind=high),
            shape(16, full - 3 * local, kind=high),
        ),
        in_specs=[SMEM] + [VMEM] * 4,
        out_specs=(VMEM,) * 7,
        scratch_shapes=[pltpu.VMEM((2, half, wide), low), pltpu.VMEM((2, half, full), low)],
        cost_estimate=cost(SMALL_COST, 4 << 20),
    )(here, own, got, d_own, d_got)


def spread_kernel(here, p_0, p_1, p_2, p_3, out):
    tokens = p_0.shape[0]
    for r, piece in enumerate((p_0, p_1, p_2, p_3)):
        first = pl.multiple_of((here[0] ^ r) * tokens, tokens)
        out[pl.ds(first, tokens), :] = piece[...].astype(out.dtype)


def spread(here, pieces, kind):
    tokens, width = pieces[0].shape
    return pl.pallas_call(
        spread_kernel,
        name="spread",
        out_shape=shape(4 * tokens, width, kind=kind),
        in_specs=[SMEM] + [VMEM] * 4,
        out_specs=VMEM,
        cost_estimate=cost(SMALL_COST, 8 << 20),
    )(here, *pieces)


def project_back_kernel(here, g_ref, edge_ref, x_ref, w_ref, keep, send, d_keep, d_send, all_ref, *, local):
    mine, c = here[0], here[2]
    rows = g_ref.shape[0]
    rim = edge_ref.shape[0]
    tokens = keep.shape[1]
    half = d_keep.shape[1]
    pad = d_keep.shape[2] - 3 * local
    all_ref[...] = g_ref[...]
    edge = pl.ds(pl.multiple_of((1 - c) * (rows - rim), rim), rim)
    all_ref[edge, local:] = (
        g_ref[edge, local:].astype(high) + edge_ref[...].astype(high)
    ).astype(low)
    for k, side in ((1, send), (0, keep)):

        def back(x, carry, k=k, side=side):
            first = pl.multiple_of((mine ^ (2 * x + k)) * tokens, tokens)
            side[x] = nt(all_ref[pl.ds(first, tokens), :], w_ref[...]).astype(low)
            return carry

        lax.fori_loop(0, 2, back, 0)
    sums = jnp.zeros((1, 3 * local), high)
    for i in range(rows // tokens):
        part = all_ref[i * tokens : (i + 1) * tokens, :].astype(high)
        sums = sums + jnp.sum(part, axis=0, keepdims=True)
    row = lax.broadcasted_iota(jnp.int32, (half, pad), 0)
    extra = jnp.zeros((half, pad), high)
    for j in range(3 * local // pad):
        extra = jnp.where(row == j, sums[:, j * pad : (j + 1) * pad], extra)
    extra = extra.astype(low)
    got = tn(x_ref[...], all_ref[...]).astype(low).reshape(-1, 2, half, 3 * local)
    for z in range(got.shape[0]):
        d_keep[z, :, 3 * local :] = extra
        d_send[z, :, 3 * local :] = extra
        for side in range(2):

            @pl.when(c == side)
            def _():
                d_keep[z, :, : 3 * local] = got[z, side]

            @pl.when(c != side)
            def _():
                d_send[z, :, : 3 * local] = got[z, side]


def project_back(here, grads, edge, x, weights, tokens, half):
    rows, width = x.shape
    local = grads.shape[1] // 3
    pad = HEAD_DIM
    return pl.pallas_call(
        lambda *refs: project_back_kernel(*refs, local=local),
        name="project_back",
        out_shape=(
            shape(2, tokens, width),
            shape(2, tokens, width),
            shape(width // half // 2, half, 3 * local + pad),
            shape(width // half // 2, half, 3 * local + pad),
        ),
        in_specs=[SMEM] + [VMEM] * 4,
        out_specs=(VMEM,) * 4,
        scratch_shapes=[pltpu.VMEM(grads.shape, low)],
        cost_estimate=cost(LAST_COST, 8 << 20),
    )(here, grads, edge, x, weights)


def attend_back_kernel(
    here, seg_q, seg_k, g_0, g_1, g_2, g_3, full_near, full_far, q_near, q_far, ka_ref, v_ref, own_ref, rim_ref,
    g_ref, full_ref, q_ref, kt_ref, va_ref, ga_ref, dka_ref, dva_ref, dqa_ref, sems, *, block, width, heads
):
    copies = [
        pltpu.make_async_copy(g, g_ref.at[r], sems.at[r]) for r, g in enumerate((g_0, g_1, g_2, g_3))
    ]
    for i, (q_part, full_part) in enumerate(((q_near, full_near), (q_far, full_far))):
        span = pl.ds(2 * i, 2)
        copies.append(pltpu.make_async_copy(q_part, q_ref.at[:, span], sems.at[4 + 2 * i]))
        copies.append(pltpu.make_async_copy(full_part, full_ref.at[span], sems.at[5 + 2 * i]))
    for copy in copies:
        copy.start()
    keys = v_ref.shape[0]
    rows = own_ref.shape[0]
    local = heads * HEAD_DIM
    scale = 1.0 / math.sqrt(HEAD_DIM)
    mine = here[0]
    for h in range(heads):
        cols = slice(h * HEAD_DIM, (h + 1) * HEAD_DIM)
        kt_ref[h] = ka_ref[h, :, :HEAD_DIM].T
        va_ref[h] = jnp.concatenate([v_ref[:, cols], jnp.ones((keys, HEAD_DIM), low)], axis=1)
    dka_ref[...] = jnp.zeros_like(dka_ref)
    dva_ref[...] = jnp.zeros_like(dva_ref)
    for copy in copies:
        copy.wait()

    def one_part(i, carry):
        first_q = pl.multiple_of((mine ^ i) * block, block)
        for h in range(heads):
            cols = slice(h * HEAD_DIM, (h + 1) * HEAD_DIM)
            grad = g_ref[i, :, cols]
            delta = jnp.sum(grad.astype(high) * full_ref[i, :, cols], axis=1, keepdims=True)
            lane = lax.broadcasted_iota(jnp.int32, (block, HEAD_DIM), 1)
            extra = jnp.zeros((block, HEAD_DIM), high)
            for j, piece in enumerate(three(-delta)):
                extra = jnp.where(lane == j, piece.astype(high), extra)
            ga_ref[h] = jnp.concatenate([grad, extra.astype(low)], axis=1)
        dqa_ref[...] = jnp.zeros_like(dqa_ref)

        def one_block(b, carry):
            first_k = b * width

            @pl.when(meets(seg_q, first_q, block, seg_k, first_k, width))
            def _():
                for h in range(heads):
                    span = pl.ds(first_k, width)
                    asks = q_ref[h, i]
                    probs = jnp.exp(nt(ka_ref[h, span, :], asks))
                    slopes = (probs * nt(va_ref[h, span, :], ga_ref[h])).astype(low)
                    dva_ref[h, span, :] += nn(probs.astype(low), ga_ref[h, :, :HEAD_DIM])
                    dka_ref[h, span, :] += nn(slopes, asks[:, :HEAD_DIM])
                    dqa_ref[h] += nn(kt_ref[h, :, span], slopes)

            return carry

        lax.fori_loop(0, keys // width, one_block, 0)
        own_ref[pl.ds(first_q, block), :local] = jnp.concatenate(
            [(dqa_ref[h] * scale).T for h in range(heads)], axis=1
        ).astype(low)
        return carry

    lax.fori_loop(0, 4, one_part, 0)
    for j, part in enumerate((dka_ref, dva_ref)):
        wide = jnp.concatenate([part[h] for h in range(heads)], axis=1).astype(low)
        own_ref[:, (1 + j) * local : (2 + j) * local] = wide[:rows]
        rim_ref[:, j * local : (j + 1) * local] = wide[rows:]


def attend_back(here, seg_q, seg_k, grads, full_near, full_far, q_near, q_far, keys, values):
    parts = len(grads)
    block, local = grads[0].shape
    rows = parts * block
    count = values.shape[0]
    heads = local // HEAD_DIM
    return pl.pallas_call(
        lambda *refs: attend_back_kernel(*refs, block=block, width=256, heads=heads),
        name="attend_back",
        out_shape=(shape(rows, 3 * local), shape(count - rows, 2 * local)),
        in_specs=[SMEM] * 3 + [ANY] * 8 + [VMEM] * 2,
        out_specs=(VMEM,) * 2,
        scratch_shapes=[
            pltpu.VMEM((parts, block, local), low),
            pltpu.VMEM((parts, block, local), high),
            pltpu.VMEM((heads, parts, block, 2 * HEAD_DIM), low),
            pltpu.VMEM((heads, HEAD_DIM, count), low),
            pltpu.VMEM((heads, count, 2 * HEAD_DIM), low),
            pltpu.VMEM((heads, block, 2 * HEAD_DIM), low),
            pltpu.VMEM((heads, count, HEAD_DIM), high),
            pltpu.VMEM((heads, count, HEAD_DIM), high),
            pltpu.VMEM((heads, HEAD_DIM, block), high),
            pltpu.SemaphoreType.DMA((parts + 4,)),
        ],
        cost_estimate=cost(BACK_COST, 8 << 20),
    )(here, seg_q, seg_k, *grads, full_near, full_far, q_near, q_far, keys, values)


def after(values, gate):
    return lax.optimization_barrier((tuple(values), gate))[0]


def add_many(pieces, plan, value, spots, in_rows):
    offset = 0
    for r, mark in spots:
        mark = None if mark is None else in_rows(mark)
        plan.append((len(pieces), offset, r, mark))
        offset += 8 if mark is None else mark(0, 0)[1]
    pieces.append(value)


def halo_of(value, c, span):
    rows = value.shape[0]
    return take(value, (1 - c) * (rows - span), span)


def shards(
    inputs, segments, w_query, b_query, w_key, w_value, b_value, w_out, b_out, gain_one, shift_one,
    w_inner, b_inner, w_outer, b_outer, gain_two, shift_two, grad_output,
):
    rows, width = inputs.shape
    local = w_query.shape[1]
    hidden = w_inner.shape[1]
    n_f, n_c, n_t = (lax.axis_size(a) for a in ("fsdp", "ctx", "tp"))
    f, c, t = (lax.axis_index(a) for a in ("fsdp", "ctx", "tp"))
    tokens = rows // n_t
    rim = MOST
    quick = n_f == 4 and n_c == 2 and n_t == 4
    piece = width // n_f
    flip = [t ^ r for r in range(n_t)]

    half = piece // 2
    blocks = (2 * n_f, half)
    here = jnp.stack([t, f, c]).astype(jnp.int32)
    bundle_a = jnp.concatenate([w_query, w_key, w_value], axis=1)

    def spot(s, side):
        def mark(f, c):
            return (f - s + n_f) % n_f * 2 + (c if side == 0 else 1 - c), 1

        return mark

    def spot_from(s):
        return lambda f, c: ((f - s + n_f) % n_f * 2, 2)

    def spot_all(f, c):
        return 0, 2 * n_f

    def in_rows(mark):
        def rows_mark(f, c):
            first, count = mark(f, c)
            return (first if isinstance(first, int) else pl.multiple_of(first * half, half)), count * half

        return rows_mark

    seg_own = segments.reshape(rows)
    if quick:
        halves_a = bundle_a.reshape(2, half, -1)
        own_a = lax.dynamic_index_in_dim(halves_a, c, 0)
        gots_a = [shift(own_a, "fsdp", s) for s in range(1, n_f)]
        joined = jnp.concatenate(gots_a, axis=0)
        mates_a = swap(joined, "ctx", 1)
        pieces_a = [halves_a, joined, mates_a]
        marks_a = [[spot_from(0)]]
        marks_a += [[spot(s, side) for s in range(1, n_f)] for side in range(2)]
    else:
        whole_a = lax.all_gather(bundle_a, "fsdp", axis=0, tiled=True)
        pieces_a, marks_a = [whole_a.reshape(blocks + (-1,))], [[spot_all]]

    if n_c == 2:
        sent = halo_of(inputs, c, rim)
        if quick:
            part = rim // 2
            ids = halo_of(seg_own, c, rim).astype(low).reshape(2, part)
            ids = jnp.pad(ids, ((0, 14), (0, width - part)))
            got = swap(jnp.concatenate([take(sent, (t & 1) * part, part), ids], axis=0), "ctx", 1)
            halo_seg = got[part : part + 2, :part].astype(jnp.int32).reshape(rim)
            got = got[:part]
            mate = swap(got, "tp", 1)
            even = (t & 1) == 0
            halo_in = jnp.concatenate([jnp.where(even, got, mate), jnp.where(even, mate, got)], axis=0)
        else:
            halo_in = swap(sent, "ctx", 1)
            halo_seg = swap(halo_of(seg_own, c, rim), "ctx", 1)
    else:
        ahead = [(i, i + 1) for i in range(n_c - 1)]
        behind = [(i + 1, i) for i in range(n_c - 1)]

        def both(value):
            return jnp.concatenate(
                [
                    lax.ppermute(value[rows - rim :], "ctx", ahead),
                    lax.ppermute(value[:rim], "ctx", behind),
                ],
                axis=0,
            )

        halo_in = both(inputs)
        halo_seg = both(seg_own + 1) - 1
        halo_seg = jnp.where(halo_seg < 0, NO_ID, halo_seg)

    bias_row = jnp.pad(b_inner[None], ((0, 7), (0, hidden + local)))
    bundle_f = jnp.concatenate([w_inner, w_outer.T, w_out.T], axis=1)
    own_rows = jnp.concatenate([bundle_f, bias_row], axis=0)
    if quick:
        far_rows = swap(own_rows, "tp", 2)
        own_f = take(bundle_f, c * half, half)
        (own_1,) = after([own_f], joined)
        gots = {s: shift(own_1, "fsdp", s) for s in (1, 3)}
        halo_in, far_rows = lax.optimization_barrier((halo_in, far_rows))
        home_mate = swap(jnp.concatenate([own_rows, far_rows], axis=0), "tp", 1)
        far_f = take(far_rows, (1 - c) * half, half)
        corners = {s: shift(far_f, "fsdp", s) for s in (1, 3)}

    bias = jnp.concatenate([b_query, jnp.zeros_like(b_query), b_value]).astype(high)[None]
    seg_all = jnp.concatenate([seg_own, halo_seg])
    lane = jnp.arange(IDS)
    near_id = seg_all[:, None] == lane
    mask_k = (near_id | ((lane >= LSE_LANE) & (lane < LSE_LANE + 3))).astype(low)
    mask_q = jnp.where(near_id[:rows] | ((lane >= LSE_LANE) & (lane < LSE_LANE + 3)), 0.0, FAR).astype(low)
    att_2, att_3, full_far, q_near, q_far, keys_wide, values, values_t, w_qkv = attend_far(
        here, seg_own, seg_all, inputs, halo_in, bias, mask_q, mask_k, pieces_a, marks_a, blocks, tokens
    )
    w_qkv = w_qkv.reshape(width, 3 * local)

    if quick:
        (own_2,) = after([own_f], att_2)
        gots[2] = shift(own_2, "fsdp", 2)
        (far_2,) = after([far_f], att_2)
        corners[2] = shift(far_2, "fsdp", 2)
        *near, corners[1], corners[3] = after([gots[1], gots[3], corners[1], corners[3]], att_2)
        near = jnp.concatenate(near, axis=0)
        home_mate, q_near = lax.optimization_barrier((home_mate, q_near))
        (q_near,) = after([q_near], (near, corners[1], corners[3]))
    att_0, att_1, full_near, q_near = attend_near(here, seg_own, seg_all, q_near, keys_wide, values_t)
    if quick:
        pieces_f, plan = [], []

        def add(r, value, marks):
            offset = 0
            for mark in marks:
                if mark is None:
                    plan.append((len(pieces_f), offset, r, None))
                    offset += 8
                else:
                    mark = in_rows(mark)
                    plan.append((len(pieces_f), offset, r, mark))
                    offset += mark(0, 0)[1]
            pieces_f.append(value)

        def add_both(r, value, marks):
            add(r, value, marks)
            add(r + 1, swap(value, "tp", 1), marks)

        for r, value in ((0, own_rows), (2, far_rows)):
            add(r, value, [spot_from(0), None])
        add_many(pieces_f, plan, home_mate, ((1, spot_from(0)), (1, None), (3, spot_from(0)), (3, None)), in_rows)
        near_x, near_y = swap(near, "tp", 2), swap(near, "ctx", 1)
        near_mate = swap(near, "tp", 1)
        near_mate, near_x, near_y, *att = lax.optimization_barrier(
            (near_mate, near_x, near_y, att_0, att_1, att_2, att_3)
        )
        att_0, att_1, att_2, att_3 = att
        att = [att_0, swap(att_1, "tp", 1), swap(att_2, "tp", 2), swap(att_3, "tp", 3)]
        (last,) = after([gots[2]], (near_x, near_y, att_0))
        last_x, last_y = swap(last, "tp", 2), swap(last, "ctx", 1)
        for r, value in ((0, near), (1, near_mate)):
            add(r, value, [spot(1, 0), spot(3, 0)])
        late = [corners[1], corners[3], near_x, near_y, last]
        corners[1], corners[3], near_x, near_y, last = after(late, (last_y, att[1]))
        add_both(2, corners[1], [spot(1, 1)])
        add_both(2, corners[3], [spot(3, 1)])
        add_both(2, near_x, [spot(1, 0), spot(3, 0)])
        add_both(0, near_y, [spot(1, 1), spot(3, 1)])
        add_both(0, last, [spot(2, 0)])
        add_both(2, last_x, [spot(2, 0)])
        add_both(0, last_y, [spot(2, 1)])
        (corner,) = after([corners[2]], (last_y, att[1], att[2]))
        add_both(2, corner, [spot(2, 1)])
    else:
        gathered = lax.all_gather(bundle_f, "fsdp", axis=0, tiled=True)
        gathered = jnp.concatenate([gathered, bias_row], axis=0)
        gathered = lax.all_gather(gathered, "tp", axis=0)
        pieces_f = [lax.dynamic_index_in_dim(gathered, i, 0, keepdims=False) for i in flip]
        plan = [(r, 0, r, in_rows(spot_all)) for r in range(n_t)]
        plan += [(r, width, r, None) for r in range(n_t)]

    if not quick:
        att = [att_0, swap(att_1, "tp", 1), swap(att_2, "tp", 2), swap(att_3, "tp", 3)]

    vectors = jnp.stack([b_out, gain_one, shift_one, b_outer, gain_two, shift_two, b_out, b_out])
    output, g_one, stats, ga_0, ga_1, ga_2, ga_3, rows_t, keep, send = feed(
        here, inputs, grad_output, att, vectors, pieces_f, plan, tokens, hidden, local
    )
    g_att = [ga_0, swap(ga_1, "tp", 1), swap(ga_2, "tp", 2), swap(ga_3, "tp", 3)]
    stats = stats[:, 0]

    if quick:
        mate_rows = swap(rows_t, "tp", 1)
        mate = swap(send, "tp", 1)
        near_sums = jnp.concatenate([stats[:6], stats[8:9], stats[10:11]], axis=0)
        away = jnp.concatenate([stats[:6], stats[9:10], stats[11:12]], axis=0)
        (away,) = after([away], mate)
        away = swap(away, "tp", 1)
        keep_a, send_a, keep_b, send_b = unit_grads(here, rows_t, mate_rows, keep, mate, half, hidden, local)
        send_a, send_b, away, *g_att = lax.optimization_barrier((send_a, send_b, away, *g_att))
        got_a = swap(send_a, "tp", 2)
        got_b = swap(send_b, "ctx", 1)
        (away,) = after([away], keep_a)
        pair = near_sums + away
        away = jnp.concatenate([pair[:6], pair[7:8], pair[7:8]], axis=0)
        away = swap(away, "tp", 2)
        *g_att, keep_a, keep_b = lax.optimization_barrier((*g_att, keep_a, keep_b))

        def everyone(value, far_value, kind):
            return spread(here, [value, swap(value, "tp", 1), far_value, swap(far_value, "tp", 1)], kind)

    else:
        ordered = []
        for r in range(n_t):
            wide = (keep, send)[r % 2][r // 2]
            ordered.append(
                jnp.concatenate(
                    [
                        nn(rows_t[0], wide[:, :hidden]),
                        nn(rows_t[1], wide[:, hidden : 2 * hidden]),
                        nn(rows_t[2], wide[:, 2 * hidden : 2 * hidden + local]),
                    ],
                    axis=1,
                )
            )
        stacked = jnp.stack(ordered)
        ordered = jnp.stack([lax.dynamic_index_in_dim(stacked, i, 0, keepdims=False) for i in flip])
        mine = lax.psum_scatter(ordered, "tp", scatter_dimension=0, tiled=False)
        mine = lax.psum(mine, ("fsdp", "ctx"))
        shard_f = take(mine, f * piece, piece)

    g_own, g_rim = attend_back(
        here, seg_own, seg_all, g_att, full_near, full_far, q_near, q_far, keys_wide, values
    )
    if quick:
        got_a, got_b = after([got_a, got_b], g_own)
        (away,) = after([away], g_own)
        pair = pair + away
        (rim_out,) = after([g_rim], (got_a, got_b, pair))
        away = swap(pair, "ctx", 1)
        edge = swap(rim_out, "ctx", 1)
        keep_a, send_a, keep_b, send_b = merge_one(here, keep_a, got_a, keep_b, got_b)
        got_a = swap(send_a, "ctx", 1)
        got_b = swap(send_b, "tp", 2)
        edge, away = after([edge, away], (send_a, send_b))
        pair = pair + away
        pair = pair + swap(pair, "fsdp", 1)
        dx_keep, dx_send, d_keep, d_send = project_back(here, g_own, edge, inputs, w_qkv, tokens, half)
        (dx_send,) = after([dx_send], (got_a, got_b, pair))
        pair = pair + swap(pair, "fsdp", 2)
        dx_got = swap(dx_send, "tp", 1)
        d_got = swap(d_send, "ctx", 1)
        outs = merge_two(here, keep_a, got_a, keep_b, got_b)
        totals = [outs[0]] + [shift(outs[s], "fsdp", s) for s in range(1, n_f)]
        near_dx = dx_keep[0] + dx_got[0]
        far_dx = dx_keep[1] + dx_got[1]
        far_got = swap(far_dx, "tp", 2)
        (d_got,) = after([d_got], outs[0])
        outs = merge_two(here, d_keep, d_got)
        d_totals = [outs[0]] + [shift(outs[s], "fsdp", s) for s in range(1, n_f)]
        (output,) = after([output], d_totals[0])
        output = everyone(output, swap(output, "tp", 2), low)
        total = merge_three(here, totals)
        (far_got,) = after([far_got], (total, d_totals[0], pair))
        mine = (near_dx.astype(high) + far_got.astype(high) + g_one).astype(low)
        (far_mine,) = after([swap(mine, "tp", 2)], d_totals)
        grad_inputs = everyone(mine, far_mine, high)
        got = swap(total, "ctx", 1)
        d_totals[1], output = lax.optimization_barrier((d_totals[1], output))
        d_total = merge_three(here, d_totals)
        d_got = swap(d_total, "ctx", 1)
        d_got, grad_inputs, pair = lax.optimization_barrier((d_got, grad_inputs, pair))
        s_inner, s_outer, s_out, s_query, s_key, s_value, s_bias = finish(
            here, total, got, d_total, d_got, hidden, local
        )
        s_outer = s_outer.T
        s_qkv = s_bias.reshape(-1)[: 3 * local]
        shared, s_b_inner = pair[:6], pair[6]
    else:
        edge_got = []
        if n_c == 2:
            edge_got.append(((1 - c) * (rows - rim), swap(g_rim, "ctx", 1)))
        else:
            edge_got.append((0, lax.ppermute(g_rim[rim:], "ctx", ahead)))
            edge_got.append((rows - rim, lax.ppermute(g_rim[:rim], "ctx", behind)))
        g_all = g_own.astype(high)
        for first, got in edge_got:
            got = jnp.pad(got.astype(high), ((0, 0), (local, 0)))
            g_all = place(g_all, take(g_all, first, rim) + got, first)
        g_all = g_all.astype(low)
        part = nt(g_all, w_qkv).reshape(n_t, tokens, width)
        mine = lax.psum_scatter(part, "tp", scatter_dimension=0, tiled=False)
        grad_inputs = lax.all_gather((mine + g_one).astype(low), "tp", axis=0, tiled=True).astype(high)
        output = lax.all_gather(output, "tp", axis=0, tiled=True)
        shard_a = take(lax.psum(tn(inputs, g_all), ("fsdp", "ctx")), f * piece, piece)
        s_query, s_key, s_value = (shard_a[:, i * local : (i + 1) * local] for i in range(3))
        s_qkv = lax.psum(jnp.sum(g_all.astype(high), axis=0), ("fsdp", "ctx"))
        s_inner, s_outer, s_out = shard_f[:, :hidden], shard_f[:, hidden : 2 * hidden].T, shard_f[:, 2 * hidden :].T
        ordered = jnp.stack([lax.dynamic_index_in_dim(stats[8:], i, 0, keepdims=False) for i in flip])
        s_b_inner = lax.psum(
            lax.psum_scatter(ordered, "tp", scatter_dimension=0, tiled=False), ("fsdp", "ctx")
        )
        shared = lax.psum(stats[:6], ("fsdp", "ctx", "tp"))
    return (
        output,
        grad_inputs,
        s_query,
        s_qkv[:local],
        s_key,
        s_value,
        s_qkv[2 * local :],
        s_out,
        shared[0],
        shared[1],
        shared[2],
        s_inner,
        s_b_inner,
        s_outer,
        shared[3],
        shared[4],
        shared[5],
    )


def solution(mesh):
    rows = P(("fsdp", "ctx"), None)
    down, flat, across = P("fsdp", "tp"), P("tp"), P("tp", "fsdp")
    return jax.shard_map(
        shards,
        mesh=mesh,
        in_specs=(
            rows, P("fsdp", "ctx"), down, flat, down, down, flat, across, P(), P(), P(), down, flat,
            across, P(), P(), P(), rows,
        ),
        out_specs=(
            rows, rows, down, flat, down, down, flat, across, P(), P(), P(), down, flat, across,
            P(), P(), P(),
        ),
        check_vma=False,
    )
```
